32 devices in a mesh: dp: 8 (over z, y), fsdp: 4 (over x, core).
Axes of the slice: x: 2, y: 2, z: 4, core: 2. Of those that a mesh axis runs over, the one named last changes fastest.
Arguments:
- tokens: bfloat16 [32768, 512], P(('dp', 'fsdp')), may hold values from -6 to 6
- cotangent: bfloat16 [32768, 512], P(('dp', 'fsdp')), may hold values from -6 to 6
- group_id: int32 [32], P(('dp', 'fsdp')), may hold values from 0 to 3
- w_qkv: bfloat16 [512, 1536], P(('dp', 'fsdp')), may hold values from -0.25 to 0.25
- w_out: bfloat16 [512, 512], P(('dp', 'fsdp')), may hold values from -1 to 1
- w_ffn_in: bfloat16 [512, 2048], P(('dp', 'fsdp')), may hold values from -0.25 to 0.25
- w_ffn_out: bfloat16 [2048, 512], P(('dp', 'fsdp')), may hold values from -0.125 to 0.125
- gain_one: bfloat16 [512], P(('dp', 'fsdp')), may hold values from 0.5 to 1.5
- shift_one: bfloat16 [512], P(('dp', 'fsdp')), may hold values from -1.5 to 1.5
- gain_two: bfloat16 [512], P(('dp', 'fsdp')), may hold values from 0.5 to 1.5
- shift_two: bfloat16 [512], P(('dp', 'fsdp')), may hold values from -1.5 to 1.5
- bias_in: bfloat16 [2048], P(('dp', 'fsdp')), may hold values from -2.5 to 2.5
- bias_out: bfloat16 [512], P(('dp', 'fsdp')), may hold values from -1.5 to 1.5
- feature_matrix: bfloat16 [8, 256, 64], replicated, may hold values from -6 to 6
Outputs:
- activations: bfloat16 [32768, 512], P(('dp', 'fsdp'))
- input_grad: bfloat16 [32768, 512], P(('dp', 'fsdp'))
- grad_w_qkv: float32 [512, 1536], P(('dp', 'fsdp'))
- grad_w_out: float32 [512, 512], P(('dp', 'fsdp'))
- grad_w_ffn_in: float32 [512, 2048], P(('dp', 'fsdp'))
- grad_w_ffn_out: float32 [2048, 512], P(('dp', 'fsdp'))
- grad_gain_one: float32 [512], P(('dp', 'fsdp'))
- grad_shift_one: float32 [512], P(('dp', 'fsdp'))
- grad_gain_two: float32 [512], P(('dp', 'fsdp'))
- grad_shift_two: float32 [512], P(('dp', 'fsdp'))
- grad_bias_in: float32 [2048], P(('dp', 'fsdp'))
- grad_bias_out: float32 [512], P(('dp', 'fsdp'))
The draws below stay inside these ranges and needn't reach their ends.
Inputs may be any that keep to these rules, and one draw needn't show every extreme that they name: `group_id`: group ids are numbered within each batch slice: sequences of different slices never share a group, whatever their ids.
All inputs are finite; a program needn't handle non-finite values.
Results may differ from the reference program's by a relative error of at most 0.019.
The reference program's roundings to bfloat16 on the way count: a program that leaves them out, or rounds other values in their place, can miss the bound.
Values may be sent and summed in bfloat16 or wider, within the bound.
A program may use at most 192 MiB of HBM per device.

```python
import math
import jax
import jax.numpy as jnp
from jax import lax

D = 512
HEADS = 8
DH = 64
FEATS = 256
FF = 2048
LEN = 1024
BLOCK = 512
SEQ_DEV = 1
SEQS = 32
TOKENS = 32768
NGROUP = 4
N_DP = 8
N_FSDP = 4


def place_ends(values, stream_key, smallest, largest):
    longest = values.shape.index(max(values.shape))
    spots = []
    for shift in (0, 1):
        where = [jax.random.randint(jax.random.fold_in(stream_key, axis), (), 0, length) for axis, length in enumerate(values.shape)]
        where[longest] = (where[longest] + shift) % values.shape[longest]
        spots.append(tuple(where))
    return values.at[spots[0]].set(smallest).at[spots[1]].set(largest)


def spiked(entries, own_key, source, target, shards_of, factor):
    owner, partner = [(jnp.arange(entries.shape[position]) // (entries.shape[position] // shards_of)).reshape([-1 if axis == position else 1 for axis in range(entries.ndim)]) for position in (source, target)]
    chosen = jax.random.permutation(own_key, shards_of)[partner]
    strong = (owner == chosen) | (owner == (partner + shards_of // 2) % shards_of)
    return jnp.where(strong, factor * entries, entries)


def steps_of(key, dims, pieces, least, largest):
    factor_of, own = 1.0, jax.random.fold_in(key, 6)
    for position, blocks in pieces:
        steps = jnp.exp(jax.random.uniform(jax.random.fold_in(own, position), (blocks,), jnp.float32, least / len(pieces), largest / len(pieces)))
        factor_of = factor_of * jnp.repeat(steps, dims[position] // blocks).reshape([-1 if axis == position else 1 for axis in range(len(dims))])
    return factor_of


def noise(own_key, extent, width, bound, split=(), kind=jnp.bfloat16):
    values = jax.random.normal(own_key, extent, jnp.float32) * width
    if len(split) > 0:
        values = steps_of(own_key, extent, split, -0.22, 0.18) * values
    return jnp.clip(values, min=-bound, max=bound).astype(kind)


def bell_draw_with(own_key, extent, deviation, bound, pieces, heavy, held_as=jnp.bfloat16):
    values = deviation * jax.random.normal(own_key, extent, jnp.float32)
    if pieces:
        values = values * steps_of(own_key, extent, pieces, -0.22, 0.18)
    return jnp.clip(spiked(values, jax.random.fold_in(own_key, 3), *heavy), -bound, bound).astype(held_as)


def setup_inputs(seed: int = 0) -> dict:
    key_list = jax.random.split(jax.random.key(seed), 15)
    tokens = bell_draw_with(key_list[0], (TOKENS, D), 1.0, 6.0, ((0, 32),), (0, 1, 32, 2.75))
    cotangent = noise(key_list[1], (TOKENS, D), 1.0, 6.0, ((0, 32),))
    group_id = place_ends(jax.random.randint(key_list[2], (SEQS,), 0, NGROUP), jax.random.fold_in(key_list[2], 1), 0, NGROUP - 1).astype(jnp.int32)
    w_qkv = noise(key_list[3], (D, 3 * D), D ** -0.5, 0.25, ((0, 32),))
    w_out = noise(key_list[4], (D, D), (D // 16) ** -0.5, 1.0, ((0, 32),))
    w_ffn_in = noise(key_list[5], (D, FF), D ** -0.5, 0.25, ((0, 32),))
    w_ffn_out = noise(key_list[6], (FF, D), FF ** -0.5, 0.125, ((0, 32),))
    gain_one = jnp.clip(1.0 + 0.1 * jax.random.normal(key_list[7], (D,), jnp.float32), 0.5, 1.5).astype(jnp.bfloat16)
    shift_one = noise(key_list[8], (D,), 0.3, 1.5, ((0, 32),))
    gain_two = jnp.clip(1.0 + 0.1 * jax.random.normal(key_list[9], (D,), jnp.float32), 0.5, 1.5).astype(jnp.bfloat16)
    shift_two = noise(key_list[10], (D,), 0.3, 1.5, ((0, 32),))
    bias_in = noise(key_list[11], (FF,), 0.5, 2.5, ((0, 32),))
    bias_out = noise(key_list[12], (D,), 0.3, 1.5, ((0, 32),))
    feature_matrix = noise(key_list[13], (HEADS, FEATS, DH), 1.0, 6.0)
    return {"tokens": tokens, "cotangent": cotangent, "group_id": group_id, "w_qkv": w_qkv, "w_out": w_out, "w_ffn_in": w_ffn_in, "w_ffn_out": w_ffn_out, "gain_one": gain_one, "shift_one": shift_one, "gain_two": gain_two, "shift_two": shift_two, "bias_in": bias_in, "bias_out": bias_out, "feature_matrix": feature_matrix}


exact_precision = lax.Precision.HIGHEST

@jax.custom_vjp
def low(v):
    return lax.optimization_barrier(v.astype(jnp.bfloat16)).astype(jnp.float32)

@jax.custom_vjp
def lowered_backward(v):
    return v

def low_keep(v):
    return (low(v), None)

def low_pass(kept, grad):
    return (grad,)

def back_keep(v):
    return (v, None)

def back_low(kept, grad):
    return (low(grad),)
low.defvjp(low_keep, low_pass)
lowered_backward.defvjp(back_keep, back_low)

def normed(values, gain_vec, shift_vec):
    average = lax.optimization_barrier(jnp.mean(values, axis=-1, keepdims=True))
    centered = values - average
    spread = lax.optimization_barrier(jnp.mean(centered * centered, axis=-1, keepdims=True))
    return centered * lax.rsqrt(spread + 1e-05) * gain_vec + shift_vec

def features(scaled_values, random_features_matrix):
    output_scores = lowered_backward(jnp.einsum('jfru,riu->jfri', scaled_values, random_features_matrix, precision=exact_precision))
    square = lax.optimization_barrier(jnp.sum(scaled_values * scaled_values, axis=-1, keepdims=True))
    return low(jnp.exp(output_scores - 0.5 * square) / math.sqrt(FEATS))

def attend(query_feat, key_feat, value_rows):
    batch_count = query_feat.shape[0]
    block_count = LEN // BLOCK
    causal = jnp.tril(jnp.ones((BLOCK, BLOCK), jnp.float32))

    def advance(carried, blocks):
        running, summed = carried
        query_block, key_block, value_block = blocks
        scores = lowered_backward(jnp.einsum('pihm,pjhm->phij', query_block, key_block, precision=exact_precision) * causal)
        numerator = jnp.einsum('phij,pjhd->pihd', low(scores), value_block, precision=exact_precision)
        numerator = lowered_backward(numerator + jnp.einsum('pihm,phmd->pihd', query_block, low(running), precision=exact_precision))
        denominator = jnp.transpose(lax.optimization_barrier(jnp.sum(scores, axis=-1)), (0, 2, 1))
        denominator = denominator + jnp.einsum('pihm,phm->pih', query_block, summed, precision=exact_precision)
        attended = numerator / denominator[..., None]
        increment = lowered_backward(jnp.einsum('pjhm,pjhd->phmd', key_block, value_block, precision=exact_precision))
        return ((running + increment, summed + lax.optimization_barrier(jnp.sum(key_block, axis=1))), attended)

    def blocked(array):
        return jnp.moveaxis(array.reshape(batch_count, block_count, BLOCK, HEADS, array.shape[-1]), 1, 0)
    initial = (jnp.zeros((batch_count, HEADS, FEATS, DH), jnp.float32), jnp.zeros((batch_count, HEADS, FEATS), jnp.float32))
    _, attended_all = lax.scan(jax.checkpoint(advance), initial, (blocked(query_feat), blocked(key_feat), blocked(value_rows)))
    return jnp.moveaxis(attended_all, 0, 1).reshape(batch_count, LEN, HEADS * DH)

def layer(row_data, params, random_features_matrix):
    w_qkv, w_out, w_ffn_in, w_ffn_out, gain_one, shift_one, gain_two, shift_two, bias_in, bias_out = params
    batch_count = row_data.shape[0]
    normal_one = low(normed(row_data, gain_one, shift_one))
    projected_features = lowered_backward(jnp.einsum('pld,de->ple', normal_one, w_qkv, precision=exact_precision))
    feature_scale = DH ** (-0.25)
    query_rows = low(projected_features[..., :D] * feature_scale).reshape(batch_count, LEN, HEADS, DH)
    key_rows = low(projected_features[..., D:2 * D] * feature_scale).reshape(batch_count, LEN, HEADS, DH)
    value_rows = low(projected_features[..., 2 * D:]).reshape(batch_count, LEN, HEADS, DH)
    attended = low(attend(features(query_rows, random_features_matrix), features(key_rows, random_features_matrix), value_rows))
    branch = lowered_backward(jnp.einsum('ple,ed->pld', attended, w_out, precision=exact_precision))
    middle = row_data + branch
    normal_two = low(normed(middle, gain_two, shift_two))
    hidden_pre = lowered_backward(jnp.einsum('pld,df->plf', normal_two, w_ffn_in, precision=exact_precision) + bias_in)
    hidden_act = low(jax.nn.gelu(hidden_pre, approximate=False))
    result = middle + lowered_backward(jnp.einsum('plf,fd->pld', hidden_act, w_ffn_out, precision=exact_precision)) + bias_out
    return result

def reference(tokens, cotangent, group_id, w_qkv, w_out, w_ffn_in, w_ffn_out, gain_one, shift_one, gain_two, shift_two, bias_in, bias_out, feature_matrix):
    group_ids = group_id.reshape(N_DP, N_FSDP, SEQ_DEV)
    labels = jnp.arange(NGROUP, dtype=jnp.int32)
    onehot = (group_ids[..., None] == labels).astype(jnp.float32)
    counts = lax.optimization_barrier(jnp.sum(onehot, axis=(0, 2)))
    group_size = lax.optimization_barrier(jnp.sum(onehot * counts[None, :, None, :], axis=-1))
    groups = lax.optimization_barrier(jnp.sum((counts > 0.5).astype(jnp.float32), axis=-1))
    weight = 2.0 * NGROUP / (groups[None, :, None] * group_size)
    weight = weight.reshape(SEQS)
    per_step = math.gcd(SEQS, max(1, 4096 // LEN))
    token_rows = tokens.astype(jnp.float32).reshape(SEQS // per_step, per_step, LEN, D)
    weighted_cot = cotangent.astype(jnp.float32).reshape(SEQS // per_step, per_step, LEN, D)
    weighted_cot = weighted_cot * weight.reshape(SEQS // per_step, per_step, 1, 1)
    params = tuple((item.astype(jnp.float32) for item in (w_qkv, w_out, w_ffn_in, w_ffn_out, gain_one, shift_one, gain_two, shift_two, bias_in, bias_out)))
    random_features_matrix = feature_matrix.astype(jnp.float32)

    def forward(rows_in, weights_in):
        return layer(rows_in, weights_in, random_features_matrix)

    def accumulate(totals, batch_item):
        block_rows, block_cot = batch_item
        layer_out, pullback = jax.vjp(forward, block_rows, params)
        row_grad, gradients = pullback(block_cot)
        return (tuple((first + second for first, second in zip(totals, gradients))), (layer_out, row_grad))
    initial = tuple((jnp.zeros_like(item) for item in params))
    totals, (layer_outs, gradient_inputs) = lax.scan(accumulate, initial, (token_rows, weighted_cot))
    return (layer_outs.reshape(TOKENS, D).astype(jnp.bfloat16), gradient_inputs.reshape(TOKENS, D).astype(jnp.bfloat16), totals[0], totals[1], totals[2], totals[3], totals[4], totals[5], totals[6], totals[7], totals[8], totals[9])
```

```python
import functools
import math

import jax
import jax.numpy as jnp
from jax import lax
from jax.experimental import pallas as pl
from jax.experimental.pallas import tpu as pltpu
from jax.sharding import PartitionSpec as P

BLOCK = 512
EPSILON = 1e-05
TILE = 256
LANES = 128
LOG2E = 1.4426950408889634
AXES = ("dp", "fsdp")
BF = jnp.bfloat16
F32 = jnp.float32


def dot(left, right):
    return lax.dot_general(left, right, (((1,), (0,)), ((), ())), preferred_element_type=F32)


def dot_bt(left, right):
    return lax.dot_general(left, right, (((1,), (1,)), ((), ())), preferred_element_type=F32)


def dot_at(left, right):
    return lax.dot_general(left, right, (((0,), (0,)), ((), ())), preferred_element_type=F32)


def lane_ids(rows, width=LANES):
    return lax.broadcasted_iota(jnp.int32, (rows, width), 1)


def tile_at(index, size=TILE):
    return pl.ds(pl.multiple_of(index * size, size), size)


def centred(values):
    mu = jnp.mean(values, axis=-1, keepdims=True)
    cen = values - mu
    inv = lax.rsqrt(jnp.mean(cen * cen, axis=-1, keepdims=True) + EPSILON)
    return cen * inv, inv


def norm_back(grad, unit, inv, gain):
    e = grad * gain
    return inv * (
        e
        - jnp.mean(e, axis=-1, keepdims=True)
        - unit * jnp.mean(e * unit, axis=-1, keepdims=True)
    )


def causal(values, offset):
    row = lax.broadcasted_iota(jnp.int32, values.shape, 0)
    col = lax.broadcasted_iota(jnp.int32, values.shape, 1)
    return jnp.where(col <= row + offset, values, 0.0).astype(BF)


def anticausal(values):
    row = lax.broadcasted_iota(jnp.int32, values.shape, 0)
    col = lax.broadcasted_iota(jnp.int32, values.shape, 1)
    return jnp.where(col >= row, values, 0.0).astype(BF)


def project_rows(i, x_ref, wq, prm_ref, h_ref, q_ref, k_ref, v_ref, factor):
    rows = tile_at(i)
    unit, _ = centred(x_ref[rows, :].astype(F32))
    h = (unit * prm_ref[0:1, :] + prm_ref[1:2, :]).astype(BF)
    h_ref[rows, :] = h
    width = h.shape[1]
    qkv = dot(h, wq)
    q_ref[rows, :] = (qkv[:, :width] * factor).astype(BF)
    k_ref[rows, :] = (qkv[:, width : 2 * width] * factor).astype(BF)
    v_ref[rows, :] = qkv[:, 2 * width :].astype(BF)


def attend_pair(p, q_ref, k_ref, v_ref, fx_ref, pq_ref, pk_ref, att_ref, attr_ref, den_ref):
    length = q_ref.shape[0]
    feats = fx_ref.shape[1]
    lanes = tile_at(p, LANES)
    shift = 0.5 * math.log2(feats)
    cols = [tile_at(2 * p + hh, feats) for hh in range(2)]
    for hh in range(2):
        fm = fx_ref[2 * p + hh][:, :LANES]
        for src, dst in ((q_ref, pq_ref), (k_ref, pk_ref)):
            for t in range(length // TILE):
                rows = slice(t * TILE, (t + 1) * TILE)
                part = src[rows, lanes]
                scores = dot_bt(part, fm)
                wide = jnp.where(lane_ids(TILE) // 64 == hh, part.astype(F32), 0.0)
                square = jnp.sum(wide * wide, axis=-1, keepdims=True)
                feat = jnp.exp2(scores * LOG2E - (square * (0.5 * LOG2E) + shift))
                dst[rows, cols[hh]] = feat.astype(BF)
    ones = jnp.ones((length, LANES), BF)
    vx = jnp.concatenate([v_ref[:, lanes], ones], axis=1)
    states = [None, None]
    low = [None, None]
    for b in range(length // BLOCK):
        base = b * BLOCK
        for i in range(BLOCK // TILE):
            rows = slice(base + i * TILE, base + (i + 1) * TILE)
            keys = slice(base, base + (i + 1) * TILE)
            got = []
            for hh in range(2):
                pq = pq_ref[rows, cols[hh]]
                weights = causal(dot_bt(pq, pk_ref[keys, cols[hh]]), i * TILE)
                both = dot(weights, vx[keys])
                if b:
                    both = both + dot(pq, low[hh])
                got.append(both)
            first = lane_ids(TILE) < 64
            num = jnp.where(first, got[0][:, :LANES], got[1][:, :LANES])
            den = jnp.where(first, got[0][:, LANES:], got[1][:, LANES:])
            att = num / den
            att_ref[rows, lanes] = att
            attr_ref[rows, lanes] = att.astype(BF)
            den_ref[rows, lanes] = den
        if base + BLOCK < length:
            block = slice(base, base + BLOCK)
            for hh in range(2):
                more = dot_at(pk_ref[block, cols[hh]], vx[block])
                states[hh] = more if b == 0 else states[hh] + more
                low[hh] = states[hh].astype(BF)


def forward_kernel(
    factor, x_ref, wq_ref, prm_ref, fx_ref,
    h_ref, q_ref, k_ref, v_ref, pq_ref, pk_ref, att_ref, attr_ref, den_ref,
):
    def rows(i, carry):
        project_rows(i, x_ref, wq_ref[...], prm_ref, h_ref, q_ref, k_ref, v_ref, factor)
        return carry

    lax.fori_loop(0, x_ref.shape[0] // TILE, rows, 0)

    def pair(p, carry):
        attend_pair(p, q_ref, k_ref, v_ref, fx_ref, pq_ref, pk_ref, att_ref, attr_ref, den_ref)
        return carry

    lax.fori_loop(0, x_ref.shape[1] // LANES, pair, 0)


def middle_kernel(
    x_ref, attr_ref, cot_ref, wo_ref, wi_ref, wf_ref, prm_ref, bin_ref, seq_ref,
    act_ref, dy_ref, datt_ref, gprm_ref, gbin_ref, gf_ref, gi_ref, go_ref,
    hid_ref, du_ref, h_ref, gr_ref, dor_ref,
):
    length, width = x_ref.shape
    hidden = wi_ref.shape[1]
    chunk = 512
    gprm_ref[...] = jnp.zeros_like(gprm_ref)
    gbin_ref[...] = jnp.zeros_like(gbin_ref)

    def rows(t, carry):
        rows = tile_at(t)
        y = x_ref[rows, :].astype(F32) + dot(attr_ref[rows, :], wo_ref[...])
        unit, inv = centred(y)
        gain = prm_ref[2:3, :]
        h = (unit * gain + prm_ref[3:4, :]).astype(BF)
        h_ref[rows, :] = h
        g = cot_ref[rows, :].astype(F32) * seq_ref[0:1, 0:1]
        gr = g.astype(BF)
        gr_ref[rows, :] = gr
        out = y + prm_ref[4:5, :]
        dh = jnp.zeros((TILE, width), F32)
        for c in range(hidden // chunk):
            cs = slice(c * chunk, (c + 1) * chunk)
            wi = wi_ref[:, cs]
            wf = wf_ref[cs, :]
            u = dot(h, wi) + bin_ref[0:1, cs]
            cdf = 0.5 + 0.5 * lax.erf(u * math.sqrt(0.5))
            slope = cdf + u * jnp.exp2(u * u * (-0.5 * LOG2E)) * (1.0 / math.sqrt(2.0 * math.pi))
            hid = (u * cdf).astype(BF)
            hid_ref[rows, cs] = hid
            out = out + dot(hid, wf)
            du = (dot_bt(gr, wf) * slope).astype(BF)
            du_ref[rows, cs] = du
            gbin_ref[0:1, cs] += jnp.sum(du.astype(F32), axis=0, keepdims=True)
            dh = dh + dot_bt(du, wi)
        act_ref[rows, :] = out.astype(BF)
        gprm_ref[2:3, :] += jnp.sum(dh * unit, axis=0, keepdims=True)
        gprm_ref[3:4, :] += jnp.sum(dh, axis=0, keepdims=True)
        gprm_ref[4:5, :] += jnp.sum(g, axis=0, keepdims=True)
        dy = g + norm_back(dh, unit, inv, gain)
        dy_ref[rows, :] = dy
        dor = dy.astype(BF)
        dor_ref[rows, :] = dor
        datt_ref[rows, :] = dot_bt(dor, wo_ref[...])
        return carry

    lax.fori_loop(0, length // TILE, rows, 0)

    def grad_f(c, carry):
        cs = tile_at(c)
        gf_ref[cs, :] = dot_at(hid_ref[:, cs], gr_ref[...]).astype(gf_ref.dtype)
        return carry

    lax.fori_loop(0, hidden // TILE, grad_f, 0)

    def grad_i(c, carry):
        cs = tile_at(c)
        gi_ref[cs, :] = dot_at(h_ref[:, cs], du_ref[...]).astype(gi_ref.dtype)
        go_ref[cs, :] = dot_at(attr_ref[:, cs], dor_ref[...]).astype(go_ref.dtype)
        return carry

    lax.fori_loop(0, width // TILE, grad_i, 0)


def back_pair(
    p, factor, q_ref, k_ref, v_ref, pq_ref, pk_ref, att_ref, den_ref, datt_ref, fx_ref,
    ht_ref, dqkv_ref, gq_ref, dn_ref, acc_ref,
):
    length = q_ref.shape[0]
    feats = fx_ref.shape[1]
    width = q_ref.shape[1]
    lanes = tile_at(p, LANES)
    blocks = length // BLOCK
    cols = [tile_at(2 * p + hh, feats) for hh in range(2)]
    v = v_ref[:, lanes]
    two = jnp.where(lane_ids(length) < 2, 1.0, 0.0).astype(BF)
    vx = jnp.concatenate([v, jnp.ones((length, LANES), BF)], axis=1)
    v2 = jnp.concatenate([v, two], axis=1)
    for t in range(length // TILE):
        rows = slice(t * TILE, (t + 1) * TILE)
        dn = datt_ref[rows, lanes] / den_ref[rows, lanes]
        prod = dn * att_ref[rows, lanes]
        lane = lane_ids(TILE)
        for hh in range(2):
            mine = lane // 64 == hh
            dden = -jnp.sum(jnp.where(mine, prod, 0.0), axis=-1, keepdims=True)
            high = dden.astype(BF).astype(F32)
            extra = jnp.where(lane == 0, high, jnp.where(lane == 1, dden - high, 0.0))
            dn_ref[hh, rows, :LANES] = jnp.where(mine, dn, 0.0).astype(BF)
            dn_ref[hh, rows, LANES:] = extra.astype(BF)
    for hh in range(2):
        mine = lane_ids(TILE) // 64 == hh
        fx = fx_ref[2 * p + hh]
        low = [None] * blocks
        total = None
        for b in range(blocks - 1):
            block = slice(b * BLOCK, (b + 1) * BLOCK)
            more = dot_at(pk_ref[block, cols[hh]], vx[block])
            total = more if total is None else total + more
            low[b + 1] = total.astype(BF)
        back = [None] * blocks
        total = None
        for b in range(blocks - 1, 0, -1):
            block = slice(b * BLOCK, (b + 1) * BLOCK)
            more = dot_at(pq_ref[block, cols[hh]], dn_ref[hh, block, :])
            total = more if total is None else total + more
            dz = total[:, LANES : LANES + 1] + total[:, LANES + 1 : LANES + 2]
            high = dz.astype(BF).astype(F32)
            lane = lane_ids(feats)
            extra = jnp.where(lane == 0, high, jnp.where(lane == 1, dz - high, 0.0))
            back[b - 1] = jnp.concatenate([total[:, :LANES], extra], axis=1).astype(BF)

        def finish(grad, feat, part, where, hh=hh, fx=fx, mine=mine):
            e = (grad * feat.astype(F32)).astype(BF)
            res = dot(e, fx)
            out = (res[:, :LANES] - part.astype(F32) * res[:, LANES:]) * factor
            rows, at = where
            if hh == 0:
                acc_ref[at, rows, :] = out
            else:
                both = jnp.where(mine, out, acc_ref[at, rows, :])
                start = pl.multiple_of(p * LANES + at * width, LANES)
                dqkv_ref[rows, pl.ds(start, LANES)] = both.astype(BF)

        for b in range(blocks):
            base = b * BLOCK
            for i in range(BLOCK // TILE):
                rows = slice(base + i * TILE, base + (i + 1) * TILE)
                keys = slice(base, base + (i + 1) * TILE)
                dn = dn_ref[hh, rows, :]
                da = causal(dot_bt(dn, v2[keys]), i * TILE)
                grad = dot(da, pk_ref[keys, cols[hh]])
                if b:
                    grad = grad + dot_bt(dn, low[b])
                finish(grad, pq_ref[rows, cols[hh]], q_ref[rows, lanes], (rows, 0))
                later = slice(base + i * TILE, base + BLOCK)
                pk = pk_ref[rows, cols[hh]]
                pql = pq_ref[later, cols[hh]]
                dnl = dn_ref[hh, later, :]
                dat = anticausal(dot_bt(v2[rows], dnl))
                grad = dot(dat, pql)
                at = anticausal(dot_bt(pk, pql))
                dv = dot(at, dnl[:, :LANES])
                if b < blocks - 1:
                    grad = grad + dot_bt(v2[rows], back[b])
                    dv = dv + dot(pk, back[b][:, :LANES])
                finish(grad, pk, k_ref[rows, lanes], (rows, 1))
                if hh == 0:
                    acc_ref[2, rows, :] = dv
                else:
                    both = acc_ref[2, rows, :] + dv
                    start = pl.multiple_of(p * LANES + 2 * width, LANES)
                    dqkv_ref[rows, pl.ds(start, LANES)] = both.astype(BF)
    for at in range(3):
        where = pl.ds(pl.multiple_of(p * LANES + at * width, LANES), LANES)
        gq_ref[:, where] = dot(ht_ref[...], dqkv_ref[:, where]).astype(gq_ref.dtype)


def input_rows(t, x_ref, wq, prm_ref, dqkv_ref, dy_ref, out_ref, gprm_ref):
    rows = tile_at(t)
    dh = dot_bt(dqkv_ref[rows, :], wq)
    unit, inv = centred(x_ref[rows, :].astype(F32))
    gprm_ref[0:1, :] += jnp.sum(dh * unit, axis=0, keepdims=True)
    gprm_ref[1:2, :] += jnp.sum(dh, axis=0, keepdims=True)
    out_ref[rows, :] = (dy_ref[rows, :] + norm_back(dh, unit, inv, prm_ref[0:1, :])).astype(BF)


def backward_kernel(
    factor, x_ref, h_ref, q_ref, k_ref, v_ref, pq_ref, pk_ref, att_ref, den_ref, datt_ref, dy_ref,
    wq_ref, fx_ref, prm_ref, gin_ref,
    out_ref, gq_ref, gprm_ref,
    ht_ref, dqkv_ref, dn_ref, acc_ref,
):
    gprm_ref[...] = gin_ref[...]
    for t in range(x_ref.shape[0] // TILE):
        rows = slice(t * TILE, (t + 1) * TILE)
        ht_ref[:, rows] = h_ref[rows, :].T

    def pair(p, carry):
        back_pair(
            p, factor, q_ref, k_ref, v_ref, pq_ref, pk_ref, att_ref, den_ref, datt_ref, fx_ref,
            ht_ref, dqkv_ref, gq_ref, dn_ref, acc_ref,
        )
        return carry

    lax.fori_loop(0, x_ref.shape[1] // LANES, pair, 0)

    def rows(t, carry):
        input_rows(t, x_ref, wq_ref[...], prm_ref, dqkv_ref, dy_ref, out_ref, gprm_ref)
        return carry

    lax.fori_loop(0, x_ref.shape[0] // TILE, rows, 0)


def call(kernel, outs, scratch, name):
    return pl.pallas_call(
        kernel,
        out_shape=[jax.ShapeDtypeStruct(s, d) for s, d in outs],
        scratch_shapes=[pltpu.VMEM(s, d) for s, d in scratch],
        compiler_params=pltpu.CompilerParams(vmem_limit_bytes=60 * 2**20),
        name=name,
    )


def body(
    tokens, cotangent, group_id, w_qkv, w_out, w_ffn_in, w_ffn_out,
    gain_one, shift_one, gain_two, shift_two, bias_in, bias_out, feature_matrix,
):
    gather = functools.partial(lax.all_gather, axis_name=AXES, axis=0, tiled=True)
    scatter = functools.partial(
        lax.psum_scatter, axis_name=AXES, scatter_dimension=0, tiled=True
    )
    length, width = tokens.shape
    heads, feats, head_size = feature_matrix.shape
    hidden = w_ffn_in.shape[1]
    factor = head_size ** (-0.25)
    wq, wo, wi, wf = gather(w_qkv), gather(w_out), gather(w_ffn_in), gather(w_ffn_out)
    prm = gather(jnp.stack([gain_one, shift_one, gain_two, shift_two, bias_out], axis=1))
    prm = jnp.pad(prm.T.astype(F32), ((0, 3), (0, 0)))
    full_bin = gather(bias_in).astype(F32)[None]

    slice_seqs = lax.axis_size("dp") * group_id.shape[0]
    labels = jnp.arange(slice_seqs // 2, dtype=jnp.int32)
    onehot = (group_id[:, None] == labels[None, :]).astype(F32)
    counts = lax.psum(jnp.sum(onehot, axis=0), "dp")
    group_size = jnp.sum(onehot * counts[None, :], axis=-1)
    groups = jnp.sum((counts > 0.5).astype(F32))
    seq_weight = jnp.broadcast_to((slice_seqs / (groups * group_size))[:, None], (1, LANES))

    fm = feature_matrix
    zero = jnp.zeros_like(fm)
    even = (jnp.arange(heads) % 2 == 0)[:, None, None]
    fx = jnp.concatenate(
        [jnp.where(even, fm, zero), jnp.where(even, zero, fm), jnp.ones((heads, feats, LANES), BF)],
        axis=-1,
    )
    big = (length, width)
    h1, q, k, v, pq, pk, att, attr, den = call(
        functools.partial(forward_kernel, factor),
        [(big, BF)] * 4 + [((length, heads * feats), BF)] * 2 + [(big, F32), (big, BF), (big, F32)],
        [],
        "forward",
    )(tokens, wq, prm, fx)
    act, dy, datt, gprm, gbin, gf, gi, go = call(
        middle_kernel,
        [
            (big, BF), (big, F32), (big, F32), ((8, width), F32), ((1, hidden), F32),
            ((hidden, width), BF), ((width, hidden), BF), ((width, width), BF),
        ],
        [((length, hidden), BF), ((length, hidden), BF), (big, BF), (big, BF), (big, BF)],
        "middle",
    )(tokens, attr, cotangent, wo, wi, wf, prm, full_bin, seq_weight)
    input_grad, gq, gprm = call(
        functools.partial(backward_kernel, factor),
        [(big, BF), ((width, 3 * width), BF), ((8, width), F32)],
        [
            ((width, length), BF), ((length, 3 * width), BF),
            ((2, length, 2 * LANES), BF), ((3, length, LANES), F32),
        ],
        "backward",
    )(tokens, h1, q, k, v, pq, pk, att, den, datt, dy, wq, fx, prm, gprm)
    small = scatter(gprm.T)
    part = [scatter(t).astype(F32) for t in (gq, go, gi, gf)]
    return (act, input_grad, *part, *(small[:, i] for i in range(4)), scatter(gbin[0]), small[:, 4])


def solution(mesh):
    rows, vec = P(AXES, None), P(AXES)
    return jax.shard_map(
        body,
        mesh=mesh,
        in_specs=(rows, rows, vec, *[rows] * 4, *[vec] * 6, P()),
        out_specs=(*[rows] * 6, *[vec] * 6),
        check_vma=False,
    )
```

```python
import functools
import math

import jax
import jax.numpy as jnp
from jax import lax
from jax.experimental import pallas as pl
from jax.experimental.pallas import tpu as pltpu
from jax.sharding import PartitionSpec as P

BLOCK = 512
EPSILON = 1e-05
TILE = 256
LANES = 128
LOG2E = 1.4426950408889634
AXES = ("dp", "fsdp")
BF = jnp.bfloat16
F32 = jnp.float32


def dot(left, right):
    return lax.dot_general(left, right, (((1,), (0,)), ((), ())), preferred_element_type=F32)


def dot_bt(left, right):
    return lax.dot_general(left, right, (((1,), (1,)), ((), ())), preferred_element_type=F32)


def dot_at(left, right):
    return lax.dot_general(left, right, (((0,), (0,)), ((), ())), preferred_element_type=F32)


def unit_rows(rows):
    row = lax.broadcasted_iota(jnp.int32, (rows, LANES), 0)
    col = lax.broadcasted_iota(jnp.int32, (rows, LANES), 1)
    return jnp.where(row == col, 1.0, 0.0).astype(BF)


def lane_ids(rows, width=LANES):
    return lax.broadcasted_iota(jnp.int32, (rows, width), 1)


def tile_at(index, size=TILE):
    return pl.ds(pl.multiple_of(index * size, size), size)


def centred(values):
    mu = jnp.mean(values, axis=-1, keepdims=True)
    cen = values - mu
    inv = lax.rsqrt(jnp.mean(cen * cen, axis=-1, keepdims=True) + EPSILON)
    return cen * inv, inv


def norm_back(grad, unit, inv, gain):
    e = grad * gain
    return inv * (
        e
        - jnp.mean(e, axis=-1, keepdims=True)
        - unit * jnp.mean(e * unit, axis=-1, keepdims=True)
    )


def causal(values, offset):
    row = lax.broadcasted_iota(jnp.int32, values.shape, 0)
    col = lax.broadcasted_iota(jnp.int32, values.shape, 1)
    return jnp.where(col <= row + offset, values, 0.0).astype(BF)


def anticausal(values):
    row = lax.broadcasted_iota(jnp.int32, values.shape, 0)
    col = lax.broadcasted_iota(jnp.int32, values.shape, 1)
    return jnp.where(col >= row, values, 0.0).astype(BF)


MESH_ID = pl.DeviceIdType.MESH


class Place:
    def __init__(self, nz):
        dp, fs = lax.axis_index("dp"), lax.axis_index("fsdp")
        self.nz = nz
        self.z, self.y = lax.div(dp, 2), lax.rem(dp, 2)
        self.x, self.c = lax.div(fs, 2), lax.rem(fs, 2)

    def device(self, z=None, y=None, x=None, c=None):
        z, y = self.z if z is None else z, self.y if y is None else y
        x, c = self.x if x is None else x, self.c if c is None else c
        return {"dp": z * 2 + y, "fsdp": x * 2 + c}

    def up(self, k):
        return lax.rem(self.z + k, self.nz)

    def down(self, k):
        return lax.rem(self.z + self.nz - k, self.nz)

    def peers(self):
        yield self.device(c=1 - self.c)
        yield self.device(x=1 - self.x)
        yield self.device(y=1 - self.y)
        for k in range(1, self.nz):
            yield self.device(z=self.up(k))

    def barrier(self):
        sem = pltpu.get_barrier_semaphore()
        for peer in self.peers():
            pl.semaphore_signal(sem, inc=1, device_id=peer, device_id_type=MESH_ID)
        pl.semaphore_wait(sem, 2 + self.nz)


def remote(src, dst, send, recv, peer):
    return pltpu.make_async_remote_copy(
        src_ref=src, dst_ref=dst, send_sem=send, recv_sem=recv, device_id=peer,
        device_id_type=MESH_ID,
    )


class Gather:
    def __init__(self, place, shard, whole, view, sems, m, y_first):
        self.place, self.shard, self.whole, self.view = place, shard, whole, view
        self.send, self.recv, self.own = sems
        self.m = m
        self.y_first = y_first

    def at(self, *index):
        return self.whole.at[(*index, *self.view)]

    def hops(self, stage):
        p = self.place
        every = slice(None)
        if stage == 0:
            src = self.shard.at[self.view]
            for k in range(1, p.nz):
                yield src, self.at(p.z, p.y, p.x, p.c), self.at(p.down(k), p.y, p.x, p.c), p.device(z=p.up(k))
        elif stage == 3:
            mine = self.at(every, every, every, p.c)
            yield mine, mine, self.at(every, every, every, 1 - p.c), p.device(c=1 - p.c)
        elif self.y_first:
            if stage == 1:
                mine = self.at(every, p.y, p.x, p.c)
                yield mine, mine, self.at(every, 1 - p.y, p.x, p.c), p.device(y=1 - p.y)
            else:
                mine = self.at(every, every, p.x, p.c)
                yield mine, mine, self.at(every, every, 1 - p.x, p.c), p.device(x=1 - p.x)
        else:
            if stage == 1:
                mine = self.at(every, p.y, p.x, p.c)
                yield mine, mine, self.at(every, p.y, 1 - p.x, p.c), p.device(x=1 - p.x)
            else:
                mine = self.at(every, p.y, every, p.c)
                yield mine, mine, self.at(every, 1 - p.y, every, p.c), p.device(y=1 - p.y)

    def copies(self, stage, arriving):
        for k, (src, dst, land, peer) in enumerate(self.hops(stage)):
            yield remote(
                src, land if arriving else dst, self.send.at[self.m, stage, k],
                self.recv.at[self.m, stage, k], peer,
            )

    def local(self):
        p = self.place
        return pltpu.make_async_copy(
            self.shard.at[self.view], self.at(p.z, p.y, p.x, p.c), self.own.at[self.m]
        )

    def start(self):
        for copy in self.copies(0, False):
            copy.start()
        self.local().start()

    def arrive(self, stage):
        for copy in self.copies(stage, True):
            copy.wait_recv()

    def step(self, stage):
        self.arrive(stage - 1)
        if stage == 1:
            self.local().wait()
        for copy in self.copies(stage, False):
            copy.start()

    def drain(self):
        for stage in range(4):
            for copy in self.copies(stage, False):
                copy.wait_send()


class Reduce:
    def __init__(self, place, source, bufs, sems, load, write):
        self.place, self.source = place, source
        self.l0, self.r0, self.l1, self.r1, self.l2, self.r2, self.r3 = bufs
        self.send, self.recv, self.own = sems
        self.load, self.write = load, write

    def hops(self, stage, c):
        p = self.place
        every = slice(None)
        if stage == 0:
            yield self.source.at[c, every, every, every, 1 - p.c], self.r0.at[c], self.r0.at[c], p.device(c=1 - p.c)
        elif stage == 1:
            yield self.l0.at[c, every, every, 1 - p.x], self.r1.at[c], self.r1.at[c], p.device(x=1 - p.x)
        elif stage == 2:
            yield self.l1.at[c, every, 1 - p.y], self.r2.at[c], self.r2.at[c], p.device(y=1 - p.y)
        else:
            for k in range(1, p.nz):
                yield self.l2.at[c, p.up(k)], self.r3.at[c, k - 1], self.r3.at[c, k - 1], p.device(z=p.up(k))

    def copies(self, stage, c):
        for k, (src, dst, _, peer) in enumerate(self.hops(stage, c)):
            yield remote(src, dst, self.send.at[c, stage, k], self.recv.at[c, stage, k], peer)

    def local(self, c):
        p = self.place
        every = slice(None)
        return pltpu.make_async_copy(
            self.source.at[c, every, every, every, p.c], self.l0.at[c], self.own.at[c]
        )

    def begin(self, stage, c):
        for copy in self.copies(stage, c):
            copy.start()

    def step(self, stage, c):
        p = self.place
        if stage == 0:
            self.begin(0, c)
            if self.load:
                self.local(c).start()
            return
        for copy in self.copies(stage - 1, c):
            copy.wait_recv()
        if stage == 1:
            if self.load:
                self.local(c).wait()
                mine = self.l0[c]
            else:
                mine = self.source[c, :, :, :, p.c]
            self.l0[c] = (mine.astype(F32) + self.r0[c].astype(F32)).astype(BF)
        elif stage == 2:
            self.l1[c] = (self.l0[c, :, :, p.x].astype(F32) + self.r1[c].astype(F32)).astype(BF)
        elif stage == 3:
            self.l2[c] = (self.l1[c, :, p.y].astype(F32) + self.r2[c].astype(F32)).astype(BF)
        else:
            total = self.l2[c, p.z].astype(F32)
            for k in range(p.nz - 1):
                total = total + self.r3[c, k].astype(F32)
            self.write(c, total)
            return
        self.begin(stage, c)

    def drain(self, c):
        for stage in range(4):
            for copy in self.copies(stage, c):
                copy.wait_send()

    @staticmethod
    def shapes(n, nz, rows, cols):
        return [
            ((n, nz, 2, 2, rows, cols), BF), ((n, nz, 2, 2, rows, cols), BF),
            ((n, nz, 2, rows, cols), BF), ((n, nz, 2, rows, cols), BF),
            ((n, nz, rows, cols), BF), ((n, nz, rows, cols), BF), ((n, nz - 1, rows, cols), BF),
        ]


def project_rows(i, x_ref, wq, prm_ref, h_ref, q_ref, k_ref, v_ref, factor):
    rows = tile_at(i)
    unit, _ = centred(x_ref[rows, :].astype(F32))
    h = (unit * prm_ref[0:1, :] + prm_ref[1:2, :]).astype(BF)
    h_ref[rows, :] = h
    width = h.shape[1]
    qkv = dot(h, wq)
    q_ref[rows, :] = (qkv[:, :width] * factor).astype(BF)
    k_ref[rows, :] = (qkv[:, width : 2 * width] * factor).astype(BF)
    v_ref[rows, :] = qkv[:, 2 * width :].astype(BF)


def attend_pair(p, q_ref, k_ref, v_ref, fx_ref, pq_ref, pk_ref, att_ref, attr_ref, den_ref):
    length = q_ref.shape[0]
    feats = fx_ref.shape[1]
    lanes = tile_at(p, LANES)
    shift = 0.5 * math.log2(feats)
    cols = [tile_at(2 * p + hh, feats) for hh in range(2)]
    for hh in range(2):
        fm = fx_ref[2 * p + hh][:, :LANES]
        for src, dst in ((q_ref, pq_ref), (k_ref, pk_ref)):
            for t in range(length // TILE):
                rows = slice(t * TILE, (t + 1) * TILE)
                part = src[rows, lanes]
                scores = dot_bt(part, fm)
                wide = jnp.where(lane_ids(TILE) // 64 == hh, part.astype(F32), 0.0)
                square = jnp.sum(wide * wide, axis=-1, keepdims=True)
                feat = jnp.exp2(scores * LOG2E - (square * (0.5 * LOG2E) + shift))
                dst[rows, cols[hh]] = feat.astype(BF)
    ones = jnp.ones((length, LANES), BF)
    vx = jnp.concatenate([v_ref[:, lanes], ones], axis=1)
    states = [None, None]
    low = [None, None]
    for b in range(length // BLOCK):
        base = b * BLOCK
        for i in range(BLOCK // TILE):
            rows = slice(base + i * TILE, base + (i + 1) * TILE)
            keys = slice(base, base + (i + 1) * TILE)
            got = []
            for hh in range(2):
                pq = pq_ref[rows, cols[hh]]
                weights = causal(dot_bt(pq, pk_ref[keys, cols[hh]]), i * TILE)
                both = dot(weights, vx[keys])
                if b:
                    both = both + dot(pq, low[hh])
                got.append(both)
            first = lane_ids(TILE) < 64
            num = jnp.where(first, got[0][:, :LANES], got[1][:, :LANES])
            den = jnp.where(first, got[0][:, LANES:], got[1][:, LANES:])
            att = num / den
            att_ref[rows, lanes] = att
            attr_ref[rows, lanes] = att.astype(BF)
            den_ref[rows, lanes] = den
        if base + BLOCK < length:
            block = slice(base, base + BLOCK)
            for hh in range(2):
                more = dot_at(pk_ref[block, cols[hh]], vx[block])
                states[hh] = more if b == 0 else states[hh] + more
                low[hh] = states[hh].astype(BF)


def forward_kernel(
    factor, x_ref, wq_ref, prm_ref, fx_ref,
    h_ref, q_ref, k_ref, v_ref, pq_ref, pk_ref, att_ref, attr_ref, den_ref,
):
    def rows(i, carry):
        project_rows(i, x_ref, wq_ref[...], prm_ref, h_ref, q_ref, k_ref, v_ref, factor)
        return carry

    lax.fori_loop(0, x_ref.shape[0] // TILE, rows, 0)

    def pair(p, carry):
        attend_pair(p, q_ref, k_ref, v_ref, fx_ref, pq_ref, pk_ref, att_ref, attr_ref, den_ref)
        return carry

    lax.fori_loop(0, x_ref.shape[1] // LANES, pair, 0)


def middle_kernel(
    x_ref, attr_ref, cot_ref, wo_ref, wi_ref, wf_ref, prm_ref, seq_ref,
    act_ref, dy_ref, datt_ref, gprm_ref, g_ref,
    hid_ref, du_ref, h_ref, gr_ref, dor_ref, bin_ref,
):
    length, width = x_ref.shape
    hidden = wi_ref.shape[1]
    chunk = width
    gprm_ref[...] = jnp.zeros_like(gprm_ref)
    bin_ref[...] = dot_bt(unit_rows(8), wf_ref[:, width:])

    def rows(t, carry):
        rows = tile_at(t)
        y = x_ref[rows, :].astype(F32) + dot(attr_ref[rows, :], wo_ref[...])
        unit, inv = centred(y)
        gain = prm_ref[2:3, :]
        h = (unit * gain + prm_ref[3:4, :]).astype(BF)
        h_ref[rows, :] = h
        g = cot_ref[rows, :].astype(F32) * seq_ref[0:1, 0:1]
        gr = g.astype(BF)
        gr_ref[rows, :] = gr
        out = y + prm_ref[4:5, :]
        dh = jnp.zeros((TILE, width), F32)
        for c in range(hidden // chunk):
            cs = slice(c * chunk, (c + 1) * chunk)
            wi = wi_ref[:, cs]
            wf = wf_ref[cs, :width]
            u = dot(h, wi) + bin_ref[0:1, cs]
            cdf = 0.5 + 0.5 * lax.erf(u * math.sqrt(0.5))
            slope = cdf + u * jnp.exp2(u * u * (-0.5 * LOG2E)) * (1.0 / math.sqrt(2.0 * math.pi))
            hid = (u * cdf).astype(BF)
            hid_ref[rows, cs] = hid
            out = out + dot(hid, wf)
            du = (dot_bt(gr, wf) * slope).astype(BF)
            du_ref[rows, cs] = du
            gprm_ref[5 + c : 6 + c, :] += jnp.sum(du.astype(F32), axis=0, keepdims=True)
            dh = dh + dot_bt(du, wi)
        act_ref[rows, :] = out.astype(BF)
        gprm_ref[2:3, :] += jnp.sum(dh * unit, axis=0, keepdims=True)
        gprm_ref[3:4, :] += jnp.sum(dh, axis=0, keepdims=True)
        gprm_ref[4:5, :] += jnp.sum(g, axis=0, keepdims=True)
        dy = g + norm_back(dh, unit, inv, gain)
        dy_ref[rows, :] = dy
        dor = dy.astype(BF)
        dor_ref[rows, :] = dor
        datt_ref[rows, :] = dot_bt(dor, wo_ref[...])
        return carry

    lax.fori_loop(0, length // TILE, rows, 0)

    def grad_f(c, carry):
        grad = dot_at(hid_ref[:, tile_at(c)], gr_ref[...]).astype(BF)
        grad = grad.reshape(4, 4, 16, width)
        for q in range(4):
            g_ref[q, c] = grad[:, q]
        return carry

    lax.fori_loop(0, hidden // TILE, grad_f, 0)

    def grad_i(c, carry):
        cs = tile_at(c)
        at = pl.ds(c * 4, 4)
        grad = dot_at(h_ref[:, cs], du_ref[...]).astype(BF)
        for k in range(hidden // chunk):
            g_ref[4 + k, at] = grad[:, k * chunk : (k + 1) * chunk].reshape(4, 4, 16, width)
        grad = dot_at(attr_ref[:, cs], dor_ref[...]).astype(BF)
        g_ref[4 + hidden // chunk, at] = grad.reshape(4, 4, 16, width)
        return carry

    lax.fori_loop(0, width // TILE, grad_i, 0)


def back_pair(
    p, factor, q_ref, k_ref, v_ref, pq_ref, pk_ref, att_ref, den_ref, datt_ref, fx_ref,
    ht_ref, dqkv_ref, dn_ref, acc_ref, tick, store,
):
    length = q_ref.shape[0]
    feats = fx_ref.shape[1]
    width = q_ref.shape[1]
    lanes = tile_at(p, LANES)
    blocks = length // BLOCK
    cols = [tile_at(2 * p + hh, feats) for hh in range(2)]
    v = v_ref[:, lanes]
    two = jnp.where(lane_ids(length) < 2, 1.0, 0.0).astype(BF)
    vx = jnp.concatenate([v, jnp.ones((length, LANES), BF)], axis=1)
    v2 = jnp.concatenate([v, two], axis=1)
    for t in range(length // TILE):
        rows = slice(t * TILE, (t + 1) * TILE)
        dn = datt_ref[rows, lanes] / den_ref[rows, lanes]
        prod = dn * att_ref[rows, lanes]
        lane = lane_ids(TILE)
        for hh in range(2):
            mine = lane // 64 == hh
            dden = -jnp.sum(jnp.where(mine, prod, 0.0), axis=-1, keepdims=True)
            high = dden.astype(BF).astype(F32)
            extra = jnp.where(lane == 0, high, jnp.where(lane == 1, dden - high, 0.0))
            dn_ref[hh, rows, :LANES] = jnp.where(mine, dn, 0.0).astype(BF)
            dn_ref[hh, rows, LANES:] = extra.astype(BF)
    for hh in range(2):
        mine = lane_ids(TILE) // 64 == hh
        fx = fx_ref[2 * p + hh]
        low = [None] * blocks
        total = None
        for b in range(blocks - 1):
            block = slice(b * BLOCK, (b + 1) * BLOCK)
            more = dot_at(pk_ref[block, cols[hh]], vx[block])
            total = more if total is None else total + more
            low[b + 1] = total.astype(BF)
        back = [None] * blocks
        total = None
        for b in range(blocks - 1, 0, -1):
            block = slice(b * BLOCK, (b + 1) * BLOCK)
            more = dot_at(pq_ref[block, cols[hh]], dn_ref[hh, block, :])
            total = more if total is None else total + more
            dz = total[:, LANES : LANES + 1] + total[:, LANES + 1 : LANES + 2]
            high = dz.astype(BF).astype(F32)
            lane = lane_ids(feats)
            extra = jnp.where(lane == 0, high, jnp.where(lane == 1, dz - high, 0.0))
            back[b - 1] = jnp.concatenate([total[:, :LANES], extra], axis=1).astype(BF)

        def finish(grad, feat, part, where, hh=hh, fx=fx, mine=mine):
            e = (grad * feat.astype(F32)).astype(BF)
            res = dot(e, fx)
            out = (res[:, :LANES] - part.astype(F32) * res[:, LANES:]) * factor
            rows, at = where
            if hh == 0:
                acc_ref[at, rows, :] = out
            else:
                both = jnp.where(mine, out, acc_ref[at, rows, :])
                start = pl.multiple_of(p * LANES + at * width, LANES)
                dqkv_ref[rows, pl.ds(start, LANES)] = both.astype(BF)

        for b in range(blocks):
            base = b * BLOCK
            for i in range(BLOCK // TILE):
                rows = slice(base + i * TILE, base + (i + 1) * TILE)
                keys = slice(base, base + (i + 1) * TILE)
                dn = dn_ref[hh, rows, :]
                da = causal(dot_bt(dn, v2[keys]), i * TILE)
                grad = dot(da, pk_ref[keys, cols[hh]])
                if b:
                    grad = grad + dot_bt(dn, low[b])
                finish(grad, pq_ref[rows, cols[hh]], q_ref[rows, lanes], (rows, 0))
                later = slice(base + i * TILE, base + BLOCK)
                pk = pk_ref[rows, cols[hh]]
                pql = pq_ref[later, cols[hh]]
                dnl = dn_ref[hh, later, :]
                dat = anticausal(dot_bt(v2[rows], dnl))
                grad = dot(dat, pql)
                at = anticausal(dot_bt(pk, pql))
                dv = dot(at, dnl[:, :LANES])
                if b < blocks - 1:
                    grad = grad + dot_bt(v2[rows], back[b])
                    dv = dv + dot(pk, back[b][:, :LANES])
                finish(grad, pk, k_ref[rows, lanes], (rows, 1))
                if hh == 0:
                    acc_ref[2, rows, :] = dv
                else:
                    both = acc_ref[2, rows, :] + dv
                    start = pl.multiple_of(p * LANES + 2 * width, LANES)
                    dqkv_ref[rows, pl.ds(start, LANES)] = both.astype(BF)
                tick((hh * blocks + b) * (BLOCK // TILE) + i)
    for at in range(3):
        where = pl.ds(pl.multiple_of(p * LANES + at * width, LANES), LANES)
        store(at, where, dot(ht_ref[...], dqkv_ref[:, where]).astype(BF))


def input_rows(t, x_ref, wq, prm_ref, dqkv_ref, dy_ref, out_ref, gprm_ref):
    rows = tile_at(t)
    dh = dot_bt(dqkv_ref[rows, :], wq)
    unit, inv = centred(x_ref[rows, :].astype(F32))
    gprm_ref[0:1, :] += jnp.sum(dh * unit, axis=0, keepdims=True)
    gprm_ref[1:2, :] += jnp.sum(dh, axis=0, keepdims=True)
    out_ref[rows, :] = (dy_ref[rows, :] + norm_back(dh, unit, inv, prm_ref[0:1, :])).astype(BF)


def flip_rows(h_ref, ht_ref):
    for t in range(h_ref.shape[0] // TILE):
        rows = slice(t * TILE, (t + 1) * TILE)
        ht_ref[:, rows] = h_ref[rows, :].T


def backward_kernel(
    factor, x_ref, h_ref, q_ref, k_ref, v_ref, pq_ref, pk_ref, att_ref, den_ref, datt_ref, dy_ref,
    wq_ref, fx_ref, prm_ref, gin_ref,
    out_ref, gq_ref, gprm_ref,
    ht_ref, dqkv_ref, dn_ref, acc_ref,
):
    gprm_ref[...] = gin_ref[...]
    flip_rows(h_ref, ht_ref)

    def store(at, where, value):
        gq_ref[:, where] = value

    def pair(p, carry):
        back_pair(
            p, factor, q_ref, k_ref, v_ref, pq_ref, pk_ref, att_ref, den_ref, datt_ref, fx_ref,
            ht_ref, dqkv_ref, dn_ref, acc_ref, lambda j: None, store,
        )
        return carry

    lax.fori_loop(0, x_ref.shape[1] // LANES, pair, 0)

    def rows(t, carry):
        input_rows(t, x_ref, wq_ref[...], prm_ref, dqkv_ref, dy_ref, out_ref, gprm_ref)
        return carry

    lax.fori_loop(0, x_ref.shape[0] // TILE, rows, 0)


def gather_forward_kernel(
    nz, factor, x_ref, wqs_ref, wos_ref, wis_ref, wfs_ref, fx_ref,
    h_ref, q_ref, k_ref, v_ref, pq_ref, pk_ref, att_ref, attr_ref, den_ref, prm_ref, seq_ref,
    wq_ref, wo_ref, wi_ref, wf_ref,
    send, recv, own,
):
    length, width = x_ref.shape
    place = Place(nz)
    every = slice(None)
    sems = (send, recv, own)
    cut = width * 3 // 2
    half = wis_ref.shape[1] // 2
    low, high = slice(0, 32), slice(32, 64)
    q0 = Gather(place, wqs_ref, wq_ref, (every, slice(0, cut)), sems, 0, True)
    q1 = Gather(place, wqs_ref, wq_ref, (every, slice(cut, wqs_ref.shape[1])), sems, 1, False)
    o = Gather(place, wos_ref, wo_ref, (every, every), sems, 2, True)
    i0 = Gather(place, wis_ref, wi_ref, (every, slice(0, half)), sems, 3, True)
    i1 = Gather(place, wis_ref, wi_ref, (every, slice(half, 2 * half)), sems, 4, False)
    f0 = Gather(place, wfs_ref, wf_ref, (low, every), sems, 5, True)
    f1 = Gather(place, wfs_ref, wf_ref, (high, every), sems, 6, False)
    first, rest = (q0, q1), (o, i0, i1, f0, f1)
    place.barrier()
    for g in (*first, *rest):
        g.start()
    for stage in (1, 2, 3):
        for g in first:
            g.step(stage)
    for g in rest:
        g.step(1)
    for g in first:
        g.arrive(3)

    wqx = wq_ref[...].reshape(width, wqs_ref.shape[1])
    small = wqx[:, 3 * width :]
    prm_ref[...] = dot_bt(unit_rows(8), small)
    nf = 4
    me = lax.axis_index("dp") * nf + lax.axis_index("fsdp")
    row = lax.broadcasted_iota(jnp.int32, small.shape, 0)
    lane = lane_ids(width).astype(F32)
    peer = lax.div(row, 16)
    ids = small[:, 5:6].astype(F32)
    hit = (lane == ids) & (lax.rem(row, 16) == 0)
    counts = jnp.sum(
        jnp.where(hit & (lax.rem(peer, nf) == lax.axis_index("fsdp")), 1.0, 0.0),
        axis=0, keepdims=True,
    )
    mine = jnp.sum(jnp.where(hit & (peer == me), 1.0, 0.0), axis=0, keepdims=True)
    size = jnp.sum(counts * mine, axis=1, keepdims=True)
    groups = jnp.sum(jnp.where(counts > 0.5, 1.0, 0.0), axis=1, keepdims=True)
    members = lax.axis_size("dp")
    seq_ref[...] = jnp.broadcast_to(members / (groups * size), seq_ref.shape)

    def rows(i, carry):
        wq = wq_ref[..., : 3 * width].reshape(width, 3 * width)
        project_rows(i, x_ref, wq, prm_ref, h_ref, q_ref, k_ref, v_ref, factor)
        return carry

    lax.fori_loop(0, length // TILE, rows, 0)
    for g in rest:
        g.step(2)

    def pair(p, carry):
        attend_pair(p, q_ref, k_ref, v_ref, fx_ref, pq_ref, pk_ref, att_ref, attr_ref, den_ref)
        return carry

    pairs = width // LANES
    lax.fori_loop(0, pairs - 2, pair, 0)
    for g in (o, i0, i1):
        g.step(3)
    lax.fori_loop(pairs - 2, pairs, pair, 0)
    for g in (f0, f1):
        g.step(3)
    for g in rest:
        g.arrive(3)
    for g in (*first, *rest):
        g.drain()


def reduce_backward_kernel(
    nz, factor, x_ref, h_ref, q_ref, k_ref, v_ref, pq_ref, pk_ref, att_ref, den_ref, datt_ref,
    dy_ref, wq_ref, fx_ref, prm_ref, gin_ref, g_ref,
    out_ref, parts_ref, partq_ref, total_ref,
    ht_ref, dqkv_ref, dn_ref, acc_ref, gq_ref, sum_ref, got_ref, *rest,
):
    place = Place(nz)
    bufs, bufs_q = rest[:7], rest[7:14]
    sems, sems_q, (send, recv) = rest[14:17], rest[17:20], rest[20:]
    width = x_ref.shape[1]
    chunks = g_ref.shape[0]
    pairs = width // LANES

    def write(c, value):
        parts_ref[c] = value

    def write_q(c, value):
        for at in range(3):
            where = pl.ds(pl.multiple_of(c * LANES + at * width, LANES), LANES)
            partq_ref[:, where] = value[:, at * LANES : (at + 1) * LANES]

    big = Reduce(place, g_ref, bufs, sems, True, write)
    own = Reduce(place, gq_ref, bufs_q, sems_q, False, write_q)

    place.barrier()

    def begin(c, carry):
        big.step(0, c)
        return carry

    lax.fori_loop(0, chunks, begin, 0)
    sum_ref[0] = gin_ref[...]
    flip_rows(h_ref, ht_ref)

    def pair(p, carry):
        def advance(ring, stage, c, count):
            @pl.when((c >= 0) & (c < count))
            def _():
                ring.step(stage, c)

        def tick(j):
            if j % 2:
                advance(big, 2, 4 * p + (j - 7) // 2, chunks)
            else:
                advance(big, 1, 4 * p + j // 2 - 1, chunks)
                advance(big, 3, 4 * p + j // 2 - 5, chunks)
                advance(big, 4, 4 * p + j // 2 - 7, chunks)
            if j == 1:
                advance(own, 1, p - 1, pairs)
                advance(own, 3, p - 2, pairs)
            if j == 5:
                advance(own, 2, p - 1, pairs)
                advance(own, 4, p - 2, pairs)

        def store(at, where, value):
            shape = (nz, 2, 2, 2, 16, LANES)
            gq_ref[p, ..., at * LANES : (at + 1) * LANES] = value.reshape(shape)

        back_pair(
            p, factor, q_ref, k_ref, v_ref, pq_ref, pk_ref, att_ref, den_ref, datt_ref, fx_ref,
            ht_ref, dqkv_ref, dn_ref, acc_ref, tick, store,
        )
        own.step(0, p)
        return carry

    lax.fori_loop(0, pairs, pair, 0)
    last = pairs - 1
    small = sum_ref.at[0]

    def rows(t, carry):
        wq = wq_ref[:, : 3 * width]
        input_rows(t, x_ref, wq, prm_ref, dqkv_ref, dy_ref, out_ref, small)
        return carry

    tiles = x_ref.shape[0] // TILE
    lax.fori_loop(0, 1, rows, 0)
    own.step(1, last)
    own.step(3, last - 1)
    lax.fori_loop(1, tiles - 1, rows, 0)
    own.step(2, last)
    own.step(4, last - 1)
    lax.fori_loop(tiles - 1, tiles, rows, 0)

    def exchange(stage):
        if stage < 3:
            at = [(0, place.device(c=1 - place.c)), (1, place.device(x=1 - place.x)),
                  (2, place.device(y=1 - place.y))][stage]
            hops = [at]
        else:
            hops = [(2 + k, place.device(z=place.up(k))) for k in range(1, nz)]
        for slot, peer in hops:
            yield slot, remote(
                sum_ref.at[stage], got_ref.at[slot], send.at[slot], recv.at[slot], peer
            )

    def combine(stage):
        value = sum_ref[stage]
        for slot, copy in exchange(stage):
            copy.wait_recv()
            value = value + got_ref[slot]
        return value

    for _, copy in exchange(0):
        copy.start()
    own.step(3, last)
    for stage in range(3):
        sum_ref[stage + 1] = combine(stage)
        for _, copy in exchange(stage + 1):
            copy.start()
        if stage == 1:
            own.step(4, last)
    total_ref[...] = combine(3)
    for stage in range(4):
        for _, copy in exchange(stage):
            copy.wait_send()

    def drain(c, carry):
        big.drain(c)
        return carry

    lax.fori_loop(0, chunks, drain, 0)

    def drain_q(c, carry):
        own.drain(c)
        return carry

    lax.fori_loop(0, pairs, drain_q, 0)


ANY = pl.BlockSpec(memory_space=pl.ANY)
VM = pl.BlockSpec(memory_space=pltpu.VMEM)


def call(kernel, outs, scratch, name, ins=None, out_specs=None, collective=None):
    extra = {} if ins is None else {"in_specs": ins, "out_specs": out_specs}
    params = {} if collective is None else {"collective_id": collective, "has_side_effects": True}
    return pl.pallas_call(
        kernel,
        out_shape=[jax.ShapeDtypeStruct(s, d) for s, d in outs],
        scratch_shapes=[pltpu.SemaphoreType.DMA(s) if d is None else pltpu.VMEM(s, d) for s, d in scratch],
        compiler_params=pltpu.CompilerParams(vmem_limit_bytes=60 * 2**20, **params),
        name=name,
        **extra,
    )


def padded_features(fm):
    heads, feats, _ = fm.shape
    zero = jnp.zeros_like(fm)
    even = (jnp.arange(heads) % 2 == 0)[:, None, None]
    return jnp.concatenate(
        [jnp.where(even, fm, zero), jnp.where(even, zero, fm), jnp.ones((heads, feats, LANES), BF)],
        axis=-1,
    )


def middle(tokens, attr, cotangent, wo, wi, wf, prm, seq_weight):
    length, width = tokens.shape
    hidden = wi.shape[1]
    big, deep = (length, width), (length, hidden)
    chunks = 5 + hidden // width
    return call(
        middle_kernel,
        [(big, BF), (big, F32), (big, F32), ((16, width), F32), ((chunks, width // 64, 4, 16, width), BF)],
        [(deep, BF), (deep, BF), (big, BF), (big, BF), (big, BF), ((8, hidden), F32)],
        "middle",
    )(tokens, attr, cotangent, wo, wi, wf, prm, seq_weight)


def forward_outs(length, width, heads, feats):
    big = (length, width)
    deep = (length, heads * feats)
    return [(big, BF)] * 4 + [(deep, BF)] * 2 + [(big, F32), (big, BF), (big, F32)]


def backward_scratch(length, width):
    return [
        ((width, length), BF), ((length, 3 * width), BF),
        ((2, length, 2 * LANES), BF), ((3, length, LANES), F32),
    ]


def plain_body(
    tokens, cotangent, group_id, w_qkv, w_out, w_ffn_in, w_ffn_out,
    gain_one, shift_one, gain_two, shift_two, bias_in, bias_out, feature_matrix,
):
    gather = functools.partial(lax.all_gather, axis_name=AXES, axis=0, tiled=True)
    scatter = functools.partial(
        lax.psum_scatter, axis_name=AXES, scatter_dimension=0, tiled=True
    )
    length, width = tokens.shape
    heads, feats, head_size = feature_matrix.shape
    hidden = w_ffn_in.shape[1]
    factor = head_size ** (-0.25)
    wq, wo, wi, wf = gather(w_qkv), gather(w_out), gather(w_ffn_in), gather(w_ffn_out)
    prm = gather(jnp.stack([gain_one, shift_one, gain_two, shift_two, bias_out], axis=1))
    prm = jnp.pad(prm.T.astype(F32), ((0, 3), (0, 0)))
    wf = jnp.concatenate([wf, jnp.pad(gather(bias_in)[:, None], ((0, 0), (0, LANES - 1)))], axis=1)

    slice_seqs = lax.axis_size("dp") * group_id.shape[0]
    labels = jnp.arange(slice_seqs // 2, dtype=jnp.int32)
    onehot = (group_id[:, None] == labels[None, :]).astype(F32)
    counts = lax.psum(jnp.sum(onehot, axis=0), "dp")
    group_size = jnp.sum(onehot * counts[None, :], axis=-1)
    groups = jnp.sum((counts > 0.5).astype(F32))
    seq_weight = jnp.broadcast_to((slice_seqs / (groups * group_size))[:, None], (8, LANES))

    fx = padded_features(feature_matrix)
    h1, q, k, v, pq, pk, att, attr, den = call(
        functools.partial(forward_kernel, factor),
        forward_outs(length, width, heads, feats), [], "forward",
    )(tokens, wq, prm, fx)
    act, dy, datt, gprm, grads = middle(tokens, attr, cotangent, wo, wi, wf, prm, seq_weight)
    input_grad, gq, gprm = call(
        functools.partial(backward_kernel, factor),
        [((length, width), BF), ((width, 3 * width), BF), ((16, width), F32)],
        backward_scratch(length, width), "backward",
    )(tokens, h1, q, k, v, pq, pk, att, den, datt, dy, wq, fx, prm, gprm)
    grads = grads.reshape(-1, width // 16, 16, width)
    gf = grads[:4].transpose(1, 0, 2, 3).reshape(hidden, width)
    gi = grads[4:-1].transpose(1, 2, 0, 3).reshape(width, hidden)
    go = grads[-1].reshape(width, width)
    small = scatter(gprm[:8].T)
    gbin = scatter(gprm[5 : 5 + hidden // width].reshape(hidden))
    part = [scatter(t).astype(F32) for t in (gq, go, gi, gf)]
    return (act, input_grad, *part, *(small[:, i] for i in range(4)), gbin, small[:, 4])


def ring_body(
    tokens, cotangent, group_id, w_qkv, w_out, w_ffn_in, w_ffn_out,
    gain_one, shift_one, gain_two, shift_two, bias_in, bias_out, feature_matrix,
):
    length, width = tokens.shape
    heads, feats, head_size = feature_matrix.shape
    hidden = w_ffn_in.shape[1]
    factor = head_size ** (-0.25)
    nz = lax.axis_size("dp") // 2
    ids = jnp.broadcast_to(group_id.astype(BF), gain_one.shape)
    small = jnp.stack([gain_one, shift_one, gain_two, shift_two, bias_out, ids], axis=1)
    wqs = jnp.concatenate([w_qkv, jnp.pad(small, ((0, 0), (0, LANES - 6)))], axis=1)
    wfs = jnp.concatenate([w_ffn_out, jnp.pad(bias_in[:, None], ((0, 0), (0, LANES - 1)))], axis=1)
    fx = padded_features(feature_matrix)
    wide = 3 * width + LANES
    grid = (nz, 2, 2, 2)
    h1, q, k, v, pq, pk, att, attr, den, prm, seq, wq, wo, wi, wf = call(
        functools.partial(gather_forward_kernel, nz, factor),
        [
            *forward_outs(length, width, heads, feats), ((8, width), F32), ((8, LANES), F32),
            ((*grid, 16, wide), BF), ((*grid, 16, width), BF), ((*grid, 16, hidden), BF),
            ((*grid, 64, width + LANES), BF),
        ],
        [((7, 4, nz - 1), None), ((7, 4, nz - 1), None), ((7,), None)],
        "gather_forward",
        [VM, ANY, ANY, ANY, ANY, VM],
        [VM] * 12 + [ANY] * 3,
        0,
    )(tokens, wqs, w_out, w_ffn_in, wfs, fx)
    wq = wq.reshape(width, wide)
    act, dy, datt, gprm, grads = middle(
        tokens, attr, cotangent, wo.reshape(width, width), wi.reshape(width, hidden),
        wf.reshape(hidden, width + LANES), prm, seq,
    )
    chunks = grads.shape[0]
    pairs = width // LANES
    input_grad, parts, gq, total = call(
        functools.partial(reduce_backward_kernel, nz, factor),
        [
            ((length, width), BF), ((chunks, 16, width), F32), ((16, 3 * width), F32),
            ((16, width), F32),
        ],
        [
            *backward_scratch(length, width),
            ((pairs, *grid, 16, 3 * LANES), BF),
            ((4, 16, width), F32), ((2 + nz, 16, width), F32),
            *Reduce.shapes(chunks, nz, 16, width),
            *Reduce.shapes(pairs, nz, 16, 3 * LANES),
            ((chunks, 4, nz - 1), None), ((chunks, 4, nz - 1), None), ((chunks,), None),
            ((pairs, 4, nz - 1), None), ((pairs, 4, nz - 1), None), ((pairs,), None),
            ((2 + nz,), None), ((2 + nz,), None),
        ],
        "reduce_backward",
        [VM] * 15 + [ANY],
        [VM] * 4,
        1,
    )(tokens, h1, q, k, v, pq, pk, att, den, datt, dy, wq, fx, prm, gprm, grads.reshape(chunks, *grid, 16, width))
    gf = parts[:4].reshape(64, width)
    gi = parts[4:-1].transpose(1, 0, 2).reshape(16, hidden)
    go = parts[-1]
    me = lax.axis_index("dp") * lax.axis_size("fsdp") + lax.axis_index("fsdp")
    vec = [lax.dynamic_slice(total[i], (me * 16,), (16,)) for i in range(5)]
    gbin = lax.dynamic_slice(total[5 : 5 + hidden // width].reshape(hidden), (me * 64,), (64,))
    return (act, input_grad, gq, go, gi, gf, *vec[:4], gbin, vec[4])


def solution(mesh):
    rows, vec = P(AXES, None), P(AXES)
    devices = mesh.shape["dp"] * mesh.shape["fsdp"]

    def body(*args):
        width = args[0].shape[1]
        ring = mesh.shape["fsdp"] == 4 and mesh.shape["dp"] % 2 == 0 and width == 16 * devices
        return (ring_body if ring else plain_body)(*args)

    return jax.shard_map(
        body,
        mesh=mesh,
        in_specs=(rows, rows, vec, *[rows] * 4, *[vec] * 6, P()),
        out_specs=(*[rows] * 6, *[vec] * 6),
        check_vma=False,
    )
```

```python
import functools
import math

import jax
import jax.numpy as jnp
from jax import lax
from jax.experimental import pallas as pl
from jax.experimental.pallas import tpu as pltpu
from jax.sharding import PartitionSpec as P

BLOCK = 512
EPSILON = 1e-05
TILE = 256
LANES = 128
LOG2E = 1.4426950408889634
AXES = ("dp", "fsdp")
BF = jnp.bfloat16
F32 = jnp.float32


def dot(left, right):
    return lax.dot_general(left, right, (((1,), (0,)), ((), ())), preferred_element_type=F32)


def dot_bt(left, right):
    return lax.dot_general(left, right, (((1,), (1,)), ((), ())), preferred_element_type=F32)


def dot_at(left, right):
    return lax.dot_general(left, right, (((0,), (0,)), ((), ())), preferred_element_type=F32)


def unit_rows(rows):
    row = lax.broadcasted_iota(jnp.int32, (rows, LANES), 0)
    col = lax.broadcasted_iota(jnp.int32, (rows, LANES), 1)
    return jnp.where(row == col, 1.0, 0.0).astype(BF)


def lane_ids(rows, width=LANES):
    return lax.broadcasted_iota(jnp.int32, (rows, width), 1)


def tile_at(index, size=TILE):
    return pl.ds(pl.multiple_of(index * size, size), size)


def centred(values):
    mu = jnp.mean(values, axis=-1, keepdims=True)
    cen = values - mu
    inv = lax.rsqrt(jnp.mean(cen * cen, axis=-1, keepdims=True) + EPSILON)
    return cen * inv, inv


def norm_back(grad, unit, inv, gain):
    e = grad * gain
    return inv * (
        e
        - jnp.mean(e, axis=-1, keepdims=True)
        - unit * jnp.mean(e * unit, axis=-1, keepdims=True)
    )


def causal(values, offset):
    row = lax.broadcasted_iota(jnp.int32, values.shape, 0)
    col = lax.broadcasted_iota(jnp.int32, values.shape, 1)
    return jnp.where(col <= row + offset, values, 0.0).astype(BF)


def anticausal(values):
    row = lax.broadcasted_iota(jnp.int32, values.shape, 0)
    col = lax.broadcasted_iota(jnp.int32, values.shape, 1)
    return jnp.where(col >= row, values, 0.0).astype(BF)


MESH_ID = pl.DeviceIdType.MESH


class Place:
    def __init__(self, nz):
        dp, fs = lax.axis_index("dp"), lax.axis_index("fsdp")
        self.nz = nz
        self.z, self.y = lax.div(dp, 2), lax.rem(dp, 2)
        self.x, self.c = lax.div(fs, 2), lax.rem(fs, 2)

    def device(self, z=None, y=None, x=None, c=None):
        z, y = self.z if z is None else z, self.y if y is None else y
        x, c = self.x if x is None else x, self.c if c is None else c
        return {"dp": z * 2 + y, "fsdp": x * 2 + c}

    def up(self, k):
        return lax.rem(self.z + k, self.nz)

    def down(self, k):
        return lax.rem(self.z + self.nz - k, self.nz)

    def peers(self):
        yield self.device(c=1 - self.c)
        yield self.device(x=1 - self.x)
        yield self.device(y=1 - self.y)
        for k in range(1, self.nz):
            yield self.device(z=self.up(k))

    def barrier(self):
        sem = pltpu.get_barrier_semaphore()
        for peer in self.peers():
            pl.semaphore_signal(sem, inc=1, device_id=peer, device_id_type=MESH_ID)
        pl.semaphore_wait(sem, 2 + self.nz)


def remote(src, dst, send, recv, peer):
    return pltpu.make_async_remote_copy(
        src_ref=src, dst_ref=dst, send_sem=send, recv_sem=recv, device_id=peer,
        device_id_type=MESH_ID,
    )


class Gather:
    def __init__(self, place, shard, whole, view, sems, m, y_first):
        self.place, self.shard, self.whole, self.view = place, shard, whole, view
        self.send, self.recv, self.own = sems
        self.m = m
        self.y_first = y_first

    def at(self, *index):
        return self.whole.at[(*index, *self.view)]

    def hops(self, stage):
        p = self.place
        every = slice(None)
        if stage == 0:
            src = self.shard.at[self.view]
            for k in range(1, p.nz):
                yield src, self.at(p.z, p.y, p.x, p.c), self.at(p.down(k), p.y, p.x, p.c), p.device(z=p.up(k))
        elif stage == 3:
            mine = self.at(every, every, every, p.c)
            yield mine, mine, self.at(every, every, every, 1 - p.c), p.device(c=1 - p.c)
        elif self.y_first:
            if stage == 1:
                mine = self.at(every, p.y, p.x, p.c)
                yield mine, mine, self.at(every, 1 - p.y, p.x, p.c), p.device(y=1 - p.y)
            else:
                mine = self.at(every, every, p.x, p.c)
                yield mine, mine, self.at(every, every, 1 - p.x, p.c), p.device(x=1 - p.x)
        else:
            if stage == 1:
                mine = self.at(every, p.y, p.x, p.c)
                yield mine, mine, self.at(every, p.y, 1 - p.x, p.c), p.device(x=1 - p.x)
            else:
                mine = self.at(every, p.y, every, p.c)
                yield mine, mine, self.at(every, 1 - p.y, every, p.c), p.device(y=1 - p.y)

    def copies(self, stage, arriving):
        for k, (src, dst, land, peer) in enumerate(self.hops(stage)):
            yield remote(
                src, land if arriving else dst, self.send.at[self.m, stage, k],
                self.recv.at[self.m, stage, k], peer,
            )

    def local(self):
        p = self.place
        return pltpu.make_async_copy(
            self.shard.at[self.view], self.at(p.z, p.y, p.x, p.c), self.own.at[self.m]
        )

    def start(self):
        for copy in self.copies(0, False):
            copy.start()
        self.local().start()

    def arrive(self, stage):
        for copy in self.copies(stage, True):
            copy.wait_recv()

    def step(self, stage):
        self.arrive(stage - 1)
        if stage == 1:
            self.local().wait()
        for copy in self.copies(stage, False):
            copy.start()

    def drain(self):
        for stage in range(4):
            for copy in self.copies(stage, False):
                copy.wait_send()


class Reduce:
    def __init__(self, place, source, bufs, sems, load, write):
        self.place, self.source = place, source
        self.l0, self.r0, self.l1, self.r1, self.l2, self.r2, self.r3 = bufs
        self.send, self.recv, self.own = sems
        self.load, self.write = load, write

    def hops(self, stage, c, x_first):
        p = self.place
        every = slice(None)
        if stage == 0:
            yield self.source.at[c, every, every, every, 1 - p.c], self.r0.at[c], p.device(c=1 - p.c)
        elif stage == 1:
            if x_first:
                yield self.l0.at[c, every, every, 1 - p.x], self.r1.at[c], p.device(x=1 - p.x)
            else:
                yield self.l0.at[c, every, 1 - p.y], self.r1.at[c], p.device(y=1 - p.y)
        elif stage == 2:
            if x_first:
                yield self.l1.at[c, every, 1 - p.y], self.r2.at[c], p.device(y=1 - p.y)
            else:
                yield self.l1.at[c, every, 1 - p.x], self.r2.at[c], p.device(x=1 - p.x)
        else:
            for k in range(1, p.nz):
                yield self.l2.at[c, p.up(k)], self.r3.at[c, k - 1], p.device(z=p.up(k))

    def copies(self, stage, c, x_first):
        for k, (src, dst, peer) in enumerate(self.hops(stage, c, x_first)):
            yield remote(src, dst, self.send.at[c, stage, k], self.recv.at[c, stage, k], peer)

    def local(self, c):
        p = self.place
        every = slice(None)
        return pltpu.make_async_copy(
            self.source.at[c, every, every, every, p.c], self.l0.at[c], self.own.at[c]
        )

    def begin(self, stage, c, x_first):
        for copy in self.copies(stage, c, x_first):
            copy.start()

    def step(self, stage, c, x_first=False):
        p = self.place
        if stage == 0:
            self.begin(0, c, x_first)
            if self.load:
                self.local(c).start()
            return
        for copy in self.copies(stage - 1, c, x_first):
            copy.wait_recv()
        if stage == 1:
            if self.load:
                self.local(c).wait()
                mine = self.l0[c]
            else:
                mine = self.source[c, :, :, :, p.c]
            self.l0[c] = (mine.astype(F32) + self.r0[c].astype(F32)).astype(BF)
        elif stage == 2:
            mine = self.l0[c, :, :, p.x] if x_first else self.l0[c, :, p.y]
            self.l1[c] = (mine.astype(F32) + self.r1[c].astype(F32)).astype(BF)
        elif stage == 3:
            mine = self.l1[c, :, p.y] if x_first else self.l1[c, :, p.x]
            self.l2[c] = (mine.astype(F32) + self.r2[c].astype(F32)).astype(BF)
        else:
            total = self.l2[c, p.z].astype(F32)
            for k in range(p.nz - 1):
                total = total + self.r3[c, k].astype(F32)
            self.write(c, total)
            return
        self.begin(stage, c, x_first)

    def drain(self, c, x_first=False):
        for stage in range(4):
            for copy in self.copies(stage, c, x_first):
                copy.wait_send()

    @staticmethod
    def shapes(n, nz, rows, cols):
        return [
            ((n, nz, 2, 2, rows, cols), BF), ((n, nz, 2, 2, rows, cols), BF),
            ((n, nz, 2, rows, cols), BF), ((n, nz, 2, rows, cols), BF),
            ((n, nz, rows, cols), BF), ((n, nz, rows, cols), BF), ((n, nz - 1, rows, cols), BF),
        ]


def project_rows(i, x_ref, wq, prm_ref, h_ref, q_ref, k_ref, v_ref, factor):
    rows = tile_at(i)
    unit, _ = centred(x_ref[rows, :].astype(F32))
    h = (unit * prm_ref[0:1, :] + prm_ref[1:2, :]).astype(BF)
    h_ref[rows, :] = h
    width = h.shape[1]
    qkv = dot(h, wq)
    q_ref[rows, :] = (qkv[:, :width] * factor).astype(BF)
    k_ref[rows, :] = (qkv[:, width : 2 * width] * factor).astype(BF)
    v_ref[rows, :] = qkv[:, 2 * width :].astype(BF)


def attend_pair(p, q_ref, k_ref, v_ref, fx_ref, pq_ref, pk_ref, att_ref, attr_ref, den_ref):
    length = q_ref.shape[0]
    feats = fx_ref.shape[1]
    lanes = tile_at(p, LANES)
    shift = 0.5 * math.log2(feats)
    cols = [tile_at(2 * p + hh, feats) for hh in range(2)]
    for hh in range(2):
        fm = fx_ref[2 * p + hh][:, :LANES]
        for src, dst in ((q_ref, pq_ref), (k_ref, pk_ref)):
            for t in range(length // TILE):
                rows = slice(t * TILE, (t + 1) * TILE)
                part = src[rows, lanes]
                scores = dot_bt(part, fm)
                wide = jnp.where(lane_ids(TILE) // 64 == hh, part.astype(F32), 0.0)
                square = jnp.sum(wide * wide, axis=-1, keepdims=True)
                feat = jnp.exp2(scores * LOG2E - (square * (0.5 * LOG2E) + shift))
                dst[rows, cols[hh]] = feat.astype(BF)
    ones = jnp.ones((length, LANES), BF)
    vx = jnp.concatenate([v_ref[:, lanes], ones], axis=1)
    states = [None, None]
    low = [None, None]
    for b in range(length // BLOCK):
        base = b * BLOCK
        for i in range(BLOCK // TILE):
            rows = slice(base + i * TILE, base + (i + 1) * TILE)
            keys = slice(base, base + (i + 1) * TILE)
            got = []
            for hh in range(2):
                pq = pq_ref[rows, cols[hh]]
                weights = causal(dot_bt(pq, pk_ref[keys, cols[hh]]), i * TILE)
                both = dot(weights, vx[keys])
                if b:
                    both = both + dot(pq, low[hh])
                got.append(both)
            first = lane_ids(TILE) < 64
            num = jnp.where(first, got[0][:, :LANES], got[1][:, :LANES])
            den = jnp.where(first, got[0][:, LANES:], got[1][:, LANES:])
            att = num / den
            att_ref[rows, lanes] = att
            attr_ref[rows, lanes] = att.astype(BF)
            den_ref[rows, lanes] = den
        if base + BLOCK < length:
            block = slice(base, base + BLOCK)
            for hh in range(2):
                more = dot_at(pk_ref[block, cols[hh]], vx[block])
                states[hh] = more if b == 0 else states[hh] + more
                low[hh] = states[hh].astype(BF)


def forward_kernel(
    factor, x_ref, wq_ref, prm_ref, fx_ref,
    h_ref, q_ref, k_ref, v_ref, pq_ref, pk_ref, att_ref, attr_ref, den_ref,
):
    def rows(i, carry):
        project_rows(i, x_ref, wq_ref[...], prm_ref, h_ref, q_ref, k_ref, v_ref, factor)
        return carry

    lax.fori_loop(0, x_ref.shape[0] // TILE, rows, 0)

    def pair(p, carry):
        attend_pair(p, q_ref, k_ref, v_ref, fx_ref, pq_ref, pk_ref, att_ref, attr_ref, den_ref)
        return carry

    lax.fori_loop(0, x_ref.shape[1] // LANES, pair, 0)


def ffn_rows(
    t, x_ref, attr_ref, cot_ref, wo, wi, wf, prm_ref, bin_ref, seq_ref,
    act_ref, dy_ref, datt_ref, gprm_ref, hid_ref, du_ref, h_ref, gr_ref, dor_ref, bin_row=0,
):
    width = x_ref.shape[1]
    chunk = width
    rows = tile_at(t)
    y = x_ref[rows, :].astype(F32) + dot(attr_ref[rows, :], wo())
    unit, inv = centred(y)
    gain = prm_ref[2:3, :]
    h = (unit * gain + prm_ref[3:4, :]).astype(BF)
    h_ref[rows, :] = h
    g = cot_ref[rows, :].astype(F32) * seq_ref[0:1, 0:1]
    gr = g.astype(BF)
    gr_ref[rows, :] = gr
    out = y + prm_ref[4:5, :]
    dh = jnp.zeros((TILE, width), F32)
    for c in range(hid_ref.shape[1] // chunk):
        cs = slice(c * chunk, (c + 1) * chunk)
        u = dot(h, wi(cs)) + bin_ref[bin_row : bin_row + 1, cs]
        cdf = 0.5 + 0.5 * lax.erf(u * math.sqrt(0.5))
        slope = cdf + u * jnp.exp2(u * u * (-0.5 * LOG2E)) * (1.0 / math.sqrt(2.0 * math.pi))
        hid = (u * cdf).astype(BF)
        hid_ref[rows, cs] = hid
        out = out + dot(hid, wf(c))
        du = (dot_bt(gr, wf(c)) * slope).astype(BF)
        du_ref[rows, cs] = du
        gprm_ref[5 + c : 6 + c, :] += jnp.sum(du.astype(F32), axis=0, keepdims=True)
        dh = dh + dot_bt(du, wi(cs))
    act_ref[rows, :] = out.astype(BF)
    gprm_ref[2:3, :] += jnp.sum(dh * unit, axis=0, keepdims=True)
    gprm_ref[3:4, :] += jnp.sum(dh, axis=0, keepdims=True)
    gprm_ref[4:5, :] += jnp.sum(g, axis=0, keepdims=True)
    dy = g + norm_back(dh, unit, inv, gain)
    dy_ref[rows, :] = dy
    dor = dy.astype(BF)
    dor_ref[rows, :] = dor
    datt_ref[rows, :] = dot_bt(dor, wo())


def grads_out(c, hid_ref, gr_ref, g_ref):
    width = gr_ref.shape[1]
    grad = dot_at(hid_ref[:, tile_at(c)], gr_ref[...]).astype(BF)
    grad = grad.reshape(4, 4, 16, width)
    for q in range(4):
        g_ref[q, c] = grad[:, q]


def grads_in(c, h_ref, du_ref, attr_ref, dor_ref, g_ref):
    width = h_ref.shape[1]
    count = du_ref.shape[1] // width
    cs = tile_at(c)
    at = pl.ds(c * 4, 4)
    grad = dot_at(h_ref[:, cs], du_ref[...]).astype(BF)
    for k in range(count):
        g_ref[4 + k, at] = grad[:, k * width : (k + 1) * width].reshape(4, 4, 16, width)
    grad = dot_at(attr_ref[:, cs], dor_ref[...]).astype(BF)
    g_ref[4 + count, at] = grad.reshape(4, 4, 16, width)


def loop(start, stop, step):
    def run(i, carry):
        step(i)
        return carry

    lax.fori_loop(start, stop, run, 0)


def middle_kernel(
    x_ref, attr_ref, cot_ref, wo_ref, wi_ref, wf_ref, prm_ref, seq_ref,
    act_ref, dy_ref, datt_ref, gprm_ref, g_ref,
    hid_ref, du_ref, h_ref, gr_ref, dor_ref, bin_ref,
):
    length, width = x_ref.shape
    gprm_ref[...] = jnp.zeros_like(gprm_ref)
    bin_ref[...] = dot_bt(unit_rows(8), wf_ref[:, width:])
    loop(0, length // TILE, lambda t: ffn_rows(
        t, x_ref, attr_ref, cot_ref, lambda: wo_ref[...], lambda cs: wi_ref[:, cs],
        lambda c: wf_ref[c * width : (c + 1) * width, :width], prm_ref, bin_ref, seq_ref,
        act_ref, dy_ref, datt_ref, gprm_ref, hid_ref, du_ref, h_ref, gr_ref, dor_ref,
    ))
    loop(0, hid_ref.shape[1] // TILE, lambda c: grads_out(c, hid_ref, gr_ref, g_ref))
    loop(0, width // TILE, lambda c: grads_in(c, h_ref, du_ref, attr_ref, dor_ref, g_ref))


def back_pair(
    p, factor, q_ref, k_ref, v_ref, pq_ref, pk_ref, att_ref, den_ref, datt_ref, fx_ref,
    ht_ref, dqkv_ref, dn_ref, acc_ref, tick, store,
):
    length = q_ref.shape[0]
    feats = fx_ref.shape[1]
    width = q_ref.shape[1]
    lanes = tile_at(p, LANES)
    blocks = length // BLOCK
    cols = [tile_at(2 * p + hh, feats) for hh in range(2)]
    v = v_ref[:, lanes]
    two = jnp.where(lane_ids(length) < 2, 1.0, 0.0).astype(BF)
    vx = jnp.concatenate([v, jnp.ones((length, LANES), BF)], axis=1)
    v2 = jnp.concatenate([v, two], axis=1)
    for t in range(length // TILE):
        rows = slice(t * TILE, (t + 1) * TILE)
        dn = datt_ref[rows, lanes] / den_ref[rows, lanes]
        prod = dn * att_ref[rows, lanes]
        lane = lane_ids(TILE)
        for hh in range(2):
            mine = lane // 64 == hh
            dden = -jnp.sum(jnp.where(mine, prod, 0.0), axis=-1, keepdims=True)
            high = dden.astype(BF).astype(F32)
            extra = jnp.where(lane == 0, high, jnp.where(lane == 1, dden - high, 0.0))
            dn_ref[hh, rows, :LANES] = jnp.where(mine, dn, 0.0).astype(BF)
            dn_ref[hh, rows, LANES:] = extra.astype(BF)
    for hh in range(2):
        mine = lane_ids(TILE) // 64 == hh
        fx = fx_ref[2 * p + hh]
        low = [None] * blocks
        total = None
        for b in range(blocks - 1):
            block = slice(b * BLOCK, (b + 1) * BLOCK)
            more = dot_at(pk_ref[block, cols[hh]], vx[block])
            total = more if total is None else total + more
            low[b + 1] = total.astype(BF)
        back = [None] * blocks
        total = None
        for b in range(blocks - 1, 0, -1):
            block = slice(b * BLOCK, (b + 1) * BLOCK)
            more = dot_at(pq_ref[block, cols[hh]], dn_ref[hh, block, :])
            total = more if total is None else total + more
            dz = total[:, LANES : LANES + 1] + total[:, LANES + 1 : LANES + 2]
            high = dz.astype(BF).astype(F32)
            lane = lane_ids(feats)
            extra = jnp.where(lane == 0, high, jnp.where(lane == 1, dz - high, 0.0))
            back[b - 1] = jnp.concatenate([total[:, :LANES], extra], axis=1).astype(BF)

        def finish(grad, feat, part, where, hh=hh, fx=fx, mine=mine):
            e = (grad * feat.astype(F32)).astype(BF)
            res = dot(e, fx)
            out = (res[:, :LANES] - part.astype(F32) * res[:, LANES:]) * factor
            rows, at = where
            if hh == 0:
                acc_ref[at, rows, :] = out
            else:
                both = jnp.where(mine, out, acc_ref[at, rows, :])
                start = pl.multiple_of(p * LANES + at * width, LANES)
                dqkv_ref[rows, pl.ds(start, LANES)] = both.astype(BF)

        for b in range(blocks):
            base = b * BLOCK
            for i in range(BLOCK // TILE):
                rows = slice(base + i * TILE, base + (i + 1) * TILE)
                keys = slice(base, base + (i + 1) * TILE)
                dn = dn_ref[hh, rows, :]
                da = causal(dot_bt(dn, v2[keys]), i * TILE)
                grad = dot(da, pk_ref[keys, cols[hh]])
                if b:
                    grad = grad + dot_bt(dn, low[b])
                finish(grad, pq_ref[rows, cols[hh]], q_ref[rows, lanes], (rows, 0))
                later = slice(base + i * TILE, base + BLOCK)
                pk = pk_ref[rows, cols[hh]]
                pql = pq_ref[later, cols[hh]]
                dnl = dn_ref[hh, later, :]
                dat = anticausal(dot_bt(v2[rows], dnl))
                grad = dot(dat, pql)
                at = anticausal(dot_bt(pk, pql))
                dv = dot(at, dnl[:, :LANES])
                if b < blocks - 1:
                    grad = grad + dot_bt(v2[rows], back[b])
                    dv = dv + dot(pk, back[b][:, :LANES])
                finish(grad, pk, k_ref[rows, lanes], (rows, 1))
                if hh == 0:
                    acc_ref[2, rows, :] = dv
                else:
                    both = acc_ref[2, rows, :] + dv
                    start = pl.multiple_of(p * LANES + 2 * width, LANES)
                    dqkv_ref[rows, pl.ds(start, LANES)] = both.astype(BF)
                tick((hh * blocks + b) * (BLOCK // TILE) + i)
    for at in range(3):
        where = pl.ds(pl.multiple_of(p * LANES + at * width, LANES), LANES)
        store(at, where, dot(ht_ref[...], dqkv_ref[:, where]).astype(BF))


def input_rows(t, x_ref, wq, prm_ref, dqkv_ref, dy_ref, out_ref, gprm_ref):
    rows = tile_at(t)
    dh = dot_bt(dqkv_ref[rows, :], wq)
    unit, inv = centred(x_ref[rows, :].astype(F32))
    gprm_ref[0:1, :] += jnp.sum(dh * unit, axis=0, keepdims=True)
    gprm_ref[1:2, :] += jnp.sum(dh, axis=0, keepdims=True)
    out_ref[rows, :] = (dy_ref[rows, :] + norm_back(dh, unit, inv, prm_ref[0:1, :])).astype(BF)


def flip_rows(h_ref, ht_ref):
    for t in range(h_ref.shape[0] // TILE):
        rows = slice(t * TILE, (t + 1) * TILE)
        ht_ref[:, rows] = h_ref[rows, :].T


def backward_kernel(
    factor, x_ref, h_ref, q_ref, k_ref, v_ref, pq_ref, pk_ref, att_ref, den_ref, datt_ref, dy_ref,
    wq_ref, fx_ref, prm_ref, gin_ref,
    out_ref, gq_ref, gprm_ref,
    ht_ref, dqkv_ref, dn_ref, acc_ref,
):
    gprm_ref[...] = gin_ref[...]
    flip_rows(h_ref, ht_ref)

    def store(at, where, value):
        gq_ref[:, where] = value

    def pair(p, carry):
        back_pair(
            p, factor, q_ref, k_ref, v_ref, pq_ref, pk_ref, att_ref, den_ref, datt_ref, fx_ref,
            ht_ref, dqkv_ref, dn_ref, acc_ref, lambda j: None, store,
        )
        return carry

    lax.fori_loop(0, x_ref.shape[1] // LANES, pair, 0)

    def rows(t, carry):
        input_rows(t, x_ref, wq_ref[...], prm_ref, dqkv_ref, dy_ref, out_ref, gprm_ref)
        return carry

    lax.fori_loop(0, x_ref.shape[0] // TILE, rows, 0)


def sequence_weight(small, seq_ref):
    nf = 4
    me = lax.axis_index("dp") * nf + lax.axis_index("fsdp")
    row = lax.broadcasted_iota(jnp.int32, small.shape, 0)
    lane = lane_ids(small.shape[0]).astype(F32)
    peer = lax.div(row, 16)
    ids = small[:, 5:6].astype(F32)
    hit = (lane == ids) & (lax.rem(row, 16) == 0)
    counts = jnp.sum(
        jnp.where(hit & (lax.rem(peer, nf) == lax.axis_index("fsdp")), 1.0, 0.0),
        axis=0, keepdims=True,
    )
    mine = jnp.sum(jnp.where(hit & (peer == me), 1.0, 0.0), axis=0, keepdims=True)
    size = jnp.sum(counts * mine, axis=1, keepdims=True)
    groups = jnp.sum(jnp.where(counts > 0.5, 1.0, 0.0), axis=1, keepdims=True)
    members = lax.axis_size("dp")
    seq_ref[...] = jnp.broadcast_to(members / (groups * size), seq_ref.shape)


def gather_forward_kernel(
    nz, factor, x_ref, cot_in, wqs_ref, wos_ref, wis_ref, wfs_ref, fm_ref, id_ref,
    g1_ref, s1_ref, g2_ref, s2_ref, bo_ref, bi_ref,
    h_out, q_out, k_out, v_out, pq_out, pk_out, att_out, den_out, wq_out,
    act_out, dy_out, datt_out, g_out, fx_out, prm_ref, gprm_ref,
    h_ref, q_ref, k_ref, v_ref, pq_ref, pk_ref, att_ref, attr_ref, den_ref,
    wq_ref, wo_ref, wi_ref, wf_ref, sp_ref, bp_ref, cot_ref, fx_ref, vec_ref, col_ref,
    act_ref, dy_ref, datt_ref, g_ref, hid_ref, du_ref, h2_ref, gr_ref, dor_ref, bin_ref, seq_ref,
    send, recv, own, one_sem, pair_sem, tile_sem, grad_sem,
):
    length, width = x_ref.shape
    place = Place(nz)
    every = slice(None)
    sems = (send, recv, own)
    cut = width * 3 // 2
    half = wis_ref.shape[1] // 2
    low, high = slice(0, 32), slice(32, 64)
    q0 = Gather(place, wqs_ref, wq_ref, (every, slice(0, cut)), sems, 0, True)
    q1 = Gather(place, wqs_ref, wq_ref, (every, slice(cut, 2 * cut)), sems, 1, False)
    o = Gather(place, wos_ref, wo_ref, (every, every), sems, 2, True)
    i0 = Gather(place, wis_ref, wi_ref, (every, slice(0, half)), sems, 3, True)
    i1 = Gather(place, wis_ref, wi_ref, (every, slice(half, 2 * half)), sems, 4, False)
    f0 = Gather(place, wfs_ref, wf_ref, (low, every), sems, 5, True)
    f1 = Gather(place, wfs_ref, wf_ref, (high, every), sems, 6, False)
    sp = Gather(place, col_ref, sp_ref, (slice(0, 16), every), sems, 7, True)
    bp = Gather(place, col_ref, bp_ref, (slice(0, 64), every), sems, 8, False)
    first, rest = (sp, q0, q1), (o, bp, i0, i1, f0, f1)

    singles = [
        pltpu.make_async_copy(src, dst, one_sem.at[n])
        for n, (src, dst) in enumerate((
            (cot_in, cot_ref), (wq_ref, wq_out), (h_ref, h_out), (q_ref, q_out),
            (k_ref, k_out), (v_ref, v_out), (fx_ref, fx_out),
        ))
    ]

    def pair_out(p):
        moves = ((pq_ref, pq_out, 4), (pk_ref, pk_out, 4), (att_ref, att_out, 1), (den_ref, den_out, 1))
        for n, (src, dst, many) in enumerate(moves):
            cols = tile_at(p, many * LANES)
            yield pltpu.make_async_copy(src.at[:, cols], dst.at[:, cols], pair_sem.at[p, n])

    def tile_out(t):
        rows = tile_at(t)
        for n, (src, dst) in enumerate(((act_ref, act_out), (dy_ref, dy_out), (datt_ref, datt_out))):
            yield pltpu.make_async_copy(src.at[rows], dst.at[rows], tile_sem.at[t, n])

    def grad_out(c):
        return pltpu.make_async_copy(g_ref.at[c], g_out.at[c], grad_sem.at[c])

    vec_ref[...] = jnp.zeros_like(vec_ref)
    for n, ref in enumerate((g1_ref, s1_ref, g2_ref, s2_ref, bo_ref)):
        vec_ref[n : n + 1, : ref.shape[1]] = ref[...].astype(F32)
    vec_ref[5:6, :] = jnp.full((1, LANES), id_ref[0], jnp.int32).astype(F32)
    vec_ref[6:7, : bi_ref.shape[1]] = bi_ref[...].astype(F32)
    col_ref[...] = dot_at(vec_ref[...].astype(BF), unit_rows(16)).astype(BF)
    place.barrier()
    for g in (*first, *rest):
        g.start()
    singles[0].start()
    head_size, feats = fm_ref.shape[1:]
    for n in range(fm_ref.shape[0]):
        row = lax.broadcasted_iota(jnp.int32, (head_size, LANES), 0)
        place_at = jnp.where(lane_ids(head_size) == row + (n % 2) * head_size, 1.0, 0.0).astype(BF)
        fx_ref[n, :, :LANES] = dot_at(fm_ref[n], place_at).astype(BF)
        fx_ref[n, :, LANES:] = jnp.ones((feats, LANES), BF)
    singles[6].start()
    for stage in (1, 2, 3):
        for g in first:
            g.step(stage)
    for g in rest:
        g.step(1)
    for g in first:
        g.arrive(3)
    singles[1].start()
    small = sp_ref[...].reshape(width, LANES)
    prm_ref[...] = dot_bt(unit_rows(8), small)
    sequence_weight(small, seq_ref)

    def rows(i):
        wq = wq_ref[...].reshape(width, 3 * width)
        project_rows(i, x_ref, wq, prm_ref, h_ref, q_ref, k_ref, v_ref, factor)

    loop(0, length // TILE, rows)
    for copy in singles[2:6]:
        copy.start()
    for g in rest:
        g.step(2)

    def pair(p):
        attend_pair(p, q_ref, k_ref, v_ref, fx_ref, pq_ref, pk_ref, att_ref, attr_ref, den_ref)
        for copy in pair_out(p):
            copy.start()

    pairs = width // LANES
    loop(0, pairs - 1, pair)
    for g in (o, bp, i0, i1):
        g.step(3)
    loop(pairs - 1, pairs, pair)
    for g in (f0, f1):
        g.step(3)
    for g in rest:
        g.arrive(3)
    singles[0].wait()

    gprm_ref[...] = jnp.zeros_like(gprm_ref)
    hidden = hid_ref.shape[1]
    bin_ref[...] = dot_bt(unit_rows(8), bp_ref[...].reshape(hidden, LANES))

    def ffn(t):
        ffn_rows(
            t, x_ref, attr_ref, cot_ref, lambda: wo_ref[...].reshape(width, width),
            lambda cs: wi_ref[..., cs].reshape(width, width),
            lambda c: wf_ref[c].reshape(width, width), prm_ref, bin_ref, seq_ref,
            act_ref, dy_ref, datt_ref, gprm_ref, hid_ref, du_ref, h2_ref, gr_ref, dor_ref, 6,
        )
        for copy in tile_out(t):
            copy.start()

    loop(0, length // TILE, ffn)
    loop(0, hidden // TILE, lambda c: grads_out(c, hid_ref, gr_ref, g_ref))
    for c in range(4):
        grad_out(c).start()
    loop(0, width // TILE, lambda c: grads_in(c, h2_ref, du_ref, attr_ref, dor_ref, g_ref))
    chunks = g_ref.shape[0]
    for c in range(4, chunks):
        grad_out(c).start()
    for copy in singles[1:]:
        copy.wait()
    for p in range(pairs):
        for copy in pair_out(p):
            copy.wait()
    for t in range(length // TILE):
        for copy in tile_out(t):
            copy.wait()
    for c in range(chunks):
        grad_out(c).wait()
    for g in (*first, *rest):
        g.drain()


def reduce_backward_kernel(
    nz, factor, x_in, h_in, q_in, k_in, v_in, pq_in, pk_in, att_in, den_in, datt_in,
    dy_in, wq_in, fx_ref, prm_ref, gin_ref, g_ref,
    out_ref, gf_ref, gi_ref, go_ref, partq_ref, small_ref,
    x_ref, h_ref, q_ref, k_ref, v_ref, pq_ref, pk_ref, att_ref, den_ref, datt_ref, dy_ref, wq_ref,
    pair_sem, full_sem,
    ht_ref, dqkv_ref, dn_ref, acc_ref, gq_ref, sum_ref, got_ref, *rest,
):
    place = Place(nz)
    bufs, bufs_q = rest[:7], rest[7:14]
    sems, sems_q, (send, recv) = rest[14:17], rest[17:20], rest[20:]
    width = x_ref.shape[1]
    chunks = g_ref.shape[0]
    pairs = width // LANES
    wide = gi_ref.shape[1] // width

    def write(c, value):
        @pl.when(c < 4)
        def _():
            gf_ref[c] = value

        @pl.when((c >= 4) & (c < 4 + wide))
        def _():
            gi_ref[:, pl.ds(pl.multiple_of((c - 4) * width, width), width)] = value

        @pl.when(c == 4 + wide)
        def _():
            go_ref[...] = value

    def write_q(c, value):
        for at in range(3):
            where = pl.ds(pl.multiple_of(c * LANES + at * width, LANES), LANES)
            partq_ref[:, where] = value[:, at * LANES : (at + 1) * LANES]

    big = Reduce(place, g_ref, bufs, sems, True, write)
    own = Reduce(place, gq_ref, bufs_q, sems_q, False, write_q)

    full = [
        pltpu.make_async_copy(src, dst, full_sem.at[n])
        for n, (src, dst) in enumerate(
            ((h_in, h_ref), (wq_in, wq_ref), (x_in, x_ref), (dy_in, dy_ref))
        )
    ]
    by_pair = (
        (pk_in, pk_ref, 4), (v_in, v_ref, 1), (datt_in, datt_ref, 1), (den_in, den_ref, 1),
        (att_in, att_ref, 1), (pq_in, pq_ref, 4), (q_in, q_ref, 1), (k_in, k_ref, 1),
    )

    def load(p):
        for n, (src, dst, many) in enumerate(by_pair):
            cols = tile_at(p, many * LANES)
            yield pltpu.make_async_copy(src.at[:, cols], dst.at[:, cols], pair_sem.at[p, n])

    for copy in load(0):
        copy.start()
    full[0].start()
    place.barrier()

    def begin(c, carry):
        big.step(0, c)
        return carry

    lax.fori_loop(0, chunks, begin, 0)

    def fetch(p, carry):
        for copy in load(p):
            copy.start()
        return carry

    lax.fori_loop(1, pairs, fetch, 0)
    for copy in full[1:]:
        copy.start()
    sum_ref[0] = gin_ref[...]
    full[0].wait()
    flip_rows(h_ref, ht_ref)

    def pair(p, carry):
        def advance(ring, stage, c, count, x_first):
            @pl.when((c >= 0) & (c < count))
            def _():
                ring.step(stage, c, x_first)

        def advance_big(stage, c0):
            advance(big, stage, 4 * p + c0, chunks, c0 % 2 == 0)

        def tick(j):
            if j % 2:
                advance_big(2, (j - 7) // 2)
            else:
                advance_big(1, j // 2 - 1)
                advance_big(3, j // 2 - 5)
                advance_big(4, j // 2 - 7)
            if j == 1:
                advance(own, 1, p - 1, pairs, False)
                advance(own, 3, p - 2, pairs, False)
            if j == 5:
                advance(own, 2, p - 1, pairs, False)
                advance(own, 4, p - 2, pairs, False)

        def store(at, where, value):
            shape = (nz, 2, 2, 2, 16, LANES)
            gq_ref[p, ..., at * LANES : (at + 1) * LANES] = value.reshape(shape)

        for copy in load(p):
            copy.wait()
        back_pair(
            p, factor, q_ref, k_ref, v_ref, pq_ref, pk_ref, att_ref, den_ref, datt_ref, fx_ref,
            ht_ref, dqkv_ref, dn_ref, acc_ref, tick, store,
        )
        own.step(0, p)
        return carry

    lax.fori_loop(0, pairs, pair, 0)
    for copy in full[1:]:
        copy.wait()
    last = pairs - 1
    small = sum_ref.at[0]

    def rows(t, carry):
        wq = wq_ref[...]
        input_rows(t, x_ref, wq, prm_ref, dqkv_ref, dy_ref, out_ref, small)
        return carry

    tiles = x_ref.shape[0] // TILE

    def exchange(stage):
        if stage < 3:
            hops = [
                [(0, place.device(c=1 - place.c))],
                [(1, place.device(x=1 - place.x))],
                [(2, place.device(y=1 - place.y))],
            ][stage]
        else:
            hops = [(2 + k, place.device(z=place.up(k))) for k in range(1, nz)]
        for slot, peer in hops:
            yield slot, remote(
                sum_ref.at[stage], got_ref.at[slot], send.at[slot], recv.at[slot], peer
            )

    def launch(stage):
        for _, copy in exchange(stage):
            copy.start()

    def combine(stage):
        value = sum_ref[stage]
        for slot, copy in exchange(stage):
            copy.wait_recv()
            value = value + got_ref[slot]
        return value

    own.step(3, last - 1)
    lax.fori_loop(0, tiles // 2, rows, 0)
    own.step(1, last)
    lax.fori_loop(tiles // 2, tiles, rows, 0)
    launch(0)
    own.step(4, last - 1)
    own.step(2, last)
    sum_ref[1] = combine(0)
    launch(1)
    own.step(3, last)
    sum_ref[2] = combine(1)
    launch(2)
    own.step(4, last)
    sum_ref[3] = combine(2)
    launch(3)
    small_ref[...] = combine(3)
    for stage in range(4):
        for _, copy in exchange(stage):
            copy.wait_send()
    for c in range(chunks):
        big.drain(c, c % 2 == 0)

    def drain_q(c, carry):
        own.drain(c)
        return carry

    lax.fori_loop(0, pairs, drain_q, 0)


def finish_kernel(
    act_in, grad_in, gq_in, gf_in, gi_in, go_in, small_in,
    act_ref, grad_ref, gq_ref, go_ref, gi_ref, gf_ref,
    g1_ref, s1_ref, g2_ref, s2_ref, bi_ref, bo_ref,
    hold_ref, in_sem, out_sem,
):
    moves = []
    for n, (src, dst) in enumerate(((act_in, act_ref), (grad_in, grad_ref))):
        for t in range(src.shape[0] // TILE):
            rows = pl.ds(t * TILE, TILE)
            hold = hold_ref.at[n, rows]
            moves.append((
                pltpu.make_async_copy(src.at[rows], hold, in_sem.at[n, t]),
                pltpu.make_async_copy(hold, dst.at[rows], out_sem.at[n, t]),
            ))
    for come, _ in moves:
        come.start()
    gq_ref[...] = gq_in[...]
    go_ref[...] = go_in[...]
    gi_ref[...] = gi_in[...]
    gf_ref[...] = gf_in[...].reshape(gf_ref.shape)
    width = small_in.shape[1]
    me = lax.axis_index("dp") * 4 + lax.axis_index("fsdp")
    row = lax.broadcasted_iota(jnp.int32, (width, LANES), 0)
    lane = lane_ids(width)

    def cut(value, start):
        pick = jnp.where(row == lane + start, 1.0, 0.0)
        return lax.dot_general(
            value, pick, (((1,), (0,)), ((), ())), precision=lax.Precision.HIGHEST,
            preferred_element_type=F32,
        )

    for come, go in moves:
        come.wait()
        go.start()
    small = small_in[...]
    part = cut(small, me * 16)
    for n, ref in enumerate((g1_ref, s1_ref, g2_ref, s2_ref, bo_ref)):
        ref[...] = part[n : n + 1, : ref.shape[1]]
    each = width // 64
    part = cut(small, lax.rem(me, each) * 64)
    which = lax.broadcasted_iota(jnp.int32, part.shape, 0)
    mine = jnp.where(which == 5 + lax.div(me, each), part, 0.0)
    bi_ref[...] = jnp.sum(mine, axis=0, keepdims=True)[:, : bi_ref.shape[1]]
    for _, go in moves:
        go.wait()


ANY = pl.BlockSpec(memory_space=pl.ANY)
VM = pl.BlockSpec(memory_space=pltpu.VMEM)


def call(kernel, outs, scratch, name, ins=None, out_specs=None, collective=None):
    extra = {} if ins is None else {"in_specs": ins, "out_specs": out_specs}
    params = {} if collective is None else {"collective_id": collective, "has_side_effects": True}
    return pl.pallas_call(
        kernel,
        out_shape=[jax.ShapeDtypeStruct(s, d) for s, d in outs],
        scratch_shapes=[pltpu.SemaphoreType.DMA(s) if d is None else pltpu.VMEM(s, d) for s, d in scratch],
        compiler_params=pltpu.CompilerParams(vmem_limit_bytes=60 * 2**20, **params),
        name=name,
        **extra,
    )


def padded_features(fm):
    heads, feats, _ = fm.shape
    zero = jnp.zeros_like(fm)
    even = (jnp.arange(heads) % 2 == 0)[:, None, None]
    return jnp.concatenate(
        [jnp.where(even, fm, zero), jnp.where(even, zero, fm), jnp.ones((heads, feats, LANES), BF)],
        axis=-1,
    )


def middle(tokens, attr, cotangent, wo, wi, wf, prm, seq_weight):
    length, width = tokens.shape
    hidden = wi.shape[1]
    big, deep = (length, width), (length, hidden)
    chunks = 5 + hidden // width
    return call(
        middle_kernel,
        [(big, BF), (big, F32), (big, F32), ((16, width), F32), ((chunks, width // 64, 4, 16, width), BF)],
        [(deep, BF), (deep, BF), (big, BF), (big, BF), (big, BF), ((8, hidden), F32)],
        "middle",
    )(tokens, attr, cotangent, wo, wi, wf, prm, seq_weight)


def forward_outs(length, width, heads, feats):
    big = (length, width)
    deep = (length, heads * feats)
    return [(big, BF)] * 4 + [(deep, BF)] * 2 + [(big, F32), (big, BF), (big, F32)]


def backward_scratch(length, width):
    return [
        ((width, length), BF), ((length, 3 * width), BF),
        ((2, length, 2 * LANES), BF), ((3, length, LANES), F32),
    ]


def plain_body(
    tokens, cotangent, group_id, w_qkv, w_out, w_ffn_in, w_ffn_out,
    gain_one, shift_one, gain_two, shift_two, bias_in, bias_out, feature_matrix,
):
    gather = functools.partial(lax.all_gather, axis_name=AXES, axis=0, tiled=True)
    scatter = functools.partial(
        lax.psum_scatter, axis_name=AXES, scatter_dimension=0, tiled=True
    )
    length, width = tokens.shape
    heads, feats, head_size = feature_matrix.shape
    hidden = w_ffn_in.shape[1]
    factor = head_size ** (-0.25)
    wq, wo, wi, wf = gather(w_qkv), gather(w_out), gather(w_ffn_in), gather(w_ffn_out)
    prm = gather(jnp.stack([gain_one, shift_one, gain_two, shift_two, bias_out], axis=1))
    prm = jnp.pad(prm.T.astype(F32), ((0, 3), (0, 0)))
    wf = jnp.concatenate([wf, jnp.pad(gather(bias_in)[:, None], ((0, 0), (0, LANES - 1)))], axis=1)

    slice_seqs = lax.axis_size("dp") * group_id.shape[0]
    labels = jnp.arange(slice_seqs // 2, dtype=jnp.int32)
    onehot = (group_id[:, None] == labels[None, :]).astype(F32)
    counts = lax.psum(jnp.sum(onehot, axis=0), "dp")
    group_size = jnp.sum(onehot * counts[None, :], axis=-1)
    groups = jnp.sum((counts > 0.5).astype(F32))
    seq_weight = jnp.broadcast_to((slice_seqs / (groups * group_size))[:, None], (8, LANES))

    fx = padded_features(feature_matrix)
    h1, q, k, v, pq, pk, att, attr, den = call(
        functools.partial(forward_kernel, factor),
        forward_outs(length, width, heads, feats), [], "forward",
    )(tokens, wq, prm, fx)
    act, dy, datt, gprm, grads = middle(tokens, attr, cotangent, wo, wi, wf, prm, seq_weight)
    input_grad, gq, gprm = call(
        functools.partial(backward_kernel, factor),
        [((length, width), BF), ((width, 3 * width), BF), ((16, width), F32)],
        backward_scratch(length, width), "backward",
    )(tokens, h1, q, k, v, pq, pk, att, den, datt, dy, wq, fx, prm, gprm)
    grads = grads.reshape(-1, width // 16, 16, width)
    gf = grads[:4].transpose(1, 0, 2, 3).reshape(hidden, width)
    gi = grads[4:-1].transpose(1, 2, 0, 3).reshape(width, hidden)
    go = grads[-1].reshape(width, width)
    small = scatter(gprm[:8].T)
    gbin = scatter(gprm[5 : 5 + hidden // width].reshape(hidden))
    part = [scatter(t).astype(F32) for t in (gq, go, gi, gf)]
    return (act, input_grad, *part, *(small[:, i] for i in range(4)), gbin, small[:, 4])


def ring_body(
    tokens, cotangent, group_id, w_qkv, w_out, w_ffn_in, w_ffn_out,
    gain_one, shift_one, gain_two, shift_two, bias_in, bias_out, feature_matrix,
):
    length, width = tokens.shape
    heads, feats, head_size = feature_matrix.shape
    hidden = w_ffn_in.shape[1]
    factor = head_size ** (-0.25)
    nz = lax.axis_size("dp") // 2
    grid = (nz, 2, 2, 2)
    wide = 3 * width
    pairs = width // LANES
    chunks = 5 + hidden // width
    big, deep, tall = (length, width), (length, heads * feats), (length, hidden)
    blocks = (chunks, width // 64, 4, 16, width)
    kept = [*[(big, BF)] * 4, *[(deep, BF)] * 2]
    h1, q, k, v, pq, pk, att, den, wq, act, dy, datt, grads, fx, prm, gprm = call(
        functools.partial(gather_forward_kernel, nz, factor),
        [
            *kept, (big, F32), (big, F32), ((*grid, 16, wide), BF), (big, BF), (big, F32),
            (big, F32), (blocks, BF), ((heads, feats, 2 * LANES), BF), ((8, width), F32), ((16, width), F32),
        ],
        [
            *kept, (big, F32), (big, BF), (big, F32),
            ((*grid, 16, wide), BF), ((*grid, 16, width), BF), ((*grid, 16, hidden), BF),
            ((*grid, 64, width), BF), ((*grid, 16, LANES), BF), ((*grid, 64, LANES), BF), (big, BF),
            ((heads, feats, 2 * LANES), BF), ((16, LANES), F32), ((LANES, LANES), BF),
            (big, BF), (big, F32), (big, F32), (blocks, BF), (tall, BF), (tall, BF),
            (big, BF), (big, BF), (big, BF), ((8, hidden), F32), ((8, LANES), F32),
            ((9, 4, nz - 1), None), ((9, 4, nz - 1), None), ((9,), None), ((7,), None),
            ((pairs, 4), None), ((length // TILE, 3), None), ((chunks,), None),
        ],
        "gather_forward",
        [VM, *[ANY] * 5, VM, pl.BlockSpec(memory_space=pltpu.SMEM), *[VM] * 6],
        [*[ANY] * 14, VM, VM],
        0,
    )(
        tokens, cotangent, w_qkv, w_out, w_ffn_in, w_ffn_out, feature_matrix.swapaxes(1, 2),
        group_id, *(t[None] for t in (gain_one, shift_one, gain_two, shift_two, bias_out, bias_in)),
    )
    wq = wq.reshape(width, wide)
    input_grad, gf, gi, go, gq, total = call(
        functools.partial(reduce_backward_kernel, nz, factor),
        [
            (big, BF), ((4, 16, width), F32), ((16, hidden), F32), ((16, width), F32),
            ((16, 3 * width), F32), ((16, width), F32),
        ],
        [
            *[(big, BF)] * 5, *[(deep, BF)] * 2, *[(big, F32)] * 4, ((width, wide), BF),
            ((pairs, 8), None), ((4,), None),
            *backward_scratch(length, width),
            ((pairs, *grid, 16, 3 * LANES), BF),
            ((4, 16, width), F32), ((2 + nz, 16, width), F32),
            *Reduce.shapes(chunks, nz, 16, width),
            *Reduce.shapes(pairs, nz, 16, 3 * LANES),
            ((chunks, 4, nz - 1), None), ((chunks, 4, nz - 1), None), ((chunks,), None),
            ((pairs, 4, nz - 1), None), ((pairs, 4, nz - 1), None), ((pairs,), None),
            ((2 + nz,), None), ((2 + nz,), None),
        ],
        "reduce_backward",
        [ANY] * 12 + [VM] * 3 + [ANY],
        [VM] * 6,
        1,
    )(tokens, h1, q, k, v, pq, pk, att, den, datt, dy, wq, fx, prm, gprm, grads.reshape(chunks, *grid, 16, width))
    act, input_grad, gq, go, gi, gf, *vecs = call(
        finish_kernel,
        [
            (big, BF), (big, BF), ((16, wide), F32), ((16, width), F32), ((16, hidden), F32),
            ((64, width), F32), *[((1, 16), F32)] * 4, ((1, 64), F32), ((1, 16), F32),
        ],
        [((2, length, width), BF), ((2, length // TILE), None), ((2, length // TILE), None)],
        "finish",
        [ANY, ANY, *[VM] * 5],
        [ANY, ANY, *[VM] * 10],
    )(act, input_grad, gq, gf, gi, go, total)
    return (act, input_grad, gq, go, gi, gf, *(t[0] for t in vecs))


def solution(mesh):
    rows, vec = P(AXES, None), P(AXES)
    devices = mesh.shape["dp"] * mesh.shape["fsdp"]

    def body(*args):
        width = args[0].shape[1]
        ring = mesh.shape["fsdp"] == 4 and mesh.shape["dp"] % 2 == 0 and width == 16 * devices
        return (ring_body if ring else plain_body)(*args)

    return jax.shard_map(
        body,
        mesh=mesh,
        in_specs=(rows, rows, vec, *[rows] * 4, *[vec] * 6, P()),
        out_specs=(*[rows] * 6, *[vec] * 6),
        check_vma=False,
    )
```

```python
import functools
import math

import jax
import jax.numpy as jnp
from jax import lax
from jax.experimental import pallas as pl
from jax.experimental.pallas import tpu as pltpu
from jax.sharding import PartitionSpec as P

BLOCK = 512
EPSILON = 1e-05
TILE = 256
FEAT_TILE = 1024
FFN_TILE = 512
LANES = 128
LOG2E = 1.4426950408889634
AXES = ("dp", "fsdp")
BF = jnp.bfloat16
F32 = jnp.float32


def dot(left, right):
    return lax.dot_general(left, right, (((1,), (0,)), ((), ())), preferred_element_type=F32)


def dot_bt(left, right):
    return lax.dot_general(left, right, (((1,), (1,)), ((), ())), preferred_element_type=F32)


def dot_at(left, right):
    return lax.dot_general(left, right, (((0,), (0,)), ((), ())), preferred_element_type=F32)


def unit_rows(rows):
    row = lax.broadcasted_iota(jnp.int32, (rows, LANES), 0)
    col = lax.broadcasted_iota(jnp.int32, (rows, LANES), 1)
    return jnp.where(row == col, 1.0, 0.0).astype(BF)


def lane_ids(rows, width=LANES):
    return lax.broadcasted_iota(jnp.int32, (rows, width), 1)


def tile_at(index, size=TILE):
    return pl.ds(pl.multiple_of(index * size, size), size)


def centred(values):
    mu = jnp.mean(values, axis=-1, keepdims=True)
    cen = values - mu
    inv = lax.rsqrt(jnp.mean(cen * cen, axis=-1, keepdims=True) + EPSILON)
    return cen * inv, inv


def norm_back(grad, unit, inv, gain):
    e = grad * gain
    return inv * (
        e
        - jnp.mean(e, axis=-1, keepdims=True)
        - unit * jnp.mean(e * unit, axis=-1, keepdims=True)
    )


def causal(values, offset):
    row = lax.broadcasted_iota(jnp.int32, values.shape, 0)
    col = lax.broadcasted_iota(jnp.int32, values.shape, 1)
    return jnp.where(col <= row + offset, values, 0.0).astype(BF)


def anticausal(values):
    row = lax.broadcasted_iota(jnp.int32, values.shape, 0)
    col = lax.broadcasted_iota(jnp.int32, values.shape, 1)
    return jnp.where(col >= row, values, 0.0).astype(BF)


MESH_ID = pl.DeviceIdType.MESH


SUMS = {
    "grad0": ((4, 0),),
    "chunk1": ((4, 1),),
    "grad1": ((5, 0),),
    "chunk2": ((5, 1), (4, 2)),
    "grad2": ((6, 0),),
    "chunk3": ((6, 1), (5, 2), (4, 3)),
    "grad3": ((7, 0), (0, 0), (1, 0), (2, 0), (3, 0)),
    "final": ((7, 1), (0, 1), (6, 2), (5, 3), (4, 4)),
    "grad_o": ((8, 0),),
    "b0:1": ((1, 1),),
    "b0:2": ((7, 2), (6, 3)),
    "b0:3": ((2, 1),),
    "b0:4": ((0, 2), (5, 4)),
    "b0:5": ((3, 1),),
    "b0:7": ((8, 1), (1, 2), (7, 3)),
    "b1:1": ((2, 2), (6, 4)),
    "b1:2": ((0, 3),),
    "b1:3": ((3, 2), (1, 3)),
    "b1:5": ((8, 2), (7, 4)),
    "b1:6": ((2, 3), (0, 4)),
    "b1:7": ((3, 3),),
    "b2:0": ((1, 4), (8, 3)),
    "b2:3": ((2, 4),),
    "b2:4": ((3, 4),),
    "b2:5": ((8, 4),),
}
OWN_SUMS = {
    "b1:2": ((0, 1),),
    "b2:1": ((0, 2),),
    "b2:2": ((1, 1),),
    "b2:6": ((0, 3),),
    "b3:1": ((1, 2),),
    "b3:2": ((2, 1),),
    "b3:4": ((0, 4),),
    "b3:6": ((1, 3),),
}
PLAN = {
    "start": (("s", 1), ("q0", 1), ("q1", 1), ("q2", 1), ("s", 2), ("q3", 1), ("q0", 2), ("o", 1), ("q1", 2), ("i0", 1), ("q2", 2), ("s", 3), ("q3", 2), ("o", 2), ("q0", 3), ("i0", 2), ("q1", 3),),
    "0:0": (("f0", 1), ("f1", 1), ("i1", 1), ("f2", 1),),
    "0:1": (("q2", 3), ("f3", 1),),
    "0:4": (("i2", 1),),
    "0:8": (("q3", 3),),
    "0:9": (("i3", 1),),
    "1:3": (("i0", 3),),
    "1:6": (("o", 3),),
    "1:8": (("f1", 2),),
    "1:11": (("f0", 2),),
    "2:0": (("f3", 2),),
    "2:4": (("i1", 2),),
    "2:5": (("i2", 2),),
    "2:8": (("f2", 2),),
    "2:10": (("i3", 2),),
    "3:7": (("f1", 3),),
    "3:9": (("f0", 3),),
    "chunk0": (("i1", 3), ("i2", 3), ("f3", 3),),
    "grad0": (("f2", 3),),
    "chunk1": (("i3", 3),),
}
Y_FIRST = {"s", "q0", "q2", "q3", "o", "i2", "i3", "f1", "f3"}


class Place:
    def __init__(self, nz):
        dp, fs = lax.axis_index("dp"), lax.axis_index("fsdp")
        self.nz = nz
        self.z, self.y = lax.div(dp, 2), lax.rem(dp, 2)
        self.x, self.c = lax.div(fs, 2), lax.rem(fs, 2)

    def device(self, z=None, y=None, x=None, c=None):
        z, y = self.z if z is None else z, self.y if y is None else y
        x, c = self.x if x is None else x, self.c if c is None else c
        return {"dp": z * 2 + y, "fsdp": x * 2 + c}

    def up(self, k):
        return lax.rem(self.z + k, self.nz)

    def down(self, k):
        return lax.rem(self.z + self.nz - k, self.nz)

    def peers(self):
        yield self.device(c=1 - self.c)
        yield self.device(x=1 - self.x)
        yield self.device(y=1 - self.y)
        yield self.device(x=1 - self.x, c=1 - self.c)
        for k in range(1, self.nz):
            yield self.device(z=self.up(k))
            yield self.device(z=self.up(k), y=1 - self.y)

    def near(self):
        yield self.device(c=1 - self.c)
        yield self.device(x=1 - self.x)
        yield self.device(x=1 - self.x, c=1 - self.c)

    def far(self):
        yield self.device(y=1 - self.y)
        for k in range(1, self.nz):
            yield self.device(z=self.up(k))
            yield self.device(z=self.up(k), y=1 - self.y)

    def barrier(self):
        sem = pltpu.get_barrier_semaphore()
        for peer in self.peers():
            pl.semaphore_signal(sem, inc=1, device_id=peer, device_id_type=MESH_ID)
        pl.semaphore_wait(sem, 2 + 2 * self.nz)


def remote(src, dst, send, recv, peer):
    return pltpu.make_async_remote_copy(
        src_ref=src, dst_ref=dst, send_sem=send, recv_sem=recv, device_id=peer,
        device_id_type=MESH_ID,
    )


class Gather:
    def __init__(self, place, shard, whole, view, sems, m, y_first, plane=None, base=None):
        self.place, self.shard, self.whole, self.view = place, shard, whole, view
        self.send, self.recv, self.own = sems
        self.m = m
        self.y_first = y_first
        self.plane, self.base = plane, base

    def at(self, *index):
        return self.whole.at[(*index, *self.view)]

    def hops(self, stage):
        p = self.place
        every = slice(None)
        zs = every if self.plane is None else self.plane
        if stage == 0:
            src = self.shard.at[self.view]
            for k in range(1, p.nz):
                yield src, self.at(p.z, p.y, p.x, p.c), self.at(p.down(k), p.y, p.x, p.c), p.device(z=p.up(k))
        elif stage == 3:
            mine = self.at(zs, every, every, p.c)
            yield mine, mine, self.at(zs, every, every, 1 - p.c), p.device(c=1 - p.c)
        elif stage == 1:
            mine = self.at(zs, p.y, p.x, p.c)
            if self.y_first:
                yield mine, mine, self.at(zs, 1 - p.y, p.x, p.c), p.device(y=1 - p.y)
            else:
                yield mine, mine, self.at(zs, p.y, 1 - p.x, p.c), p.device(x=1 - p.x)
        elif self.y_first:
            mine = self.at(zs, every, p.x, p.c)
            yield mine, mine, self.at(zs, every, 1 - p.x, p.c), p.device(x=1 - p.x)
        else:
            mine = self.at(zs, p.y, every, p.c)
            yield mine, mine, self.at(zs, 1 - p.y, every, p.c), p.device(y=1 - p.y)

    def copies(self, stage, arriving):
        for k, (src, dst, land, peer) in enumerate(self.hops(stage)):
            yield remote(
                src, land if arriving else dst, self.send.at[self.m, stage, k],
                self.recv.at[self.m, stage, k], peer,
            )

    def local(self):
        p = self.place
        return pltpu.make_async_copy(
            self.shard.at[self.view], self.at(p.z, p.y, p.x, p.c), self.own.at[self.m]
        )

    def start(self):
        for copy in self.copies(0, False):
            copy.start()
        self.local().start()

    def arrive(self, stage):
        for copy in self.copies(stage, True):
            copy.wait_recv()

    def enter(self):
        if self.plane is None:
            self.arrive(0)
            self.local().wait()
            return
        p = self.place
        hop = lax.rem(p.z + p.nz - self.plane, p.nz)

        @pl.when(hop == 0)
        def _():
            self.base.local().wait()

        @pl.when(hop != 0)
        def _():
            k = jnp.maximum(hop, 1) - 1
            remote(
                self.shard.at[self.view], self.at(self.plane, p.y, p.x, p.c),
                self.send.at[self.base.m, 0, k], self.recv.at[self.base.m, 0, k],
                p.device(z=p.up(1)),
            ).wait_recv()

    def step(self, stage):
        if stage == 1:
            self.enter()
        else:
            self.arrive(stage - 1)
        for copy in self.copies(stage, False):
            copy.start()

    def drain(self, stages=range(4)):
        for stage in stages:
            for copy in self.copies(stage, False):
                copy.wait_send()


class Reduce:
    def __init__(self, place, source, bufs, sems, write):
        self.place, self.source = place, source
        self.r0, self.r1, self.r2, self.r3 = bufs
        self.send, self.recv = sems
        self.write = write

    def hops(self, stage, c, x_first):
        p = self.place
        every = slice(None)
        if stage == 0:
            yield self.source.at[c, every, every, every, 1 - p.c], self.r0.at[c], p.device(c=1 - p.c)
        elif stage == 1:
            if x_first:
                yield self.r0.at[c, every, every, 1 - p.x], self.r1.at[c], p.device(x=1 - p.x)
            else:
                yield self.r0.at[c, every, 1 - p.y], self.r1.at[c], p.device(y=1 - p.y)
        elif stage == 2:
            if x_first:
                yield self.r1.at[c, every, 1 - p.y], self.r2.at[c], p.device(y=1 - p.y)
            else:
                yield self.r1.at[c, every, 1 - p.x], self.r2.at[c], p.device(x=1 - p.x)
        else:
            for k in range(1, p.nz):
                yield self.r2.at[c, p.up(k)], self.r3.at[c, k - 1], p.device(z=p.up(k))

    def copies(self, stage, c, x_first):
        for k, (src, dst, peer) in enumerate(self.hops(stage, c, x_first)):
            yield remote(src, dst, self.send.at[c, stage, k], self.recv.at[c, stage, k], peer)

    def step(self, stage, c, x_first=False):
        p = self.place
        if stage:
            for copy in self.copies(stage - 1, c, x_first):
                copy.wait_recv()
        if stage == 1:
            mine = self.source[c, :, :, :, p.c]
            self.r0[c] = mine + self.r0[c]
        elif stage == 2:
            mine = self.r0[c, :, :, p.x] if x_first else self.r0[c, :, p.y]
            self.r1[c] = mine + self.r1[c]
        elif stage == 3:
            mine = self.r1[c, :, p.y] if x_first else self.r1[c, :, p.x]
            self.r2[c] = mine + self.r2[c]
        elif stage == 4:
            total = self.r2[c, p.z].astype(F32)
            for k in range(p.nz - 1):
                total = total + self.r3[c, k].astype(F32)
            self.write(c, total)
            return
        for copy in self.copies(stage, c, x_first):
            copy.start()

    def drain(self, c, x_first=False):
        for stage in range(4):
            for copy in self.copies(stage, c, x_first):
                copy.wait_send()

    @staticmethod
    def shapes(n, nz, rows, cols):
        return [
            ((n, nz, 2, 2, rows, cols), BF), ((n, nz, 2, rows, cols), BF),
            ((n, nz, rows, cols), BF), ((n, nz - 1, rows, cols), BF),
        ]


def project_rows(i, x_ref, wq, prm_ref, h_ref, q_ref, k_ref, v_ref, factor):
    rows = tile_at(i)
    unit, _ = centred(x_ref[rows, :].astype(F32))
    h = (unit * prm_ref[0:1, :] + prm_ref[1:2, :]).astype(BF)
    h_ref[rows, :] = h
    width = h.shape[1]
    qkv = dot(h, wq)
    q_ref[rows, :] = (qkv[:, :width] * factor).astype(BF)
    k_ref[rows, :] = (qkv[:, width : 2 * width] * factor).astype(BF)
    v_ref[rows, :] = qkv[:, 2 * width :].astype(BF)


def attend_pair(
    p, q_ref, k_ref, v_ref, fx_ref, pq_ref, pk_ref, attr_ref, den_ref, low_ref,
    site=lambda j: None,
):
    length = q_ref.shape[0]
    feats = fx_ref.shape[1]
    lanes = tile_at(p, LANES)
    shift = 0.5 * math.log2(feats)
    cols = [tile_at(2 * p + hh, feats) for hh in range(2)]
    step = FEAT_TILE
    for hh in range(2):
        fm = fx_ref[2 * p + hh][:, :LANES]
        for src, dst in ((q_ref, pq_ref), (k_ref, pk_ref)):
            for t in range(length // step):
                rows = slice(t * step, (t + 1) * step)
                part = src[rows, lanes]
                scores = dot_bt(part, fm)
                wide = jnp.where(lane_ids(step) // 64 == hh, part.astype(F32), 0.0)
                square = jnp.sum(wide * wide, axis=-1, keepdims=True)
                feat = jnp.exp2(scores * LOG2E - (square * (0.5 * LOG2E) + shift))
                dst[rows, cols[hh]] = feat.astype(BF)
            site(2 * hh + int(src is k_ref))
    ones = jnp.ones((length, LANES), BF)
    vx = jnp.concatenate([v_ref[:, lanes], ones], axis=1)
    states = [None, None]
    for b in range(length // BLOCK):
        base = b * BLOCK
        for i in range(BLOCK // TILE):
            rows = slice(base + i * TILE, base + (i + 1) * TILE)
            keys = slice(base, base + (i + 1) * TILE)
            got = []
            for hh in range(2):
                pq = pq_ref[rows, cols[hh]]
                weights = causal(dot_bt(pq, pk_ref[keys, cols[hh]]), i * TILE)
                both = dot(weights, vx[keys])
                if b:
                    both = both + dot(pq, low_ref[2 * p + hh, b - 1])
                got.append(both)
            first = lane_ids(TILE) < 64
            num = jnp.where(first, got[0][:, :LANES], got[1][:, :LANES])
            den = jnp.where(first, got[0][:, LANES:], got[1][:, LANES:])
            attr_ref[rows, lanes] = (num / den).astype(BF)
            den_ref[rows, lanes] = den
            site(4 + b * (BLOCK // TILE) + i)
        if base + BLOCK < length:
            block = slice(base, base + BLOCK)
            for hh in range(2):
                more = dot_at(pk_ref[block, cols[hh]], vx[block])
                states[hh] = more if b == 0 else states[hh] + more
                low_ref[2 * p + hh, b] = states[hh].astype(BF)


def forward_kernel(
    factor, x_ref, wq_ref, prm_ref, fx_ref,
    h_ref, q_ref, k_ref, v_ref, pq_ref, pk_ref, attr_ref, den_ref, low_ref,
):
    def rows(i, carry):
        project_rows(i, x_ref, wq_ref[...], prm_ref, h_ref, q_ref, k_ref, v_ref, factor)
        return carry

    lax.fori_loop(0, x_ref.shape[0] // TILE, rows, 0)

    def pair(p, carry):
        attend_pair(
            p, q_ref, k_ref, v_ref, fx_ref, pq_ref, pk_ref, attr_ref, den_ref, low_ref
        )
        return carry

    lax.fori_loop(0, x_ref.shape[1] // LANES, pair, 0)


def ffn_rows(
    t, x_ref, attr_ref, cot_ref, wo, wi, wf, prm_ref, bin_ref, seq_ref,
    act_ref, dy_ref, datt_ref, gprm_ref, hid_ref, du_ref, h_ref, gr_ref, dor_ref, bin_row=0,
):
    width = x_ref.shape[1]
    chunk = width
    rows = tile_at(t, FFN_TILE)
    y = x_ref[rows, :].astype(F32) + dot(attr_ref[rows, :], wo())
    unit, inv = centred(y)
    gain = prm_ref[2:3, :]
    h = (unit * gain + prm_ref[3:4, :]).astype(BF)
    h_ref[rows, :] = h
    g = cot_ref[rows, :].astype(F32) * seq_ref[0:1, 0:1]
    gr = g.astype(BF)
    gr_ref[rows, :] = gr
    out = y + prm_ref[4:5, :]
    dh = jnp.zeros((FFN_TILE, width), F32)
    for c in range(hid_ref.shape[1] // chunk):
        cs = slice(c * chunk, (c + 1) * chunk)
        u = dot(h, wi(cs)) + bin_ref[bin_row : bin_row + 1, cs]
        cdf = 0.5 + 0.5 * lax.erf(u * math.sqrt(0.5))
        slope = cdf + u * jnp.exp2(u * u * (-0.5 * LOG2E)) * (1.0 / math.sqrt(2.0 * math.pi))
        hid = (u * cdf).astype(BF)
        hid_ref[rows, cs] = hid
        out = out + dot(hid, wf(c))
        du = (dot_bt(gr, wf(c)) * slope).astype(BF)
        du_ref[rows, cs] = du
        gprm_ref[5 + c : 6 + c, :] += jnp.sum(du.astype(F32), axis=0, keepdims=True)
        dh = dh + dot_bt(du, wi(cs))
    act_ref[rows, :] = out.astype(BF)
    gprm_ref[2:3, :] += jnp.sum(dh * unit, axis=0, keepdims=True)
    gprm_ref[3:4, :] += jnp.sum(dh, axis=0, keepdims=True)
    gprm_ref[4:5, :] += jnp.sum(g, axis=0, keepdims=True)
    dy = g + norm_back(dh, unit, inv, gain)
    dy_ref[rows, :] = dy
    dor = dy.astype(BF)
    dor_ref[rows, :] = dor
    datt_ref[rows, :] = dot_bt(dor, wo())


def ffn_norm(t, x_ref, attr_ref, cot_ref, wo, prm_ref, seq_ref, y_ref, h_ref, gr_ref):
    rows = tile_at(t, FFN_TILE)
    y = x_ref[rows, :].astype(F32) + dot(attr_ref[rows, :], wo)
    y_ref[rows, :] = y
    unit, _ = centred(y)
    h_ref[rows, :] = (unit * prm_ref[2:3, :] + prm_ref[3:4, :]).astype(BF)
    gr_ref[rows, :] = (cot_ref[rows, :].astype(F32) * seq_ref[0:1, 0:1]).astype(BF)


def ffn_chunk(t, c, wi, wf, bias, h_ref, gr_ref, hid_ref, du_ref, gprm_ref):
    rows = tile_at(t, FFN_TILE)
    width = h_ref.shape[1]
    cs = slice(c * width, (c + 1) * width)
    u = dot(h_ref[rows, :], wi) + bias
    cdf = 0.5 + 0.5 * lax.erf(u * math.sqrt(0.5))
    slope = cdf + u * jnp.exp2(u * u * (-0.5 * LOG2E)) * (1.0 / math.sqrt(2.0 * math.pi))
    hid_ref[rows, cs] = (u * cdf).astype(BF)
    du = (dot_bt(gr_ref[rows, :], wf) * slope).astype(BF)
    du_ref[rows, cs] = du
    gprm_ref[5 + c : 6 + c, :] += jnp.sum(du.astype(F32), axis=0, keepdims=True)


def ffn_final(
    t, cot_ref, wo, wi, wf, prm_ref, seq_ref, y_ref, hid_ref, du_ref,
    act_ref, dy_ref, dor_ref, datt_ref, gprm_ref,
):
    rows = tile_at(t, FFN_TILE)
    y = y_ref[rows, :]
    act_ref[rows, :] = (y + dot(hid_ref[rows, :], wf) + prm_ref[4:5, :]).astype(BF)
    dh = dot_bt(du_ref[rows, :], wi)
    unit, inv = centred(y)
    g = cot_ref[rows, :].astype(F32) * seq_ref[0:1, 0:1]
    gprm_ref[2:3, :] += jnp.sum(dh * unit, axis=0, keepdims=True)
    gprm_ref[3:4, :] += jnp.sum(dh, axis=0, keepdims=True)
    gprm_ref[4:5, :] += jnp.sum(g, axis=0, keepdims=True)
    dy = g + norm_back(dh, unit, inv, prm_ref[2:3, :])
    dy_ref[rows, :] = dy
    dor = dy.astype(BF)
    dor_ref[rows, :] = dor
    datt_ref[rows, :] = dot_bt(dor, wo)


def put_rows(g_ref, chunk, c, value):
    if len(g_ref.shape) == 5:
        g_ref[chunk, c] = value
    else:
        g_ref[chunk, lax.div(c, 2), lax.rem(c, 2)] = value.reshape(2, 2, *value.shape[1:])


def grads_out(c, hid_ref, gr_ref, g_ref):
    width = gr_ref.shape[1]
    grad = dot_at(hid_ref[:, tile_at(c)], gr_ref[...]).astype(BF)
    grad = grad.reshape(4, 4, 16, width)
    for q in range(4):
        put_rows(g_ref, q, c, grad[:, q])


def grads_in(c, h_ref, du_ref, attr_ref, dor_ref, g_ref):
    width = h_ref.shape[1]
    count = du_ref.shape[1] // width
    cs = tile_at(c)
    at = pl.ds(c * 4, 4)
    grad = dot_at(h_ref[:, cs], du_ref[...]).astype(BF)
    for k in range(count):
        g_ref[4 + k, at] = grad[:, k * width : (k + 1) * width].reshape(4, 4, 16, width)
    grad = dot_at(attr_ref[:, cs], dor_ref[...]).astype(BF)
    g_ref[4 + count, at] = grad.reshape(4, 4, 16, width)


def loop(start, stop, step):
    def run(i, carry):
        step(i)
        return carry

    lax.fori_loop(start, stop, run, 0)


def middle_kernel(
    x_ref, attr_ref, cot_ref, wo_ref, wi_ref, wf_ref, prm_ref, seq_ref,
    act_ref, dy_ref, datt_ref, gprm_ref, g_ref,
    hid_ref, du_ref, h_ref, gr_ref, dor_ref, bin_ref,
):
    length, width = x_ref.shape
    gprm_ref[...] = jnp.zeros_like(gprm_ref)
    bin_ref[...] = dot_bt(unit_rows(8), wf_ref[:, width:])
    loop(0, length // FFN_TILE, lambda t: ffn_rows(
        t, x_ref, attr_ref, cot_ref, lambda: wo_ref[...], lambda cs: wi_ref[:, cs],
        lambda c: wf_ref[c * width : (c + 1) * width, :width], prm_ref, bin_ref, seq_ref,
        act_ref, dy_ref, datt_ref, gprm_ref, hid_ref, du_ref, h_ref, gr_ref, dor_ref,
    ))
    loop(0, hid_ref.shape[1] // TILE, lambda c: grads_out(c, hid_ref, gr_ref, g_ref))
    loop(0, width // TILE, lambda c: grads_in(c, h_ref, du_ref, attr_ref, dor_ref, g_ref))


def back_pair(
    p, factor, q_ref, k_ref, v_ref, pq_ref, pk_ref, att_ref, den_ref, datt_ref, fx_ref, low_ref,
    ht_ref, dqkv_ref, dn_ref, e_ref, da_ref, tick, store,
):
    length = q_ref.shape[0]
    feats = fx_ref.shape[1]
    lanes = tile_at(p, LANES)
    blocks = length // BLOCK
    cols = [tile_at(2 * p + hh, feats) for hh in range(2)]
    two = jnp.where(lane_ids(length) < 2, 1.0, 0.0).astype(BF)
    v2 = jnp.concatenate([v_ref[:, lanes], two], axis=1)
    for t in range(length // TILE):
        rows = slice(t * TILE, (t + 1) * TILE)
        dn = datt_ref[rows, lanes] / den_ref[rows, lanes]
        prod = dn * att_ref[rows, lanes].astype(F32)
        lane = lane_ids(TILE)
        for hh in range(2):
            mine = lane // 64 == hh
            dden = -jnp.sum(jnp.where(mine, prod, 0.0), axis=-1, keepdims=True)
            high = dden.astype(BF).astype(F32)
            extra = jnp.where(lane == 0, high, jnp.where(lane == 1, dden - high, 0.0))
            dn_ref[hh, rows, :LANES] = jnp.where(mine, dn, 0.0).astype(BF)
            dn_ref[hh, rows, LANES:] = extra.astype(BF)
    for hh in range(2):
        fx = fx_ref[2 * p + hh]
        back = [None] * blocks
        total = None
        for b in range(blocks - 1, 0, -1):
            block = slice(b * BLOCK, (b + 1) * BLOCK)
            more = dot_at(pq_ref[block, cols[hh]], dn_ref[hh, block, :])
            total = more if total is None else total + more
            dz = total[:, LANES : LANES + 1] + total[:, LANES + 1 : LANES + 2]
            high = dz.astype(BF).astype(F32)
            lane = lane_ids(feats)
            extra = jnp.where(lane == 0, high, jnp.where(lane == 1, dz - high, 0.0))
            back[b - 1] = jnp.concatenate([total[:, :LANES], extra], axis=1).astype(BF)

        def put(value, rows, at, hh=hh):
            where = pl.ds(pl.multiple_of((3 * p + at) * LANES, LANES), LANES)
            if hh:
                mine = lane_ids(value.shape[0]) >= 64
                value = jnp.where(mine, value, dqkv_ref[rows, where].astype(F32))
            dqkv_ref[rows, where] = value.astype(BF)

        for b in range(blocks):
            base = b * BLOCK
            for i in range(BLOCK // TILE):
                rows = slice(base + i * TILE, base + (i + 1) * TILE)
                keys = slice(base, base + (i + 1) * TILE)
                dn = dn_ref[hh, rows, :]
                da = causal(dot_bt(dn, v2[keys]), i * TILE)
                da_ref[i * TILE : (i + 1) * TILE, : (i + 1) * TILE] = da
                grad = dot(da, pk_ref[keys, cols[hh]])
                if b:
                    grad = grad + dot_bt(dn, low_ref[2 * p + hh, b - 1])
                e_ref[0, rows, :] = (grad * pq_ref[rows, cols[hh]].astype(F32)).astype(BF)
            tick((hh * blocks + b) * 2)
            for i in range(BLOCK // TILE):
                rows = slice(base + i * TILE, base + (i + 1) * TILE)
                later = slice(base + i * TILE, base + BLOCK)
                pk = pk_ref[rows, cols[hh]]
                pql = pq_ref[later, cols[hh]]
                grad = dot_at(da_ref[i * TILE :, i * TILE : (i + 1) * TILE], pql)
                at = anticausal(dot_bt(pk, pql))
                dv = dot(at, dn_ref[hh, later, :LANES])
                if b < blocks - 1:
                    grad = grad + dot_bt(v2[rows], back[b])
                    dv = dv + dot(pk, back[b][:, :LANES])
                e_ref[1, rows, :] = (grad * pk.astype(F32)).astype(BF)
                put(dv, rows, 2)
            tick((hh * blocks + b) * 2 + 1)
        for at, src in ((0, q_ref), (1, k_ref)):
            res = dot(e_ref[at], fx)
            out = (res[:, :LANES] - src[:, lanes].astype(F32) * res[:, LANES:]) * factor
            put(out, slice(0, length), at)
    store(dot(ht_ref[...], dqkv_ref[:, tile_at(p, 3 * LANES)]).astype(BF))


def input_rows(t, x_ref, wq, prm_ref, dqkv_ref, dy_ref, out_ref, gprm_ref):
    rows = tile_at(t, FFN_TILE)
    dh = dot_bt(dqkv_ref[rows, : wq.shape[1]], wq)
    unit, inv = centred(x_ref[rows, :].astype(F32))
    gprm_ref[0:1, :] += jnp.sum(dh * unit, axis=0, keepdims=True)
    gprm_ref[1:2, :] += jnp.sum(dh, axis=0, keepdims=True)
    out_ref[rows, :] = (dy_ref[rows, :] + norm_back(dh, unit, inv, prm_ref[0:1, :])).astype(BF)


def flip_rows(h_ref, ht_ref):
    for t in range(h_ref.shape[0] // TILE):
        rows = slice(t * TILE, (t + 1) * TILE)
        ht_ref[:, rows] = h_ref[rows, :].T


def backward_kernel(
    factor, x_ref, h_ref, q_ref, k_ref, v_ref, pq_ref, pk_ref, att_ref, den_ref, datt_ref, dy_ref,
    wq_ref, fx_ref, prm_ref, gin_ref, low_ref,
    out_ref, gq_ref, gprm_ref,
    ht_ref, dqkv_ref, dn_ref, e_ref, da_ref,
):
    gprm_ref[...] = gin_ref[...]
    flip_rows(h_ref, ht_ref)

    def pair(p, carry):
        def store(value):
            gq_ref[:, tile_at(p, 3 * LANES)] = value

        back_pair(
            p, factor, q_ref, k_ref, v_ref, pq_ref, pk_ref, att_ref, den_ref, datt_ref, fx_ref, low_ref,
            ht_ref, dqkv_ref, dn_ref, e_ref, da_ref, lambda j: None, store,
        )
        return carry

    lax.fori_loop(0, x_ref.shape[1] // LANES, pair, 0)

    def rows(t, carry):
        input_rows(t, x_ref, wq_ref[...], prm_ref, dqkv_ref, dy_ref, out_ref, gprm_ref)
        return carry

    lax.fori_loop(0, x_ref.shape[0] // FFN_TILE, rows, 0)


def sequence_weight(small, seq_ref):
    nf = 4
    me = lax.axis_index("dp") * nf + lax.axis_index("fsdp")
    row = lax.broadcasted_iota(jnp.int32, small.shape, 0)
    lane = lane_ids(small.shape[0]).astype(F32)
    peer = lax.div(row, 16)
    ids = small[:, 5:6].astype(F32)
    hit = (lane == ids) & (lax.rem(row, 16) == 0)
    counts = jnp.sum(
        jnp.where(hit & (lax.rem(peer, nf) == lax.axis_index("fsdp")), 1.0, 0.0),
        axis=0, keepdims=True,
    )
    mine = jnp.sum(jnp.where(hit & (peer == me), 1.0, 0.0), axis=0, keepdims=True)
    size = jnp.sum(counts * mine, axis=1, keepdims=True)
    groups = jnp.sum(jnp.where(counts > 0.5, 1.0, 0.0), axis=1, keepdims=True)
    members = lax.axis_size("dp")
    seq_ref[...] = jnp.broadcast_to(members / (groups * size), seq_ref.shape)


class Columns:
    def __init__(self, ref, start, size):
        self.ref, self.start, self.size = ref, start, size

    def where(self, index):
        n, *rest = index if isinstance(index, tuple) else (index,)
        rows, cols = [*rest, slice(None), slice(None)][:2]
        base = self.start + n * self.size
        low, high = cols.start or 0, self.size if cols.stop is None else cols.stop
        return rows, slice(base + low, base + high)

    def __getitem__(self, index):
        return self.ref[self.where(index)]

    def __setitem__(self, index, value):
        self.ref[self.where(index)] = value


class Total:
    def __init__(self, place, ref, part, near, far, sems):
        self.place, self.ref, self.part, self.near, self.far = place, ref, part, near, far
        self.send, self.recv = sems

    def copies(self, stage):
        peers = self.place.far() if stage else self.place.near()
        src, dst = (self.part, self.far) if stage else (self.ref, self.near)
        for k, peer in enumerate(peers):
            yield remote(src, dst.at[k], self.send.at[stage, k], self.recv.at[stage, k], peer)

    def start(self):
        for copy in self.copies(0):
            copy.start()

    def turn(self):
        for copy in self.copies(0):
            copy.wait_recv()
        self.part[...] = self.ref[...] + sum(self.near[k] for k in range(self.near.shape[0]))
        for copy in self.copies(1):
            copy.start()

    def result(self):
        for copy in self.copies(1):
            copy.wait_recv()
        return self.part[...] + sum(self.far[k] for k in range(self.far.shape[0]))

    def drain(self):
        for stage in range(2):
            for copy in self.copies(stage):
                copy.wait_send()


def layer_kernel(
    nz, factor, x_ref, cot_in, wqs_ref, wos_ref, wis_ref, wfs_ref, fm_ref, id_ref,
    g1_ref, s1_ref, g2_ref, s2_ref, bo_ref, bi_ref,
    act_out, grad_out, partq_ref, gf_ref, gi_ref, go_ref, rest_out, first_out,
    h_ref, q_ref, k_ref, v_ref, pq_ref, pk_ref, attr_ref, den_ref, low_ref,
    wqt_ref, wq_ref, wo_ref, wi_ref, wf_ref, sp_ref, cot_ref, fx_ref, vec_ref, col_ref, prm_ref,
    act_ref, dy_ref, y_ref, g_ref, gprm_ref, hid_ref, du_ref, h2_ref, gr_ref, dor_ref,
    bin_ref, seq_ref, lhs_ref, gq_ref,
    b0, b1, b2, b3, c0, c1, c2, c3,
    rest_ref, rest_part, rest_near, rest_far, first_ref, first_part, first_near, first_far,
    send, recv, own, big_send, big_recv, q_send, q_recv, rest_send, rest_recv, first_send, first_recv,
    local_sem, tile_sem,
):
    length, width = x_ref.shape
    hidden = hid_ref.shape[1]
    place = Place(nz)
    every = slice(None)
    sems = (send, recv, own)
    pairs, tiles, parts = width // LANES, length // TILE, hidden // width
    slabs = length // FFN_TILE

    def gather(name, shard, whole, view, m, plane=None, base=None):
        return Gather(place, shard, whole, view, sems, m, name in Y_FIRST, plane, base)

    both = (every, every)
    sp = gather("s", col_ref, sp_ref, (slice(0, 16), every), 0)
    o = gather("o", wos_ref, wo_ref, both, 1)
    f = gather("f", wfs_ref, wf_ref, both, 2)
    wq = [gather(f"q{p}", wqt_ref.at[p], wq_ref.at[p], both, 3 + p) for p in range(pairs)]
    wi = [
        gather(f"i{c}", wis_ref, wi_ref, (every, slice(c * width, (c + 1) * width)), 3 + pairs + c)
        for c in range(parts)
    ]
    wf = [
        gather(f"f{c}", wfs_ref, wf_ref, both, 3 + pairs + parts + c, c, f) for c in range(parts)
    ]
    named = {"s": sp, "o": o}
    for n in range(pairs):
        named[f"q{n}"] = wq[n]
    for n in range(parts):
        named[f"i{n}"] = wi[n]
        named[f"f{n}"] = wf[n]

    def write(c, value):
        if c < 4:
            gf_ref[c] = value
        elif c < 4 + parts:
            gi_ref[:, (c - 4) * width : (c - 3) * width] = value
        else:
            go_ref[...] = value

    def write_q(c, value):
        for at in range(3):
            where = pl.ds(pl.multiple_of(c * LANES + at * width, LANES), LANES)
            partq_ref[:, where] = value[:, at * LANES : (at + 1) * LANES]

    grid = (nz, 2, 2, 2)
    big = Reduce(place, g_ref, (b0, b1, b2, b3), (big_send, big_recv), write)
    mine = Reduce(place, gq_ref, (c0, c1, c2, c3), (q_send, q_recv), write_q)
    rest = Total(place, rest_ref, rest_part, rest_near, rest_far, (rest_send, rest_recv))
    first = Total(place, first_ref, first_part, first_near, first_far, (first_send, first_recv))
    cot_copy = pltpu.make_async_copy(cot_in, cot_ref, local_sem)

    def slab_out(t, src, dst, n):
        rows = tile_at(t, FFN_TILE)
        return pltpu.make_async_copy(src.at[rows], dst.at[rows], tile_sem.at[n, t])

    def at_site(name):
        for who, stage in PLAN.get(name, ()):
            named[who].step(stage)
        for c, stage in SUMS.get(name, ()):
            big.step(stage, c, c % 2 == 0)
        for c, stage in OWN_SUMS.get(name, ()):
            mine.step(stage, c)

    def sites(p, prefix):
        def site(j):
            for n in range(pairs):
                name = f"{prefix}{n}:{j}"
                if name in PLAN or name in SUMS or name in OWN_SUMS:
                    pl.when(p == n)(functools.partial(at_site, name))

        return site

    vec_ref[...] = jnp.zeros_like(vec_ref)
    for n, ref in enumerate((g1_ref, s1_ref, g2_ref, s2_ref, bo_ref)):
        vec_ref[n : n + 1, : ref.shape[1]] = ref[...].astype(F32)
    vec_ref[5:6, :] = jnp.full((1, LANES), id_ref[0], jnp.int32).astype(F32)
    for n in range(4):
        vec_ref[8 + n : 9 + n, :16] = bi_ref[:, n * 16 : (n + 1) * 16].astype(F32)
    col_ref[...] = dot_at(vec_ref[...].astype(BF), unit_rows(16)).astype(BF)
    for p in range(pairs):
        for n in range(3):
            at = n * width + p * LANES
            wqt_ref[p, :, n * LANES : (n + 1) * LANES] = wqs_ref[:, at : at + LANES]
    place.barrier()
    for g in (sp, *wq, o, wi[0], f, *wi[1:]):
        g.start()
    cot_copy.start()
    head_size, feats = fm_ref.shape[1:]
    for n in range(fm_ref.shape[0]):
        row = lax.broadcasted_iota(jnp.int32, (head_size, LANES), 0)
        place_at = jnp.where(lane_ids(head_size) == row + (n % 2) * head_size, 1.0, 0.0).astype(BF)
        fx_ref[n, :, :LANES] = dot_at(fm_ref[n], place_at).astype(BF)
        fx_ref[n, :, LANES:] = jnp.ones((feats, LANES), BF)
    at_site("start")
    sp.arrive(3)
    small = sp_ref[...].reshape(width, LANES)
    prm = dot_bt(unit_rows(16), small)
    prm_ref[...] = prm[:8]
    sequence_weight(small, seq_ref)
    for c in range(parts):
        for n in range(4):
            lhs_ref[n, c : c + 1, :] = prm[8 + n : 9 + n, c * LANES : (c + 1) * LANES]
    row = lax.broadcasted_iota(jnp.int32, (LANES, width), 0)
    col = lax.broadcasted_iota(jnp.int32, (LANES, width), 1)
    bias = jnp.zeros((8, width), F32)
    for n in range(4):
        spread = (lax.div(row, 16) == lax.div(col, 64)) & (
            lax.rem(row, 16) + n * 16 == lax.rem(col, 64)
        )
        bias = bias + dot(lhs_ref[n].astype(BF), jnp.where(spread, 1.0, 0.0).astype(BF))
    bin_ref[...] = bias
    gprm_ref[...] = jnp.zeros_like(gprm_ref)

    def rows(i):
        rows = tile_at(i)
        unit, _ = centred(x_ref[rows, :].astype(F32))
        h_ref[rows, :] = (unit * prm_ref[0:1, :] + prm_ref[1:2, :]).astype(BF)

    loop(0, tiles, rows)

    def pair(p):
        site = sites(p, "")
        for n in range(pairs):
            pl.when(p == n)(functools.partial(wq[n].arrive, 3))
        lanes = tile_at(p, LANES)
        for t in range(tiles):
            rows = slice(t * TILE, (t + 1) * TILE)
            qkv = dot(h_ref[rows, :], wq_ref[p].reshape(width, 3 * LANES))
            q_ref[rows, lanes] = (qkv[:, :LANES] * factor).astype(BF)
            k_ref[rows, lanes] = (qkv[:, LANES : 2 * LANES] * factor).astype(BF)
            v_ref[rows, lanes] = qkv[:, 2 * LANES :].astype(BF)
            site(t)
        attend_pair(
            p, q_ref, k_ref, v_ref, fx_ref, pq_ref, pk_ref, attr_ref, den_ref, low_ref,
            lambda j: site(tiles + j),
        )

    loop(0, pairs, pair)
    o.arrive(3)
    cot_copy.wait()

    def norm(t):
        wo = wo_ref[...].reshape(width, width)
        ffn_norm(t, x_ref, attr_ref, cot_ref, wo, prm_ref, seq_ref, y_ref, h2_ref, gr_ref)

    loop(0, slabs, norm)
    at_site("norm")
    for c in range(parts):
        wi[c].arrive(3)
        wf[c].arrive(3)
        cs = slice(c * width, (c + 1) * width)

        def chunk(t, c=c, cs=cs):
            w_in, w_out = wi_ref[..., cs].reshape(width, width), wf_ref[c].reshape(width, width)
            bias = bin_ref[c : c + 1, :]
            ffn_chunk(t, c, w_in, w_out, bias, h2_ref, gr_ref, hid_ref, du_ref, gprm_ref)

        loop(0, slabs, chunk)
        at_site(f"chunk{c}")
        loop(2 * c, 2 * c + 2, lambda n: grads_out(n, hid_ref, gr_ref, g_ref))

        def grad(n, c=c, cs=cs):
            value = dot_at(h2_ref[:, tile_at(n)], du_ref[:, cs]).astype(BF)
            g_ref[4 + c, pl.ds(n * 2, 2)] = value.reshape(2, 2, 2, 2, 16, width)

        loop(0, width // TILE, grad)
        at_site(f"grad{c}")

    def final(t):
        ffn_final(
            t, cot_ref, wo_ref[...].reshape(width, width), wi_ref[...].reshape(width, hidden),
            wf_ref[...].reshape(hidden, width), prm_ref, seq_ref, y_ref, hid_ref, du_ref,
            act_ref, dy_ref, dor_ref, y_ref, gprm_ref,
        )
        slab_out(t, act_ref, act_out, 0).start()

    loop(0, slabs, final)
    at_site("final")

    def grad_o(n):
        value = dot_at(attr_ref[:, tile_at(n)], dor_ref[...]).astype(BF)
        g_ref[4 + parts, pl.ds(n * 2, 2)] = value.reshape(2, 2, 2, 2, 16, width)

    loop(0, width // TILE, grad_o)
    at_site("grad_o")
    for n in range(3 + parts):
        for c in range(pairs):
            rest_ref[n * pairs + c : n * pairs + c + 1, :] = gprm_ref[2 + n : 3 + n, c * LANES : (c + 1) * LANES]
    for n in range((3 + parts) * pairs, rest_ref.shape[0]):
        rest_ref[n : n + 1, :] = jnp.zeros((1, LANES), F32)
    rest.start()

    ht_ref = du_ref.at[0:width, 0:length]
    da_ref = du_ref.at[width : 2 * width, 0:BLOCK]
    dn_ref = Columns(du_ref, length, 2 * LANES)
    e_ref = Columns(du_ref, length + 4 * LANES, 2 * LANES)
    dqkv_ref = hid_ref
    out_ref = h2_ref
    flip_rows(h_ref, ht_ref)

    def back(p):
        def store(value):
            gq_ref[p] = value.reshape(*grid, 16, 3 * LANES)

        back_pair(
            p, factor, q_ref, k_ref, v_ref, pq_ref, pk_ref, attr_ref, den_ref, y_ref, fx_ref,
            low_ref, ht_ref, dqkv_ref, dn_ref, e_ref, da_ref, sites(p, "b"), store,
        )
        mine.step(0, p)

        @pl.when(p == 0)
        def _():
            rest.turn()

    loop(0, pairs, back)
    last = pairs - 1

    def rows_back(t):
        weights = [wq_ref[p].reshape(width, 3 * LANES) for p in range(pairs)]
        input_rows(
            t, x_ref, jnp.concatenate(weights, axis=1), prm_ref, dqkv_ref, dy_ref, out_ref, gprm_ref
        )
        slab_out(t, out_ref, grad_out, 1).start()

    mine.step(2, last - 1)
    loop(0, slabs // 2, rows_back)
    mine.step(1, last)
    mine.step(4, last - 2)
    loop(slabs // 2, slabs, rows_back)
    for n in range(2):
        for c in range(pairs):
            first_ref[n * pairs + c : n * pairs + c + 1, :] = gprm_ref[n : n + 1, c * LANES : (c + 1) * LANES]
    first.start()
    mine.step(3, last - 1)
    mine.step(2, last)
    first.turn()
    rest_out[...] = rest.result()
    mine.step(3, last)
    first_out[...] = first.result()
    mine.step(4, last - 1)
    mine.step(4, last)
    for t in range(slabs):
        slab_out(t, act_ref, act_out, 0).wait()
        slab_out(t, out_ref, grad_out, 1).wait()
    for g in (sp, o, *wq, *wi):
        g.drain()
    f.drain((0,))
    for g in wf:
        g.drain((1, 2, 3))
    for c in range(g_ref.shape[0]):
        big.drain(c, c % 2 == 0)
    loop(0, pairs, mine.drain)
    rest.drain()
    first.drain()


def finish_kernel(
    act_in, grad_in, gq_in, gf_in, gi_in, go_in, rest_in, first_in,
    act_ref, grad_ref, gq_ref, go_ref, gi_ref, gf_ref,
    g1_ref, s1_ref, g2_ref, s2_ref, bi_ref, bo_ref,
    hold_ref, in_sem, out_sem,
):
    moves = []
    for n, (src, dst) in enumerate(((act_in, act_ref), (grad_in, grad_ref))):
        for t in range(src.shape[0] // TILE):
            rows = pl.ds(t * TILE, TILE)
            hold = hold_ref.at[n, rows]
            moves.append((
                pltpu.make_async_copy(src.at[rows], hold, in_sem.at[n, t]),
                pltpu.make_async_copy(hold, dst.at[rows], out_sem.at[n, t]),
            ))
    for come, _ in moves:
        come.start()
    gq_ref[...] = gq_in[...]
    go_ref[...] = go_in[...]
    gi_ref[...] = gi_in[...]
    gf_ref[...] = gf_in[...].reshape(gf_ref.shape)
    me = lax.axis_index("dp") * 4 + lax.axis_index("fsdp")
    row = lax.broadcasted_iota(jnp.int32, (LANES, LANES), 0)
    lane = lane_ids(LANES)

    def cut(value, start):
        pick = jnp.where(row == lane + start, 1.0, 0.0)
        return lax.dot_general(
            value, pick, (((1,), (0,)), ((), ())), precision=lax.Precision.HIGHEST,
            preferred_element_type=F32,
        )

    def only(value, base, count, which):
        part = value[base : base + count]
        at = lax.broadcasted_iota(jnp.int32, part.shape, 0)
        return jnp.sum(jnp.where(at == which, part, 0.0), axis=0, keepdims=True)

    for come, go in moves:
        come.wait()
        go.start()
    pairs = first_in.shape[0] // 2
    spot = lax.rem(me, 8) * 16
    first, rest = cut(first_in[...], spot), cut(rest_in[...], spot)
    which = lax.div(me, 8)
    for n, ref in enumerate((g1_ref, s1_ref)):
        ref[...] = only(first, n * pairs, pairs, which)[:, :16]
    for n, ref in enumerate((g2_ref, s2_ref, bo_ref)):
        ref[...] = only(rest, n * pairs, pairs, which)[:, :16]
    wide = cut(rest_in[...], lax.rem(me, 2) * 64)
    each = pairs * pairs
    bi_ref[...] = only(wide, 3 * pairs, each, lax.div(me, 2))[:, :64]
    for _, go in moves:
        go.wait()


ANY = pl.BlockSpec(memory_space=pl.ANY)
VM = pl.BlockSpec(memory_space=pltpu.VMEM)


def call(kernel, outs, scratch, name, ins=None, out_specs=None, collective=None):
    extra = {} if ins is None else {"in_specs": ins, "out_specs": out_specs}
    params = {} if collective is None else {"collective_id": collective, "has_side_effects": True}
    return pl.pallas_call(
        kernel,
        out_shape=[jax.ShapeDtypeStruct(s, d) for s, d in outs],
        scratch_shapes=[pltpu.SemaphoreType.DMA(s) if d is None else pltpu.VMEM(s, d) for s, d in scratch],
        compiler_params=pltpu.CompilerParams(vmem_limit_bytes=60 * 2**20, **params),
        name=name,
        **extra,
    )


def padded_features(fm):
    heads, feats, _ = fm.shape
    zero = jnp.zeros_like(fm)
    even = (jnp.arange(heads) % 2 == 0)[:, None, None]
    return jnp.concatenate(
        [jnp.where(even, fm, zero), jnp.where(even, zero, fm), jnp.ones((heads, feats, LANES), BF)],
        axis=-1,
    )


def by_pair(columns, outer):
    rows, count = columns.shape
    split = columns.reshape(rows, outer, count // (outer * LANES), LANES)
    return split.swapaxes(1, 2).reshape(rows, count)


def middle(tokens, attr, cotangent, wo, wi, wf, prm, seq_weight):
    length, width = tokens.shape
    hidden = wi.shape[1]
    big, deep = (length, width), (length, hidden)
    chunks = 5 + hidden // width
    return call(
        middle_kernel,
        [(big, BF), (big, F32), (big, F32), ((16, width), F32), ((chunks, width // 64, 4, 16, width), BF)],
        [(deep, BF), (deep, BF), (big, BF), (big, BF), (big, BF), ((8, hidden), F32)],
        "middle",
    )(tokens, attr, cotangent, wo, wi, wf, prm, seq_weight)


def forward_outs(length, width, heads, feats):
    big = (length, width)
    deep = (length, heads * feats)
    low = (heads, length // BLOCK - 1, feats, 2 * LANES)
    return [(big, BF)] * 4 + [(deep, BF)] * 2 + [(big, BF), (big, F32), (low, BF)]


def backward_scratch(length, width):
    return [
        ((width, length), BF), ((length, 3 * width), BF),
        ((2, length, 2 * LANES), BF), ((2, length, 2 * LANES), BF), ((BLOCK, BLOCK), BF),
    ]


def plain_body(
    tokens, cotangent, group_id, w_qkv, w_out, w_ffn_in, w_ffn_out,
    gain_one, shift_one, gain_two, shift_two, bias_in, bias_out, feature_matrix,
):
    gather = functools.partial(lax.all_gather, axis_name=AXES, axis=0, tiled=True)
    scatter = functools.partial(
        lax.psum_scatter, axis_name=AXES, scatter_dimension=0, tiled=True
    )
    length, width = tokens.shape
    heads, feats, head_size = feature_matrix.shape
    hidden = w_ffn_in.shape[1]
    factor = head_size ** (-0.25)
    wq, wo, wi, wf = gather(w_qkv), gather(w_out), gather(w_ffn_in), gather(w_ffn_out)
    prm = gather(jnp.stack([gain_one, shift_one, gain_two, shift_two, bias_out], axis=1))
    prm = jnp.pad(prm.T.astype(F32), ((0, 3), (0, 0)))
    wf = jnp.concatenate([wf, jnp.pad(gather(bias_in)[:, None], ((0, 0), (0, LANES - 1)))], axis=1)

    slice_seqs = lax.axis_size("dp") * group_id.shape[0]
    labels = jnp.arange(slice_seqs // 2, dtype=jnp.int32)
    onehot = (group_id[:, None] == labels[None, :]).astype(F32)
    counts = lax.psum(jnp.sum(onehot, axis=0), "dp")
    group_size = jnp.sum(onehot * counts[None, :], axis=-1)
    groups = jnp.sum((counts > 0.5).astype(F32))
    seq_weight = jnp.broadcast_to((slice_seqs / (groups * group_size))[:, None], (8, LANES))

    fx = padded_features(feature_matrix)
    h1, q, k, v, pq, pk, attr, den, low = call(
        functools.partial(forward_kernel, factor),
        forward_outs(length, width, heads, feats), [], "forward",
    )(tokens, wq, prm, fx)
    act, dy, datt, gprm, grads = middle(tokens, attr, cotangent, wo, wi, wf, prm, seq_weight)
    input_grad, gq, gprm = call(
        functools.partial(backward_kernel, factor),
        [((length, width), BF), ((width, 3 * width), BF), ((16, width), F32)],
        backward_scratch(length, width), "backward",
    )(tokens, h1, q, k, v, pq, pk, attr, den, datt, dy, by_pair(wq, 3), fx, prm, gprm, low)
    gq = by_pair(gq, width // LANES)
    grads = grads.reshape(-1, width // 16, 16, width)
    gf = grads[:4].transpose(1, 0, 2, 3).reshape(hidden, width)
    gi = grads[4:-1].transpose(1, 2, 0, 3).reshape(width, hidden)
    go = grads[-1].reshape(width, width)
    small = scatter(gprm[:8].T)
    gbin = scatter(gprm[5 : 5 + hidden // width].reshape(hidden))
    part = [scatter(t).astype(F32) for t in (gq, go, gi, gf)]
    return (act, input_grad, *part, *(small[:, i] for i in range(4)), gbin, small[:, 4])


def ring_body(
    tokens, cotangent, group_id, w_qkv, w_out, w_ffn_in, w_ffn_out,
    gain_one, shift_one, gain_two, shift_two, bias_in, bias_out, feature_matrix,
):
    length, width = tokens.shape
    heads, feats, head_size = feature_matrix.shape
    hidden = w_ffn_in.shape[1]
    factor = head_size ** (-0.25)
    nz = lax.axis_size("dp") // 2
    grid = (nz, 2, 2, 2)
    wide = 3 * width
    pairs = width // LANES
    parts = hidden // width
    chunks, many = 5 + parts, 3 + pairs + 2 * parts
    wqs = (pairs, *grid, 16, 3 * LANES)
    big, deep, tall = (length, width), (length, heads * feats), (length, hidden)
    half = (-(-(3 + parts) * pairs // 8) * 8, LANES)
    pair_rows = (2 * pairs, LANES)
    near, far = 3, 2 * nz - 1
    act, input_grad, gq, gf, gi, go, rest, first = call(
        functools.partial(layer_kernel, nz, factor),
        [
            (big, BF), (big, BF), ((16, wide), F32), ((4, 16, width), F32), ((16, hidden), F32),
            ((16, width), F32), (half, F32), (pair_rows, F32),
        ],
        [
            *[(big, BF)] * 4, *[(deep, BF)] * 2, (big, BF), (big, F32),
            ((heads, length // BLOCK - 1, feats, 2 * LANES), BF),
            ((pairs, 16, 3 * LANES), BF), (wqs, BF), ((*grid, 16, width), BF),
            ((*grid, 16, hidden), BF), ((*grid, 64, width), BF), ((*grid, 16, LANES), BF), (big, BF),
            ((heads, feats, 2 * LANES), BF), ((16, LANES), F32), ((LANES, LANES), BF),
            ((8, width), F32),
            (big, BF), (big, F32), (big, F32), ((chunks, *grid, 16, width), BF), ((16, width), F32),
            (tall, BF), (tall, BF), (big, BF), (big, BF), (big, BF),
            ((8, width), F32), ((8, LANES), F32), ((4, 8, LANES), F32),
            ((pairs, *grid, 16, 3 * LANES), BF),
            *Reduce.shapes(chunks, nz, 16, width),
            *Reduce.shapes(pairs, nz, 16, 3 * LANES),
            (half, F32), (half, F32), ((near, *half), F32), ((far, *half), F32),
            (pair_rows, F32), (pair_rows, F32), ((near, *pair_rows), F32), ((far, *pair_rows), F32),
            ((many, 4, nz - 1), None), ((many, 4, nz - 1), None), ((many,), None),
            ((chunks, 4, nz - 1), None), ((chunks, 4, nz - 1), None),
            ((pairs, 4, nz - 1), None), ((pairs, 4, nz - 1), None),
            ((2, far), None), ((2, far), None), ((2, far), None), ((2, far), None),
            ((), None), ((2, length // FFN_TILE), None),
        ],
        "layer",
        [VM, ANY, VM, ANY, ANY, ANY, VM, pl.BlockSpec(memory_space=pltpu.SMEM), *[VM] * 6],
        [ANY, ANY, *[VM] * 6],
        0,
    )(
        tokens, cotangent, w_qkv, w_out, w_ffn_in, w_ffn_out, feature_matrix.swapaxes(1, 2),
        group_id, *(t[None] for t in (gain_one, shift_one, gain_two, shift_two, bias_out, bias_in)),
    )
    act, input_grad, gq, go, gi, gf, *vecs = call(
        finish_kernel,
        [
            (big, BF), (big, BF), ((16, wide), F32), ((16, width), F32), ((16, hidden), F32),
            ((64, width), F32), *[((1, 16), F32)] * 4, ((1, 64), F32), ((1, 16), F32),
        ],
        [((2, length, width), BF), ((2, length // TILE), None), ((2, length // TILE), None)],
        "finish",
        [ANY, ANY, *[VM] * 6],
        [ANY, ANY, *[VM] * 10],
    )(act, input_grad, gq, gf, gi, go, rest, first)
    return (act, input_grad, gq, go, gi, gf, *(t[0] for t in vecs))


def solution(mesh):
    rows, vec = P(AXES, None), P(AXES)
    devices = mesh.shape["dp"] * mesh.shape["fsdp"]

    def body(*args):
        width = args[0].shape[1]
        ring = mesh.shape["fsdp"] == 4 and mesh.shape["dp"] % 2 == 0 and width == 16 * devices
        return (ring_body if ring else plain_body)(*args)

    return jax.shard_map(
        body,
        mesh=mesh,
        in_specs=(rows, rows, vec, *[rows] * 4, *[vec] * 6, P()),
        out_specs=(*[rows] * 6, *[vec] * 6),
        check_vma=False,
    )
```

```python
import functools
import math

import jax
import jax.numpy as jnp
from jax import lax
from jax.experimental import pallas as pl
from jax.experimental.pallas import tpu as pltpu
from jax.sharding import PartitionSpec as P

BLOCK = 512
EPSILON = 1e-05
TILE = 256
FEAT_TILE = 1024
FFN_TILE = 512
LANES = 128
LOG2E = 1.4426950408889634
AXES = ("dp", "fsdp")
BF = jnp.bfloat16
F32 = jnp.float32


def dot(left, right):
    return lax.dot_general(left, right, (((1,), (0,)), ((), ())), preferred_element_type=F32)


def dot_bt(left, right):
    return lax.dot_general(left, right, (((1,), (1,)), ((), ())), preferred_element_type=F32)


def dot_at(left, right):
    return lax.dot_general(left, right, (((0,), (0,)), ((), ())), preferred_element_type=F32)


def unit_rows(rows):
    row = lax.broadcasted_iota(jnp.int32, (rows, LANES), 0)
    col = lax.broadcasted_iota(jnp.int32, (rows, LANES), 1)
    return jnp.where(row == col, 1.0, 0.0).astype(BF)


def lane_ids(rows, width=LANES):
    return lax.broadcasted_iota(jnp.int32, (rows, width), 1)


def tile_at(index, size=TILE):
    return pl.ds(pl.multiple_of(index * size, size), size)


def centred(values):
    mu = jnp.mean(values, axis=-1, keepdims=True)
    cen = values - mu
    inv = lax.rsqrt(jnp.mean(cen * cen, axis=-1, keepdims=True) + EPSILON)
    return cen * inv, inv


def norm_back(grad, unit, inv, gain):
    e = grad * gain
    return inv * (
        e
        - jnp.mean(e, axis=-1, keepdims=True)
        - unit * jnp.mean(e * unit, axis=-1, keepdims=True)
    )


def causal(values, offset):
    row = lax.broadcasted_iota(jnp.int32, values.shape, 0)
    col = lax.broadcasted_iota(jnp.int32, values.shape, 1)
    return jnp.where(col <= row + offset, values, 0.0).astype(BF)


def anticausal(values):
    row = lax.broadcasted_iota(jnp.int32, values.shape, 0)
    col = lax.broadcasted_iota(jnp.int32, values.shape, 1)
    return jnp.where(col >= row, values, 0.0).astype(BF)


MESH_ID = pl.DeviceIdType.MESH


SUMS = {
    "grad0": ((4, 0),),
    "chunk1": ((4, 1),),
    "grad1": ((5, 0),),
    "chunk2": ((5, 1), (4, 2)),
    "grad2": ((6, 0),),
    "chunk3": ((6, 1), (5, 2), (4, 3)),
    "grad3": ((7, 0), (0, 0), (1, 0), (2, 0), (3, 0)),
    "final": ((7, 1), (0, 1), (1, 1), (6, 2), (5, 3), (4, 4)),
    "grad_o": ((8, 0),),
    "b0:0": ((2, 1), (3, 1), (8, 1)),
    "b0:1": ((7, 2), (0, 2), (1, 2), (6, 3), (5, 4)),
    "b1:0": ((2, 2), (3, 2), (8, 2)),
    "b1:1": ((7, 3), (0, 3), (1, 3), (6, 4)),
    "b2:0": ((2, 3), (3, 3), (8, 3)),
    "b2:1": ((7, 4), (0, 4), (1, 4)),
    "b3:0": ((2, 4), (3, 4), (8, 4)),
}
OWN_SUMS = {
    "b1:0": ((0, 1),),
    "b2:0": ((0, 2), (1, 1)),
    "b3:0": ((0, 3), (1, 2), (2, 1)),
}
PLAN = {
    "start": (("s", 1), ("q0", 1), ("q1", 1), ("q2", 1), ("s", 2), ("q3", 1), ("q0", 2), ("o", 1), ("q1", 2), ("i0", 1), ("s", 3), ("q2", 2), ("q3", 2), ("o", 2), ("q0", 3), ("i0", 2),),
    "params": (("q1", 3), ("f0", 1), ("f1", 1), ("f2", 1), ("f3", 1),),
    "0:0": (("q2", 3), ("q3", 3), ("i1", 1),),
    "0:1": (("i2", 1),),
    "0:2": (("o", 3), ("i3", 1),),
    "1:0": (("i0", 3), ("f0", 2),),
    "1:1": (("f1", 2),),
    "1:2": (("i1", 2), ("f2", 2),),
    "2:0": (("i2", 2),),
    "2:1": (("i3", 2), ("f3", 2),),
    "3:0": (("f0", 3),),
    "3:1": (("f1", 3),),
    "norm": (("i1", 3), ("f2", 3),),
    "chunk0": (("i2", 3), ("f3", 3),),
    "grad0": (("i3", 3),),
}
Y_FIRST = {"s", "q1", "q2", "i0", "i1", "i2", "i3", "f0"}
LEAVE = ("s", "q0", "q1", "q2", "q3", "o", "i0", "F", "i1", "i2", "i3")


class Place:
    def __init__(self, nz):
        dp, fs = lax.axis_index("dp"), lax.axis_index("fsdp")
        self.nz = nz
        self.z, self.y = lax.div(dp, 2), lax.rem(dp, 2)
        self.x, self.c = lax.div(fs, 2), lax.rem(fs, 2)

    def device(self, z=None, y=None, x=None, c=None):
        z, y = self.z if z is None else z, self.y if y is None else y
        x, c = self.x if x is None else x, self.c if c is None else c
        return {"dp": z * 2 + y, "fsdp": x * 2 + c}

    def up(self, k):
        return lax.rem(self.z + k, self.nz)

    def down(self, k):
        return lax.rem(self.z + self.nz - k, self.nz)

    def around(self):
        for k in range(1, 4 * self.nz):
            y = 1 - self.y if k // 2 % 2 else self.y
            x = 1 - self.x if k % 2 else self.x
            yield (self.up(k // 4), y, x), (self.down(k // 4), y, x)

    def peers(self):
        yield self.device(c=1 - self.c)
        yield self.device(x=1 - self.x, c=1 - self.c)
        for (z, y, x), _ in self.around():
            yield self.device(z, y, x)

    def near(self):
        yield self.device(c=1 - self.c)
        yield self.device(x=1 - self.x)
        yield self.device(x=1 - self.x, c=1 - self.c)

    def far(self):
        yield self.device(y=1 - self.y)
        for k in range(1, self.nz):
            yield self.device(z=self.up(k))
            yield self.device(z=self.up(k), y=1 - self.y)

    def barrier(self):
        sem = pltpu.get_barrier_semaphore()
        for peer in self.peers():
            pl.semaphore_signal(sem, inc=1, device_id=peer, device_id_type=MESH_ID)
        pl.semaphore_wait(sem, 1 + 4 * self.nz)


def remote(src, dst, send, recv, peer):
    return pltpu.make_async_remote_copy(
        src_ref=src, dst_ref=dst, send_sem=send, recv_sem=recv, device_id=peer,
        device_id_type=MESH_ID,
    )


class Gather:
    def __init__(self, place, shard, whole, view, sems, m, y_first, plane=None, base=None):
        self.place, self.shard, self.whole, self.view = place, shard, whole, view
        self.send, self.recv, self.own = sems
        self.m = m
        self.y_first = y_first
        self.plane, self.base = plane, base

    def at(self, *index):
        return self.whole.at[(*index, *self.view)]

    def hops(self, stage):
        p = self.place
        every = slice(None)
        zs = every if self.plane is None else self.plane
        if stage == 0:
            src = self.shard.at[self.view]
            for k in range(1, p.nz):
                yield src, self.at(p.z, p.y, p.x, p.c), self.at(p.down(k), p.y, p.x, p.c), p.device(z=p.up(k))
        elif stage == 3:
            mine = self.at(zs, every, every, p.c)
            yield mine, mine, self.at(zs, every, every, 1 - p.c), p.device(c=1 - p.c)
        elif stage == 1:
            mine = self.at(zs, p.y, p.x, p.c)
            if self.y_first:
                yield mine, mine, self.at(zs, 1 - p.y, p.x, p.c), p.device(y=1 - p.y)
            else:
                yield mine, mine, self.at(zs, p.y, 1 - p.x, p.c), p.device(x=1 - p.x)
        elif self.y_first:
            mine = self.at(zs, every, p.x, p.c)
            yield mine, mine, self.at(zs, every, 1 - p.x, p.c), p.device(x=1 - p.x)
        else:
            mine = self.at(zs, p.y, every, p.c)
            yield mine, mine, self.at(zs, 1 - p.y, every, p.c), p.device(y=1 - p.y)

    def copies(self, stage, arriving):
        for k, (src, dst, land, peer) in enumerate(self.hops(stage)):
            yield remote(
                src, land if arriving else dst, self.send.at[self.m, stage, k],
                self.recv.at[self.m, stage, k], peer,
            )

    def local(self):
        p = self.place
        return pltpu.make_async_copy(
            self.shard.at[self.view], self.at(p.z, p.y, p.x, p.c), self.own.at[self.m]
        )

    def start(self):
        for copy in self.copies(0, False):
            copy.start()
        self.local().start()

    def arrive(self, stage):
        for copy in self.copies(stage, True):
            copy.wait_recv()

    def enter(self):
        if self.plane is None:
            self.arrive(0)
            self.local().wait()
            return
        p = self.place
        hop = lax.rem(p.z + p.nz - self.plane, p.nz)

        @pl.when(hop == 0)
        def _():
            self.base.local().wait()

        @pl.when(hop != 0)
        def _():
            k = jnp.maximum(hop, 1) - 1
            remote(
                self.shard.at[self.view], self.at(self.plane, p.y, p.x, p.c),
                self.send.at[self.base.m, 0, k], self.recv.at[self.base.m, 0, k],
                p.device(z=p.up(1)),
            ).wait_recv()

    def step(self, stage):
        if stage == 1:
            self.enter()
        else:
            self.arrive(stage - 1)
        for copy in self.copies(stage, False):
            copy.start()

    def drain(self, stages=range(4)):
        for stage in stages:
            for copy in self.copies(stage, False):
                copy.wait_send()


class Reduce:
    def __init__(self, place, source, bufs, sems, write):
        self.place, self.source = place, source
        self.r0, self.r1, self.r2, self.r3 = bufs
        self.send, self.recv = sems
        self.write = write

    def hops(self, stage, c, x_first):
        p = self.place
        every = slice(None)
        if stage == 0:
            yield self.source.at[c, every, every, every, 1 - p.c], self.r0.at[c], p.device(c=1 - p.c)
        elif stage == 1:
            if x_first:
                yield self.r0.at[c, every, every, 1 - p.x], self.r1.at[c], p.device(x=1 - p.x)
            else:
                yield self.r0.at[c, every, 1 - p.y], self.r1.at[c], p.device(y=1 - p.y)
        elif stage == 2:
            if x_first:
                yield self.r1.at[c, every, 1 - p.y], self.r2.at[c], p.device(y=1 - p.y)
            else:
                yield self.r1.at[c, every, 1 - p.x], self.r2.at[c], p.device(x=1 - p.x)
        else:
            for k in range(1, p.nz):
                yield self.r2.at[c, p.up(k)], self.r3.at[c, k - 1], p.device(z=p.up(k))

    def copies(self, stage, c, x_first):
        for k, (src, dst, peer) in enumerate(self.hops(stage, c, x_first)):
            yield remote(src, dst, self.send.at[c, stage, k], self.recv.at[c, stage, k], peer)

    def step(self, stage, c, x_first=False):
        p = self.place
        if stage:
            for copy in self.copies(stage - 1, c, x_first):
                copy.wait_recv()
        if stage == 1:
            mine = self.source[c, :, :, :, p.c]
            self.r0[c] = mine + self.r0[c]
        elif stage == 2:
            mine = self.r0[c, :, :, p.x] if x_first else self.r0[c, :, p.y]
            self.r1[c] = mine + self.r1[c]
        elif stage == 3:
            mine = self.r1[c, :, p.y] if x_first else self.r1[c, :, p.x]
            self.r2[c] = mine + self.r2[c]
        elif stage == 4:
            total = self.r2[c, p.z].astype(F32)
            for k in range(p.nz - 1):
                total = total + self.r3[c, k].astype(F32)
            self.write(c, total)
            return
        for copy in self.copies(stage, c, x_first):
            copy.start()

    def drain(self, c, x_first=False, stages=range(4)):
        for stage in stages:
            for copy in self.copies(stage, c, x_first):
                copy.wait_send()

    def short(self, c, land, sems):
        p = self.place
        for k, (to, _) in enumerate(p.around()):
            yield remote(self.r0.at[(c, *to)], land.at[k], sems[0].at[k], sems[1].at[k], p.device(*to))

    def short_start(self, c, land, sems):
        for copy in self.copies(0, c, False):
            copy.wait_recv()
        self.r0[c] = self.source[c, :, :, :, self.place.c] + self.r0[c]
        for copy in self.short(c, land, sems):
            copy.start()

    def short_end(self, c, land, sems):
        p = self.place
        total = self.r0[c, p.z, p.y, p.x].astype(F32)
        for k, copy in enumerate(self.short(c, land, sems)):
            copy.wait_recv()
            total = total + land[k].astype(F32)
        self.write(c, total)

    @staticmethod
    def shapes(n, nz, rows, cols):
        return [
            ((n, nz, 2, 2, rows, cols), BF), ((n, nz, 2, rows, cols), BF),
            ((n, nz, rows, cols), BF), ((n, nz - 1, rows, cols), BF),
        ]


def project_rows(i, x_ref, wq, prm_ref, h_ref, q_ref, k_ref, v_ref, factor):
    rows = tile_at(i)
    unit, _ = centred(x_ref[rows, :].astype(F32))
    h = (unit * prm_ref[0:1, :] + prm_ref[1:2, :]).astype(BF)
    h_ref[rows, :] = h
    width = h.shape[1]
    qkv = dot(h, wq)
    q_ref[rows, :] = (qkv[:, :width] * factor).astype(BF)
    k_ref[rows, :] = (qkv[:, width : 2 * width] * factor).astype(BF)
    v_ref[rows, :] = qkv[:, 2 * width :].astype(BF)


def attend_pair(
    p, q_ref, k_ref, v_ref, fx_ref, pq_ref, pk_ref, attr_ref, den_ref, low_ref,
    site=lambda j: None,
):
    length = q_ref.shape[0]
    feats = fx_ref.shape[1]
    lanes = tile_at(p, LANES)
    shift = 0.5 * math.log2(feats)
    cols = [tile_at(2 * p + hh, feats) for hh in range(2)]
    step = FEAT_TILE
    for hh in range(2):
        fm = fx_ref[2 * p + hh][:, :LANES]
        for src, dst in ((q_ref, pq_ref), (k_ref, pk_ref)):
            for t in range(length // step):
                rows = slice(t * step, (t + 1) * step)
                part = src[rows, lanes]
                scores = dot_bt(part, fm)
                wide = jnp.where(lane_ids(step) // 64 == hh, part.astype(F32), 0.0)
                square = jnp.sum(wide * wide, axis=-1, keepdims=True)
                feat = jnp.exp2(scores * LOG2E - (square * (0.5 * LOG2E) + shift))
                dst[rows, cols[hh]] = feat.astype(BF)
    site(1)
    ones = jnp.ones((length, LANES), BF)
    vx = jnp.concatenate([v_ref[:, lanes], ones], axis=1)
    states = [None, None]
    for b in range(length // BLOCK):
        base = b * BLOCK
        for i in range(BLOCK // TILE):
            rows = slice(base + i * TILE, base + (i + 1) * TILE)
            keys = slice(base, base + (i + 1) * TILE)
            got = []
            for hh in range(2):
                pq = pq_ref[rows, cols[hh]]
                weights = causal(dot_bt(pq, pk_ref[keys, cols[hh]]), i * TILE)
                both = dot(weights, vx[keys])
                if b:
                    both = both + dot(pq, low_ref[2 * p + hh, b - 1])
                got.append(both)
            first = lane_ids(TILE) < 64
            num = jnp.where(first, got[0][:, :LANES], got[1][:, :LANES])
            den = jnp.where(first, got[0][:, LANES:], got[1][:, LANES:])
            attr_ref[rows, lanes] = (num / den).astype(BF)
            den_ref[rows, lanes] = den
        if base + BLOCK < length:
            block = slice(base, base + BLOCK)
            for hh in range(2):
                more = dot_at(pk_ref[block, cols[hh]], vx[block])
                states[hh] = more if b == 0 else states[hh] + more
                low_ref[2 * p + hh, b] = states[hh].astype(BF)


def forward_kernel(
    factor, x_ref, wq_ref, prm_ref, fx_ref,
    h_ref, q_ref, k_ref, v_ref, pq_ref, pk_ref, attr_ref, den_ref, low_ref,
):
    def rows(i, carry):
        project_rows(i, x_ref, wq_ref[...], prm_ref, h_ref, q_ref, k_ref, v_ref, factor)
        return carry

    lax.fori_loop(0, x_ref.shape[0] // TILE, rows, 0)

    def pair(p, carry):
        attend_pair(
            p, q_ref, k_ref, v_ref, fx_ref, pq_ref, pk_ref, attr_ref, den_ref, low_ref
        )
        return carry

    lax.fori_loop(0, x_ref.shape[1] // LANES, pair, 0)


def ffn_rows(
    t, x_ref, attr_ref, cot_ref, wo, wi, wf, prm_ref, bin_ref, seq_ref,
    act_ref, dy_ref, datt_ref, gprm_ref, hid_ref, du_ref, h_ref, gr_ref, dor_ref, bin_row=0,
):
    width = x_ref.shape[1]
    chunk = width
    rows = tile_at(t, FFN_TILE)
    y = x_ref[rows, :].astype(F32) + dot(attr_ref[rows, :], wo())
    unit, inv = centred(y)
    gain = prm_ref[2:3, :]
    h = (unit * gain + prm_ref[3:4, :]).astype(BF)
    h_ref[rows, :] = h
    g = cot_ref[rows, :].astype(F32) * seq_ref[0:1, 0:1]
    gr = g.astype(BF)
    gr_ref[rows, :] = gr
    out = y + prm_ref[4:5, :]
    dh = jnp.zeros((FFN_TILE, width), F32)
    for c in range(hid_ref.shape[1] // chunk):
        cs = slice(c * chunk, (c + 1) * chunk)
        u = dot(h, wi(cs)) + bin_ref[bin_row : bin_row + 1, cs]
        cdf = 0.5 + 0.5 * lax.erf(u * math.sqrt(0.5))
        slope = cdf + u * jnp.exp2(u * u * (-0.5 * LOG2E)) * (1.0 / math.sqrt(2.0 * math.pi))
        hid = (u * cdf).astype(BF)
        hid_ref[rows, cs] = hid
        out = out + dot(hid, wf(c))
        du = (dot_bt(gr, wf(c)) * slope).astype(BF)
        du_ref[rows, cs] = du
        gprm_ref[5 + c : 6 + c, :] += jnp.sum(du.astype(F32), axis=0, keepdims=True)
        dh = dh + dot_bt(du, wi(cs))
    act_ref[rows, :] = out.astype(BF)
    gprm_ref[2:3, :] += jnp.sum(dh * unit, axis=0, keepdims=True)
    gprm_ref[3:4, :] += jnp.sum(dh, axis=0, keepdims=True)
    gprm_ref[4:5, :] += jnp.sum(g, axis=0, keepdims=True)
    dy = g + norm_back(dh, unit, inv, gain)
    dy_ref[rows, :] = dy
    dor = dy.astype(BF)
    dor_ref[rows, :] = dor
    datt_ref[rows, :] = dot_bt(dor, wo())


def ffn_norm(t, x_ref, attr_ref, cot_ref, wo, prm_ref, seq_ref, y_ref, h_ref, gr_ref):
    rows = tile_at(t, FFN_TILE)
    y = x_ref[rows, :].astype(F32) + dot(attr_ref[rows, :], wo)
    y_ref[rows, :] = y
    unit, _ = centred(y)
    h_ref[rows, :] = (unit * prm_ref[2:3, :] + prm_ref[3:4, :]).astype(BF)
    gr_ref[rows, :] = (cot_ref[rows, :].astype(F32) * seq_ref[0:1, 0:1]).astype(BF)


def ffn_chunk(t, c, wi, wf, bias, h_ref, gr_ref, hid_ref, du_ref, gprm_ref):
    rows = tile_at(t, FFN_TILE)
    width = h_ref.shape[1]
    cs = slice(c * width, (c + 1) * width)
    u = dot(h_ref[rows, :], wi) + bias
    cdf = 0.5 + 0.5 * lax.erf(u * math.sqrt(0.5))
    slope = cdf + u * jnp.exp2(u * u * (-0.5 * LOG2E)) * (1.0 / math.sqrt(2.0 * math.pi))
    hid_ref[rows, cs] = (u * cdf).astype(BF)
    du = (dot_bt(gr_ref[rows, :], wf) * slope).astype(BF)
    du_ref[rows, cs] = du
    gprm_ref[5 + c : 6 + c, :] += jnp.sum(du.astype(F32), axis=0, keepdims=True)


def ffn_final(
    t, cot_ref, wo, wi, wf, prm_ref, seq_ref, y_ref, hid_ref, du_ref,
    act_ref, dy_ref, dor_ref, datt_ref, gprm_ref,
):
    rows = tile_at(t, FFN_TILE)
    y = y_ref[rows, :]
    act_ref[rows, :] = (y + dot(hid_ref[rows, :], wf) + prm_ref[4:5, :]).astype(BF)
    dh = dot_bt(du_ref[rows, :], wi)
    unit, inv = centred(y)
    g = cot_ref[rows, :].astype(F32) * seq_ref[0:1, 0:1]
    gprm_ref[2:3, :] += jnp.sum(dh * unit, axis=0, keepdims=True)
    gprm_ref[3:4, :] += jnp.sum(dh, axis=0, keepdims=True)
    gprm_ref[4:5, :] += jnp.sum(g, axis=0, keepdims=True)
    dy = g + norm_back(dh, unit, inv, prm_ref[2:3, :])
    dy_ref[rows, :] = dy
    dor = dy.astype(BF)
    dor_ref[rows, :] = dor
    datt_ref[rows, :] = dot_bt(dor, wo)


def put_rows(g_ref, chunk, c, value):
    if len(g_ref.shape) == 5:
        g_ref[chunk, c] = value
    else:
        g_ref[chunk, lax.div(c, 2), lax.rem(c, 2)] = value.reshape(2, 2, *value.shape[1:])


def grads_out(c, hid_ref, gr_ref, g_ref):
    width = gr_ref.shape[1]
    grad = dot_at(hid_ref[:, tile_at(c)], gr_ref[...]).astype(BF)
    grad = grad.reshape(4, 4, 16, width)
    for q in range(4):
        put_rows(g_ref, q, c, grad[:, q])


def grads_in(c, h_ref, du_ref, attr_ref, dor_ref, g_ref):
    width = h_ref.shape[1]
    count = du_ref.shape[1] // width
    cs = tile_at(c)
    at = pl.ds(c * 4, 4)
    grad = dot_at(h_ref[:, cs], du_ref[...]).astype(BF)
    for k in range(count):
        g_ref[4 + k, at] = grad[:, k * width : (k + 1) * width].reshape(4, 4, 16, width)
    grad = dot_at(attr_ref[:, cs], dor_ref[...]).astype(BF)
    g_ref[4 + count, at] = grad.reshape(4, 4, 16, width)


def loop(start, stop, step):
    def run(i, carry):
        step(i)
        return carry

    lax.fori_loop(start, stop, run, 0)


def middle_kernel(
    x_ref, attr_ref, cot_ref, wo_ref, wi_ref, wf_ref, prm_ref, seq_ref,
    act_ref, dy_ref, datt_ref, gprm_ref, g_ref,
    hid_ref, du_ref, h_ref, gr_ref, dor_ref, bin_ref,
):
    length, width = x_ref.shape
    gprm_ref[...] = jnp.zeros_like(gprm_ref)
    bin_ref[...] = dot_bt(unit_rows(8), wf_ref[:, width:])
    loop(0, length // FFN_TILE, lambda t: ffn_rows(
        t, x_ref, attr_ref, cot_ref, lambda: wo_ref[...], lambda cs: wi_ref[:, cs],
        lambda c: wf_ref[c * width : (c + 1) * width, :width], prm_ref, bin_ref, seq_ref,
        act_ref, dy_ref, datt_ref, gprm_ref, hid_ref, du_ref, h_ref, gr_ref, dor_ref,
    ))
    loop(0, hid_ref.shape[1] // TILE, lambda c: grads_out(c, hid_ref, gr_ref, g_ref))
    loop(0, width // TILE, lambda c: grads_in(c, h_ref, du_ref, attr_ref, dor_ref, g_ref))


def back_pair(
    p, factor, q_ref, k_ref, v_ref, pq_ref, pk_ref, att_ref, den_ref, datt_ref, fx_ref, low_ref,
    ht_ref, dqkv_ref, dn_ref, e_ref, da_ref, tick, store,
):
    length = q_ref.shape[0]
    feats = fx_ref.shape[1]
    lanes = tile_at(p, LANES)
    blocks = length // BLOCK
    cols = [tile_at(2 * p + hh, feats) for hh in range(2)]
    two = jnp.where(lane_ids(length) < 2, 1.0, 0.0).astype(BF)
    v2 = jnp.concatenate([v_ref[:, lanes], two], axis=1)
    for t in range(length // TILE):
        rows = slice(t * TILE, (t + 1) * TILE)
        dn = datt_ref[rows, lanes] / den_ref[rows, lanes]
        prod = dn * att_ref[rows, lanes].astype(F32)
        lane = lane_ids(TILE)
        for hh in range(2):
            mine = lane // 64 == hh
            dden = -jnp.sum(jnp.where(mine, prod, 0.0), axis=-1, keepdims=True)
            high = dden.astype(BF).astype(F32)
            extra = jnp.where(lane == 0, high, jnp.where(lane == 1, dden - high, 0.0))
            dn_ref[hh, rows, :LANES] = jnp.where(mine, dn, 0.0).astype(BF)
            dn_ref[hh, rows, LANES:] = extra.astype(BF)
    for hh in range(2):
        fx = fx_ref[2 * p + hh]
        back = [None] * blocks
        total = None
        for b in range(blocks - 1, 0, -1):
            block = slice(b * BLOCK, (b + 1) * BLOCK)
            more = dot_at(pq_ref[block, cols[hh]], dn_ref[hh, block, :])
            total = more if total is None else total + more
            dz = total[:, LANES : LANES + 1] + total[:, LANES + 1 : LANES + 2]
            high = dz.astype(BF).astype(F32)
            lane = lane_ids(feats)
            extra = jnp.where(lane == 0, high, jnp.where(lane == 1, dz - high, 0.0))
            back[b - 1] = jnp.concatenate([total[:, :LANES], extra], axis=1).astype(BF)

        def put(value, rows, at, hh=hh):
            where = pl.ds(pl.multiple_of((3 * p + at) * LANES, LANES), LANES)
            if hh:
                mine = lane_ids(value.shape[0]) >= 64
                value = jnp.where(mine, value, dqkv_ref[rows, where].astype(F32))
            dqkv_ref[rows, where] = value.astype(BF)

        for b in range(blocks):
            base = b * BLOCK
            for i in range(BLOCK // TILE):
                rows = slice(base + i * TILE, base + (i + 1) * TILE)
                keys = slice(base, base + (i + 1) * TILE)
                dn = dn_ref[hh, rows, :]
                da = causal(dot_bt(dn, v2[keys]), i * TILE)
                da_ref[i * TILE : (i + 1) * TILE, : (i + 1) * TILE] = da
                grad = dot(da, pk_ref[keys, cols[hh]])
                if b:
                    grad = grad + dot_bt(dn, low_ref[2 * p + hh, b - 1])
                e_ref[0, rows, :] = (grad * pq_ref[rows, cols[hh]].astype(F32)).astype(BF)
            for i in range(BLOCK // TILE):
                rows = slice(base + i * TILE, base + (i + 1) * TILE)
                later = slice(base + i * TILE, base + BLOCK)
                pk = pk_ref[rows, cols[hh]]
                pql = pq_ref[later, cols[hh]]
                grad = dot_at(da_ref[i * TILE :, i * TILE : (i + 1) * TILE], pql)
                at = anticausal(dot_bt(pk, pql))
                dv = dot(at, dn_ref[hh, later, :LANES])
                if b < blocks - 1:
                    grad = grad + dot_bt(v2[rows], back[b])
                    dv = dv + dot(pk, back[b][:, :LANES])
                e_ref[1, rows, :] = (grad * pk.astype(F32)).astype(BF)
                put(dv, rows, 2)
        for at, src in ((0, q_ref), (1, k_ref)):
            res = dot(e_ref[at], fx)
            out = (res[:, :LANES] - src[:, lanes].astype(F32) * res[:, LANES:]) * factor
            put(out, slice(0, length), at)
        if hh == 0:
            tick(0)
    store(dot(ht_ref[...], dqkv_ref[:, tile_at(p, 3 * LANES)]).astype(BF))


def input_rows(t, x_ref, wq, prm_ref, dqkv_ref, dy_ref, out_ref, gprm_ref):
    rows = tile_at(t, FFN_TILE)
    dh = dot_bt(dqkv_ref[rows, : wq.shape[1]], wq)
    unit, inv = centred(x_ref[rows, :].astype(F32))
    gprm_ref[0:1, :] += jnp.sum(dh * unit, axis=0, keepdims=True)
    gprm_ref[1:2, :] += jnp.sum(dh, axis=0, keepdims=True)
    out_ref[rows, :] = (dy_ref[rows, :] + norm_back(dh, unit, inv, prm_ref[0:1, :])).astype(BF)


def flip_rows(h_ref, ht_ref):
    for t in range(h_ref.shape[0] // TILE):
        rows = slice(t * TILE, (t + 1) * TILE)
        ht_ref[:, rows] = h_ref[rows, :].T


def backward_kernel(
    factor, x_ref, h_ref, q_ref, k_ref, v_ref, pq_ref, pk_ref, att_ref, den_ref, datt_ref, dy_ref,
    wq_ref, fx_ref, prm_ref, gin_ref, low_ref,
    out_ref, gq_ref, gprm_ref,
    ht_ref, dqkv_ref, dn_ref, e_ref, da_ref,
):
    gprm_ref[...] = gin_ref[...]
    flip_rows(h_ref, ht_ref)

    def pair(p, carry):
        def store(value):
            gq_ref[:, tile_at(p, 3 * LANES)] = value

        back_pair(
            p, factor, q_ref, k_ref, v_ref, pq_ref, pk_ref, att_ref, den_ref, datt_ref, fx_ref, low_ref,
            ht_ref, dqkv_ref, dn_ref, e_ref, da_ref, lambda j: None, store,
        )
        return carry

    lax.fori_loop(0, x_ref.shape[1] // LANES, pair, 0)

    def rows(t, carry):
        input_rows(t, x_ref, wq_ref[...], prm_ref, dqkv_ref, dy_ref, out_ref, gprm_ref)
        return carry

    lax.fori_loop(0, x_ref.shape[0] // FFN_TILE, rows, 0)


def sequence_weight(small, seq_ref):
    nf = 4
    me = lax.axis_index("dp") * nf + lax.axis_index("fsdp")
    row = lax.broadcasted_iota(jnp.int32, small.shape, 0)
    lane = lane_ids(small.shape[0]).astype(F32)
    peer = lax.div(row, 16)
    ids = small[:, 5:6].astype(F32)
    hit = (lane == ids) & (lax.rem(row, 16) == 0)
    counts = jnp.sum(
        jnp.where(hit & (lax.rem(peer, nf) == lax.axis_index("fsdp")), 1.0, 0.0),
        axis=0, keepdims=True,
    )
    mine = jnp.sum(jnp.where(hit & (peer == me), 1.0, 0.0), axis=0, keepdims=True)
    size = jnp.sum(counts * mine, axis=1, keepdims=True)
    groups = jnp.sum(jnp.where(counts > 0.5, 1.0, 0.0), axis=1, keepdims=True)
    members = lax.axis_size("dp")
    seq_ref[...] = jnp.broadcast_to(members / (groups * size), seq_ref.shape)


class Columns:
    def __init__(self, ref, start, size):
        self.ref, self.start, self.size = ref, start, size

    def where(self, index):
        n, *rest = index if isinstance(index, tuple) else (index,)
        rows, cols = [*rest, slice(None), slice(None)][:2]
        base = self.start + n * self.size
        low, high = cols.start or 0, self.size if cols.stop is None else cols.stop
        return rows, slice(base + low, base + high)

    def __getitem__(self, index):
        return self.ref[self.where(index)]

    def __setitem__(self, index, value):
        self.ref[self.where(index)] = value


class Total:
    def __init__(self, place, ref, part, near, far, sems):
        self.place, self.ref, self.part, self.near, self.far = place, ref, part, near, far
        self.send, self.recv = sems

    def copies(self, stage):
        peers = self.place.far() if stage else self.place.near()
        src, dst = (self.part, self.far) if stage else (self.ref, self.near)
        for k, peer in enumerate(peers):
            yield remote(src, dst.at[k], self.send.at[stage, k], self.recv.at[stage, k], peer)

    def start(self):
        for copy in self.copies(0):
            copy.start()

    def turn(self):
        for copy in self.copies(0):
            copy.wait_recv()
        self.part[...] = self.ref[...] + sum(self.near[k] for k in range(self.near.shape[0]))
        for copy in self.copies(1):
            copy.start()

    def result(self):
        for copy in self.copies(1):
            copy.wait_recv()
        return self.part[...] + sum(self.far[k] for k in range(self.far.shape[0]))

    def drain(self):
        for stage in range(2):
            for copy in self.copies(stage):
                copy.wait_send()


def layer_kernel(
    nz, factor, x_ref, cot_in, wqs_ref, wos_ref, wis_ref, wfs_ref, fm_ref, id_ref,
    g1_ref, s1_ref, g2_ref, s2_ref, bo_ref, bi_ref,
    act_out, grad_out, partq_ref, gf_ref, gi_ref, go_ref, rest_out, first_out,
    h_ref, q_ref, k_ref, v_ref, pq_ref, pk_ref, attr_ref, den_ref, low_ref,
    wqt_ref, wq_ref, wo_ref, wi_ref, wf_ref, sp_ref, cot_ref, fx_ref, vec_ref, col_ref, prm_ref,
    act_ref, dy_ref, y_ref, g_ref, gprm_ref, hid_ref, du_ref, h2_ref, gr_ref, dor_ref,
    bin_ref, seq_ref, lhs_ref, gq_ref,
    b0, b1, b2, b3, c0, c1, c2, c3,
    rest_ref, rest_part, rest_near, rest_far, first_ref, first_part, first_near, first_far,
    land_ref,
    send, recv, own, big_send, big_recv, q_send, q_recv, rest_send, rest_recv, first_send, first_recv,
    short_send, short_recv, local_sem, tile_sem,
):
    length, width = x_ref.shape
    hidden = hid_ref.shape[1]
    place = Place(nz)
    every = slice(None)
    sems = (send, recv, own)
    pairs, tiles, parts = width // LANES, length // TILE, hidden // width
    slabs = length // FFN_TILE

    def gather(name, shard, whole, view, m, plane=None, base=None):
        return Gather(place, shard, whole, view, sems, m, name in Y_FIRST, plane, base)

    both = (every, every)
    sp = gather("s", col_ref, sp_ref, (slice(0, 16), every), 0)
    o = gather("o", wos_ref, wo_ref, both, 1)
    f = gather("f", wfs_ref, wf_ref, both, 2)
    wq = [gather(f"q{p}", wqt_ref.at[p], wq_ref.at[p], both, 3 + p) for p in range(pairs)]
    wi = [
        gather(f"i{c}", wis_ref, wi_ref, (every, slice(c * width, (c + 1) * width)), 3 + pairs + c)
        for c in range(parts)
    ]
    wf = [
        gather(f"f{c}", wfs_ref, wf_ref, both, 3 + pairs + parts + c, c, f) for c in range(parts)
    ]
    named = {"s": sp, "o": o, "F": f}
    for n in range(pairs):
        named[f"q{n}"] = wq[n]
    for n in range(parts):
        named[f"i{n}"] = wi[n]
        named[f"f{n}"] = wf[n]

    def write(c, value):
        if c < 4:
            gf_ref[c] = value
        elif c < 4 + parts:
            gi_ref[:, (c - 4) * width : (c - 3) * width] = value
        else:
            go_ref[...] = value

    def write_q(c, value):
        for at in range(3):
            where = pl.ds(pl.multiple_of(c * LANES + at * width, LANES), LANES)
            partq_ref[:, where] = value[:, at * LANES : (at + 1) * LANES]

    grid = (nz, 2, 2, 2)
    big = Reduce(place, g_ref, (b0, b1, b2, b3), (big_send, big_recv), write)
    mine = Reduce(place, gq_ref, (c0, c1, c2, c3), (q_send, q_recv), write_q)
    rest = Total(place, rest_ref, rest_part, rest_near, rest_far, (rest_send, rest_recv))
    first = Total(place, first_ref, first_part, first_near, first_far, (first_send, first_recv))
    short_sems = (short_send, short_recv)
    cot_copy = pltpu.make_async_copy(cot_in, cot_ref, local_sem)

    def slab_out(t, src, dst, n):
        rows = tile_at(t, FFN_TILE)
        return pltpu.make_async_copy(src.at[rows], dst.at[rows], tile_sem.at[n, t])

    def at_site(name):
        for who, stage in PLAN.get(name, ()):
            named[who].step(stage)
        for c, stage in SUMS.get(name, ()):
            big.step(stage, c, c % 2 == 0)
        for c, stage in OWN_SUMS.get(name, ()):
            mine.step(stage, c)

    def sites(p, prefix):
        def site(j):
            for n in range(pairs):
                name = f"{prefix}{n}:{j}"
                if name in PLAN or name in SUMS or name in OWN_SUMS:
                    pl.when(p == n)(functools.partial(at_site, name))

        return site

    vec_ref[...] = jnp.zeros_like(vec_ref)
    for n, ref in enumerate((g1_ref, s1_ref, g2_ref, s2_ref, bo_ref)):
        vec_ref[n : n + 1, : ref.shape[1]] = ref[...].astype(F32)
    vec_ref[5:6, :] = jnp.full((1, LANES), id_ref[0], jnp.int32).astype(F32)
    for n in range(4):
        vec_ref[8 + n : 9 + n, :16] = bi_ref[:, n * 16 : (n + 1) * 16].astype(F32)
    col_ref[...] = dot_at(vec_ref[...].astype(BF), unit_rows(16)).astype(BF)
    for p in range(pairs):
        for n in range(3):
            at = n * width + p * LANES
            wqt_ref[p, :, n * LANES : (n + 1) * LANES] = wqs_ref[:, at : at + LANES]
    place.barrier()
    for who in LEAVE:
        named[who].start()
    cot_copy.start()
    head_size, feats = fm_ref.shape[1:]
    for n in range(fm_ref.shape[0]):
        row = lax.broadcasted_iota(jnp.int32, (head_size, LANES), 0)
        place_at = jnp.where(lane_ids(head_size) == row + (n % 2) * head_size, 1.0, 0.0).astype(BF)
        fx_ref[n, :, :LANES] = dot_at(fm_ref[n], place_at).astype(BF)
        fx_ref[n, :, LANES:] = jnp.ones((feats, LANES), BF)
    at_site("start")
    sp.arrive(3)
    small = sp_ref[...].reshape(width, LANES)
    prm = dot_bt(unit_rows(16), small)
    prm_ref[...] = prm[:8]
    at_site("params")
    sequence_weight(small, seq_ref)
    for c in range(parts):
        for n in range(4):
            lhs_ref[n, c : c + 1, :] = prm[8 + n : 9 + n, c * LANES : (c + 1) * LANES]
    row = lax.broadcasted_iota(jnp.int32, (LANES, width), 0)
    col = lax.broadcasted_iota(jnp.int32, (LANES, width), 1)
    bias = jnp.zeros((8, width), F32)
    for n in range(4):
        spread = (lax.div(row, 16) == lax.div(col, 64)) & (
            lax.rem(row, 16) + n * 16 == lax.rem(col, 64)
        )
        bias = bias + dot(lhs_ref[n].astype(BF), jnp.where(spread, 1.0, 0.0).astype(BF))
    bin_ref[...] = bias
    gprm_ref[...] = jnp.zeros_like(gprm_ref)

    def rows(i):
        rows = tile_at(i)
        unit, _ = centred(x_ref[rows, :].astype(F32))
        h_ref[rows, :] = (unit * prm_ref[0:1, :] + prm_ref[1:2, :]).astype(BF)

    loop(0, tiles, rows)
    at_site("rows")

    def pair(p):
        site = sites(p, "")
        for n in range(pairs):
            pl.when(p == n)(functools.partial(wq[n].arrive, 3))
        lanes = tile_at(p, LANES)
        for t in range(tiles):
            rows = slice(t * TILE, (t + 1) * TILE)
            qkv = dot(h_ref[rows, :], wq_ref[p].reshape(width, 3 * LANES))
            q_ref[rows, lanes] = (qkv[:, :LANES] * factor).astype(BF)
            k_ref[rows, lanes] = (qkv[:, LANES : 2 * LANES] * factor).astype(BF)
            v_ref[rows, lanes] = qkv[:, 2 * LANES :].astype(BF)
        site(0)
        attend_pair(
            p, q_ref, k_ref, v_ref, fx_ref, pq_ref, pk_ref, attr_ref, den_ref, low_ref,
            site,
        )
        site(2)

    loop(0, pairs, pair)
    o.arrive(3)
    cot_copy.wait()

    def norm(t):
        wo = wo_ref[...].reshape(width, width)
        ffn_norm(t, x_ref, attr_ref, cot_ref, wo, prm_ref, seq_ref, y_ref, h2_ref, gr_ref)

    loop(0, slabs, norm)
    at_site("norm")
    for c in range(parts):
        wi[c].arrive(3)
        wf[c].arrive(3)
        cs = slice(c * width, (c + 1) * width)

        def chunk(t, c=c, cs=cs):
            w_in, w_out = wi_ref[..., cs].reshape(width, width), wf_ref[c].reshape(width, width)
            bias = bin_ref[c : c + 1, :]
            ffn_chunk(t, c, w_in, w_out, bias, h2_ref, gr_ref, hid_ref, du_ref, gprm_ref)

        loop(0, slabs, chunk)
        at_site(f"chunk{c}")
        loop(2 * c, 2 * c + 2, lambda n: grads_out(n, hid_ref, gr_ref, g_ref))

        def grad(n, c=c, cs=cs):
            value = dot_at(h2_ref[:, tile_at(n)], du_ref[:, cs]).astype(BF)
            g_ref[4 + c, pl.ds(n * 2, 2)] = value.reshape(2, 2, 2, 2, 16, width)

        loop(0, width // TILE, grad)
        at_site(f"grad{c}")

    def final(t):
        ffn_final(
            t, cot_ref, wo_ref[...].reshape(width, width), wi_ref[...].reshape(width, hidden),
            wf_ref[...].reshape(hidden, width), prm_ref, seq_ref, y_ref, hid_ref, du_ref,
            act_ref, dy_ref, dor_ref, y_ref, gprm_ref,
        )
        slab_out(t, act_ref, act_out, 0).start()

    loop(0, slabs, final)
    at_site("final")

    def grad_o(n):
        value = dot_at(attr_ref[:, tile_at(n)], dor_ref[...]).astype(BF)
        g_ref[4 + parts, pl.ds(n * 2, 2)] = value.reshape(2, 2, 2, 2, 16, width)

    loop(0, width // TILE, grad_o)
    at_site("grad_o")
    for n in range(3 + parts):
        for c in range(pairs):
            rest_ref[n * pairs + c : n * pairs + c + 1, :] = gprm_ref[2 + n : 3 + n, c * LANES : (c + 1) * LANES]
    for n in range((3 + parts) * pairs, rest_ref.shape[0]):
        rest_ref[n : n + 1, :] = jnp.zeros((1, LANES), F32)
    rest.start()

    ht_ref = du_ref.at[0:width, 0:length]
    da_ref = du_ref.at[width : 2 * width, 0:BLOCK]
    dn_ref = Columns(du_ref, length, 2 * LANES)
    e_ref = Columns(du_ref, length + 4 * LANES, 2 * LANES)
    dqkv_ref = hid_ref
    out_ref = h2_ref
    flip_rows(h_ref, ht_ref)

    def back(p):
        def store(value):
            gq_ref[p] = value.reshape(*grid, 16, 3 * LANES)

        back_pair(
            p, factor, q_ref, k_ref, v_ref, pq_ref, pk_ref, attr_ref, den_ref, y_ref, fx_ref,
            low_ref, ht_ref, dqkv_ref, dn_ref, e_ref, da_ref, sites(p, "b"), store,
        )
        mine.step(0, p)
        sites(p, "b")(1)

        @pl.when(p == 0)
        def _():
            rest.turn()

    loop(0, pairs, back)
    last = pairs - 1

    def rows_back(t):
        weights = [wq_ref[p].reshape(width, 3 * LANES) for p in range(pairs)]
        input_rows(
            t, x_ref, jnp.concatenate(weights, axis=1), prm_ref, dqkv_ref, dy_ref, out_ref, gprm_ref
        )
        slab_out(t, out_ref, grad_out, 1).start()

    mine.step(3, last - 2)
    mine.step(2, last - 1)
    loop(0, slabs // 2, rows_back)
    mine.short_start(last, land_ref, short_sems)
    loop(slabs // 2, slabs, rows_back)
    for n in range(2):
        for c in range(pairs):
            first_ref[n * pairs + c : n * pairs + c + 1, :] = gprm_ref[n : n + 1, c * LANES : (c + 1) * LANES]
    first.start()
    mine.step(3, last - 1)
    first.turn()
    rest_out[...] = rest.result()
    mine.step(4, last - 3)
    mine.step(4, last - 2)
    mine.step(4, last - 1)
    first_out[...] = first.result()
    mine.short_end(last, land_ref, short_sems)
    for t in range(slabs):
        slab_out(t, act_ref, act_out, 0).wait()
        slab_out(t, out_ref, grad_out, 1).wait()
    for g in (sp, o, *wq, *wi):
        g.drain()
    f.drain((0,))
    for g in wf:
        g.drain((1, 2, 3))
    for c in range(g_ref.shape[0]):
        big.drain(c, c % 2 == 0)
    loop(0, last, mine.drain)
    mine.drain(last, stages=(0,))
    for copy in mine.short(last, land_ref, short_sems):
        copy.wait_send()
    rest.drain()
    first.drain()


def finish_kernel(
    act_in, grad_in, gq_in, gf_in, gi_in, go_in, rest_in, first_in,
    act_ref, grad_ref, gq_ref, go_ref, gi_ref, gf_ref,
    g1_ref, s1_ref, g2_ref, s2_ref, bi_ref, bo_ref,
    hold_ref, in_sem, out_sem,
):
    moves = []
    for n, (src, dst) in enumerate(((act_in, act_ref), (grad_in, grad_ref))):
        for t in range(src.shape[0] // TILE):
            rows = pl.ds(t * TILE, TILE)
            hold = hold_ref.at[n, rows]
            moves.append((
                pltpu.make_async_copy(src.at[rows], hold, in_sem.at[n, t]),
                pltpu.make_async_copy(hold, dst.at[rows], out_sem.at[n, t]),
            ))
    for come, _ in moves:
        come.start()
    gq_ref[...] = gq_in[...]
    go_ref[...] = go_in[...]
    gi_ref[...] = gi_in[...]
    gf_ref[...] = gf_in[...].reshape(gf_ref.shape)
    me = lax.axis_index("dp") * 4 + lax.axis_index("fsdp")
    row = lax.broadcasted_iota(jnp.int32, (LANES, LANES), 0)
    lane = lane_ids(LANES)

    def cut(value, start):
        pick = jnp.where(row == lane + start, 1.0, 0.0)
        return lax.dot_general(
            value, pick, (((1,), (0,)), ((), ())), precision=lax.Precision.HIGHEST,
            preferred_element_type=F32,
        )

    def only(value, base, count, which):
        part = value[base : base + count]
        at = lax.broadcasted_iota(jnp.int32, part.shape, 0)
        return jnp.sum(jnp.where(at == which, part, 0.0), axis=0, keepdims=True)

    for come, go in moves:
        come.wait()
        go.start()
    pairs = first_in.shape[0] // 2
    spot = lax.rem(me, 8) * 16
    first, rest = cut(first_in[...], spot), cut(rest_in[...], spot)
    which = lax.div(me, 8)
    for n, ref in enumerate((g1_ref, s1_ref)):
        ref[...] = only(first, n * pairs, pairs, which)[:, :16]
    for n, ref in enumerate((g2_ref, s2_ref, bo_ref)):
        ref[...] = only(rest, n * pairs, pairs, which)[:, :16]
    wide = cut(rest_in[...], lax.rem(me, 2) * 64)
    each = pairs * pairs
    bi_ref[...] = only(wide, 3 * pairs, each, lax.div(me, 2))[:, :64]
    for _, go in moves:
        go.wait()


ANY = pl.BlockSpec(memory_space=pl.ANY)
VM = pl.BlockSpec(memory_space=pltpu.VMEM)


def call(kernel, outs, scratch, name, ins=None, out_specs=None, collective=None):
    extra = {} if ins is None else {"in_specs": ins, "out_specs": out_specs}
    params = {} if collective is None else {"collective_id": collective, "has_side_effects": True}
    return pl.pallas_call(
        kernel,
        out_shape=[jax.ShapeDtypeStruct(s, d) for s, d in outs],
        scratch_shapes=[pltpu.SemaphoreType.DMA(s) if d is None else pltpu.VMEM(s, d) for s, d in scratch],
        compiler_params=pltpu.CompilerParams(vmem_limit_bytes=60 * 2**20, **params),
        name=name,
        **extra,
    )


def padded_features(fm):
    heads, feats, _ = fm.shape
    zero = jnp.zeros_like(fm)
    even = (jnp.arange(heads) % 2 == 0)[:, None, None]
    return jnp.concatenate(
        [jnp.where(even, fm, zero), jnp.where(even, zero, fm), jnp.ones((heads, feats, LANES), BF)],
        axis=-1,
    )


def by_pair(columns, outer):
    rows, count = columns.shape
    split = columns.reshape(rows, outer, count // (outer * LANES), LANES)
    return split.swapaxes(1, 2).reshape(rows, count)


def middle(tokens, attr, cotangent, wo, wi, wf, prm, seq_weight):
    length, width = tokens.shape
    hidden = wi.shape[1]
    big, deep = (length, width), (length, hidden)
    chunks = 5 + hidden // width
    return call(
        middle_kernel,
        [(big, BF), (big, F32), (big, F32), ((16, width), F32), ((chunks, width // 64, 4, 16, width), BF)],
        [(deep, BF), (deep, BF), (big, BF), (big, BF), (big, BF), ((8, hidden), F32)],
        "middle",
    )(tokens, attr, cotangent, wo, wi, wf, prm, seq_weight)


def forward_outs(length, width, heads, feats):
    big = (length, width)
    deep = (length, heads * feats)
    low = (heads, length // BLOCK - 1, feats, 2 * LANES)
    return [(big, BF)] * 4 + [(deep, BF)] * 2 + [(big, BF), (big, F32), (low, BF)]


def backward_scratch(length, width):
    return [
        ((width, length), BF), ((length, 3 * width), BF),
        ((2, length, 2 * LANES), BF), ((2, length, 2 * LANES), BF), ((BLOCK, BLOCK), BF),
    ]


def plain_body(
    tokens, cotangent, group_id, w_qkv, w_out, w_ffn_in, w_ffn_out,
    gain_one, shift_one, gain_two, shift_two, bias_in, bias_out, feature_matrix,
):
    gather = functools.partial(lax.all_gather, axis_name=AXES, axis=0, tiled=True)
    scatter = functools.partial(
        lax.psum_scatter, axis_name=AXES, scatter_dimension=0, tiled=True
    )
    length, width = tokens.shape
    heads, feats, head_size = feature_matrix.shape
    hidden = w_ffn_in.shape[1]
    factor = head_size ** (-0.25)
    wq, wo, wi, wf = gather(w_qkv), gather(w_out), gather(w_ffn_in), gather(w_ffn_out)
    prm = gather(jnp.stack([gain_one, shift_one, gain_two, shift_two, bias_out], axis=1))
    prm = jnp.pad(prm.T.astype(F32), ((0, 3), (0, 0)))
    wf = jnp.concatenate([wf, jnp.pad(gather(bias_in)[:, None], ((0, 0), (0, LANES - 1)))], axis=1)

    slice_seqs = lax.axis_size("dp") * group_id.shape[0]
    labels = jnp.arange(slice_seqs // 2, dtype=jnp.int32)
    onehot = (group_id[:, None] == labels[None, :]).astype(F32)
    counts = lax.psum(jnp.sum(onehot, axis=0), "dp")
    group_size = jnp.sum(onehot * counts[None, :], axis=-1)
    groups = jnp.sum((counts > 0.5).astype(F32))
    seq_weight = jnp.broadcast_to((slice_seqs / (groups * group_size))[:, None], (8, LANES))

    fx = padded_features(feature_matrix)
    h1, q, k, v, pq, pk, attr, den, low = call(
        functools.partial(forward_kernel, factor),
        forward_outs(length, width, heads, feats), [], "forward",
    )(tokens, wq, prm, fx)
    act, dy, datt, gprm, grads = middle(tokens, attr, cotangent, wo, wi, wf, prm, seq_weight)
    input_grad, gq, gprm = call(
        functools.partial(backward_kernel, factor),
        [((length, width), BF), ((width, 3 * width), BF), ((16, width), F32)],
        backward_scratch(length, width), "backward",
    )(tokens, h1, q, k, v, pq, pk, attr, den, datt, dy, by_pair(wq, 3), fx, prm, gprm, low)
    gq = by_pair(gq, width // LANES)
    grads = grads.reshape(-1, width // 16, 16, width)
    gf = grads[:4].transpose(1, 0, 2, 3).reshape(hidden, width)
    gi = grads[4:-1].transpose(1, 2, 0, 3).reshape(width, hidden)
    go = grads[-1].reshape(width, width)
    small = scatter(gprm[:8].T)
    gbin = scatter(gprm[5 : 5 + hidden // width].reshape(hidden))
    part = [scatter(t).astype(F32) for t in (gq, go, gi, gf)]
    return (act, input_grad, *part, *(small[:, i] for i in range(4)), gbin, small[:, 4])


def ring_body(
    tokens, cotangent, group_id, w_qkv, w_out, w_ffn_in, w_ffn_out,
    gain_one, shift_one, gain_two, shift_two, bias_in, bias_out, feature_matrix,
):
    length, width = tokens.shape
    heads, feats, head_size = feature_matrix.shape
    hidden = w_ffn_in.shape[1]
    factor = head_size ** (-0.25)
    nz = lax.axis_size("dp") // 2
    grid = (nz, 2, 2, 2)
    wide = 3 * width
    pairs = width // LANES
    parts = hidden // width
    chunks, many = 5 + parts, 3 + pairs + 2 * parts
    wqs = (pairs, *grid, 16, 3 * LANES)
    big, deep, tall = (length, width), (length, heads * feats), (length, hidden)
    half = (-(-(3 + parts) * pairs // 8) * 8, LANES)
    pair_rows = (2 * pairs, LANES)
    near, far = 3, 2 * nz - 1
    act, input_grad, gq, gf, gi, go, rest, first = call(
        functools.partial(layer_kernel, nz, factor),
        [
            (big, BF), (big, BF), ((16, wide), F32), ((4, 16, width), F32), ((16, hidden), F32),
            ((16, width), F32), (half, F32), (pair_rows, F32),
        ],
        [
            *[(big, BF)] * 4, *[(deep, BF)] * 2, (big, BF), (big, F32),
            ((heads, length // BLOCK - 1, feats, 2 * LANES), BF),
            ((pairs, 16, 3 * LANES), BF), (wqs, BF), ((*grid, 16, width), BF),
            ((*grid, 16, hidden), BF), ((*grid, 64, width), BF), ((*grid, 16, LANES), BF), (big, BF),
            ((heads, feats, 2 * LANES), BF), ((16, LANES), F32), ((LANES, LANES), BF),
            ((8, width), F32),
            (big, BF), (big, F32), (big, F32), ((chunks, *grid, 16, width), BF), ((16, width), F32),
            (tall, BF), (tall, BF), (big, BF), (big, BF), (big, BF),
            ((8, width), F32), ((8, LANES), F32), ((4, 8, LANES), F32),
            ((pairs, *grid, 16, 3 * LANES), BF),
            *Reduce.shapes(chunks, nz, 16, width),
            *Reduce.shapes(pairs, nz, 16, 3 * LANES),
            (half, F32), (half, F32), ((near, *half), F32), ((far, *half), F32),
            (pair_rows, F32), (pair_rows, F32), ((near, *pair_rows), F32), ((far, *pair_rows), F32),
            ((4 * nz - 1, 16, 3 * LANES), BF),
            ((many, 4, nz - 1), None), ((many, 4, nz - 1), None), ((many,), None),
            ((chunks, 4, nz - 1), None), ((chunks, 4, nz - 1), None),
            ((pairs, 4, nz - 1), None), ((pairs, 4, nz - 1), None),
            ((2, far), None), ((2, far), None), ((2, far), None), ((2, far), None),
            ((4 * nz - 1,), None), ((4 * nz - 1,), None),
            ((), None), ((2, length // FFN_TILE), None),
        ],
        "layer",
        [VM, ANY, VM, ANY, ANY, ANY, VM, pl.BlockSpec(memory_space=pltpu.SMEM), *[VM] * 6],
        [ANY, ANY, *[VM] * 6],
        0,
    )(
        tokens, cotangent, w_qkv, w_out, w_ffn_in, w_ffn_out, feature_matrix.swapaxes(1, 2),
        group_id, *(t[None] for t in (gain_one, shift_one, gain_two, shift_two, bias_out, bias_in)),
    )
    act, input_grad, gq, go, gi, gf, *vecs = call(
        finish_kernel,
        [
            (big, BF), (big, BF), ((16, wide), F32), ((16, width), F32), ((16, hidden), F32),
            ((64, width), F32), *[((1, 16), F32)] * 4, ((1, 64), F32), ((1, 16), F32),
        ],
        [((2, length, width), BF), ((2, length // TILE), None), ((2, length // TILE), None)],
        "finish",
        [ANY, ANY, *[VM] * 6],
        [ANY, ANY, *[VM] * 10],
    )(act, input_grad, gq, gf, gi, go, rest, first)
    return (act, input_grad, gq, go, gi, gf, *(t[0] for t in vecs))


def solution(mesh):
    rows, vec = P(AXES, None), P(AXES)
    devices = mesh.shape["dp"] * mesh.shape["fsdp"]

    def body(*args):
        width = args[0].shape[1]
        ring = mesh.shape["fsdp"] == 4 and mesh.shape["dp"] % 2 == 0 and width == 16 * devices
        return (ring_body if ring else plain_body)(*args)

    return jax.shard_map(
        body,
        mesh=mesh,
        in_specs=(rows, rows, vec, *[rows] * 4, *[vec] * 6, P()),
        out_specs=(*[rows] * 6, *[vec] * 6),
        check_vma=False,
    )
```

```python
import functools
import math

import jax
import jax.numpy as jnp
from jax import lax
from jax.experimental import pallas as pl
from jax.experimental.pallas import tpu as pltpu
from jax.sharding import PartitionSpec as P

BLOCK = 512
EPSILON = 1e-05
TILE = 256
FEAT_TILE = 1024
FFN_TILE = 512
LANES = 128
LOG2E = 1.4426950408889634
AXES = ("dp", "fsdp")
BF = jnp.bfloat16
F32 = jnp.float32


def dot(left, right):
    return lax.dot_general(left, right, (((1,), (0,)), ((), ())), preferred_element_type=F32)


def dot_bt(left, right):
    return lax.dot_general(left, right, (((1,), (1,)), ((), ())), preferred_element_type=F32)


def dot_at(left, right):
    return lax.dot_general(left, right, (((0,), (0,)), ((), ())), preferred_element_type=F32)


def unit_rows(rows):
    row = lax.broadcasted_iota(jnp.int32, (rows, LANES), 0)
    col = lax.broadcasted_iota(jnp.int32, (rows, LANES), 1)
    return jnp.where(row == col, 1.0, 0.0).astype(BF)


def lane_ids(rows, width=LANES):
    return lax.broadcasted_iota(jnp.int32, (rows, width), 1)


def tile_at(index, size=TILE):
    return pl.ds(pl.multiple_of(index * size, size), size)


def centred(values):
    mu = jnp.mean(values, axis=-1, keepdims=True)
    cen = values - mu
    inv = lax.rsqrt(jnp.mean(cen * cen, axis=-1, keepdims=True) + EPSILON)
    return cen * inv, inv


def norm_back(grad, unit, inv, gain):
    e = grad * gain
    return inv * (
        e
        - jnp.mean(e, axis=-1, keepdims=True)
        - unit * jnp.mean(e * unit, axis=-1, keepdims=True)
    )


def causal(values, offset):
    row = lax.broadcasted_iota(jnp.int32, values.shape, 0)
    col = lax.broadcasted_iota(jnp.int32, values.shape, 1)
    return jnp.where(col <= row + offset, values, 0.0).astype(BF)


def anticausal(values):
    row = lax.broadcasted_iota(jnp.int32, values.shape, 0)
    col = lax.broadcasted_iota(jnp.int32, values.shape, 1)
    return jnp.where(col >= row, values, 0.0).astype(BF)


MESH_ID = pl.DeviceIdType.MESH


SUMS = {
    "grad0": ((4, 0),),
    "chunk1": ((4, 1),),
    "grad1": ((5, 0),),
    "chunk2": ((5, 1), (4, 2)),
    "grad2": ((6, 0),),
    "chunk3": ((6, 1), (5, 2), (4, 3)),
    "grad3": ((7, 0), (0, 0), (1, 0), (2, 0), (3, 0)),
    "final": ((7, 1), (0, 1), (1, 1), (6, 2), (5, 3)),
    "grad_o": ((8, 0),),
    "b0:0": ((2, 1), (3, 1), (8, 1)),
    "b0:1": ((7, 2), (0, 2), (1, 2), (6, 3)),
    "b1:0": ((2, 2), (3, 2), (8, 2)),
    "b1:1": ((7, 3), (0, 3), (1, 3)),
    "b2:0": ((2, 3), (3, 3), (8, 3)),
    "tail": ((4, 4), (5, 4), (6, 4), (7, 4), (0, 4), (1, 4), (2, 4), (3, 4), (8, 4)),
}
OWN_SUMS = {
    "b1:0": ((0, 1),),
    "b2:0": ((0, 2), (1, 1)),
    "b3:0": ((0, 3), (1, 2), (2, 1)),
}
PLAN = {
    "start": (("s", 1), ("q0", 1), ("q1", 1), ("q2", 1), ("s", 2), ("q3", 1), ("q0", 2), ("o", 1), ("q1", 2), ("i0", 1), ("s", 3), ("q2", 2), ("q3", 2), ("o", 2), ("q0", 3), ("i0", 2),),
    "params": (("q1", 3), ("f0", 1), ("f1", 1), ("f2", 1), ("f3", 1),),
    "0:0": (("q2", 3), ("q3", 3), ("i1", 1),),
    "0:1": (("i2", 1),),
    "0:2": (("o", 3), ("i3", 1),),
    "1:0": (("i0", 3), ("f0", 2),),
    "1:1": (("f1", 2),),
    "1:2": (("i1", 2), ("f2", 2),),
    "2:0": (("i2", 2),),
    "2:1": (("i3", 2), ("f3", 2),),
    "3:0": (("f0", 3),),
    "3:1": (("f1", 3),),
    "norm": (("i1", 3), ("f2", 3),),
    "chunk0": (("i2", 3), ("f3", 3),),
    "grad0": (("i3", 3),),
}
Y_FIRST = {"s", "q1", "q2", "i0", "i1", "i2", "i3", "f0"}
LEAVE = ("s", "q0", "q1", "q2", "q3", "o", "i0", "F", "i1", "i2", "i3")


class Place:
    def __init__(self, nz):
        dp, fs = lax.axis_index("dp"), lax.axis_index("fsdp")
        self.nz = nz
        self.z, self.y = lax.div(dp, 2), lax.rem(dp, 2)
        self.x, self.c = lax.div(fs, 2), lax.rem(fs, 2)

    def device(self, z=None, y=None, x=None, c=None):
        z, y = self.z if z is None else z, self.y if y is None else y
        x, c = self.x if x is None else x, self.c if c is None else c
        return {"dp": z * 2 + y, "fsdp": x * 2 + c}

    def up(self, k):
        return lax.rem(self.z + k, self.nz)

    def down(self, k):
        return lax.rem(self.z + self.nz - k, self.nz)

    def around(self):
        for k in range(1, 4 * self.nz):
            y = 1 - self.y if k // 2 % 2 else self.y
            x = 1 - self.x if k % 2 else self.x
            yield (self.up(k // 4), y, x), (self.down(k // 4), y, x)

    def peers(self):
        yield self.device(c=1 - self.c)
        yield self.device(x=1 - self.x, c=1 - self.c)
        for (z, y, x), _ in self.around():
            yield self.device(z, y, x)

    def near(self):
        yield self.device(c=1 - self.c)
        yield self.device(x=1 - self.x)
        yield self.device(x=1 - self.x, c=1 - self.c)

    def far(self):
        yield self.device(y=1 - self.y)
        for k in range(1, self.nz):
            yield self.device(z=self.up(k))
            yield self.device(z=self.up(k), y=1 - self.y)

    def barrier(self):
        sem = pltpu.get_barrier_semaphore()
        for peer in self.peers():
            pl.semaphore_signal(sem, inc=1, device_id=peer, device_id_type=MESH_ID)
        pl.semaphore_wait(sem, 1 + 4 * self.nz)


def remote(src, dst, send, recv, peer):
    return pltpu.make_async_remote_copy(
        src_ref=src, dst_ref=dst, send_sem=send, recv_sem=recv, device_id=peer,
        device_id_type=MESH_ID,
    )


class Gather:
    def __init__(self, place, shard, whole, view, sems, m, y_first, plane=None, base=None):
        self.place, self.shard, self.whole, self.view = place, shard, whole, view
        self.send, self.recv, self.own = sems
        self.m = m
        self.y_first = y_first
        self.plane, self.base = plane, base

    def at(self, *index):
        return self.whole.at[(*index, *self.view)]

    def hops(self, stage):
        p = self.place
        every = slice(None)
        zs = every if self.plane is None else self.plane
        if stage == 0:
            src = self.shard.at[self.view]
            for k in range(1, p.nz):
                yield src, self.at(p.z, p.y, p.x, p.c), self.at(p.down(k), p.y, p.x, p.c), p.device(z=p.up(k))
        elif stage == 3:
            mine = self.at(zs, every, every, p.c)
            yield mine, mine, self.at(zs, every, every, 1 - p.c), p.device(c=1 - p.c)
        elif stage == 1:
            mine = self.at(zs, p.y, p.x, p.c)
            if self.y_first:
                yield mine, mine, self.at(zs, 1 - p.y, p.x, p.c), p.device(y=1 - p.y)
            else:
                yield mine, mine, self.at(zs, p.y, 1 - p.x, p.c), p.device(x=1 - p.x)
        elif self.y_first:
            mine = self.at(zs, every, p.x, p.c)
            yield mine, mine, self.at(zs, every, 1 - p.x, p.c), p.device(x=1 - p.x)
        else:
            mine = self.at(zs, p.y, every, p.c)
            yield mine, mine, self.at(zs, 1 - p.y, every, p.c), p.device(y=1 - p.y)

    def copies(self, stage, arriving):
        for k, (src, dst, land, peer) in enumerate(self.hops(stage)):
            yield remote(
                src, land if arriving else dst, self.send.at[self.m, stage, k],
                self.recv.at[self.m, stage, k], peer,
            )

    def local(self):
        p = self.place
        return pltpu.make_async_copy(
            self.shard.at[self.view], self.at(p.z, p.y, p.x, p.c), self.own.at[self.m]
        )

    def start(self):
        for copy in self.copies(0, False):
            copy.start()
        self.local().start()

    def arrive(self, stage):
        for copy in self.copies(stage, True):
            copy.wait_recv()

    def enter(self):
        if self.plane is None:
            self.arrive(0)
            self.local().wait()
            return
        p = self.place
        hop = lax.rem(p.z + p.nz - self.plane, p.nz)

        @pl.when(hop == 0)
        def _():
            self.base.local().wait()

        @pl.when(hop != 0)
        def _():
            k = jnp.maximum(hop, 1) - 1
            remote(
                self.shard.at[self.view], self.at(self.plane, p.y, p.x, p.c),
                self.send.at[self.base.m, 0, k], self.recv.at[self.base.m, 0, k],
                p.device(z=p.up(1)),
            ).wait_recv()

    def step(self, stage):
        if stage == 1:
            self.enter()
        else:
            self.arrive(stage - 1)
        for copy in self.copies(stage, False):
            copy.start()

    def drain(self, stages=range(4)):
        for stage in stages:
            for copy in self.copies(stage, False):
                copy.wait_send()


class Reduce:
    def __init__(self, place, source, bufs, sems, write):
        self.place, self.source = place, source
        self.r0, self.r1, self.r2, self.r3 = bufs
        self.send, self.recv = sems
        self.write = write

    def hops(self, stage, cs, x_first):
        p = self.place
        every = slice(None)
        r0, r1, r2, r3 = (ref.at[cs] for ref in (self.r0, self.r1, self.r2, self.r3))
        if stage == 0:
            yield self.source.at[cs, every, every, every, 1 - p.c], r0, p.device(c=1 - p.c)
        elif stage == 1:
            if x_first:
                yield r0.at[every, every, every, 1 - p.x], r1, p.device(x=1 - p.x)
            else:
                yield r0.at[every, every, 1 - p.y], r1, p.device(y=1 - p.y)
        elif stage == 2:
            if x_first:
                yield r1.at[every, every, 1 - p.y], r2, p.device(y=1 - p.y)
            else:
                yield r1.at[every, every, 1 - p.x], r2, p.device(x=1 - p.x)
        else:
            for k in range(1, p.nz):
                yield r2.at[every, p.up(k)], r3.at[every, k - 1], p.device(z=p.up(k))

    def copies(self, stage, c, x_first, count=1):
        for k, (src, dst, peer) in enumerate(self.hops(stage, pl.ds(c, count), x_first)):
            yield remote(src, dst, self.send.at[c, stage, k], self.recv.at[c, stage, k], peer)

    def step(self, stage, c, x_first=False, count=1):
        p = self.place
        cs = pl.ds(c, count)
        if stage:
            for copy in self.copies(stage - 1, c, x_first, count):
                copy.wait_recv()
        if stage == 1:
            self.r0[cs] = self.source[cs, :, :, :, p.c] + self.r0[cs]
        elif stage == 2:
            mine = self.r0[cs, :, :, p.x] if x_first else self.r0[cs, :, p.y]
            self.r1[cs] = mine + self.r1[cs]
        elif stage == 3:
            mine = self.r1[cs, :, p.y] if x_first else self.r1[cs, :, p.x]
            self.r2[cs] = mine + self.r2[cs]
        elif stage == 4:
            for n in range(count):
                total = self.r2[c + n, p.z].astype(F32)
                for k in range(p.nz - 1):
                    total = total + self.r3[c + n, k].astype(F32)
                self.write(c + n, total)
            return
        for copy in self.copies(stage, c, x_first, count):
            copy.start()

    def drain(self, c, x_first=False, count=1, stages=range(4)):
        for stage in stages:
            for copy in self.copies(stage, c, x_first, count):
                copy.wait_send()

    def short(self, c, land, sems):
        p = self.place
        for k, (to, _) in enumerate(p.around()):
            yield remote(self.r0.at[(c, *to)], land.at[k], sems[0].at[k], sems[1].at[k], p.device(*to))

    def short_start(self, c, land, sems):
        for copy in self.copies(0, c, False):
            copy.wait_recv()
        self.r0[c] = self.source[c, :, :, :, self.place.c] + self.r0[c]
        for copy in self.short(c, land, sems):
            copy.start()

    def short_end(self, c, land, sems):
        p = self.place
        total = self.r0[c, p.z, p.y, p.x].astype(F32)
        for k, copy in enumerate(self.short(c, land, sems)):
            copy.wait_recv()
            total = total + land[k].astype(F32)
        self.write(c, total)

    @staticmethod
    def shapes(n, nz, rows, cols):
        return [
            ((n, nz, 2, 2, rows, cols), BF), ((n, nz, 2, rows, cols), BF),
            ((n, nz, rows, cols), BF), ((n, nz - 1, rows, cols), BF),
        ]


def project_rows(i, x_ref, wq, prm_ref, h_ref, q_ref, k_ref, v_ref, factor):
    rows = tile_at(i)
    unit, _ = centred(x_ref[rows, :].astype(F32))
    h = (unit * prm_ref[0:1, :] + prm_ref[1:2, :]).astype(BF)
    h_ref[rows, :] = h
    width = h.shape[1]
    qkv = dot(h, wq)
    q_ref[rows, :] = (qkv[:, :width] * factor).astype(BF)
    k_ref[rows, :] = (qkv[:, width : 2 * width] * factor).astype(BF)
    v_ref[rows, :] = qkv[:, 2 * width :].astype(BF)


def attend_pair(
    p, q_ref, k_ref, v_ref, fx_ref, pq_ref, pk_ref, attr_ref, den_ref, low_ref,
    site=lambda j: None,
):
    length = q_ref.shape[0]
    feats = fx_ref.shape[1]
    lanes = tile_at(p, LANES)
    shift = 0.5 * math.log2(feats)
    cols = [tile_at(2 * p + hh, feats) for hh in range(2)]
    step = FEAT_TILE
    for hh in range(2):
        fm = fx_ref[2 * p + hh][:, :LANES]
        for src, dst in ((q_ref, pq_ref), (k_ref, pk_ref)):
            for t in range(length // step):
                rows = slice(t * step, (t + 1) * step)
                part = src[rows, lanes]
                scores = dot_bt(part, fm)
                wide = jnp.where(lane_ids(step) // 64 == hh, part.astype(F32), 0.0)
                square = jnp.sum(wide * wide, axis=-1, keepdims=True)
                feat = jnp.exp2(scores * LOG2E - (square * (0.5 * LOG2E) + shift))
                dst[rows, cols[hh]] = feat.astype(BF)
    site(1)
    ones = jnp.ones((length, LANES), BF)
    vx = jnp.concatenate([v_ref[:, lanes], ones], axis=1)
    states = [None, None]
    for b in range(length // BLOCK):
        base = b * BLOCK
        for i in range(BLOCK // TILE):
            rows = slice(base + i * TILE, base + (i + 1) * TILE)
            keys = slice(base, base + (i + 1) * TILE)
            got = []
            for hh in range(2):
                pq = pq_ref[rows, cols[hh]]
                weights = causal(dot_bt(pq, pk_ref[keys, cols[hh]]), i * TILE)
                both = dot(weights, vx[keys])
                if b:
                    both = both + dot(pq, low_ref[2 * p + hh, b - 1])
                got.append(both)
            first = lane_ids(TILE) < 64
            num = jnp.where(first, got[0][:, :LANES], got[1][:, :LANES])
            den = jnp.where(first, got[0][:, LANES:], got[1][:, LANES:])
            attr_ref[rows, lanes] = (num / den).astype(BF)
            den_ref[rows, lanes] = den
        if base + BLOCK < length:
            block = slice(base, base + BLOCK)
            for hh in range(2):
                more = dot_at(pk_ref[block, cols[hh]], vx[block])
                states[hh] = more if b == 0 else states[hh] + more
                low_ref[2 * p + hh, b] = states[hh].astype(BF)


def forward_kernel(
    factor, x_ref, wq_ref, prm_ref, fx_ref,
    h_ref, q_ref, k_ref, v_ref, pq_ref, pk_ref, attr_ref, den_ref, low_ref,
):
    def rows(i, carry):
        project_rows(i, x_ref, wq_ref[...], prm_ref, h_ref, q_ref, k_ref, v_ref, factor)
        return carry

    lax.fori_loop(0, x_ref.shape[0] // TILE, rows, 0)

    def pair(p, carry):
        attend_pair(
            p, q_ref, k_ref, v_ref, fx_ref, pq_ref, pk_ref, attr_ref, den_ref, low_ref
        )
        return carry

    lax.fori_loop(0, x_ref.shape[1] // LANES, pair, 0)


def ffn_rows(
    t, x_ref, attr_ref, cot_ref, wo, wi, wf, prm_ref, bin_ref, seq_ref,
    act_ref, dy_ref, datt_ref, gprm_ref, hid_ref, du_ref, h_ref, gr_ref, dor_ref, bin_row=0,
):
    width = x_ref.shape[1]
    chunk = width
    rows = tile_at(t, FFN_TILE)
    y = x_ref[rows, :].astype(F32) + dot(attr_ref[rows, :], wo())
    unit, inv = centred(y)
    gain = prm_ref[2:3, :]
    h = (unit * gain + prm_ref[3:4, :]).astype(BF)
    h_ref[rows, :] = h
    g = cot_ref[rows, :].astype(F32) * seq_ref[0:1, 0:1]
    gr = g.astype(BF)
    gr_ref[rows, :] = gr
    out = y + prm_ref[4:5, :]
    dh = jnp.zeros((FFN_TILE, width), F32)
    for c in range(hid_ref.shape[1] // chunk):
        cs = slice(c * chunk, (c + 1) * chunk)
        u = dot(h, wi(cs)) + bin_ref[bin_row : bin_row + 1, cs]
        cdf = 0.5 + 0.5 * lax.erf(u * math.sqrt(0.5))
        slope = cdf + u * jnp.exp2(u * u * (-0.5 * LOG2E)) * (1.0 / math.sqrt(2.0 * math.pi))
        hid = (u * cdf).astype(BF)
        hid_ref[rows, cs] = hid
        out = out + dot(hid, wf(c))
        du = (dot_bt(gr, wf(c)) * slope).astype(BF)
        du_ref[rows, cs] = du
        gprm_ref[5 + c : 6 + c, :] += jnp.sum(du.astype(F32), axis=0, keepdims=True)
        dh = dh + dot_bt(du, wi(cs))
    act_ref[rows, :] = out.astype(BF)
    gprm_ref[2:3, :] += jnp.sum(dh * unit, axis=0, keepdims=True)
    gprm_ref[3:4, :] += jnp.sum(dh, axis=0, keepdims=True)
    gprm_ref[4:5, :] += jnp.sum(g, axis=0, keepdims=True)
    dy = g + norm_back(dh, unit, inv, gain)
    dy_ref[rows, :] = dy
    dor = dy.astype(BF)
    dor_ref[rows, :] = dor
    datt_ref[rows, :] = dot_bt(dor, wo())


def ffn_norm(t, x_ref, attr_ref, cot_ref, wo, prm_ref, seq_ref, y_ref, h_ref, gr_ref):
    rows = tile_at(t, FFN_TILE)
    y = x_ref[rows, :].astype(F32) + dot(attr_ref[rows, :], wo)
    y_ref[rows, :] = y
    unit, _ = centred(y)
    h_ref[rows, :] = (unit * prm_ref[2:3, :] + prm_ref[3:4, :]).astype(BF)
    gr_ref[rows, :] = (cot_ref[rows, :].astype(F32) * seq_ref[0:1, 0:1]).astype(BF)


def ffn_chunk(t, c, wi, wf, bias, h_ref, gr_ref, hid_ref, du_ref, gprm_ref):
    rows = tile_at(t, FFN_TILE)
    width = h_ref.shape[1]
    cs = slice(c * width, (c + 1) * width)
    u = dot(h_ref[rows, :], wi) + bias
    cdf = 0.5 + 0.5 * lax.erf(u * math.sqrt(0.5))
    slope = cdf + u * jnp.exp2(u * u * (-0.5 * LOG2E)) * (1.0 / math.sqrt(2.0 * math.pi))
    hid_ref[rows, cs] = (u * cdf).astype(BF)
    du = (dot_bt(gr_ref[rows, :], wf) * slope).astype(BF)
    du_ref[rows, cs] = du
    gprm_ref[5 + c : 6 + c, :] += jnp.sum(du.astype(F32), axis=0, keepdims=True)


def ffn_final(
    t, cot_ref, wo, wi, prm_ref, seq_ref, y_ref, du_ref, dy_ref, dor_ref, datt_ref, gprm_ref
):
    rows = tile_at(t, FFN_TILE)
    y = y_ref[rows, :]
    dh = dot_bt(du_ref[rows, :], wi)
    unit, inv = centred(y)
    g = cot_ref[rows, :].astype(F32) * seq_ref[0:1, 0:1]
    gprm_ref[2:3, :] += jnp.sum(dh * unit, axis=0, keepdims=True)
    gprm_ref[3:4, :] += jnp.sum(dh, axis=0, keepdims=True)
    gprm_ref[4:5, :] += jnp.sum(g, axis=0, keepdims=True)
    dy = g + norm_back(dh, unit, inv, prm_ref[2:3, :])
    dy_ref[rows, :] = dy
    dor = dy.astype(BF)
    dor_ref[rows, :] = dor
    datt_ref[rows, :] = dot_bt(dor, wo)


def put_rows(g_ref, chunk, c, value):
    if len(g_ref.shape) == 5:
        g_ref[chunk, c] = value
    else:
        g_ref[chunk, lax.div(c, 2), lax.rem(c, 2)] = value.reshape(2, 2, *value.shape[1:])


def grads_out(c, hid_ref, gr_ref, g_ref):
    width = gr_ref.shape[1]
    grad = dot_at(hid_ref[:, tile_at(c)], gr_ref[...]).astype(BF)
    grad = grad.reshape(4, 4, 16, width)
    for q in range(4):
        put_rows(g_ref, q, c, grad[:, q])


def grads_in(c, h_ref, du_ref, attr_ref, dor_ref, g_ref):
    width = h_ref.shape[1]
    count = du_ref.shape[1] // width
    cs = tile_at(c)
    at = pl.ds(c * 4, 4)
    grad = dot_at(h_ref[:, cs], du_ref[...]).astype(BF)
    for k in range(count):
        g_ref[4 + k, at] = grad[:, k * width : (k + 1) * width].reshape(4, 4, 16, width)
    grad = dot_at(attr_ref[:, cs], dor_ref[...]).astype(BF)
    g_ref[4 + count, at] = grad.reshape(4, 4, 16, width)


def loop(start, stop, step):
    def run(i, carry):
        step(i)
        return carry

    lax.fori_loop(start, stop, run, 0)


def middle_kernel(
    x_ref, attr_ref, cot_ref, wo_ref, wi_ref, wf_ref, prm_ref, seq_ref,
    act_ref, dy_ref, datt_ref, gprm_ref, g_ref,
    hid_ref, du_ref, h_ref, gr_ref, dor_ref, bin_ref,
):
    length, width = x_ref.shape
    gprm_ref[...] = jnp.zeros_like(gprm_ref)
    bin_ref[...] = dot_bt(unit_rows(8), wf_ref[:, width:])
    loop(0, length // FFN_TILE, lambda t: ffn_rows(
        t, x_ref, attr_ref, cot_ref, lambda: wo_ref[...], lambda cs: wi_ref[:, cs],
        lambda c: wf_ref[c * width : (c + 1) * width, :width], prm_ref, bin_ref, seq_ref,
        act_ref, dy_ref, datt_ref, gprm_ref, hid_ref, du_ref, h_ref, gr_ref, dor_ref,
    ))
    loop(0, hid_ref.shape[1] // TILE, lambda c: grads_out(c, hid_ref, gr_ref, g_ref))
    loop(0, width // TILE, lambda c: grads_in(c, h_ref, du_ref, attr_ref, dor_ref, g_ref))


def back_pair(
    p, factor, q_ref, k_ref, v_ref, pq_ref, pk_ref, att_ref, den_ref, datt_ref, fx_ref, low_ref,
    ht_ref, dqkv_refs, dn_ref, e_ref, da_ref, tick, store,
):
    length = q_ref.shape[0]
    feats = fx_ref.shape[1]
    lanes = tile_at(p, LANES)
    blocks = length // BLOCK
    cols = [tile_at(2 * p + hh, feats) for hh in range(2)]
    two = jnp.where(lane_ids(length) < 2, 1.0, 0.0).astype(BF)
    v2 = jnp.concatenate([v_ref[:, lanes], two], axis=1)
    for t in range(length // TILE):
        rows = slice(t * TILE, (t + 1) * TILE)
        dn = datt_ref[rows, lanes] / den_ref[rows, lanes]
        prod = dn * att_ref[rows, lanes].astype(F32)
        lane = lane_ids(TILE)
        for hh in range(2):
            mine = lane // 64 == hh
            dden = -jnp.sum(jnp.where(mine, prod, 0.0), axis=-1, keepdims=True)
            high = dden.astype(BF).astype(F32)
            extra = jnp.where(lane == 0, high, jnp.where(lane == 1, dden - high, 0.0))
            dn_ref[hh, rows, :LANES] = jnp.where(mine, dn, 0.0).astype(BF)
            dn_ref[hh, rows, LANES:] = extra.astype(BF)
    for hh in range(2):
        fx = fx_ref[2 * p + hh]
        back = [None] * blocks
        total = None
        for b in range(blocks - 1, 0, -1):
            block = slice(b * BLOCK, (b + 1) * BLOCK)
            more = dot_at(pq_ref[block, cols[hh]], dn_ref[hh, block, :])
            total = more if total is None else total + more
            dz = total[:, LANES : LANES + 1] + total[:, LANES + 1 : LANES + 2]
            high = dz.astype(BF).astype(F32)
            lane = lane_ids(feats)
            extra = jnp.where(lane == 0, high, jnp.where(lane == 1, dz - high, 0.0))
            back[b - 1] = jnp.concatenate([total[:, :LANES], extra], axis=1).astype(BF)

        def put(value, rows, at, hh=hh):
            ref = dqkv_refs[at]
            if hh:
                mine = lane_ids(value.shape[0]) >= 64
                value = jnp.where(mine, value, ref[rows, lanes].astype(F32))
            ref[rows, lanes] = value.astype(BF)

        for b in range(blocks):
            base = b * BLOCK
            for i in range(BLOCK // TILE):
                rows = slice(base + i * TILE, base + (i + 1) * TILE)
                keys = slice(base, base + (i + 1) * TILE)
                dn = dn_ref[hh, rows, :]
                da = causal(dot_bt(dn, v2[keys]), i * TILE)
                da_ref[i * TILE : (i + 1) * TILE, : (i + 1) * TILE] = da
                grad = dot(da, pk_ref[keys, cols[hh]])
                if b:
                    grad = grad + dot_bt(dn, low_ref[2 * p + hh, b - 1])
                e_ref[0, rows, :] = (grad * pq_ref[rows, cols[hh]].astype(F32)).astype(BF)
            for i in range(BLOCK // TILE):
                rows = slice(base + i * TILE, base + (i + 1) * TILE)
                later = slice(base + i * TILE, base + BLOCK)
                pk = pk_ref[rows, cols[hh]]
                pql = pq_ref[later, cols[hh]]
                grad = dot_at(da_ref[i * TILE :, i * TILE : (i + 1) * TILE], pql)
                at = anticausal(dot_bt(pk, pql))
                dv = dot(at, dn_ref[hh, later, :LANES])
                if b < blocks - 1:
                    grad = grad + dot_bt(v2[rows], back[b])
                    dv = dv + dot(pk, back[b][:, :LANES])
                e_ref[1, rows, :] = (grad * pk.astype(F32)).astype(BF)
                put(dv, rows, 2)
        for at, src in ((0, q_ref), (1, k_ref)):
            res = dot(e_ref[at], fx)
            out = (res[:, :LANES] - src[:, lanes].astype(F32) * res[:, LANES:]) * factor
            put(out, slice(0, length), at)
        if hh == 0:
            tick(0)
    store(dot(ht_ref[...], jnp.concatenate([ref[:, lanes] for ref in dqkv_refs], axis=1)).astype(BF))


def input_rows(t, x_ref, wq, prm_ref, dqkv_refs, dy_ref, out_ref, gprm_ref):
    rows = tile_at(t, FFN_TILE)
    dh = dot_bt(jnp.concatenate([ref[rows, :] for ref in dqkv_refs], axis=1), wq)
    unit, inv = centred(x_ref[rows, :].astype(F32))
    gprm_ref[0:1, :] += jnp.sum(dh * unit, axis=0, keepdims=True)
    gprm_ref[1:2, :] += jnp.sum(dh, axis=0, keepdims=True)
    out_ref[rows, :] = (dy_ref[rows, :] + norm_back(dh, unit, inv, prm_ref[0:1, :])).astype(BF)


def flip_rows(h_ref, ht_ref):
    for t in range(h_ref.shape[0] // TILE):
        rows = slice(t * TILE, (t + 1) * TILE)
        ht_ref[:, rows] = h_ref[rows, :].T


def backward_kernel(
    factor, x_ref, h_ref, q_ref, k_ref, v_ref, pq_ref, pk_ref, att_ref, den_ref, datt_ref, dy_ref,
    wq_ref, fx_ref, prm_ref, gin_ref, low_ref,
    out_ref, gq_ref, gprm_ref,
    ht_ref, dqkv_ref, dn_ref, e_ref, da_ref,
):
    gprm_ref[...] = gin_ref[...]
    width = x_ref.shape[1]
    dqkv_refs = [dqkv_ref.at[:, n * width : (n + 1) * width] for n in range(3)]
    flip_rows(h_ref, ht_ref)

    def pair(p, carry):
        def store(value):
            gq_ref[:, tile_at(p, 3 * LANES)] = value

        back_pair(
            p, factor, q_ref, k_ref, v_ref, pq_ref, pk_ref, att_ref, den_ref, datt_ref, fx_ref, low_ref,
            ht_ref, dqkv_refs, dn_ref, e_ref, da_ref, lambda j: None, store,
        )
        return carry

    lax.fori_loop(0, x_ref.shape[1] // LANES, pair, 0)

    def rows(t, carry):
        input_rows(t, x_ref, wq_ref[...], prm_ref, dqkv_refs, dy_ref, out_ref, gprm_ref)
        return carry

    lax.fori_loop(0, x_ref.shape[0] // FFN_TILE, rows, 0)


def sequence_weight(small, seq_ref):
    nf = 4
    me = lax.axis_index("dp") * nf + lax.axis_index("fsdp")
    row = lax.broadcasted_iota(jnp.int32, small.shape, 0)
    lane = lane_ids(small.shape[0]).astype(F32)
    peer = lax.div(row, 16)
    ids = small[:, 5:6].astype(F32)
    hit = (lane == ids) & (lax.rem(row, 16) == 0)
    counts = jnp.sum(
        jnp.where(hit & (lax.rem(peer, nf) == lax.axis_index("fsdp")), 1.0, 0.0),
        axis=0, keepdims=True,
    )
    mine = jnp.sum(jnp.where(hit & (peer == me), 1.0, 0.0), axis=0, keepdims=True)
    size = jnp.sum(counts * mine, axis=1, keepdims=True)
    groups = jnp.sum(jnp.where(counts > 0.5, 1.0, 0.0), axis=1, keepdims=True)
    members = lax.axis_size("dp")
    seq_ref[...] = jnp.broadcast_to(members / (groups * size), seq_ref.shape)


class Columns:
    def __init__(self, ref, start, size):
        self.ref, self.start, self.size = ref, start, size

    def where(self, index):
        n, *rest = index if isinstance(index, tuple) else (index,)
        rows, cols = [*rest, slice(None), slice(None)][:2]
        base = self.start + n * self.size
        low, high = cols.start or 0, self.size if cols.stop is None else cols.stop
        return rows, slice(base + low, base + high)

    def __getitem__(self, index):
        return self.ref[self.where(index)]

    def __setitem__(self, index, value):
        self.ref[self.where(index)] = value


class Total:
    def __init__(self, place, ref, part, near, far, sems):
        self.place, self.ref, self.part, self.near, self.far = place, ref, part, near, far
        self.send, self.recv = sems

    def copies(self, stage):
        peers = self.place.far() if stage else self.place.near()
        src, dst = (self.part, self.far) if stage else (self.ref, self.near)
        for k, peer in enumerate(peers):
            yield remote(src, dst.at[k], self.send.at[stage, k], self.recv.at[stage, k], peer)

    def start(self):
        for copy in self.copies(0):
            copy.start()

    def turn(self):
        for copy in self.copies(0):
            copy.wait_recv()
        self.part[...] = self.ref[...] + sum(self.near[k] for k in range(self.near.shape[0]))
        for copy in self.copies(1):
            copy.start()

    def result(self):
        for copy in self.copies(1):
            copy.wait_recv()
        return self.part[...] + sum(self.far[k] for k in range(self.far.shape[0]))

    def drain(self):
        for stage in range(2):
            for copy in self.copies(stage):
                copy.wait_send()


def layer_kernel(
    nz, factor, x_ref, cot_in, wqs_ref, wos_ref, wis_ref, wfs_ref, fm_ref, id_ref,
    g1_ref, s1_ref, g2_ref, s2_ref, bo_ref, bi_ref,
    act_out, grad_out, partq_ref, gf_ref, gi_ref, go_ref, rest_out, first_out,
    h_ref, q_ref, k_ref, v_ref, pq_ref, pk_ref, attr_ref, den_ref, low_ref,
    wqt_ref, wq_ref, wo_ref, wi_ref, wf_ref, sp_ref, cot_ref, fx_ref, vec_ref, col_ref, prm_ref,
    act_ref, dy_ref, y_ref, g_ref, gprm_ref, hid_ref, du_ref, h2_ref, gr_ref, dor_ref,
    bin_ref, seq_ref, lhs_ref, gq_ref,
    b0, b1, b2, b3, c0, c1, c2, c3,
    rest_ref, rest_part, rest_near, rest_far, first_ref, first_part, first_near, first_far,
    land_ref,
    send, recv, own, big_send, big_recv, q_send, q_recv, rest_send, rest_recv, first_send, first_recv,
    short_send, short_recv, local_sem, tile_sem,
):
    length, width = x_ref.shape
    hidden = hid_ref.shape[1]
    place = Place(nz)
    every = slice(None)
    sems = (send, recv, own)
    pairs, tiles, parts = width // LANES, length // TILE, hidden // width
    slabs = length // FFN_TILE

    def gather(name, shard, whole, view, m, plane=None, base=None):
        return Gather(place, shard, whole, view, sems, m, name in Y_FIRST, plane, base)

    both = (every, every)
    sp = gather("s", col_ref, sp_ref, (slice(0, 16), every), 0)
    o = gather("o", wos_ref, wo_ref, both, 1)
    f = gather("f", wfs_ref, wf_ref, both, 2)
    wq = [gather(f"q{p}", wqt_ref.at[p], wq_ref.at[p], both, 3 + p) for p in range(pairs)]
    wi = [
        gather(f"i{c}", wis_ref, wi_ref, (every, slice(c * width, (c + 1) * width)), 3 + pairs + c)
        for c in range(parts)
    ]
    wf = [
        gather(f"f{c}", wfs_ref, wf_ref, both, 3 + pairs + parts + c, c, f) for c in range(parts)
    ]
    named = {"s": sp, "o": o, "F": f}
    for n in range(pairs):
        named[f"q{n}"] = wq[n]
    for n in range(parts):
        named[f"i{n}"] = wi[n]
        named[f"f{n}"] = wf[n]

    def write(c, value):
        if c < 4:
            gf_ref[c] = value
        elif c < 4 + parts:
            gi_ref[:, (c - 4) * width : (c - 3) * width] = value
        else:
            go_ref[...] = value

    def write_q(c, value):
        for at in range(3):
            where = pl.ds(pl.multiple_of(c * LANES + at * width, LANES), LANES)
            partq_ref[:, where] = value[:, at * LANES : (at + 1) * LANES]

    grid = (nz, 2, 2, 2)
    big = Reduce(place, g_ref, (b0, b1, b2, b3), (big_send, big_recv), write)
    mine = Reduce(place, gq_ref, (c0, c1, c2, c3), (q_send, q_recv), write_q)
    rest = Total(place, rest_ref, rest_part, rest_near, rest_far, (rest_send, rest_recv))
    first = Total(place, first_ref, first_part, first_near, first_far, (first_send, first_recv))
    short_sems = (short_send, short_recv)
    cot_copy = pltpu.make_async_copy(cot_in, cot_ref, local_sem)

    def slab_out(t, src, dst, n):
        rows = tile_at(t, FFN_TILE)
        return pltpu.make_async_copy(src.at[rows], dst.at[rows], tile_sem.at[n, t])

    def at_site(name):
        for who, stage in PLAN.get(name, ()):
            named[who].step(stage)
        for c, stage in SUMS.get(name, ()):
            big.step(stage, c, c % 2 == 0)
        for c, stage in OWN_SUMS.get(name, ()):
            mine.step(stage, c)

    def sites(p, prefix):
        def site(j):
            for n in range(pairs):
                name = f"{prefix}{n}:{j}"
                if name in PLAN or name in SUMS or name in OWN_SUMS:
                    pl.when(p == n)(functools.partial(at_site, name))

        return site

    vec_ref[...] = jnp.zeros_like(vec_ref)
    for n, ref in enumerate((g1_ref, s1_ref, g2_ref, s2_ref, bo_ref)):
        vec_ref[n : n + 1, : ref.shape[1]] = ref[...].astype(F32)
    vec_ref[5:6, :] = jnp.full((1, LANES), id_ref[0], jnp.int32).astype(F32)
    for n in range(4):
        vec_ref[8 + n : 9 + n, :16] = bi_ref[:, n * 16 : (n + 1) * 16].astype(F32)
    col_ref[...] = dot_at(vec_ref[...].astype(BF), unit_rows(16)).astype(BF)
    for p in range(pairs):
        for n in range(3):
            at = n * width + p * LANES
            wqt_ref[p, :, n * LANES : (n + 1) * LANES] = wqs_ref[:, at : at + LANES]
    place.barrier()
    for who in LEAVE:
        named[who].start()
    cot_copy.start()
    head_size, feats = fm_ref.shape[1:]
    for n in range(fm_ref.shape[0]):
        row = lax.broadcasted_iota(jnp.int32, (head_size, LANES), 0)
        place_at = jnp.where(lane_ids(head_size) == row + (n % 2) * head_size, 1.0, 0.0).astype(BF)
        fx_ref[n, :, :LANES] = dot_at(fm_ref[n], place_at).astype(BF)
        fx_ref[n, :, LANES:] = jnp.ones((feats, LANES), BF)
    at_site("start")
    sp.arrive(3)
    small = sp_ref[...].reshape(width, LANES)
    prm = dot_bt(unit_rows(16), small)
    prm_ref[...] = prm[:8]
    at_site("params")
    sequence_weight(small, seq_ref)
    for c in range(parts):
        for n in range(4):
            lhs_ref[n, c : c + 1, :] = prm[8 + n : 9 + n, c * LANES : (c + 1) * LANES]
    row = lax.broadcasted_iota(jnp.int32, (LANES, width), 0)
    col = lax.broadcasted_iota(jnp.int32, (LANES, width), 1)
    bias = jnp.zeros((8, width), F32)
    for n in range(4):
        spread = (lax.div(row, 16) == lax.div(col, 64)) & (
            lax.rem(row, 16) + n * 16 == lax.rem(col, 64)
        )
        bias = bias + dot(lhs_ref[n].astype(BF), jnp.where(spread, 1.0, 0.0).astype(BF))
    bin_ref[...] = bias
    gprm_ref[...] = jnp.zeros_like(gprm_ref)

    def rows(i):
        rows = tile_at(i)
        unit, _ = centred(x_ref[rows, :].astype(F32))
        h_ref[rows, :] = (unit * prm_ref[0:1, :] + prm_ref[1:2, :]).astype(BF)

    loop(0, tiles, rows)
    at_site("rows")

    def pair(p):
        site = sites(p, "")
        for n in range(pairs):
            pl.when(p == n)(functools.partial(wq[n].arrive, 3))
        lanes = tile_at(p, LANES)
        for t in range(tiles):
            rows = slice(t * TILE, (t + 1) * TILE)
            qkv = dot(h_ref[rows, :], wq_ref[p].reshape(width, 3 * LANES))
            q_ref[rows, lanes] = (qkv[:, :LANES] * factor).astype(BF)
            k_ref[rows, lanes] = (qkv[:, LANES : 2 * LANES] * factor).astype(BF)
            v_ref[rows, lanes] = qkv[:, 2 * LANES :].astype(BF)
        site(0)
        attend_pair(
            p, q_ref, k_ref, v_ref, fx_ref, pq_ref, pk_ref, attr_ref, den_ref, low_ref,
            site,
        )
        site(2)

    loop(0, pairs, pair)
    o.arrive(3)
    cot_copy.wait()

    def norm(t):
        wo = wo_ref[...].reshape(width, width)
        ffn_norm(t, x_ref, attr_ref, cot_ref, wo, prm_ref, seq_ref, y_ref, h2_ref, gr_ref)

    loop(0, slabs, norm)
    at_site("norm")
    for c in range(parts):
        wi[c].arrive(3)
        wf[c].arrive(3)
        cs = slice(c * width, (c + 1) * width)

        def chunk(t, c=c, cs=cs):
            w_in, w_out = wi_ref[..., cs].reshape(width, width), wf_ref[c].reshape(width, width)
            bias = bin_ref[c : c + 1, :]
            ffn_chunk(t, c, w_in, w_out, bias, h2_ref, gr_ref, hid_ref, du_ref, gprm_ref)

        loop(0, slabs, chunk)
        at_site(f"chunk{c}")
        loop(2 * c, 2 * c + 2, lambda n: grads_out(n, hid_ref, gr_ref, g_ref))

        def grad(n, c=c, cs=cs):
            value = dot_at(h2_ref[:, tile_at(n)], du_ref[:, cs]).astype(BF)
            g_ref[4 + c, pl.ds(n * 2, 2)] = value.reshape(2, 2, 2, 2, 16, width)

        loop(0, width // TILE, grad)
        at_site(f"grad{c}")

    def final(t):
        ffn_final(
            t, cot_ref, wo_ref[...].reshape(width, width), wi_ref[...].reshape(width, hidden),
            prm_ref, seq_ref, y_ref, du_ref, dy_ref, dor_ref, y_ref, gprm_ref,
        )

    loop(0, slabs, final)
    at_site("final")

    def grad_o(n):
        value = dot_at(attr_ref[:, tile_at(n)], dor_ref[...]).astype(BF)
        g_ref[4 + parts, pl.ds(n * 2, 2)] = value.reshape(2, 2, 2, 2, 16, width)

    loop(0, width // TILE, grad_o)
    at_site("grad_o")
    for n in range(3 + parts):
        for c in range(pairs):
            rest_ref[n * pairs + c : n * pairs + c + 1, :] = gprm_ref[2 + n : 3 + n, c * LANES : (c + 1) * LANES]
    for n in range((3 + parts) * pairs, rest_ref.shape[0]):
        rest_ref[n : n + 1, :] = jnp.zeros((1, LANES), F32)
    rest.start()

    ht_ref = du_ref.at[0:width, 0:length]
    da_ref = du_ref.at[width : 2 * width, 0:BLOCK]
    dn_ref = Columns(du_ref, length, 2 * LANES)
    e_ref = Columns(du_ref, length + 4 * LANES, 2 * LANES)
    dqkv_refs = (cot_ref, gr_ref, dor_ref)
    out_ref = h2_ref
    flip_rows(h_ref, ht_ref)

    def back(p):
        def store(value):
            gq_ref[p] = value.reshape(*grid, 16, 3 * LANES)

        back_pair(
            p, factor, q_ref, k_ref, v_ref, pq_ref, pk_ref, attr_ref, den_ref, y_ref, fx_ref,
            low_ref, ht_ref, dqkv_refs, dn_ref, e_ref, da_ref, sites(p, "b"), store,
        )
        mine.step(0, p)
        sites(p, "b")(1)

        @pl.when(p == 0)
        def _():
            rest.turn()

        @pl.when(p == 2)
        def _():
            rest_out[...] = rest.result()

    loop(0, pairs, back)
    last = pairs - 1

    def rows_back(t):
        weights = [
            wq_ref[p, ..., n * LANES : (n + 1) * LANES].reshape(width, LANES)
            for n in range(3)
            for p in range(pairs)
        ]
        input_rows(
            t, x_ref, jnp.concatenate(weights, axis=1), prm_ref, dqkv_refs, dy_ref, out_ref, gprm_ref
        )
        slab_out(t, out_ref, grad_out, 1).start()

    def output(t):
        rows = tile_at(t, FFN_TILE)
        out = x_ref[rows, :].astype(F32) + dot(attr_ref[rows, :], wo_ref[...].reshape(width, width))
        out = out + dot(hid_ref[rows, :], wf_ref[...].reshape(hidden, width)) + prm_ref[4:5, :]
        act_ref[rows, :] = out.astype(BF)
        slab_out(t, act_ref, act_out, 0).start()

    mine.step(3, last - 2)
    mine.step(2, last - 1)
    loop(0, slabs // 2, rows_back)
    mine.short_start(last, land_ref, short_sems)
    loop(slabs // 2, slabs, rows_back)
    for n in range(2):
        for c in range(pairs):
            first_ref[n * pairs + c : n * pairs + c + 1, :] = gprm_ref[n : n + 1, c * LANES : (c + 1) * LANES]
    first.start()
    mine.step(3, last - 1)
    loop(0, slabs // 2, output)
    first.turn()
    loop(slabs // 2, slabs, output)
    at_site("tail")
    mine.step(4, last - 3)
    mine.step(4, last - 2)
    mine.step(4, last - 1)
    first_out[...] = first.result()
    mine.short_end(last, land_ref, short_sems)
    for t in range(slabs):
        slab_out(t, act_ref, act_out, 0).wait()
        slab_out(t, out_ref, grad_out, 1).wait()
    for g in (sp, o, *wq, *wi):
        g.drain()
    f.drain((0,))
    for g in wf:
        g.drain((1, 2, 3))
    for c in range(g_ref.shape[0]):
        big.drain(c, c % 2 == 0)
    loop(0, last, mine.drain)
    mine.drain(last, stages=(0,))
    for copy in mine.short(last, land_ref, short_sems):
        copy.wait_send()
    rest.drain()
    first.drain()


def finish_kernel(
    act_in, grad_in, gq_in, gf_in, gi_in, go_in, rest_in, first_in,
    act_ref, grad_ref, gq_ref, go_ref, gi_ref, gf_ref,
    g1_ref, s1_ref, g2_ref, s2_ref, bi_ref, bo_ref,
    hold_ref, holdq_ref, holdf_ref, holdi_ref, holdo_ref, in_sem, out_sem,
):
    moves = []

    def move(src, hold, dst):
        n = len(moves)
        moves.append((
            pltpu.make_async_copy(src, hold, in_sem.at[n]),
            pltpu.make_async_copy(hold, dst, out_sem.at[n]),
        ))
        moves[n][0].start()

    for n, (src, dst) in enumerate(((act_in, act_ref), (grad_in, grad_ref))):
        for t in range(src.shape[0] // TILE):
            rows = pl.ds(t * TILE, TILE)
            move(src.at[rows], hold_ref.at[n, rows], dst.at[rows])
    move(gq_in, holdq_ref, gq_ref)
    move(gi_in, holdi_ref, gi_ref)
    move(go_in, holdo_ref, go_ref)
    for n in range(4):
        move(gf_in.at[n], holdf_ref.at[n], gf_ref.at[pl.ds(16 * n, 16)])
    me = lax.axis_index("dp") * 4 + lax.axis_index("fsdp")
    row = lax.broadcasted_iota(jnp.int32, (LANES, LANES), 0)
    lane = lane_ids(LANES)

    def cut(value, start):
        pick = jnp.where(row == lane + start, 1.0, 0.0)
        return lax.dot_general(
            value, pick, (((1,), (0,)), ((), ())), precision=lax.Precision.HIGHEST,
            preferred_element_type=F32,
        )

    def only(value, base, count, which):
        part = value[base : base + count]
        at = lax.broadcasted_iota(jnp.int32, part.shape, 0)
        return jnp.sum(jnp.where(at == which, part, 0.0), axis=0, keepdims=True)

    for come, go in moves:
        come.wait()
        go.start()
    pairs = first_in.shape[0] // 2
    spot = lax.rem(me, 8) * 16
    first, rest = cut(first_in[...], spot), cut(rest_in[...], spot)
    which = lax.div(me, 8)
    for n, ref in enumerate((g1_ref, s1_ref)):
        ref[...] = only(first, n * pairs, pairs, which)[:, :16]
    for n, ref in enumerate((g2_ref, s2_ref, bo_ref)):
        ref[...] = only(rest, n * pairs, pairs, which)[:, :16]
    wide = cut(rest_in[...], lax.rem(me, 2) * 64)
    each = pairs * pairs
    bi_ref[...] = only(wide, 3 * pairs, each, lax.div(me, 2))[:, :64]
    for _, go in moves:
        go.wait()


ANY = pl.BlockSpec(memory_space=pl.ANY)
VM = pl.BlockSpec(memory_space=pltpu.VMEM)


def call(kernel, outs, scratch, name, ins=None, out_specs=None, collective=None):
    extra = {} if ins is None else {"in_specs": ins, "out_specs": out_specs}
    params = {} if collective is None else {"collective_id": collective, "has_side_effects": True}
    return pl.pallas_call(
        kernel,
        out_shape=[jax.ShapeDtypeStruct(s, d) for s, d in outs],
        scratch_shapes=[pltpu.SemaphoreType.DMA(s) if d is None else pltpu.VMEM(s, d) for s, d in scratch],
        compiler_params=pltpu.CompilerParams(vmem_limit_bytes=60 * 2**20, **params),
        name=name,
        **extra,
    )


def padded_features(fm):
    heads, feats, _ = fm.shape
    zero = jnp.zeros_like(fm)
    even = (jnp.arange(heads) % 2 == 0)[:, None, None]
    return jnp.concatenate(
        [jnp.where(even, fm, zero), jnp.where(even, zero, fm), jnp.ones((heads, feats, LANES), BF)],
        axis=-1,
    )


def by_pair(columns, outer):
    rows, count = columns.shape
    split = columns.reshape(rows, outer, count // (outer * LANES), LANES)
    return split.swapaxes(1, 2).reshape(rows, count)


def middle(tokens, attr, cotangent, wo, wi, wf, prm, seq_weight):
    length, width = tokens.shape
    hidden = wi.shape[1]
    big, deep = (length, width), (length, hidden)
    chunks = 5 + hidden // width
    return call(
        middle_kernel,
        [(big, BF), (big, F32), (big, F32), ((16, width), F32), ((chunks, width // 64, 4, 16, width), BF)],
        [(deep, BF), (deep, BF), (big, BF), (big, BF), (big, BF), ((8, hidden), F32)],
        "middle",
    )(tokens, attr, cotangent, wo, wi, wf, prm, seq_weight)


def forward_outs(length, width, heads, feats):
    big = (length, width)
    deep = (length, heads * feats)
    low = (heads, length // BLOCK - 1, feats, 2 * LANES)
    return [(big, BF)] * 4 + [(deep, BF)] * 2 + [(big, BF), (big, F32), (low, BF)]


def backward_scratch(length, width):
    return [
        ((width, length), BF), ((length, 3 * width), BF),
        ((2, length, 2 * LANES), BF), ((2, length, 2 * LANES), BF), ((BLOCK, BLOCK), BF),
    ]


def plain_body(
    tokens, cotangent, group_id, w_qkv, w_out, w_ffn_in, w_ffn_out,
    gain_one, shift_one, gain_two, shift_two, bias_in, bias_out, feature_matrix,
):
    gather = functools.partial(lax.all_gather, axis_name=AXES, axis=0, tiled=True)
    scatter = functools.partial(
        lax.psum_scatter, axis_name=AXES, scatter_dimension=0, tiled=True
    )
    length, width = tokens.shape
    heads, feats, head_size = feature_matrix.shape
    hidden = w_ffn_in.shape[1]
    factor = head_size ** (-0.25)
    wq, wo, wi, wf = gather(w_qkv), gather(w_out), gather(w_ffn_in), gather(w_ffn_out)
    prm = gather(jnp.stack([gain_one, shift_one, gain_two, shift_two, bias_out], axis=1))
    prm = jnp.pad(prm.T.astype(F32), ((0, 3), (0, 0)))
    wf = jnp.concatenate([wf, jnp.pad(gather(bias_in)[:, None], ((0, 0), (0, LANES - 1)))], axis=1)

    slice_seqs = lax.axis_size("dp") * group_id.shape[0]
    labels = jnp.arange(slice_seqs // 2, dtype=jnp.int32)
    onehot = (group_id[:, None] == labels[None, :]).astype(F32)
    counts = lax.psum(jnp.sum(onehot, axis=0), "dp")
    group_size = jnp.sum(onehot * counts[None, :], axis=-1)
    groups = jnp.sum((counts > 0.5).astype(F32))
    seq_weight = jnp.broadcast_to((slice_seqs / (groups * group_size))[:, None], (8, LANES))

    fx = padded_features(feature_matrix)
    h1, q, k, v, pq, pk, attr, den, low = call(
        functools.partial(forward_kernel, factor),
        forward_outs(length, width, heads, feats), [], "forward",
    )(tokens, wq, prm, fx)
    act, dy, datt, gprm, grads = middle(tokens, attr, cotangent, wo, wi, wf, prm, seq_weight)
    input_grad, gq, gprm = call(
        functools.partial(backward_kernel, factor),
        [((length, width), BF), ((width, 3 * width), BF), ((16, width), F32)],
        backward_scratch(length, width), "backward",
    )(tokens, h1, q, k, v, pq, pk, attr, den, datt, dy, wq, fx, prm, gprm, low)
    gq = by_pair(gq, width // LANES)
    grads = grads.reshape(-1, width // 16, 16, width)
    gf = grads[:4].transpose(1, 0, 2, 3).reshape(hidden, width)
    gi = grads[4:-1].transpose(1, 2, 0, 3).reshape(width, hidden)
    go = grads[-1].reshape(width, width)
    small = scatter(gprm[:8].T)
    gbin = scatter(gprm[5 : 5 + hidden // width].reshape(hidden))
    part = [scatter(t).astype(F32) for t in (gq, go, gi, gf)]
    return (act, input_grad, *part, *(small[:, i] for i in range(4)), gbin, small[:, 4])


def ring_body(
    tokens, cotangent, group_id, w_qkv, w_out, w_ffn_in, w_ffn_out,
    gain_one, shift_one, gain_two, shift_two, bias_in, bias_out, feature_matrix,
):
    length, width = tokens.shape
    heads, feats, head_size = feature_matrix.shape
    hidden = w_ffn_in.shape[1]
    factor = head_size ** (-0.25)
    nz = lax.axis_size("dp") // 2
    grid = (nz, 2, 2, 2)
    wide = 3 * width
    pairs = width // LANES
    parts = hidden // width
    chunks, many = 5 + parts, 3 + pairs + 2 * parts
    wqs = (pairs, *grid, 16, 3 * LANES)
    big, deep, tall = (length, width), (length, heads * feats), (length, hidden)
    half = (-(-(3 + parts) * pairs // 8) * 8, LANES)
    pair_rows = (2 * pairs, LANES)
    near, far = 3, 2 * nz - 1
    act, input_grad, gq, gf, gi, go, rest, first = call(
        functools.partial(layer_kernel, nz, factor),
        [
            (big, BF), (big, BF), ((16, wide), F32), ((4, 16, width), F32), ((16, hidden), F32),
            ((16, width), F32), (half, F32), (pair_rows, F32),
        ],
        [
            *[(big, BF)] * 4, *[(deep, BF)] * 2, (big, BF), (big, F32),
            ((heads, length // BLOCK - 1, feats, 2 * LANES), BF),
            ((pairs, 16, 3 * LANES), BF), (wqs, BF), ((*grid, 16, width), BF),
            ((*grid, 16, hidden), BF), ((*grid, 64, width), BF), ((*grid, 16, LANES), BF), (big, BF),
            ((heads, feats, 2 * LANES), BF), ((16, LANES), F32), ((LANES, LANES), BF),
            ((8, width), F32),
            (big, BF), (big, F32), (big, F32), ((chunks, *grid, 16, width), BF), ((16, width), F32),
            (tall, BF), (tall, BF), (big, BF), (big, BF), (big, BF),
            ((8, width), F32), ((8, LANES), F32), ((4, 8, LANES), F32),
            ((pairs, *grid, 16, 3 * LANES), BF),
            *Reduce.shapes(chunks, nz, 16, width),
            *Reduce.shapes(pairs, nz, 16, 3 * LANES),
            (half, F32), (half, F32), ((near, *half), F32), ((far, *half), F32),
            (pair_rows, F32), (pair_rows, F32), ((near, *pair_rows), F32), ((far, *pair_rows), F32),
            ((4 * nz - 1, 16, 3 * LANES), BF),
            ((many, 4, nz - 1), None), ((many, 4, nz - 1), None), ((many,), None),
            ((chunks, 4, nz - 1), None), ((chunks, 4, nz - 1), None),
            ((pairs, 4, nz - 1), None), ((pairs, 4, nz - 1), None),
            ((2, far), None), ((2, far), None), ((2, far), None), ((2, far), None),
            ((4 * nz - 1,), None), ((4 * nz - 1,), None),
            ((), None), ((2, length // FFN_TILE), None),
        ],
        "layer",
        [VM, ANY, VM, ANY, ANY, ANY, VM, pl.BlockSpec(memory_space=pltpu.SMEM), *[VM] * 6],
        [ANY, ANY, *[VM] * 6],
        0,
    )(
        tokens, cotangent, w_qkv, w_out, w_ffn_in, w_ffn_out, feature_matrix.swapaxes(1, 2),
        group_id, *(t[None] for t in (gain_one, shift_one, gain_two, shift_two, bias_out, bias_in)),
    )
    act, input_grad, gq, go, gi, gf, *vecs = call(
        finish_kernel,
        [
            (big, BF), (big, BF), ((16, wide), F32), ((16, width), F32), ((16, hidden), F32),
            ((64, width), F32), *[((1, 16), F32)] * 4, ((1, 64), F32), ((1, 16), F32),
        ],
        [
            ((2, length, width), BF), ((16, wide), F32), ((4, 16, width), F32), ((16, hidden), F32),
            ((16, width), F32), ((2 * length // TILE + 7,), None), ((2 * length // TILE + 7,), None),
        ],
        "finish",
        [*[ANY] * 6, VM, VM],
        [*[ANY] * 6, *[VM] * 6],
    )(act, input_grad, gq, gf, gi, go, rest, first)
    return (act, input_grad, gq, go, gi, gf, *(t[0] for t in vecs))


def solution(mesh):
    rows, vec = P(AXES, None), P(AXES)
    devices = mesh.shape["dp"] * mesh.shape["fsdp"]

    def body(*args):
        width = args[0].shape[1]
        ring = mesh.shape["fsdp"] == 4 and mesh.shape["dp"] % 2 == 0 and width == 16 * devices
        return (ring_body if ring else plain_body)(*args)

    return jax.shard_map(
        body,
        mesh=mesh,
        in_specs=(rows, rows, vec, *[rows] * 4, *[vec] * 6, P()),
        out_specs=(*[rows] * 6, *[vec] * 6),
        check_vma=False,
    )
```

```python
import functools
import math

import jax
import jax.numpy as jnp
from jax import lax
from jax.experimental import pallas as pl
from jax.experimental.pallas import tpu as pltpu
from jax.sharding import PartitionSpec as P

BLOCK = 512
EPSILON = 1e-05
TILE = 256
FEAT_TILE = 1024
FFN_TILE = 512
LANES = 128
LOG2E = 1.4426950408889634
AXES = ("dp", "fsdp")
BF = jnp.bfloat16
F32 = jnp.float32


def dot(left, right):
    return lax.dot_general(left, right, (((1,), (0,)), ((), ())), preferred_element_type=F32)


def dot_bt(left, right):
    return lax.dot_general(left, right, (((1,), (1,)), ((), ())), preferred_element_type=F32)


def dot_at(left, right):
    return lax.dot_general(left, right, (((0,), (0,)), ((), ())), preferred_element_type=F32)


def unit_rows(rows):
    row = lax.broadcasted_iota(jnp.int32, (rows, LANES), 0)
    col = lax.broadcasted_iota(jnp.int32, (rows, LANES), 1)
    return jnp.where(row == col, 1.0, 0.0).astype(BF)


def lane_ids(rows, width=LANES):
    return lax.broadcasted_iota(jnp.int32, (rows, width), 1)


def tile_at(index, size=TILE):
    return pl.ds(pl.multiple_of(index * size, size), size)


def centred(values):
    mu = jnp.mean(values, axis=-1, keepdims=True)
    cen = values - mu
    inv = lax.rsqrt(jnp.mean(cen * cen, axis=-1, keepdims=True) + EPSILON)
    return cen * inv, inv


def norm_back(grad, unit, inv, gain):
    e = grad * gain
    return inv * (
        e
        - jnp.mean(e, axis=-1, keepdims=True)
        - unit * jnp.mean(e * unit, axis=-1, keepdims=True)
    )


def causal(values, offset):
    row = lax.broadcasted_iota(jnp.int32, values.shape, 0)
    col = lax.broadcasted_iota(jnp.int32, values.shape, 1)
    return jnp.where(col <= row + offset, values, 0.0).astype(BF)


def anticausal(values):
    row = lax.broadcasted_iota(jnp.int32, values.shape, 0)
    col = lax.broadcasted_iota(jnp.int32, values.shape, 1)
    return jnp.where(col >= row, values, 0.0).astype(BF)


MESH_ID = pl.DeviceIdType.MESH


SUMS = {
    "grad0": ((4, 0),),
    "chunk1": ((4, 1),),
    "grad1": ((5, 0),),
    "chunk2": ((5, 1), (4, 2)),
    "grad2": ((6, 0),),
    "chunk3": ((6, 1), (5, 2), (4, 3)),
    "grad3": ((7, 0), (0, 0), (1, 0), (2, 0), (3, 0)),
    "final": ((7, 1), (0, 1), (6, 2), (5, 3)),
    "grad_o": ((8, 0), (1, 1), (2, 1)),
    "b0:0": ((3, 1), (8, 1)),
    "b0:1": ((7, 2), (0, 2), (1, 2), (6, 3)),
    "b1:0": ((2, 2), (3, 2), (8, 2)),
    "b1:1": ((7, 3), (0, 3), (1, 3)),
    "b2:0": ((2, 3), (3, 3), (8, 3)),
    "tail": ((4, 4), (5, 4), (6, 4), (7, 4), (0, 4), (1, 4), (2, 4), (3, 4), (8, 4)),
}
OWN_SUMS = {
    "b1:0": ((0, 1),),
    "b2:0": ((0, 2), (1, 1)),
    "b3:0": ((0, 3), (1, 2), (2, 1)),
}
PLAN = {
    "start": (("s", 1), ("q0", 1), ("q1", 1), ("q2", 1), ("s", 2), ("q3", 1), ("q0", 2), ("o", 1), ("q1", 2), ("s", 3), ("i0", 1), ("q2", 2), ("q3", 2), ("q0", 3), ("q1", 3), ("o", 2),),
    "rows": (("f3", 1), ("i0", 2), ("f0", 1), ("f1", 1), ("f2", 1),),
    "0:0": (("q2", 3), ("i1", 1),),
    "0:2": (("q3", 3), ("i2", 1),),
    "1:0": (("f3", 2), ("o", 3), ("i3", 1),),
    "1:1": (("f0", 2),),
    "1:2": (("i0", 3), ("f1", 2),),
    "2:1": (("i1", 2), ("f2", 2),),
    "2:2": (("i2", 2),),
    "3:1": (("f0", 3),),
    "3:2": (("f3", 3),),
    "norm": (("f1", 3), ("i3", 2),),
    "chunk0": (("i1", 3), ("f2", 3),),
    "grad0": (("i2", 3),),
    "chunk1": (("i3", 3),),
}
Y_FIRST = {"q1", "o", "f2", "f3"}
LEAVE = ("s", "q0", "q1", "q2", "q3", "o", "i0", "F", "i1", "i2", "i3")


class Place:
    def __init__(self, nz):
        dp, fs = lax.axis_index("dp"), lax.axis_index("fsdp")
        self.nz = nz
        self.z, self.y = lax.div(dp, 2), lax.rem(dp, 2)
        self.x, self.c = lax.div(fs, 2), lax.rem(fs, 2)

    def device(self, z=None, y=None, x=None, c=None):
        z, y = self.z if z is None else z, self.y if y is None else y
        x, c = self.x if x is None else x, self.c if c is None else c
        return {"dp": z * 2 + y, "fsdp": x * 2 + c}

    def up(self, k):
        return lax.rem(self.z + k, self.nz)

    def down(self, k):
        return lax.rem(self.z + self.nz - k, self.nz)

    def around(self):
        for k in range(1, 4 * self.nz):
            y = 1 - self.y if k // 2 % 2 else self.y
            x = 1 - self.x if k % 2 else self.x
            yield (self.up(k // 4), y, x), (self.down(k // 4), y, x)

    def peers(self):
        yield self.device(c=1 - self.c)
        yield self.device(x=1 - self.x, c=1 - self.c)
        for (z, y, x), _ in self.around():
            yield self.device(z, y, x)

    def near(self):
        yield self.device(c=1 - self.c)
        yield self.device(x=1 - self.x)
        yield self.device(x=1 - self.x, c=1 - self.c)

    def far(self):
        yield self.device(y=1 - self.y)
        for k in range(1, self.nz):
            yield self.device(z=self.up(k))
            yield self.device(z=self.up(k), y=1 - self.y)

    def greet(self):
        for peer in self.peers():
            pl.semaphore_signal(
                pltpu.get_barrier_semaphore(), inc=1, device_id=peer, device_id_type=MESH_ID
            )

    def all_here(self):
        pl.semaphore_wait(pltpu.get_barrier_semaphore(), 1 + 4 * self.nz)


def remote(src, dst, send, recv, peer):
    return pltpu.make_async_remote_copy(
        src_ref=src, dst_ref=dst, send_sem=send, recv_sem=recv, device_id=peer,
        device_id_type=MESH_ID,
    )


class Gather:
    def __init__(self, place, shard, whole, view, sems, m, y_first, plane=None, base=None):
        self.place, self.shard, self.whole, self.view = place, shard, whole, view
        self.send, self.recv, self.own = sems
        self.m = m
        self.y_first = y_first
        self.plane, self.base = plane, base

    def at(self, *index):
        return self.whole.at[(*index, *self.view)]

    def hops(self, stage):
        p = self.place
        every = slice(None)
        zs = every if self.plane is None else self.plane
        if stage == 0:
            src = self.shard.at[self.view]
            for k in range(1, p.nz):
                yield src, self.at(p.z, p.y, p.x, p.c), self.at(p.down(k), p.y, p.x, p.c), p.device(z=p.up(k))
        elif stage == 3:
            mine = self.at(zs, every, every, p.c)
            yield mine, mine, self.at(zs, every, every, 1 - p.c), p.device(c=1 - p.c)
        elif stage == 1:
            mine = self.at(zs, p.y, p.x, p.c)
            if self.y_first:
                yield mine, mine, self.at(zs, 1 - p.y, p.x, p.c), p.device(y=1 - p.y)
            else:
                yield mine, mine, self.at(zs, p.y, 1 - p.x, p.c), p.device(x=1 - p.x)
        elif self.y_first:
            mine = self.at(zs, every, p.x, p.c)
            yield mine, mine, self.at(zs, every, 1 - p.x, p.c), p.device(x=1 - p.x)
        else:
            mine = self.at(zs, p.y, every, p.c)
            yield mine, mine, self.at(zs, 1 - p.y, every, p.c), p.device(y=1 - p.y)

    def copies(self, stage, arriving):
        for k, (src, dst, land, peer) in enumerate(self.hops(stage)):
            yield remote(
                src, land if arriving else dst, self.send.at[self.m, stage, k],
                self.recv.at[self.m, stage, k], peer,
            )

    def local(self):
        p = self.place
        return pltpu.make_async_copy(
            self.shard.at[self.view], self.at(p.z, p.y, p.x, p.c), self.own.at[self.m]
        )

    def start(self):
        for copy in self.copies(0, False):
            copy.start()
        self.local().start()

    def arrive(self, stage):
        for copy in self.copies(stage, True):
            copy.wait_recv()

    def enter(self):
        if self.plane is None:
            self.arrive(0)
            self.local().wait()
            return
        p = self.place
        hop = lax.rem(p.z + p.nz - self.plane, p.nz)

        @pl.when(hop == 0)
        def _():
            self.base.local().wait()

        @pl.when(hop != 0)
        def _():
            k = jnp.maximum(hop, 1) - 1
            remote(
                self.shard.at[self.view], self.at(self.plane, p.y, p.x, p.c),
                self.send.at[self.base.m, 0, k], self.recv.at[self.base.m, 0, k],
                p.device(z=p.up(1)),
            ).wait_recv()

    def step(self, stage):
        if stage == 1:
            self.enter()
        else:
            self.arrive(stage - 1)
        for copy in self.copies(stage, False):
            copy.start()

    def drain(self, stages=range(4)):
        for stage in stages:
            for copy in self.copies(stage, False):
                copy.wait_send()


class Reduce:
    def __init__(self, place, source, bufs, sems, write):
        self.place, self.source = place, source
        self.r0, self.r1, self.r2, self.r3 = bufs
        self.send, self.recv = sems
        self.write = write

    def hops(self, stage, cs, x_first):
        p = self.place
        every = slice(None)
        r0, r1, r2, r3 = (ref.at[cs] for ref in (self.r0, self.r1, self.r2, self.r3))
        if stage == 0:
            yield self.source.at[cs, every, every, every, 1 - p.c], r0, p.device(c=1 - p.c)
        elif stage == 1:
            if x_first:
                yield r0.at[every, every, every, 1 - p.x], r1, p.device(x=1 - p.x)
            else:
                yield r0.at[every, every, 1 - p.y], r1, p.device(y=1 - p.y)
        elif stage == 2:
            if x_first:
                yield r1.at[every, every, 1 - p.y], r2, p.device(y=1 - p.y)
            else:
                yield r1.at[every, every, 1 - p.x], r2, p.device(x=1 - p.x)
        else:
            for k in range(1, p.nz):
                yield r2.at[every, p.up(k)], r3.at[every, k - 1], p.device(z=p.up(k))

    def copies(self, stage, c, x_first, count=1):
        for k, (src, dst, peer) in enumerate(self.hops(stage, pl.ds(c, count), x_first)):
            yield remote(src, dst, self.send.at[c, stage, k], self.recv.at[c, stage, k], peer)

    def step(self, stage, c, x_first=False, count=1):
        p = self.place
        cs = pl.ds(c, count)
        if stage:
            for copy in self.copies(stage - 1, c, x_first, count):
                copy.wait_recv()
        if stage == 1:
            self.r0[cs] = self.source[cs, :, :, :, p.c] + self.r0[cs]
        elif stage == 2:
            mine = self.r0[cs, :, :, p.x] if x_first else self.r0[cs, :, p.y]
            self.r1[cs] = mine + self.r1[cs]
        elif stage == 3:
            mine = self.r1[cs, :, p.y] if x_first else self.r1[cs, :, p.x]
            self.r2[cs] = mine + self.r2[cs]
        elif stage == 4:
            for n in range(count):
                total = self.r2[c + n, p.z].astype(F32)
                for k in range(p.nz - 1):
                    total = total + self.r3[c + n, k].astype(F32)
                self.write(c + n, total)
            return
        for copy in self.copies(stage, c, x_first, count):
            copy.start()

    def drain(self, c, x_first=False, count=1, stages=range(4)):
        for stage in stages:
            for copy in self.copies(stage, c, x_first, count):
                copy.wait_send()

    def short(self, c, land, sems):
        p = self.place
        for k, (to, _) in enumerate(p.around()):
            yield remote(self.r0.at[(c, *to)], land.at[k], sems[0].at[k], sems[1].at[k], p.device(*to))

    def short_start(self, c, land, sems):
        for copy in self.copies(0, c, False):
            copy.wait_recv()
        self.r0[c] = self.source[c, :, :, :, self.place.c] + self.r0[c]
        for copy in self.short(c, land, sems):
            copy.start()

    def short_end(self, c, land, sems):
        p = self.place
        total = self.r0[c, p.z, p.y, p.x].astype(F32)
        for k, copy in enumerate(self.short(c, land, sems)):
            copy.wait_recv()
            total = total + land[k].astype(F32)
        self.write(c, total)

    @staticmethod
    def shapes(n, nz, rows, cols):
        return [
            ((n, nz, 2, 2, rows, cols), BF), ((n, nz, 2, rows, cols), BF),
            ((n, nz, rows, cols), BF), ((n, nz - 1, rows, cols), BF),
        ]


def project_rows(i, x_ref, wq, prm_ref, h_ref, q_ref, k_ref, v_ref, factor):
    rows = tile_at(i)
    unit, _ = centred(x_ref[rows, :].astype(F32))
    h = (unit * prm_ref[0:1, :] + prm_ref[1:2, :]).astype(BF)
    h_ref[rows, :] = h
    width = h.shape[1]
    qkv = dot(h, wq)
    q_ref[rows, :] = (qkv[:, :width] * factor).astype(BF)
    k_ref[rows, :] = (qkv[:, width : 2 * width] * factor).astype(BF)
    v_ref[rows, :] = qkv[:, 2 * width :].astype(BF)


def attend_pair(
    p, q_ref, k_ref, v_ref, fx_ref, pq_ref, pk_ref, attr_ref, den_ref, low_ref,
    site=lambda j: None,
):
    length = q_ref.shape[0]
    feats = fx_ref.shape[1]
    lanes = tile_at(p, LANES)
    shift = 0.5 * math.log2(feats)
    cols = [tile_at(2 * p + hh, feats) for hh in range(2)]
    step = FEAT_TILE
    for hh in range(2):
        fm = fx_ref[2 * p + hh][:, :LANES]
        for src, dst in ((q_ref, pq_ref), (k_ref, pk_ref)):
            for t in range(length // step):
                rows = slice(t * step, (t + 1) * step)
                part = src[rows, lanes]
                scores = dot_bt(part, fm)
                wide = jnp.where(lane_ids(step) // 64 == hh, part.astype(F32), 0.0)
                square = jnp.sum(wide * wide, axis=-1, keepdims=True)
                feat = jnp.exp2(scores * LOG2E - (square * (0.5 * LOG2E) + shift))
                dst[rows, cols[hh]] = feat.astype(BF)
    site(1)
    ones = jnp.ones((length, LANES), BF)
    vx = jnp.concatenate([v_ref[:, lanes], ones], axis=1)
    states = [None, None]
    for b in range(length // BLOCK):
        base = b * BLOCK
        for i in range(BLOCK // TILE):
            rows = slice(base + i * TILE, base + (i + 1) * TILE)
            keys = slice(base, base + (i + 1) * TILE)
            got = []
            for hh in range(2):
                pq = pq_ref[rows, cols[hh]]
                weights = causal(dot_bt(pq, pk_ref[keys, cols[hh]]), i * TILE)
                both = dot(weights, vx[keys])
                if b:
                    both = both + dot(pq, low_ref[2 * p + hh, b - 1])
                got.append(both)
            first = lane_ids(TILE) < 64
            num = jnp.where(first, got[0][:, :LANES], got[1][:, :LANES])
            den = jnp.where(first, got[0][:, LANES:], got[1][:, LANES:])
            attr_ref[rows, lanes] = (num / den).astype(BF)
            den_ref[rows, lanes] = den
        if base + BLOCK < length:
            block = slice(base, base + BLOCK)
            for hh in range(2):
                more = dot_at(pk_ref[block, cols[hh]], vx[block])
                states[hh] = more if b == 0 else states[hh] + more
                low_ref[2 * p + hh, b] = states[hh].astype(BF)


def forward_kernel(
    factor, x_ref, wq_ref, prm_ref, fx_ref,
    h_ref, q_ref, k_ref, v_ref, pq_ref, pk_ref, attr_ref, den_ref, low_ref,
):
    def rows(i, carry):
        project_rows(i, x_ref, wq_ref[...], prm_ref, h_ref, q_ref, k_ref, v_ref, factor)
        return carry

    lax.fori_loop(0, x_ref.shape[0] // TILE, rows, 0)

    def pair(p, carry):
        attend_pair(
            p, q_ref, k_ref, v_ref, fx_ref, pq_ref, pk_ref, attr_ref, den_ref, low_ref
        )
        return carry

    lax.fori_loop(0, x_ref.shape[1] // LANES, pair, 0)


def ffn_rows(
    t, x_ref, attr_ref, cot_ref, wo, wi, wf, prm_ref, bin_ref, seq_ref,
    act_ref, dy_ref, datt_ref, gprm_ref, hid_ref, du_ref, h_ref, gr_ref, dor_ref, bin_row=0,
):
    width = x_ref.shape[1]
    chunk = width
    rows = tile_at(t, FFN_TILE)
    y = x_ref[rows, :].astype(F32) + dot(attr_ref[rows, :], wo())
    unit, inv = centred(y)
    gain = prm_ref[2:3, :]
    h = (unit * gain + prm_ref[3:4, :]).astype(BF)
    h_ref[rows, :] = h
    g = cot_ref[rows, :].astype(F32) * seq_ref[0:1, 0:1]
    gr = g.astype(BF)
    gr_ref[rows, :] = gr
    out = y + prm_ref[4:5, :]
    dh = jnp.zeros((FFN_TILE, width), F32)
    for c in range(hid_ref.shape[1] // chunk):
        cs = slice(c * chunk, (c + 1) * chunk)
        u = dot(h, wi(cs)) + bin_ref[bin_row : bin_row + 1, cs]
        cdf = 0.5 + 0.5 * lax.erf(u * math.sqrt(0.5))
        slope = cdf + u * jnp.exp2(u * u * (-0.5 * LOG2E)) * (1.0 / math.sqrt(2.0 * math.pi))
        hid = (u * cdf).astype(BF)
        hid_ref[rows, cs] = hid
        out = out + dot(hid, wf(c))
        du = (dot_bt(gr, wf(c)) * slope).astype(BF)
        du_ref[rows, cs] = du
        gprm_ref[5 + c : 6 + c, :] += jnp.sum(du.astype(F32), axis=0, keepdims=True)
        dh = dh + dot_bt(du, wi(cs))
    act_ref[rows, :] = out.astype(BF)
    gprm_ref[2:3, :] += jnp.sum(dh * unit, axis=0, keepdims=True)
    gprm_ref[3:4, :] += jnp.sum(dh, axis=0, keepdims=True)
    gprm_ref[4:5, :] += jnp.sum(g, axis=0, keepdims=True)
    dy = g + norm_back(dh, unit, inv, gain)
    dy_ref[rows, :] = dy
    dor = dy.astype(BF)
    dor_ref[rows, :] = dor
    datt_ref[rows, :] = dot_bt(dor, wo())


def ffn_norm(t, x_ref, attr_ref, cot_ref, wo, prm_ref, seq_ref, y_ref, h_ref, gr_ref):
    rows = tile_at(t, FFN_TILE)
    y = x_ref[rows, :].astype(F32) + dot(attr_ref[rows, :], wo)
    y_ref[rows, :] = y
    unit, _ = centred(y)
    h_ref[rows, :] = (unit * prm_ref[2:3, :] + prm_ref[3:4, :]).astype(BF)
    gr_ref[rows, :] = (cot_ref[rows, :].astype(F32) * seq_ref[0:1, 0:1]).astype(BF)


def ffn_chunk(t, c, wi, wf, bias, h_ref, gr_ref, hid_ref, du_ref, gprm_ref):
    rows = tile_at(t, FFN_TILE)
    width = h_ref.shape[1]
    cs = slice(c * width, (c + 1) * width)
    u = dot(h_ref[rows, :], wi) + bias
    cdf = 0.5 + 0.5 * lax.erf(u * math.sqrt(0.5))
    slope = cdf + u * jnp.exp2(u * u * (-0.5 * LOG2E)) * (1.0 / math.sqrt(2.0 * math.pi))
    hid_ref[rows, cs] = (u * cdf).astype(BF)
    du = (dot_bt(gr_ref[rows, :], wf) * slope).astype(BF)
    du_ref[rows, cs] = du
    gprm_ref[5 + c : 6 + c, :] += jnp.sum(du.astype(F32), axis=0, keepdims=True)


def ffn_final(
    t, cot_ref, wo, wi, prm_ref, seq_ref, y_ref, du_ref, dy_ref, dor_ref, datt_ref, gprm_ref
):
    rows = tile_at(t, FFN_TILE)
    y = y_ref[rows, :]
    dh = dot_bt(du_ref[rows, :], wi)
    unit, inv = centred(y)
    g = cot_ref[rows, :].astype(F32) * seq_ref[0:1, 0:1]
    gprm_ref[2:3, :] += jnp.sum(dh * unit, axis=0, keepdims=True)
    gprm_ref[3:4, :] += jnp.sum(dh, axis=0, keepdims=True)
    gprm_ref[4:5, :] += jnp.sum(g, axis=0, keepdims=True)
    dy = g + norm_back(dh, unit, inv, prm_ref[2:3, :])
    dy_ref[rows, :] = dy
    dor = dy.astype(BF)
    dor_ref[rows, :] = dor
    datt_ref[rows, :] = dot_bt(dor, wo)


def grads_out(c, hid_ref, gr_ref, g_ref):
    width = gr_ref.shape[1]
    grad = dot_at(hid_ref[:, tile_at(c)], gr_ref[...]).astype(BF)
    grad = grad.reshape(4, 4, 16, width)
    for q in range(4):
        g_ref[q, c] = grad[:, q]


def grads_in(c, h_ref, du_ref, attr_ref, dor_ref, g_ref):
    width = h_ref.shape[1]
    count = du_ref.shape[1] // width
    cs = tile_at(c)
    at = pl.ds(c * 4, 4)
    grad = dot_at(h_ref[:, cs], du_ref[...]).astype(BF)
    for k in range(count):
        g_ref[4 + k, at] = grad[:, k * width : (k + 1) * width].reshape(4, 4, 16, width)
    grad = dot_at(attr_ref[:, cs], dor_ref[...]).astype(BF)
    g_ref[4 + count, at] = grad.reshape(4, 4, 16, width)


def loop(start, stop, step):
    def run(i, carry):
        step(i)
        return carry

    lax.fori_loop(start, stop, run, 0)


def middle_kernel(
    x_ref, attr_ref, cot_ref, wo_ref, wi_ref, wf_ref, prm_ref, seq_ref,
    act_ref, dy_ref, datt_ref, gprm_ref, g_ref,
    hid_ref, du_ref, h_ref, gr_ref, dor_ref, bin_ref,
):
    length, width = x_ref.shape
    gprm_ref[...] = jnp.zeros_like(gprm_ref)
    bin_ref[...] = dot_bt(unit_rows(8), wf_ref[:, width:])
    loop(0, length // FFN_TILE, lambda t: ffn_rows(
        t, x_ref, attr_ref, cot_ref, lambda: wo_ref[...], lambda cs: wi_ref[:, cs],
        lambda c: wf_ref[c * width : (c + 1) * width, :width], prm_ref, bin_ref, seq_ref,
        act_ref, dy_ref, datt_ref, gprm_ref, hid_ref, du_ref, h_ref, gr_ref, dor_ref,
    ))
    loop(0, hid_ref.shape[1] // TILE, lambda c: grads_out(c, hid_ref, gr_ref, g_ref))
    loop(0, width // TILE, lambda c: grads_in(c, h_ref, du_ref, attr_ref, dor_ref, g_ref))


def back_pair(
    p, factor, q_ref, k_ref, v_ref, pq_ref, pk_ref, att_ref, den_ref, datt_ref, fx_ref, low_ref,
    ht_ref, dqkv_refs, dn_ref, e_ref, da_ref, tick, store,
):
    length = q_ref.shape[0]
    feats = fx_ref.shape[1]
    lanes = tile_at(p, LANES)
    blocks = length // BLOCK
    cols = [tile_at(2 * p + hh, feats) for hh in range(2)]
    two = jnp.where(lane_ids(length) < 2, 1.0, 0.0).astype(BF)
    v2 = jnp.concatenate([v_ref[:, lanes], two], axis=1)
    for t in range(length // TILE):
        rows = slice(t * TILE, (t + 1) * TILE)
        dn = datt_ref[rows, lanes] / den_ref[rows, lanes]
        prod = dn * att_ref[rows, lanes].astype(F32)
        lane = lane_ids(TILE)
        for hh in range(2):
            mine = lane // 64 == hh
            dden = -jnp.sum(jnp.where(mine, prod, 0.0), axis=-1, keepdims=True)
            high = dden.astype(BF).astype(F32)
            extra = jnp.where(lane == 0, high, jnp.where(lane == 1, dden - high, 0.0))
            dn_ref[hh, rows, :LANES] = jnp.where(mine, dn, 0.0).astype(BF)
            dn_ref[hh, rows, LANES:] = extra.astype(BF)
    for hh in range(2):
        fx = fx_ref[2 * p + hh]
        back = [None] * blocks
        total = None
        for b in range(blocks - 1, 0, -1):
            block = slice(b * BLOCK, (b + 1) * BLOCK)
            more = dot_at(pq_ref[block, cols[hh]], dn_ref[hh, block, :])
            total = more if total is None else total + more
            dz = total[:, LANES : LANES + 1] + total[:, LANES + 1 : LANES + 2]
            high = dz.astype(BF).astype(F32)
            lane = lane_ids(feats)
            extra = jnp.where(lane == 0, high, jnp.where(lane == 1, dz - high, 0.0))
            back[b - 1] = jnp.concatenate([total[:, :LANES], extra], axis=1).astype(BF)

        def put(value, rows, at, hh=hh):
            ref = dqkv_refs[at]
            if hh:
                mine = lane_ids(value.shape[0]) >= 64
                value = jnp.where(mine, value, ref[rows, lanes].astype(F32))
            ref[rows, lanes] = value.astype(BF)

        for b in range(blocks):
            base = b * BLOCK
            for i in range(BLOCK // TILE):
                rows = slice(base + i * TILE, base + (i + 1) * TILE)
                keys = slice(base, base + (i + 1) * TILE)
                dn = dn_ref[hh, rows, :]
                da = causal(dot_bt(dn, v2[keys]), i * TILE)
                da_ref[i * TILE : (i + 1) * TILE, : (i + 1) * TILE] = da
                grad = dot(da, pk_ref[keys, cols[hh]])
                if b:
                    grad = grad + dot_bt(dn, low_ref[2 * p + hh, b - 1])
                e_ref[0, rows, :] = (grad * pq_ref[rows, cols[hh]].astype(F32)).astype(BF)
            for i in range(BLOCK // TILE):
                rows = slice(base + i * TILE, base + (i + 1) * TILE)
                later = slice(base + i * TILE, base + BLOCK)
                pk = pk_ref[rows, cols[hh]]
                pql = pq_ref[later, cols[hh]]
                grad = dot_at(da_ref[i * TILE :, i * TILE : (i + 1) * TILE], pql)
                at = anticausal(dot_bt(pk, pql))
                dv = dot(at, dn_ref[hh, later, :LANES])
                if b < blocks - 1:
                    grad = grad + dot_bt(v2[rows], back[b])
                    dv = dv + dot(pk, back[b][:, :LANES])
                e_ref[1, rows, :] = (grad * pk.astype(F32)).astype(BF)
                put(dv, rows, 2)
        for at, src in ((0, q_ref), (1, k_ref)):
            res = dot(e_ref[at], fx)
            out = (res[:, :LANES] - src[:, lanes].astype(F32) * res[:, LANES:]) * factor
            put(out, slice(0, length), at)
        if hh == 0:
            tick(0)
    store(dot(ht_ref[...], jnp.concatenate([ref[:, lanes] for ref in dqkv_refs], axis=1)).astype(BF))


def input_rows(t, x_ref, wq, prm_ref, dqkv_refs, dy_ref, out_ref, gprm_ref):
    rows = tile_at(t, FFN_TILE)
    dh = dot_bt(jnp.concatenate([ref[rows, :] for ref in dqkv_refs], axis=1), wq)
    unit, inv = centred(x_ref[rows, :].astype(F32))
    gprm_ref[0:1, :] += jnp.sum(dh * unit, axis=0, keepdims=True)
    gprm_ref[1:2, :] += jnp.sum(dh, axis=0, keepdims=True)
    out_ref[rows, :] = (dy_ref[rows, :] + norm_back(dh, unit, inv, prm_ref[0:1, :])).astype(BF)


def flip_rows(h_ref, ht_ref):
    for t in range(h_ref.shape[0] // TILE):
        rows = slice(t * TILE, (t + 1) * TILE)
        ht_ref[:, rows] = h_ref[rows, :].T


def backward_kernel(
    factor, x_ref, h_ref, q_ref, k_ref, v_ref, pq_ref, pk_ref, att_ref, den_ref, datt_ref, dy_ref,
    wq_ref, fx_ref, prm_ref, gin_ref, low_ref,
    out_ref, gq_ref, gprm_ref,
    ht_ref, dqkv_ref, dn_ref, e_ref, da_ref,
):
    gprm_ref[...] = gin_ref[...]
    width = x_ref.shape[1]
    dqkv_refs = [dqkv_ref.at[:, n * width : (n + 1) * width] for n in range(3)]
    flip_rows(h_ref, ht_ref)

    def pair(p, carry):
        def store(value):
            gq_ref[:, tile_at(p, 3 * LANES)] = value

        back_pair(
            p, factor, q_ref, k_ref, v_ref, pq_ref, pk_ref, att_ref, den_ref, datt_ref, fx_ref, low_ref,
            ht_ref, dqkv_refs, dn_ref, e_ref, da_ref, lambda j: None, store,
        )
        return carry

    lax.fori_loop(0, x_ref.shape[1] // LANES, pair, 0)

    def rows(t, carry):
        input_rows(t, x_ref, wq_ref[...], prm_ref, dqkv_refs, dy_ref, out_ref, gprm_ref)
        return carry

    lax.fori_loop(0, x_ref.shape[0] // FFN_TILE, rows, 0)


def sequence_weight(small, seq_ref):
    nf = 4
    me = lax.axis_index("dp") * nf + lax.axis_index("fsdp")
    row = lax.broadcasted_iota(jnp.int32, small.shape, 0)
    lane = lane_ids(small.shape[0]).astype(F32)
    peer = lax.div(row, 16)
    ids = small[:, 5:6].astype(F32)
    hit = (lane == ids) & (lax.rem(row, 16) == 0)
    counts = jnp.sum(
        jnp.where(hit & (lax.rem(peer, nf) == lax.axis_index("fsdp")), 1.0, 0.0),
        axis=0, keepdims=True,
    )
    mine = jnp.sum(jnp.where(hit & (peer == me), 1.0, 0.0), axis=0, keepdims=True)
    size = jnp.sum(counts * mine, axis=1, keepdims=True)
    groups = jnp.sum(jnp.where(counts > 0.5, 1.0, 0.0), axis=1, keepdims=True)
    members = lax.axis_size("dp")
    seq_ref[...] = jnp.broadcast_to(members / (groups * size), seq_ref.shape)


class Columns:
    def __init__(self, ref, start, size):
        self.ref, self.start, self.size = ref, start, size

    def where(self, index):
        n, *rest = index if isinstance(index, tuple) else (index,)
        rows, cols = [*rest, slice(None), slice(None)][:2]
        base = self.start + n * self.size
        low, high = cols.start or 0, self.size if cols.stop is None else cols.stop
        return rows, slice(base + low, base + high)

    def __getitem__(self, index):
        return self.ref[self.where(index)]

    def __setitem__(self, index, value):
        self.ref[self.where(index)] = value


class Total:
    def __init__(self, place, ref, part, near, far, sems):
        self.place, self.ref, self.part, self.near, self.far = place, ref, part, near, far
        self.send, self.recv = sems

    def copies(self, stage):
        peers = self.place.far() if stage else self.place.near()
        src, dst = (self.part, self.far) if stage else (self.ref, self.near)
        for k, peer in enumerate(peers):
            yield remote(src, dst.at[k], self.send.at[stage, k], self.recv.at[stage, k], peer)

    def start(self):
        for copy in self.copies(0):
            copy.start()

    def turn(self):
        for copy in self.copies(0):
            copy.wait_recv()
        self.part[...] = self.ref[...] + sum(self.near[k] for k in range(self.near.shape[0]))
        for copy in self.copies(1):
            copy.start()

    def result(self):
        for copy in self.copies(1):
            copy.wait_recv()
        return self.part[...] + sum(self.far[k] for k in range(self.far.shape[0]))

    def drain(self):
        for stage in range(2):
            for copy in self.copies(stage):
                copy.wait_send()


def layer_kernel(
    nz, factor, x_ref, cot_in, wqs_ref, wos_ref, wis_ref, wfs_ref, fm_ref, id_ref,
    g1_ref, s1_ref, g2_ref, s2_ref, bo_ref, bi_ref,
    act_out, grad_out, partq_ref, gf_ref, gi_ref, go_ref, rest_out, first_out,
    h_ref, q_ref, k_ref, v_ref, pq_ref, pk_ref, attr_ref, den_ref, low_ref,
    wqt_ref, wq_ref, wo_ref, wi_ref, wf_ref, sp_ref, cot_ref, fx_ref, vec_ref, col_ref, prm_ref,
    act_ref, dy_ref, y_ref, g_ref, gprm_ref, hid_ref, du_ref, h2_ref, gr_ref, dor_ref,
    bin_ref, seq_ref, lhs_ref, gq_ref,
    b0, b1, b2, b3, c0, c1, c2, c3,
    rest_ref, rest_part, rest_near, rest_far, first_ref, first_part, first_near, first_far,
    land_ref,
    send, recv, own, big_send, big_recv, q_send, q_recv, rest_send, rest_recv, first_send, first_recv,
    short_send, short_recv, local_sem, tile_sem,
):
    length, width = x_ref.shape
    hidden = hid_ref.shape[1]
    place = Place(nz)
    every = slice(None)
    sems = (send, recv, own)
    pairs, tiles, parts = width // LANES, length // TILE, hidden // width
    slabs = length // FFN_TILE

    def gather(name, shard, whole, view, m, plane=None, base=None):
        return Gather(place, shard, whole, view, sems, m, name in Y_FIRST, plane, base)

    both = (every, every)
    sp = gather("s", col_ref, sp_ref, (slice(0, 16), every), 0)
    o = gather("o", wos_ref, wo_ref, both, 1)
    f = gather("f", wfs_ref, wf_ref, both, 2)
    wq = [gather(f"q{p}", wqt_ref.at[p], wq_ref.at[p], both, 3 + p) for p in range(pairs)]
    wi = [
        gather(f"i{c}", wis_ref, wi_ref, (every, slice(c * width, (c + 1) * width)), 3 + pairs + c)
        for c in range(parts)
    ]
    wf = [
        gather(f"f{c}", wfs_ref, wf_ref, both, 3 + pairs + parts + c, c, f) for c in range(parts)
    ]
    named = {"s": sp, "o": o, "F": f}
    for n in range(pairs):
        named[f"q{n}"] = wq[n]
    for n in range(parts):
        named[f"i{n}"] = wi[n]
        named[f"f{n}"] = wf[n]

    def write(c, value):
        if c < 4:
            gf_ref[c] = value
        elif c < 4 + parts:
            gi_ref[:, (c - 4) * width : (c - 3) * width] = value
        else:
            go_ref[...] = value

    def write_q(c, value):
        for at in range(3):
            where = pl.ds(pl.multiple_of(c * LANES + at * width, LANES), LANES)
            partq_ref[:, where] = value[:, at * LANES : (at + 1) * LANES]

    grid = (nz, 2, 2, 2)
    big = Reduce(place, g_ref, (b0, b1, b2, b3), (big_send, big_recv), write)
    mine = Reduce(place, gq_ref, (c0, c1, c2, c3), (q_send, q_recv), write_q)
    rest = Total(place, rest_ref, rest_part, rest_near, rest_far, (rest_send, rest_recv))
    first = Total(place, first_ref, first_part, first_near, first_far, (first_send, first_recv))
    short_sems = (short_send, short_recv)
    cot_copy = pltpu.make_async_copy(cot_in, cot_ref, local_sem)

    def slab_out(t, src, dst, n):
        rows = tile_at(t, FFN_TILE)
        return pltpu.make_async_copy(src.at[rows], dst.at[rows], tile_sem.at[n, t])

    def at_site(name):
        for who, stage in PLAN.get(name, ()):
            named[who].step(stage)
        for c, stage in SUMS.get(name, ()):
            big.step(stage, c, c % 2 == 0)
        for c, stage in OWN_SUMS.get(name, ()):
            mine.step(stage, c)

    def sites(p, prefix):
        def site(j):
            for n in range(pairs):
                name = f"{prefix}{n}:{j}"
                if name in PLAN or name in SUMS or name in OWN_SUMS:
                    pl.when(p == n)(functools.partial(at_site, name))

        return site

    place.greet()
    vec_ref[...] = jnp.zeros_like(vec_ref)
    for n, ref in enumerate((g1_ref, s1_ref, g2_ref, s2_ref, bo_ref)):
        vec_ref[n : n + 1, : ref.shape[1]] = ref[...].astype(F32)
    vec_ref[5:6, :] = jnp.full((1, LANES), id_ref[0], jnp.int32).astype(F32)
    for n in range(4):
        vec_ref[8 + n : 9 + n, :16] = bi_ref[:, n * 16 : (n + 1) * 16].astype(F32)
    col_ref[...] = dot_at(vec_ref[...].astype(BF), unit_rows(16)).astype(BF)
    for p in range(pairs):
        for n in range(3):
            at = n * width + p * LANES
            wqt_ref[p, :, n * LANES : (n + 1) * LANES] = wqs_ref[:, at : at + LANES]
    place.all_here()
    for who in LEAVE:
        named[who].start()
    cot_copy.start()
    head_size, feats = fm_ref.shape[1:]
    for n in range(fm_ref.shape[0]):
        row = lax.broadcasted_iota(jnp.int32, (head_size, LANES), 0)
        place_at = jnp.where(lane_ids(head_size) == row + (n % 2) * head_size, 1.0, 0.0).astype(BF)
        fx_ref[n, :, :LANES] = dot_at(fm_ref[n], place_at).astype(BF)
        fx_ref[n, :, LANES:] = jnp.ones((feats, LANES), BF)
    at_site("start")
    sp.arrive(3)
    small = sp_ref[...].reshape(width, LANES)
    prm = dot_bt(unit_rows(16), small)
    prm_ref[...] = prm[:8]
    at_site("params")
    sequence_weight(small, seq_ref)
    for c in range(parts):
        for n in range(4):
            lhs_ref[n, c : c + 1, :] = prm[8 + n : 9 + n, c * LANES : (c + 1) * LANES]
    row = lax.broadcasted_iota(jnp.int32, (LANES, width), 0)
    col = lax.broadcasted_iota(jnp.int32, (LANES, width), 1)
    bias = jnp.zeros((8, width), F32)
    for n in range(4):
        spread = (lax.div(row, 16) == lax.div(col, 64)) & (
            lax.rem(row, 16) + n * 16 == lax.rem(col, 64)
        )
        bias = bias + dot(lhs_ref[n].astype(BF), jnp.where(spread, 1.0, 0.0).astype(BF))
    bin_ref[...] = bias
    gprm_ref[...] = jnp.zeros_like(gprm_ref)

    def rows(i):
        rows = tile_at(i)
        unit, _ = centred(x_ref[rows, :].astype(F32))
        h_ref[rows, :] = (unit * prm_ref[0:1, :] + prm_ref[1:2, :]).astype(BF)

    loop(0, tiles, rows)
    at_site("rows")

    def pair(p):
        site = sites(p, "")
        for n in range(pairs):
            pl.when(p == n)(functools.partial(wq[n].arrive, 3))
        lanes = tile_at(p, LANES)
        for t in range(tiles):
            rows = slice(t * TILE, (t + 1) * TILE)
            qkv = dot(h_ref[rows, :], wq_ref[p].reshape(width, 3 * LANES))
            q_ref[rows, lanes] = (qkv[:, :LANES] * factor).astype(BF)
            k_ref[rows, lanes] = (qkv[:, LANES : 2 * LANES] * factor).astype(BF)
            v_ref[rows, lanes] = qkv[:, 2 * LANES :].astype(BF)
        site(0)
        attend_pair(
            p, q_ref, k_ref, v_ref, fx_ref, pq_ref, pk_ref, attr_ref, den_ref, low_ref,
            site,
        )
        site(2)

    loop(0, pairs, pair)
    o.arrive(3)
    cot_copy.wait()

    def norm(t):
        wo = wo_ref[...].reshape(width, width)
        ffn_norm(t, x_ref, attr_ref, cot_ref, wo, prm_ref, seq_ref, y_ref, h2_ref, gr_ref)

    loop(0, slabs, norm)
    at_site("norm")
    for c in range(parts):
        wi[c].arrive(3)
        wf[c].arrive(3)
        cs = slice(c * width, (c + 1) * width)

        def chunk(t, c=c, cs=cs):
            w_in, w_out = wi_ref[..., cs].reshape(width, width), wf_ref[c].reshape(width, width)
            bias = bin_ref[c : c + 1, :]
            ffn_chunk(t, c, w_in, w_out, bias, h2_ref, gr_ref, hid_ref, du_ref, gprm_ref)

        loop(0, slabs, chunk)
        at_site(f"chunk{c}")
        value = dot_at(hid_ref[:, cs], gr_ref[...]).astype(BF).reshape(8, 4, 16, width)
        for q in range(4):
            g_ref[q, c] = value[:, q].reshape(2, 2, 2, 16, width)
        value = dot_at(h2_ref[...], du_ref[:, cs]).astype(BF)
        g_ref[4 + c] = value.reshape(*grid, 16, width)
        at_site(f"grad{c}")

    def final(t):
        ffn_final(
            t, cot_ref, wo_ref[...].reshape(width, width), wi_ref[...].reshape(width, hidden),
            prm_ref, seq_ref, y_ref, du_ref, dy_ref, dor_ref, y_ref, gprm_ref,
        )

    loop(0, slabs, final)
    at_site("final")

    value = dot_at(attr_ref[...], dor_ref[...]).astype(BF)
    g_ref[4 + parts] = value.reshape(*grid, 16, width)
    at_site("grad_o")
    for n in range(3 + parts):
        for c in range(pairs):
            rest_ref[n * pairs + c : n * pairs + c + 1, :] = gprm_ref[2 + n : 3 + n, c * LANES : (c + 1) * LANES]
    for n in range((3 + parts) * pairs, rest_ref.shape[0]):
        rest_ref[n : n + 1, :] = jnp.zeros((1, LANES), F32)
    rest.start()

    ht_ref = du_ref.at[0:width, 0:length]
    da_ref = du_ref.at[width : 2 * width, 0:BLOCK]
    dn_ref = Columns(du_ref, length, 2 * LANES)
    e_ref = Columns(du_ref, length + 4 * LANES, 2 * LANES)
    dqkv_refs = (cot_ref, gr_ref, dor_ref)
    out_ref = h2_ref
    flip_rows(h_ref, ht_ref)

    def back(p):
        def store(value):
            gq_ref[p] = value.reshape(*grid, 16, 3 * LANES)

        back_pair(
            p, factor, q_ref, k_ref, v_ref, pq_ref, pk_ref, attr_ref, den_ref, y_ref, fx_ref,
            low_ref, ht_ref, dqkv_refs, dn_ref, e_ref, da_ref, sites(p, "b"), store,
        )
        mine.step(0, p)
        sites(p, "b")(1)

        @pl.when(p == 0)
        def _():
            rest.turn()

        @pl.when(p == 2)
        def _():
            rest_out[...] = rest.result()

    loop(0, pairs, back)
    last = pairs - 1

    def rows_back(t):
        weights = [
            wq_ref[p, ..., n * LANES : (n + 1) * LANES].reshape(width, LANES)
            for n in range(3)
            for p in range(pairs)
        ]
        input_rows(
            t, x_ref, jnp.concatenate(weights, axis=1), prm_ref, dqkv_refs, dy_ref, out_ref, gprm_ref
        )
        slab_out(t, out_ref, grad_out, 1).start()

    def output(t):
        rows = tile_at(t, FFN_TILE)
        out = x_ref[rows, :].astype(F32) + dot(attr_ref[rows, :], wo_ref[...].reshape(width, width))
        out = out + dot(hid_ref[rows, :], wf_ref[...].reshape(hidden, width)) + prm_ref[4:5, :]
        act_ref[rows, :] = out.astype(BF)
        slab_out(t, act_ref, act_out, 0).start()

    mine.step(3, last - 2)
    mine.step(2, last - 1)
    loop(0, slabs // 2, rows_back)
    mine.short_start(last, land_ref, short_sems)
    loop(slabs // 2, slabs, rows_back)
    for n in range(2):
        for c in range(pairs):
            first_ref[n * pairs + c : n * pairs + c + 1, :] = gprm_ref[n : n + 1, c * LANES : (c + 1) * LANES]
    first.start()
    mine.step(3, last - 1)
    loop(0, slabs // 2, output)
    first.turn()
    loop(slabs // 2, slabs, output)
    at_site("tail")
    mine.step(4, last - 3)
    mine.step(4, last - 2)
    mine.step(4, last - 1)
    first_out[...] = first.result()
    mine.short_end(last, land_ref, short_sems)
    for t in range(slabs):
        slab_out(t, act_ref, act_out, 0).wait()
        slab_out(t, out_ref, grad_out, 1).wait()
    for g in (sp, o, *wq, *wi):
        g.drain()
    f.drain((0,))
    for g in wf:
        g.drain((1, 2, 3))
    for c in range(g_ref.shape[0]):
        big.drain(c, c % 2 == 0)
    loop(0, last, mine.drain)
    mine.drain(last, stages=(0,))
    for copy in mine.short(last, land_ref, short_sems):
        copy.wait_send()
    rest.drain()
    first.drain()


def finish_kernel(
    act_in, grad_in, gq_in, gf_in, gi_in, go_in, rest_in, first_in,
    act_ref, grad_ref, gq_ref, go_ref, gi_ref, gf_ref,
    g1_ref, s1_ref, g2_ref, s2_ref, bi_ref, bo_ref,
    hold_ref, holdq_ref, holdf_ref, holdi_ref, holdo_ref, in_sem, out_sem,
):
    moves = []

    def move(src, hold, dst):
        n = len(moves)
        moves.append((
            pltpu.make_async_copy(src, hold, in_sem.at[n]),
            pltpu.make_async_copy(hold, dst, out_sem.at[n]),
        ))
        moves[n][0].start()

    for n, (src, dst) in enumerate(((act_in, act_ref), (grad_in, grad_ref))):
        for t in range(src.shape[0] // TILE):
            rows = pl.ds(t * TILE, TILE)
            move(src.at[rows], hold_ref.at[n, rows], dst.at[rows])
    move(gq_in, holdq_ref, gq_ref)
    move(gi_in, holdi_ref, gi_ref)
    move(go_in, holdo_ref, go_ref)
    for n in range(4):
        move(gf_in.at[n], holdf_ref.at[n], gf_ref.at[pl.ds(16 * n, 16)])
    me = lax.axis_index("dp") * 4 + lax.axis_index("fsdp")
    row = lax.broadcasted_iota(jnp.int32, (LANES, LANES), 0)
    lane = lane_ids(LANES)

    def cut(value, start):
        pick = jnp.where(row == lane + start, 1.0, 0.0)
        return lax.dot_general(
            value, pick, (((1,), (0,)), ((), ())), precision=lax.Precision.HIGHEST,
            preferred_element_type=F32,
        )

    def only(value, base, count, which):
        part = value[base : base + count]
        at = lax.broadcasted_iota(jnp.int32, part.shape, 0)
        return jnp.sum(jnp.where(at == which, part, 0.0), axis=0, keepdims=True)

    for come, go in moves:
        come.wait()
        go.start()
    pairs = first_in.shape[0] // 2
    spot = lax.rem(me, 8) * 16
    first, rest = cut(first_in[...], spot), cut(rest_in[...], spot)
    which = lax.div(me, 8)
    for n, ref in enumerate((g1_ref, s1_ref)):
        ref[...] = only(first, n * pairs, pairs, which)[:, :16]
    for n, ref in enumerate((g2_ref, s2_ref, bo_ref)):
        ref[...] = only(rest, n * pairs, pairs, which)[:, :16]
    wide = cut(rest_in[...], lax.rem(me, 2) * 64)
    each = pairs * pairs
    bi_ref[...] = only(wide, 3 * pairs, each, lax.div(me, 2))[:, :64]
    for _, go in moves:
        go.wait()


ANY = pl.BlockSpec(memory_space=pl.ANY)
VM = pl.BlockSpec(memory_space=pltpu.VMEM)


def call(kernel, outs, scratch, name, ins=None, out_specs=None, collective=None):
    extra = {} if ins is None else {"in_specs": ins, "out_specs": out_specs}
    params = {} if collective is None else {"collective_id": collective, "has_side_effects": True}
    return pl.pallas_call(
        kernel,
        out_shape=[jax.ShapeDtypeStruct(s, d) for s, d in outs],
        scratch_shapes=[pltpu.SemaphoreType.DMA(s) if d is None else pltpu.VMEM(s, d) for s, d in scratch],
        compiler_params=pltpu.CompilerParams(vmem_limit_bytes=60 * 2**20, **params),
        name=name,
        **extra,
    )


def padded_features(fm):
    heads, feats, _ = fm.shape
    zero = jnp.zeros_like(fm)
    even = (jnp.arange(heads) % 2 == 0)[:, None, None]
    return jnp.concatenate(
        [jnp.where(even, fm, zero), jnp.where(even, zero, fm), jnp.ones((heads, feats, LANES), BF)],
        axis=-1,
    )


def by_pair(columns, outer):
    rows, count = columns.shape
    split = columns.reshape(rows, outer, count // (outer * LANES), LANES)
    return split.swapaxes(1, 2).reshape(rows, count)


def middle(tokens, attr, cotangent, wo, wi, wf, prm, seq_weight):
    length, width = tokens.shape
    hidden = wi.shape[1]
    big, deep = (length, width), (length, hidden)
    chunks = 5 + hidden // width
    return call(
        middle_kernel,
        [(big, BF), (big, F32), (big, F32), ((16, width), F32), ((chunks, width // 64, 4, 16, width), BF)],
        [(deep, BF), (deep, BF), (big, BF), (big, BF), (big, BF), ((8, hidden), F32)],
        "middle",
    )(tokens, attr, cotangent, wo, wi, wf, prm, seq_weight)


def forward_outs(length, width, heads, feats):
    big = (length, width)
    deep = (length, heads * feats)
    low = (heads, length // BLOCK - 1, feats, 2 * LANES)
    return [(big, BF)] * 4 + [(deep, BF)] * 2 + [(big, BF), (big, F32), (low, BF)]


def backward_scratch(length, width):
    return [
        ((width, length), BF), ((length, 3 * width), BF),
        ((2, length, 2 * LANES), BF), ((2, length, 2 * LANES), BF), ((BLOCK, BLOCK), BF),
    ]


def plain_body(
    tokens, cotangent, group_id, w_qkv, w_out, w_ffn_in, w_ffn_out,
    gain_one, shift_one, gain_two, shift_two, bias_in, bias_out, feature_matrix,
):
    gather = functools.partial(lax.all_gather, axis_name=AXES, axis=0, tiled=True)
    scatter = functools.partial(
        lax.psum_scatter, axis_name=AXES, scatter_dimension=0, tiled=True
    )
    length, width = tokens.shape
    heads, feats, head_size = feature_matrix.shape
    hidden = w_ffn_in.shape[1]
    factor = head_size ** (-0.25)
    wq, wo, wi, wf = gather(w_qkv), gather(w_out), gather(w_ffn_in), gather(w_ffn_out)
    prm = gather(jnp.stack([gain_one, shift_one, gain_two, shift_two, bias_out], axis=1))
    prm = jnp.pad(prm.T.astype(F32), ((0, 3), (0, 0)))
    wf = jnp.concatenate([wf, jnp.pad(gather(bias_in)[:, None], ((0, 0), (0, LANES - 1)))], axis=1)

    slice_seqs = lax.axis_size("dp") * group_id.shape[0]
    labels = jnp.arange(slice_seqs // 2, dtype=jnp.int32)
    onehot = (group_id[:, None] == labels[None, :]).astype(F32)
    counts = lax.psum(jnp.sum(onehot, axis=0), "dp")
    group_size = jnp.sum(onehot * counts[None, :], axis=-1)
    groups = jnp.sum((counts > 0.5).astype(F32))
    seq_weight = jnp.broadcast_to((slice_seqs / (groups * group_size))[:, None], (8, LANES))

    fx = padded_features(feature_matrix)
    h1, q, k, v, pq, pk, attr, den, low = call(
        functools.partial(forward_kernel, factor),
        forward_outs(length, width, heads, feats), [], "forward",
    )(tokens, wq, prm, fx)
    act, dy, datt, gprm, grads = middle(tokens, attr, cotangent, wo, wi, wf, prm, seq_weight)
    input_grad, gq, gprm = call(
        functools.partial(backward_kernel, factor),
        [((length, width), BF), ((width, 3 * width), BF), ((16, width), F32)],
        backward_scratch(length, width), "backward",
    )(tokens, h1, q, k, v, pq, pk, attr, den, datt, dy, wq, fx, prm, gprm, low)
    gq = by_pair(gq, width // LANES)
    grads = grads.reshape(-1, width // 16, 16, width)
    gf = grads[:4].transpose(1, 0, 2, 3).reshape(hidden, width)
    gi = grads[4:-1].transpose(1, 2, 0, 3).reshape(width, hidden)
    go = grads[-1].reshape(width, width)
    small = scatter(gprm[:8].T)
    gbin = scatter(gprm[5 : 5 + hidden // width].reshape(hidden))
    part = [scatter(t).astype(F32) for t in (gq, go, gi, gf)]
    return (act, input_grad, *part, *(small[:, i] for i in range(4)), gbin, small[:, 4])


def ring_body(
    tokens, cotangent, group_id, w_qkv, w_out, w_ffn_in, w_ffn_out,
    gain_one, shift_one, gain_two, shift_two, bias_in, bias_out, feature_matrix,
):
    length, width = tokens.shape
    heads, feats, head_size = feature_matrix.shape
    hidden = w_ffn_in.shape[1]
    factor = head_size ** (-0.25)
    nz = lax.axis_size("dp") // 2
    grid = (nz, 2, 2, 2)
    wide = 3 * width
    pairs = width // LANES
    parts = hidden // width
    chunks, many = 5 + parts, 3 + pairs + 2 * parts
    wqs = (pairs, *grid, 16, 3 * LANES)
    big, deep, tall = (length, width), (length, heads * feats), (length, hidden)
    half = (-(-(3 + parts) * pairs // 8) * 8, LANES)
    pair_rows = (2 * pairs, LANES)
    near, far = 3, 2 * nz - 1
    act, input_grad, gq, gf, gi, go, rest, first = call(
        functools.partial(layer_kernel, nz, factor),
        [
            (big, BF), (big, BF), ((16, wide), F32), ((4, 16, width), F32), ((16, hidden), F32),
            ((16, width), F32), (half, F32), (pair_rows, F32),
        ],
        [
            *[(big, BF)] * 4, *[(deep, BF)] * 2, (big, BF), (big, F32),
            ((heads, length // BLOCK - 1, feats, 2 * LANES), BF),
            ((pairs, 16, 3 * LANES), BF), (wqs, BF), ((*grid, 16, width), BF),
            ((*grid, 16, hidden), BF), ((*grid, 64, width), BF), ((*grid, 16, LANES), BF), (big, BF),
            ((heads, feats, 2 * LANES), BF), ((16, LANES), F32), ((LANES, LANES), BF),
            ((8, width), F32),
            (big, BF), (big, F32), (big, F32), ((chunks, *grid, 16, width), BF), ((16, width), F32),
            (tall, BF), (tall, BF), (big, BF), (big, BF), (big, BF),
            ((8, width), F32), ((8, LANES), F32), ((4, 8, LANES), F32),
            ((pairs, *grid, 16, 3 * LANES), BF),
            *Reduce.shapes(chunks, nz, 16, width),
            *Reduce.shapes(pairs, nz, 16, 3 * LANES),
            (half, F32), (half, F32), ((near, *half), F32), ((far, *half), F32),
            (pair_rows, F32), (pair_rows, F32), ((near, *pair_rows), F32), ((far, *pair_rows), F32),
            ((4 * nz - 1, 16, 3 * LANES), BF),
            ((many, 4, nz - 1), None), ((many, 4, nz - 1), None), ((many,), None),
            ((chunks, 4, nz - 1), None), ((chunks, 4, nz - 1), None),
            ((pairs, 4, nz - 1), None), ((pairs, 4, nz - 1), None),
            ((2, far), None), ((2, far), None), ((2, far), None), ((2, far), None),
            ((4 * nz - 1,), None), ((4 * nz - 1,), None),
            ((), None), ((2, length // FFN_TILE), None),
        ],
        "layer",
        [VM, ANY, VM, ANY, ANY, ANY, VM, pl.BlockSpec(memory_space=pltpu.SMEM), *[VM] * 6],
        [ANY, ANY, *[VM] * 6],
        0,
    )(
        tokens, cotangent, w_qkv, w_out, w_ffn_in, w_ffn_out, feature_matrix.swapaxes(1, 2),
        group_id, *(t[None] for t in (gain_one, shift_one, gain_two, shift_two, bias_out, bias_in)),
    )
    act, input_grad, gq, go, gi, gf, *vecs = call(
        finish_kernel,
        [
            (big, BF), (big, BF), ((16, wide), F32), ((16, width), F32), ((16, hidden), F32),
            ((64, width), F32), *[((1, 16), F32)] * 4, ((1, 64), F32), ((1, 16), F32),
        ],
        [
            ((2, length, width), BF), ((16, wide), F32), ((4, 16, width), F32), ((16, hidden), F32),
            ((16, width), F32), ((2 * length // TILE + 7,), None), ((2 * length // TILE + 7,), None),
        ],
        "finish",
        [*[ANY] * 6, VM, VM],
        [*[ANY] * 6, *[VM] * 6],
    )(act, input_grad, gq, gf, gi, go, rest, first)
    return (act, input_grad, gq, go, gi, gf, *(t[0] for t in vecs))


def solution(mesh):
    rows, vec = P(AXES, None), P(AXES)
    devices = mesh.shape["dp"] * mesh.shape["fsdp"]

    def body(*args):
        width = args[0].shape[1]
        ring = mesh.shape["fsdp"] == 4 and mesh.shape["dp"] % 2 == 0 and width == 16 * devices
        return (ring_body if ring else plain_body)(*args)

    return jax.shard_map(
        body,
        mesh=mesh,
        in_specs=(rows, rows, vec, *[rows] * 4, *[vec] * 6, P()),
        out_specs=(*[rows] * 6, *[vec] * 6),
        check_vma=False,
    )
```

```python
import functools
import math

import jax
import jax.numpy as jnp
from jax import lax
from jax.experimental import pallas as pl
from jax.experimental.pallas import tpu as pltpu
from jax.sharding import PartitionSpec as P

BLOCK = 512
EPSILON = 1e-05
TILE = 256
FEAT_TILE = 1024
FFN_TILE = 512
LANES = 128
LOG2E = 1.4426950408889634
AXES = ("dp", "fsdp")
BF = jnp.bfloat16
F32 = jnp.float32


def dot(left, right):
    return lax.dot_general(left, right, (((1,), (0,)), ((), ())), preferred_element_type=F32)


def dot_bt(left, right):
    return lax.dot_general(left, right, (((1,), (1,)), ((), ())), preferred_element_type=F32)


def dot_at(left, right):
    return lax.dot_general(left, right, (((0,), (0,)), ((), ())), preferred_element_type=F32)


def unit_rows(rows):
    row = lax.broadcasted_iota(jnp.int32, (rows, LANES), 0)
    col = lax.broadcasted_iota(jnp.int32, (rows, LANES), 1)
    return jnp.where(row == col, 1.0, 0.0).astype(BF)


def lane_ids(rows, width=LANES):
    return lax.broadcasted_iota(jnp.int32, (rows, width), 1)


def tile_at(index, size=TILE):
    return pl.ds(pl.multiple_of(index * size, size), size)


def centred(values):
    mu = jnp.mean(values, axis=-1, keepdims=True)
    cen = values - mu
    inv = lax.rsqrt(jnp.mean(cen * cen, axis=-1, keepdims=True) + EPSILON)
    return cen * inv, inv


def norm_back(grad, unit, inv, gain):
    e = grad * gain
    return inv * (
        e
        - jnp.mean(e, axis=-1, keepdims=True)
        - unit * jnp.mean(e * unit, axis=-1, keepdims=True)
    )


def causal(values, offset):
    row = lax.broadcasted_iota(jnp.int32, values.shape, 0)
    col = lax.broadcasted_iota(jnp.int32, values.shape, 1)
    return jnp.where(col <= row + offset, values, 0.0).astype(BF)


def anticausal(values):
    row = lax.broadcasted_iota(jnp.int32, values.shape, 0)
    col = lax.broadcasted_iota(jnp.int32, values.shape, 1)
    return jnp.where(col >= row, values, 0.0).astype(BF)


MESH_ID = pl.DeviceIdType.MESH


SUMS = {
    "grad0": ((4, 0),),
    "chunk1": ((4, 1),),
    "grad1": ((5, 0),),
    "chunk2": ((5, 1), (4, 2)),
    "grad2": ((6, 0),),
    "chunk3": ((6, 1), (5, 2), (4, 3)),
    "grad3": ((7, 0), (0, 0), (1, 0), (2, 0), (3, 0)),
    "final": ((7, 1), (0, 1), (6, 2), (5, 3)),
    "grad_o": ((8, 0), (1, 1), (2, 1)),
    "b0:0": ((3, 1), (8, 1)),
    "b0:1": ((7, 2), (0, 2), (1, 2), (6, 3)),
    "b1:0": ((2, 2), (3, 2), (8, 2)),
    "b1:1": ((7, 3), (0, 3), (1, 3)),
    "b2:0": ((2, 3), (3, 3), (8, 3)),
    "tail": ((4, 4), (5, 4), (6, 4), (7, 4), (0, 4), (1, 4), (2, 4), (3, 4), (8, 4)),
}
OWN_SUMS = {
    "b1:0": ((0, 1),),
    "b2:0": ((0, 2), (1, 1)),
    "b3:0": ((0, 3), (1, 2), (2, 1)),
}
PLAN = {
    "start": (("s", 1), ("q0", 1), ("q1", 1), ("q2", 1), ("s", 2), ("q3", 1), ("q0", 2), ("o", 1), ("q1", 2), ("s", 3), ("i0", 1), ("q2", 2), ("q3", 2), ("q0", 3), ("q1", 3), ("o", 2),),
    "rows": (("f3", 1), ("i0", 2), ("f0", 1), ("f1", 1), ("f2", 1),),
    "0:0": (("q2", 3), ("i1", 1),),
    "0:2": (("q3", 3), ("i2", 1),),
    "1:0": (("f3", 2), ("o", 3), ("i3", 1),),
    "1:1": (("f0", 2),),
    "1:2": (("i0", 3), ("f1", 2),),
    "2:1": (("i1", 2), ("f2", 2),),
    "2:2": (("i2", 2),),
    "3:1": (("f0", 3),),
    "3:2": (("f3", 3),),
    "norm": (("f1", 3), ("i3", 2),),
    "chunk0": (("i1", 3), ("f2", 3),),
    "grad0": (("i2", 3),),
    "chunk1": (("i3", 3),),
}
Y_FIRST = {"q1", "o", "f2", "f3"}
LEAVE = ("s", "q0", "q1", "q2", "q3", "o", "i0", "F", "i1", "i2", "i3")


class Place:
    def __init__(self, nz):
        dp, fs = lax.axis_index("dp"), lax.axis_index("fsdp")
        self.nz = nz
        self.z, self.y = lax.div(dp, 2), lax.rem(dp, 2)
        self.x, self.c = lax.div(fs, 2), lax.rem(fs, 2)

    def device(self, z=None, y=None, x=None, c=None):
        z, y = self.z if z is None else z, self.y if y is None else y
        x, c = self.x if x is None else x, self.c if c is None else c
        return {"dp": z * 2 + y, "fsdp": x * 2 + c}

    def up(self, k):
        return lax.rem(self.z + k, self.nz)

    def down(self, k):
        return lax.rem(self.z + self.nz - k, self.nz)

    def around(self):
        for k in range(1, 4 * self.nz):
            y = 1 - self.y if k // 2 % 2 else self.y
            x = 1 - self.x if k % 2 else self.x
            yield (self.up(k // 4), y, x), (self.down(k // 4), y, x)

    def peers(self):
        yield self.device(c=1 - self.c)
        yield self.device(x=1 - self.x, c=1 - self.c)
        for (z, y, x), _ in self.around():
            yield self.device(z, y, x)

    def near(self):
        yield self.device(c=1 - self.c)
        yield self.device(x=1 - self.x)
        yield self.device(x=1 - self.x, c=1 - self.c)

    def far(self):
        yield self.device(y=1 - self.y)
        for k in range(1, self.nz):
            yield self.device(z=self.up(k))
            yield self.device(z=self.up(k), y=1 - self.y)

    def greet(self):
        for peer in self.peers():
            pl.semaphore_signal(
                pltpu.get_barrier_semaphore(), inc=1, device_id=peer, device_id_type=MESH_ID
            )

    def all_here(self):
        pl.semaphore_wait(pltpu.get_barrier_semaphore(), 1 + 4 * self.nz)


def remote(src, dst, send, recv, peer):
    return pltpu.make_async_remote_copy(
        src_ref=src, dst_ref=dst, send_sem=send, recv_sem=recv, device_id=peer,
        device_id_type=MESH_ID,
    )


class Gather:
    def __init__(self, place, shard, whole, view, sems, m, y_first, plane=None, base=None):
        self.place, self.shard, self.whole, self.view = place, shard, whole, view
        self.send, self.recv, self.own = sems
        self.m = m
        self.y_first = y_first
        self.plane, self.base = plane, base

    def at(self, *index):
        return self.whole.at[(*index, *self.view)]

    def hops(self, stage):
        p = self.place
        every = slice(None)
        zs = every if self.plane is None else self.plane
        if stage == 0:
            src = self.shard.at[self.view]
            for k in range(1, p.nz):
                yield src, self.at(p.z, p.y, p.x, p.c), self.at(p.down(k), p.y, p.x, p.c), p.device(z=p.up(k))
        elif stage == 3:
            mine = self.at(zs, every, every, p.c)
            yield mine, mine, self.at(zs, every, every, 1 - p.c), p.device(c=1 - p.c)
        elif stage == 1:
            mine = self.at(zs, p.y, p.x, p.c)
            if self.y_first:
                yield mine, mine, self.at(zs, 1 - p.y, p.x, p.c), p.device(y=1 - p.y)
            else:
                yield mine, mine, self.at(zs, p.y, 1 - p.x, p.c), p.device(x=1 - p.x)
        elif self.y_first:
            mine = self.at(zs, every, p.x, p.c)
            yield mine, mine, self.at(zs, every, 1 - p.x, p.c), p.device(x=1 - p.x)
        else:
            mine = self.at(zs, p.y, every, p.c)
            yield mine, mine, self.at(zs, 1 - p.y, every, p.c), p.device(y=1 - p.y)

    def copies(self, stage, arriving):
        for k, (src, dst, land, peer) in enumerate(self.hops(stage)):
            yield remote(
                src, land if arriving else dst, self.send.at[self.m, stage, k],
                self.recv.at[self.m, stage, k], peer,
            )

    def local(self):
        p = self.place
        return pltpu.make_async_copy(
            self.shard.at[self.view], self.at(p.z, p.y, p.x, p.c), self.own.at[self.m]
        )

    def start(self):
        for copy in self.copies(0, False):
            copy.start()
        self.local().start()

    def arrive(self, stage):
        for copy in self.copies(stage, True):
            copy.wait_recv()

    def enter(self):
        if self.plane is None:
            self.arrive(0)
            self.local().wait()
            return
        p = self.place
        hop = lax.rem(p.z + p.nz - self.plane, p.nz)

        @pl.when(hop == 0)
        def _():
            self.base.local().wait()

        @pl.when(hop != 0)
        def _():
            k = jnp.maximum(hop, 1) - 1
            remote(
                self.shard.at[self.view], self.at(self.plane, p.y, p.x, p.c),
                self.send.at[self.base.m, 0, k], self.recv.at[self.base.m, 0, k],
                p.device(z=p.up(1)),
            ).wait_recv()

    def step(self, stage):
        if stage == 1:
            self.enter()
        else:
            self.arrive(stage - 1)
        for copy in self.copies(stage, False):
            copy.start()

    def drain(self, stages=range(4)):
        for stage in stages:
            for copy in self.copies(stage, False):
                copy.wait_send()


class Reduce:
    def __init__(self, place, source, bufs, sems, write):
        self.place, self.source = place, source
        self.r0, self.r1, self.r2, self.r3 = bufs
        self.send, self.recv = sems
        self.write = write

    def hops(self, stage, cs, x_first):
        p = self.place
        every = slice(None)
        r0, r1, r2, r3 = (ref.at[cs] for ref in (self.r0, self.r1, self.r2, self.r3))
        if stage == 0:
            yield self.source.at[cs, every, every, every, 1 - p.c], r0, p.device(c=1 - p.c)
        elif stage == 1:
            if x_first:
                yield r0.at[every, every, every, 1 - p.x], r1, p.device(x=1 - p.x)
            else:
                yield r0.at[every, every, 1 - p.y], r1, p.device(y=1 - p.y)
        elif stage == 2:
            if x_first:
                yield r1.at[every, every, 1 - p.y], r2, p.device(y=1 - p.y)
            else:
                yield r1.at[every, every, 1 - p.x], r2, p.device(x=1 - p.x)
        else:
            for k in range(1, p.nz):
                yield r2.at[every, p.up(k)], r3.at[every, k - 1], p.device(z=p.up(k))

    def copies(self, stage, c, x_first, count=1):
        for k, (src, dst, peer) in enumerate(self.hops(stage, pl.ds(c, count), x_first)):
            yield remote(src, dst, self.send.at[c, stage, k], self.recv.at[c, stage, k], peer)

    def step(self, stage, c, x_first=False, count=1):
        p = self.place
        cs = pl.ds(c, count)
        if stage:
            for copy in self.copies(stage - 1, c, x_first, count):
                copy.wait_recv()
        if stage == 1:
            self.r0[cs] = self.source[cs, :, :, :, p.c] + self.r0[cs]
        elif stage == 2:
            mine = self.r0[cs, :, :, p.x] if x_first else self.r0[cs, :, p.y]
            self.r1[cs] = mine + self.r1[cs]
        elif stage == 3:
            mine = self.r1[cs, :, p.y] if x_first else self.r1[cs, :, p.x]
            self.r2[cs] = mine + self.r2[cs]
        elif stage == 4:
            for n in range(count):
                total = self.r2[c + n, p.z].astype(F32)
                for k in range(p.nz - 1):
                    total = total + self.r3[c + n, k].astype(F32)
                self.write(c + n, total)
            return
        for copy in self.copies(stage, c, x_first, count):
            copy.start()

    def drain(self, c, x_first=False, count=1, stages=range(4)):
        for stage in stages:
            for copy in self.copies(stage, c, x_first, count):
                copy.wait_send()

    def short(self, c, land, sems):
        p = self.place
        for k, (to, _) in enumerate(p.around()):
            yield remote(self.r0.at[(c, *to)], land.at[k], sems[0].at[k], sems[1].at[k], p.device(*to))

    def short_start(self, c, land, sems):
        for copy in self.copies(0, c, False):
            copy.wait_recv()
        self.r0[c] = self.source[c, :, :, :, self.place.c] + self.r0[c]
        for copy in self.short(c, land, sems):
            copy.start()

    def short_end(self, c, land, sems):
        p = self.place
        total = self.r0[c, p.z, p.y, p.x].astype(F32)
        for k, copy in enumerate(self.short(c, land, sems)):
            copy.wait_recv()
            total = total + land[k].astype(F32)
        self.write(c, total)

    @staticmethod
    def shapes(n, nz, rows, cols):
        return [
            ((n, nz, 2, 2, rows, cols), BF), ((n, nz, 2, rows, cols), BF),
            ((n, nz, rows, cols), BF), ((n, nz - 1, rows, cols), BF),
        ]


def project_rows(i, x_ref, wq, prm_ref, h_ref, q_ref, k_ref, v_ref, factor):
    rows = tile_at(i)
    unit, _ = centred(x_ref[rows, :].astype(F32))
    h = (unit * prm_ref[0:1, :] + prm_ref[1:2, :]).astype(BF)
    h_ref[rows, :] = h
    width = h.shape[1]
    qkv = dot(h, wq)
    q_ref[rows, :] = (qkv[:, :width] * factor).astype(BF)
    k_ref[rows, :] = (qkv[:, width : 2 * width] * factor).astype(BF)
    v_ref[rows, :] = qkv[:, 2 * width :].astype(BF)


def attend_pair(
    p, q_ref, k_ref, v_ref, fx_ref, pq_ref, pk_ref, attr_ref, den_ref, low_ref,
    site=lambda j: None,
):
    length = q_ref.shape[0]
    feats = fx_ref.shape[1]
    lanes = tile_at(p, LANES)
    shift = 0.5 * math.log2(feats)
    cols = [tile_at(2 * p + hh, feats) for hh in range(2)]
    step = FEAT_TILE
    for hh in range(2):
        fm = fx_ref[2 * p + hh][:, :LANES]
        for src, dst in ((q_ref, pq_ref), (k_ref, pk_ref)):
            for t in range(length // step):
                rows = slice(t * step, (t + 1) * step)
                part = src[rows, lanes]
                scores = dot_bt(part, fm)
                wide = jnp.where(lane_ids(step) // 64 == hh, part.astype(F32), 0.0)
                square = jnp.sum(wide * wide, axis=-1, keepdims=True)
                feat = jnp.exp2(scores * LOG2E - (square * (0.5 * LOG2E) + shift))
                dst[rows, cols[hh]] = feat.astype(BF)
    site(1)
    ones = jnp.ones((length, LANES), BF)
    vx = jnp.concatenate([v_ref[:, lanes], ones], axis=1)
    states = [None, None]
    for b in range(length // BLOCK):
        base = b * BLOCK
        for i in range(BLOCK // TILE):
            rows = slice(base + i * TILE, base + (i + 1) * TILE)
            keys = slice(base, base + (i + 1) * TILE)
            got = []
            for hh in range(2):
                pq = pq_ref[rows, cols[hh]]
                weights = causal(dot_bt(pq, pk_ref[keys, cols[hh]]), i * TILE)
                both = dot(weights, vx[keys])
                if b:
                    both = both + dot(pq, low_ref[2 * p + hh, b - 1])
                got.append(both)
            first = lane_ids(TILE) < 64
            num = jnp.where(first, got[0][:, :LANES], got[1][:, :LANES])
            den = jnp.where(first, got[0][:, LANES:], got[1][:, LANES:])
            attr_ref[rows, lanes] = (num / den).astype(BF)
            den_ref[rows, lanes] = den
        if base + BLOCK < length:
            block = slice(base, base + BLOCK)
            for hh in range(2):
                more = dot_at(pk_ref[block, cols[hh]], vx[block])
                states[hh] = more if b == 0 else states[hh] + more
                low_ref[2 * p + hh, b] = states[hh].astype(BF)


def forward_kernel(
    factor, x_ref, wq_ref, prm_ref, fx_ref,
    h_ref, q_ref, k_ref, v_ref, pq_ref, pk_ref, attr_ref, den_ref, low_ref,
):
    def rows(i, carry):
        project_rows(i, x_ref, wq_ref[...], prm_ref, h_ref, q_ref, k_ref, v_ref, factor)
        return carry

    lax.fori_loop(0, x_ref.shape[0] // TILE, rows, 0)

    def pair(p, carry):
        attend_pair(
            p, q_ref, k_ref, v_ref, fx_ref, pq_ref, pk_ref, attr_ref, den_ref, low_ref
        )
        return carry

    lax.fori_loop(0, x_ref.shape[1] // LANES, pair, 0)


def ffn_rows(
    t, x_ref, attr_ref, cot_ref, wo, wi, wf, prm_ref, bin_ref, seq_ref,
    act_ref, dy_ref, datt_ref, gprm_ref, hid_ref, du_ref, h_ref, gr_ref, dor_ref, bin_row=0,
):
    width = x_ref.shape[1]
    chunk = width
    rows = tile_at(t, FFN_TILE)
    y = x_ref[rows, :].astype(F32) + dot(attr_ref[rows, :], wo())
    unit, inv = centred(y)
    gain = prm_ref[2:3, :]
    h = (unit * gain + prm_ref[3:4, :]).astype(BF)
    h_ref[rows, :] = h
    g = cot_ref[rows, :].astype(F32) * seq_ref[0:1, 0:1]
    gr = g.astype(BF)
    gr_ref[rows, :] = gr
    out = y + prm_ref[4:5, :]
    dh = jnp.zeros((FFN_TILE, width), F32)
    for c in range(hid_ref.shape[1] // chunk):
        cs = slice(c * chunk, (c + 1) * chunk)
        u = dot(h, wi(cs)) + bin_ref[bin_row : bin_row + 1, cs]
        cdf = 0.5 + 0.5 * lax.erf(u * math.sqrt(0.5))
        slope = cdf + u * jnp.exp2(u * u * (-0.5 * LOG2E)) * (1.0 / math.sqrt(2.0 * math.pi))
        hid = (u * cdf).astype(BF)
        hid_ref[rows, cs] = hid
        out = out + dot(hid, wf(c))
        du = (dot_bt(gr, wf(c)) * slope).astype(BF)
        du_ref[rows, cs] = du
        gprm_ref[5 + c : 6 + c, :] += jnp.sum(du.astype(F32), axis=0, keepdims=True)
        dh = dh + dot_bt(du, wi(cs))
    act_ref[rows, :] = out.astype(BF)
    gprm_ref[2:3, :] += jnp.sum(dh * unit, axis=0, keepdims=True)
    gprm_ref[3:4, :] += jnp.sum(dh, axis=0, keepdims=True)
    gprm_ref[4:5, :] += jnp.sum(g, axis=0, keepdims=True)
    dy = g + norm_back(dh, unit, inv, gain)
    dy_ref[rows, :] = dy
    dor = dy.astype(BF)
    dor_ref[rows, :] = dor
    datt_ref[rows, :] = dot_bt(dor, wo())


def ffn_norm(t, x_ref, attr_ref, cot_ref, wo, prm_ref, seq_ref, y_ref, h_ref, gr_ref):
    rows = tile_at(t, FFN_TILE)
    y = x_ref[rows, :].astype(F32) + dot(attr_ref[rows, :], wo)
    y_ref[rows, :] = y
    unit, _ = centred(y)
    h_ref[rows, :] = (unit * prm_ref[2:3, :] + prm_ref[3:4, :]).astype(BF)
    gr_ref[rows, :] = (cot_ref[rows, :].astype(F32) * seq_ref[0:1, 0:1]).astype(BF)


def ffn_chunk(t, c, wi, wf, bias, h_ref, gr_ref, hid_ref, du_ref, gprm_ref):
    rows = tile_at(t, FFN_TILE)
    width = h_ref.shape[1]
    cs = slice(c * width, (c + 1) * width)
    u = dot(h_ref[rows, :], wi) + bias
    cdf = 0.5 + 0.5 * lax.erf(u * math.sqrt(0.5))
    slope = cdf + u * jnp.exp2(u * u * (-0.5 * LOG2E)) * (1.0 / math.sqrt(2.0 * math.pi))
    hid_ref[rows, cs] = (u * cdf).astype(BF)
    du = (dot_bt(gr_ref[rows, :], wf) * slope).astype(BF)
    du_ref[rows, cs] = du
    gprm_ref[5 + c : 6 + c, :] += jnp.sum(du.astype(F32), axis=0, keepdims=True)


def ffn_final(
    t, cot_ref, wo, wi, prm_ref, seq_ref, y_ref, du_ref, dy_ref, dor_ref, datt_ref, gprm_ref
):
    rows = tile_at(t, FFN_TILE)
    y = y_ref[rows, :]
    dh = dot_bt(du_ref[rows, :], wi)
    unit, inv = centred(y)
    g = cot_ref[rows, :].astype(F32) * seq_ref[0:1, 0:1]
    gprm_ref[2:3, :] += jnp.sum(dh * unit, axis=0, keepdims=True)
    gprm_ref[3:4, :] += jnp.sum(dh, axis=0, keepdims=True)
    gprm_ref[4:5, :] += jnp.sum(g, axis=0, keepdims=True)
    dy = g + norm_back(dh, unit, inv, prm_ref[2:3, :])
    dy_ref[rows, :] = dy
    dor = dy.astype(BF)
    dor_ref[rows, :] = dor
    datt_ref[rows, :] = dot_bt(dor, wo)


def grads_out(c, hid_ref, gr_ref, g_ref):
    width = gr_ref.shape[1]
    grad = dot_at(hid_ref[:, tile_at(c)], gr_ref[...]).astype(BF)
    grad = grad.reshape(4, 4, 16, width)
    for q in range(4):
        g_ref[q, c] = grad[:, q]


def grads_in(c, h_ref, du_ref, attr_ref, dor_ref, g_ref):
    width = h_ref.shape[1]
    count = du_ref.shape[1] // width
    cs = tile_at(c)
    at = pl.ds(c * 4, 4)
    grad = dot_at(h_ref[:, cs], du_ref[...]).astype(BF)
    for k in range(count):
        g_ref[4 + k, at] = grad[:, k * width : (k + 1) * width].reshape(4, 4, 16, width)
    grad = dot_at(attr_ref[:, cs], dor_ref[...]).astype(BF)
    g_ref[4 + count, at] = grad.reshape(4, 4, 16, width)


def loop(start, stop, step):
    def run(i, carry):
        step(i)
        return carry

    lax.fori_loop(start, stop, run, 0)


def middle_kernel(
    x_ref, attr_ref, cot_ref, wo_ref, wi_ref, wf_ref, prm_ref, seq_ref,
    act_ref, dy_ref, datt_ref, gprm_ref, g_ref,
    hid_ref, du_ref, h_ref, gr_ref, dor_ref, bin_ref,
):
    length, width = x_ref.shape
    gprm_ref[...] = jnp.zeros_like(gprm_ref)
    bin_ref[...] = dot_bt(unit_rows(8), wf_ref[:, width:])
    loop(0, length // FFN_TILE, lambda t: ffn_rows(
        t, x_ref, attr_ref, cot_ref, lambda: wo_ref[...], lambda cs: wi_ref[:, cs],
        lambda c: wf_ref[c * width : (c + 1) * width, :width], prm_ref, bin_ref, seq_ref,
        act_ref, dy_ref, datt_ref, gprm_ref, hid_ref, du_ref, h_ref, gr_ref, dor_ref,
    ))
    loop(0, hid_ref.shape[1] // TILE, lambda c: grads_out(c, hid_ref, gr_ref, g_ref))
    loop(0, width // TILE, lambda c: grads_in(c, h_ref, du_ref, attr_ref, dor_ref, g_ref))


def back_pair(
    p, factor, q_ref, k_ref, v_ref, pq_ref, pk_ref, att_ref, den_ref, datt_ref, fx_ref, low_ref,
    ht_ref, dqkv_refs, dn_ref, e_ref, da_ref, tick, store,
):
    length = q_ref.shape[0]
    feats = fx_ref.shape[1]
    lanes = tile_at(p, LANES)
    blocks = length // BLOCK
    cols = [tile_at(2 * p + hh, feats) for hh in range(2)]
    two = jnp.where(lane_ids(length) < 2, 1.0, 0.0).astype(BF)
    v2 = jnp.concatenate([v_ref[:, lanes], two], axis=1)
    for t in range(length // TILE):
        rows = slice(t * TILE, (t + 1) * TILE)
        dn = datt_ref[rows, lanes] / den_ref[rows, lanes]
        prod = dn * att_ref[rows, lanes].astype(F32)
        lane = lane_ids(TILE)
        for hh in range(2):
            mine = lane // 64 == hh
            dden = -jnp.sum(jnp.where(mine, prod, 0.0), axis=-1, keepdims=True)
            high = dden.astype(BF).astype(F32)
            extra = jnp.where(lane == 0, high, jnp.where(lane == 1, dden - high, 0.0))
            dn_ref[hh, rows, :LANES] = jnp.where(mine, dn, 0.0).astype(BF)
            dn_ref[hh, rows, LANES:] = extra.astype(BF)
    for hh in range(2):
        fx = fx_ref[2 * p + hh]
        back = [None] * blocks
        total = None
        for b in range(blocks - 1, 0, -1):
            block = slice(b * BLOCK, (b + 1) * BLOCK)
            more = dot_at(pq_ref[block, cols[hh]], dn_ref[hh, block, :])
            total = more if total is None else total + more
            dz = total[:, LANES : LANES + 1] + total[:, LANES + 1 : LANES + 2]
            high = dz.astype(BF).astype(F32)
            lane = lane_ids(feats)
            extra = jnp.where(lane == 0, high, jnp.where(lane == 1, dz - high, 0.0))
            back[b - 1] = jnp.concatenate([total[:, :LANES], extra], axis=1).astype(BF)

        def put(value, rows, at, hh=hh):
            ref = dqkv_refs[at]
            if hh:
                mine = lane_ids(value.shape[0]) >= 64
                value = jnp.where(mine, value, ref[rows, lanes].astype(F32))
            ref[rows, lanes] = value.astype(BF)

        for b in range(blocks):
            base = b * BLOCK
            for i in range(BLOCK // TILE):
                rows = slice(base + i * TILE, base + (i + 1) * TILE)
                keys = slice(base, base + (i + 1) * TILE)
                dn = dn_ref[hh, rows, :]
                da = causal(dot_bt(dn, v2[keys]), i * TILE)
                da_ref[i * TILE : (i + 1) * TILE, : (i + 1) * TILE] = da
                grad = dot(da, pk_ref[keys, cols[hh]])
                if b:
                    grad = grad + dot_bt(dn, low_ref[2 * p + hh, b - 1])
                e_ref[0, rows, :] = (grad * pq_ref[rows, cols[hh]].astype(F32)).astype(BF)
            for i in range(BLOCK // TILE):
                rows = slice(base + i * TILE, base + (i + 1) * TILE)
                later = slice(base + i * TILE, base + BLOCK)
                pk = pk_ref[rows, cols[hh]]
                pql = pq_ref[later, cols[hh]]
                grad = dot_at(da_ref[i * TILE :, i * TILE : (i + 1) * TILE], pql)
                at = anticausal(dot_bt(pk, pql))
                dv = dot(at, dn_ref[hh, later, :LANES])
                if b < blocks - 1:
                    grad = grad + dot_bt(v2[rows], back[b])
                    dv = dv + dot(pk, back[b][:, :LANES])
                e_ref[1, rows, :] = (grad * pk.astype(F32)).astype(BF)
                put(dv, rows, 2)
        for at, src in ((0, q_ref), (1, k_ref)):
            res = dot(e_ref[at], fx)
            out = (res[:, :LANES] - src[:, lanes].astype(F32) * res[:, LANES:]) * factor
            put(out, slice(0, length), at)
        if hh == 0:
            tick(0)
    store(dot(ht_ref[...], jnp.concatenate([ref[:, lanes] for ref in dqkv_refs], axis=1)).astype(BF))


def input_rows(t, x_ref, wq, prm_ref, dqkv_refs, dy_ref, out_ref, gprm_ref):
    rows = tile_at(t, FFN_TILE)
    dh = dot_bt(jnp.concatenate([ref[rows, :] for ref in dqkv_refs], axis=1), wq)
    unit, inv = centred(x_ref[rows, :].astype(F32))
    gprm_ref[0:1, :] += jnp.sum(dh * unit, axis=0, keepdims=True)
    gprm_ref[1:2, :] += jnp.sum(dh, axis=0, keepdims=True)
    out_ref[rows, :] = (dy_ref[rows, :] + norm_back(dh, unit, inv, prm_ref[0:1, :])).astype(BF)


def flip_rows(h_ref, ht_ref):
    for t in range(h_ref.shape[0] // TILE):
        rows = slice(t * TILE, (t + 1) * TILE)
        ht_ref[:, rows] = h_ref[rows, :].T


def backward_kernel(
    factor, x_ref, h_ref, q_ref, k_ref, v_ref, pq_ref, pk_ref, att_ref, den_ref, datt_ref, dy_ref,
    wq_ref, fx_ref, prm_ref, gin_ref, low_ref,
    out_ref, gq_ref, gprm_ref,
    ht_ref, dqkv_ref, dn_ref, e_ref, da_ref,
):
    gprm_ref[...] = gin_ref[...]
    width = x_ref.shape[1]
    dqkv_refs = [dqkv_ref.at[:, n * width : (n + 1) * width] for n in range(3)]
    flip_rows(h_ref, ht_ref)

    def pair(p, carry):
        def store(value):
            gq_ref[:, tile_at(p, 3 * LANES)] = value

        back_pair(
            p, factor, q_ref, k_ref, v_ref, pq_ref, pk_ref, att_ref, den_ref, datt_ref, fx_ref, low_ref,
            ht_ref, dqkv_refs, dn_ref, e_ref, da_ref, lambda j: None, store,
        )
        return carry

    lax.fori_loop(0, x_ref.shape[1] // LANES, pair, 0)

    def rows(t, carry):
        input_rows(t, x_ref, wq_ref[...], prm_ref, dqkv_refs, dy_ref, out_ref, gprm_ref)
        return carry

    lax.fori_loop(0, x_ref.shape[0] // FFN_TILE, rows, 0)


def sequence_weight(small, seq_ref):
    nf = 4
    me = lax.axis_index("dp") * nf + lax.axis_index("fsdp")
    row = lax.broadcasted_iota(jnp.int32, small.shape, 0)
    lane = lane_ids(small.shape[0]).astype(F32)
    peer = lax.div(row, 16)
    ids = small[:, 5:6].astype(F32)
    hit = (lane == ids) & (lax.rem(row, 16) == 0)
    counts = jnp.sum(
        jnp.where(hit & (lax.rem(peer, nf) == lax.axis_index("fsdp")), 1.0, 0.0),
        axis=0, keepdims=True,
    )
    mine = jnp.sum(jnp.where(hit & (peer == me), 1.0, 0.0), axis=0, keepdims=True)
    size = jnp.sum(counts * mine, axis=1, keepdims=True)
    groups = jnp.sum(jnp.where(counts > 0.5, 1.0, 0.0), axis=1, keepdims=True)
    members = lax.axis_size("dp")
    seq_ref[...] = jnp.broadcast_to(members / (groups * size), seq_ref.shape)


class Columns:
    def __init__(self, ref, start, size):
        self.ref, self.start, self.size = ref, start, size

    def where(self, index):
        n, *rest = index if isinstance(index, tuple) else (index,)
        rows, cols = [*rest, slice(None), slice(None)][:2]
        base = self.start + n * self.size
        low, high = cols.start or 0, self.size if cols.stop is None else cols.stop
        return rows, slice(base + low, base + high)

    def __getitem__(self, index):
        return self.ref[self.where(index)]

    def __setitem__(self, index, value):
        self.ref[self.where(index)] = value


class Total:
    def __init__(self, place, ref, part, near, far, sems):
        self.place, self.ref, self.part, self.near, self.far = place, ref, part, near, far
        self.send, self.recv = sems

    def copies(self, stage):
        peers = self.place.far() if stage else self.place.near()
        src, dst = (self.part, self.far) if stage else (self.ref, self.near)
        for k, peer in enumerate(peers):
            yield remote(src, dst.at[k], self.send.at[stage, k], self.recv.at[stage, k], peer)

    def start(self):
        for copy in self.copies(0):
            copy.start()

    def turn(self):
        for copy in self.copies(0):
            copy.wait_recv()
        self.part[...] = self.ref[...] + sum(self.near[k] for k in range(self.near.shape[0]))
        for copy in self.copies(1):
            copy.start()

    def result(self):
        for copy in self.copies(1):
            copy.wait_recv()
        return self.part[...] + sum(self.far[k] for k in range(self.far.shape[0]))

    def drain(self):
        for stage in range(2):
            for copy in self.copies(stage):
                copy.wait_send()


def layer_kernel(
    nz, factor, x_ref, cot_in, wqs_ref, wos_ref, wis_ref, wfs_ref, fm_ref, id_ref,
    g1_ref, s1_ref, g2_ref, s2_ref, bo_ref, bi_ref,
    act_out, grad_out, partq_ref, gf_ref, gi_ref, go_ref, rest_out, first_out,
    h_ref, q_ref, k_ref, v_ref, pq_ref, pk_ref, attr_ref, den_ref, low_ref,
    wqt_ref, wq_ref, wo_ref, wi_ref, wf_ref, sp_ref, cot_ref, fx_ref, vec_ref, col_ref, prm_ref,
    act_ref, dy_ref, y_ref, g_ref, gprm_ref, hid_ref, du_ref, h2_ref, gr_ref, dor_ref,
    bin_ref, seq_ref, lhs_ref, gq_ref,
    b0, b1, b2, b3, c0, c1, c2, c3,
    rest_ref, rest_part, rest_near, rest_far, first_ref, first_part, first_near, first_far,
    land_ref,
    send, recv, own, big_send, big_recv, q_send, q_recv, rest_send, rest_recv, first_send, first_recv,
    short_send, short_recv, local_sem, tile_sem,
):
    length, width = x_ref.shape
    hidden = hid_ref.shape[1]
    place = Place(nz)
    every = slice(None)
    sems = (send, recv, own)
    pairs, tiles, parts = width // LANES, length // TILE, hidden // width
    slabs = length // FFN_TILE

    def gather(name, shard, whole, view, m, plane=None, base=None):
        return Gather(place, shard, whole, view, sems, m, name in Y_FIRST, plane, base)

    both = (every, every)
    sp = gather("s", col_ref, sp_ref, (slice(0, 16), every), 0)
    o = gather("o", wos_ref, wo_ref, both, 1)
    f = gather("f", wfs_ref, wf_ref, both, 2)
    wq = [gather(f"q{p}", wqt_ref.at[p], wq_ref.at[p], both, 3 + p) for p in range(pairs)]
    wi = [
        gather(f"i{c}", wis_ref, wi_ref, (every, slice(c * width, (c + 1) * width)), 3 + pairs + c)
        for c in range(parts)
    ]
    wf = [
        gather(f"f{c}", wfs_ref, wf_ref, both, 3 + pairs + parts + c, c, f) for c in range(parts)
    ]
    named = {"s": sp, "o": o, "F": f}
    for n in range(pairs):
        named[f"q{n}"] = wq[n]
    for n in range(parts):
        named[f"i{n}"] = wi[n]
        named[f"f{n}"] = wf[n]

    def write(c, value):
        if c < 4:
            gf_ref[c] = value
        elif c < 4 + parts:
            gi_ref[:, (c - 4) * width : (c - 3) * width] = value
        else:
            go_ref[...] = value

    def write_q(c, value):
        for at in range(3):
            where = pl.ds(pl.multiple_of(c * LANES + at * width, LANES), LANES)
            partq_ref[:, where] = value[:, at * LANES : (at + 1) * LANES]

    grid = (nz, 2, 2, 2)
    big = Reduce(place, g_ref, (b0, b1, b2, b3), (big_send, big_recv), write)
    mine = Reduce(place, gq_ref, (c0, c1, c2, c3), (q_send, q_recv), write_q)
    rest = Total(place, rest_ref, rest_part, rest_near, rest_far, (rest_send, rest_recv))
    first = Total(place, first_ref, first_part, first_near, first_far, (first_send, first_recv))
    short_sems = (short_send, short_recv)
    cot_copy = pltpu.make_async_copy(cot_in, cot_ref, local_sem)

    def slab_out(t, src, dst, n):
        rows = tile_at(t, FFN_TILE)
        return pltpu.make_async_copy(src.at[rows], dst.at[rows], tile_sem.at[n, t])

    def at_site(name):
        for who, stage in PLAN.get(name, ()):
            named[who].step(stage)
        for c, stage in SUMS.get(name, ()):
            big.step(stage, c, c % 2 == 0)
        for c, stage in OWN_SUMS.get(name, ()):
            mine.step(stage, c)

    def sites(p, prefix):
        def site(j):
            for n in range(pairs):
                name = f"{prefix}{n}:{j}"
                if name in PLAN or name in SUMS or name in OWN_SUMS:
                    pl.when(p == n)(functools.partial(at_site, name))

        return site

    place.greet()
    vec_ref[...] = jnp.zeros_like(vec_ref)
    for n, ref in enumerate((g1_ref, s1_ref, g2_ref, s2_ref, bo_ref)):
        vec_ref[n : n + 1, : ref.shape[1]] = ref[...].astype(F32)
    vec_ref[5:6, :] = jnp.full((1, LANES), id_ref[0], jnp.int32).astype(F32)
    for n in range(4):
        vec_ref[8 + n : 9 + n, :16] = bi_ref[:, n * 16 : (n + 1) * 16].astype(F32)
    col_ref[...] = dot_at(vec_ref[...].astype(BF), unit_rows(16)).astype(BF)
    for p in range(pairs):
        for n in range(3):
            at = n * width + p * LANES
            wqt_ref[p, :, n * LANES : (n + 1) * LANES] = wqs_ref[:, at : at + LANES]
    place.all_here()
    for who in LEAVE:
        named[who].start()
    cot_copy.start()
    head_size, feats = fm_ref.shape[1:]
    for n in range(fm_ref.shape[0]):
        row = lax.broadcasted_iota(jnp.int32, (head_size, LANES), 0)
        place_at = jnp.where(lane_ids(head_size) == row + (n % 2) * head_size, 1.0, 0.0).astype(BF)
        fx_ref[n, :, :LANES] = dot_at(fm_ref[n], place_at).astype(BF)
        fx_ref[n, :, LANES:] = jnp.ones((feats, LANES), BF)
    at_site("start")
    sp.arrive(3)
    small = sp_ref[...].reshape(width, LANES)
    prm = dot_bt(unit_rows(16), small)
    prm_ref[...] = prm[:8]
    at_site("params")
    sequence_weight(small, seq_ref)
    for c in range(parts):
        for n in range(4):
            lhs_ref[n, c : c + 1, :] = prm[8 + n : 9 + n, c * LANES : (c + 1) * LANES]
    row = lax.broadcasted_iota(jnp.int32, (LANES, width), 0)
    col = lax.broadcasted_iota(jnp.int32, (LANES, width), 1)
    bias = jnp.zeros((8, width), F32)
    for n in range(4):
        spread = (lax.div(row, 16) == lax.div(col, 64)) & (
            lax.rem(row, 16) + n * 16 == lax.rem(col, 64)
        )
        bias = bias + dot(lhs_ref[n].astype(BF), jnp.where(spread, 1.0, 0.0).astype(BF))
    bin_ref[...] = bias
    gprm_ref[...] = jnp.zeros_like(gprm_ref)

    def rows(i):
        rows = tile_at(i)
        unit, _ = centred(x_ref[rows, :].astype(F32))
        h_ref[rows, :] = (unit * prm_ref[0:1, :] + prm_ref[1:2, :]).astype(BF)

    loop(0, tiles, rows)
    at_site("rows")

    def pair(p):
        site = sites(p, "")
        for n in range(pairs):
            pl.when(p == n)(functools.partial(wq[n].arrive, 3))
        lanes = tile_at(p, LANES)
        for t in range(tiles):
            rows = slice(t * TILE, (t + 1) * TILE)
            qkv = dot(h_ref[rows, :], wq_ref[p].reshape(width, 3 * LANES))
            q_ref[rows, lanes] = (qkv[:, :LANES] * factor).astype(BF)
            k_ref[rows, lanes] = (qkv[:, LANES : 2 * LANES] * factor).astype(BF)
            v_ref[rows, lanes] = qkv[:, 2 * LANES :].astype(BF)
        site(0)
        attend_pair(
            p, q_ref, k_ref, v_ref, fx_ref, pq_ref, pk_ref, attr_ref, den_ref, low_ref,
            site,
        )
        site(2)

    loop(0, pairs, pair)
    o.arrive(3)
    cot_copy.wait()

    def norm(t):
        wo = wo_ref[...].reshape(width, width)
        ffn_norm(t, x_ref, attr_ref, cot_ref, wo, prm_ref, seq_ref, y_ref, h2_ref, gr_ref)

    loop(0, slabs, norm)
    at_site("norm")
    for c in range(parts):
        wi[c].arrive(3)
        wf[c].arrive(3)
        cs = slice(c * width, (c + 1) * width)

        def chunk(t, c=c, cs=cs):
            w_in, w_out = wi_ref[..., cs].reshape(width, width), wf_ref[c].reshape(width, width)
            bias = bin_ref[c : c + 1, :]
            ffn_chunk(t, c, w_in, w_out, bias, h2_ref, gr_ref, hid_ref, du_ref, gprm_ref)

        loop(0, slabs, chunk)
        at_site(f"chunk{c}")
        value = dot_at(hid_ref[:, cs], gr_ref[...]).astype(BF).reshape(8, 4, 16, width)
        for q in range(4):
            g_ref[q, c] = value[:, q].reshape(2, 2, 2, 16, width)
        value = dot_at(h2_ref[...], du_ref[:, cs]).astype(BF)
        g_ref[4 + c] = value.reshape(*grid, 16, width)
        at_site(f"grad{c}")

    def final(t):
        ffn_final(
            t, cot_ref, wo_ref[...].reshape(width, width), wi_ref[...].reshape(width, hidden),
            prm_ref, seq_ref, y_ref, du_ref, dy_ref, dor_ref, y_ref, gprm_ref,
        )

    loop(0, slabs, final)
    at_site("final")

    value = dot_at(attr_ref[...], dor_ref[...]).astype(BF)
    g_ref[4 + parts] = value.reshape(*grid, 16, width)
    at_site("grad_o")
    for n in range(3 + parts):
        for c in range(pairs):
            rest_ref[n * pairs + c : n * pairs + c + 1, :] = gprm_ref[2 + n : 3 + n, c * LANES : (c + 1) * LANES]
    for n in range((3 + parts) * pairs, rest_ref.shape[0]):
        rest_ref[n : n + 1, :] = jnp.zeros((1, LANES), F32)
    rest.start()

    ht_ref = du_ref.at[0:width, 0:length]
    da_ref = du_ref.at[width : 2 * width, 0:BLOCK]
    dn_ref = Columns(du_ref, length, 2 * LANES)
    e_ref = Columns(du_ref, length + 4 * LANES, 2 * LANES)
    dqkv_refs = (cot_ref, gr_ref, dor_ref)
    out_ref = h2_ref
    flip_rows(h_ref, ht_ref)

    def back(p):
        def store(value):
            gq_ref[p] = value.reshape(*grid, 16, 3 * LANES)

        back_pair(
            p, factor, q_ref, k_ref, v_ref, pq_ref, pk_ref, attr_ref, den_ref, y_ref, fx_ref,
            low_ref, ht_ref, dqkv_refs, dn_ref, e_ref, da_ref, sites(p, "b"), store,
        )
        mine.step(0, p)
        sites(p, "b")(1)

        @pl.when(p == 0)
        def _():
            rest.turn()

        @pl.when(p == 2)
        def _():
            rest_out[...] = rest.result()

    loop(0, pairs, back)
    last = pairs - 1

    def rows_back(t):
        weights = [
            wq_ref[p, ..., n * LANES : (n + 1) * LANES].reshape(width, LANES)
            for n in range(3)
            for p in range(pairs)
        ]
        input_rows(
            t, x_ref, jnp.concatenate(weights, axis=1), prm_ref, dqkv_refs, dy_ref, out_ref, gprm_ref
        )
        slab_out(t, out_ref, grad_out, 1).start()

    def output(t):
        rows = tile_at(t, FFN_TILE)
        out = x_ref[rows, :].astype(F32) + dot(attr_ref[rows, :], wo_ref[...].reshape(width, width))
        out = out + dot(hid_ref[rows, :], wf_ref[...].reshape(hidden, width)) + prm_ref[4:5, :]
        act_ref[rows, :] = out.astype(BF)
        slab_out(t, act_ref, act_out, 0).start()

    loop(0, slabs // 2, rows_back)
    mine.short_start(last, land_ref, short_sems)
    loop(slabs // 2, slabs, rows_back)
    for n in range(2):
        for c in range(pairs):
            first_ref[n * pairs + c : n * pairs + c + 1, :] = gprm_ref[n : n + 1, c * LANES : (c + 1) * LANES]
    first.start()
    mine.step(3, last - 2)
    mine.step(2, last - 1)
    loop(0, slabs // 2, output)
    first.turn()
    mine.step(3, last - 1)
    loop(slabs // 2, slabs, output)
    at_site("tail")
    mine.step(4, last - 3)
    mine.step(4, last - 2)
    mine.step(4, last - 1)
    first_out[...] = first.result()
    mine.short_end(last, land_ref, short_sems)
    for t in range(slabs):
        slab_out(t, act_ref, act_out, 0).wait()
        slab_out(t, out_ref, grad_out, 1).wait()
    for g in (sp, o, *wq, *wi):
        g.drain()
    f.drain((0,))
    for g in wf:
        g.drain((1, 2, 3))
    for c in range(g_ref.shape[0]):
        big.drain(c, c % 2 == 0)
    loop(0, last, mine.drain)
    mine.drain(last, stages=(0,))
    for copy in mine.short(last, land_ref, short_sems):
        copy.wait_send()
    rest.drain()
    first.drain()


def finish_kernel(
    act_in, grad_in, gq_in, gf_in, gi_in, go_in, rest_in, first_in,
    act_ref, grad_ref, gq_ref, go_ref, gi_ref, gf_ref,
    g1_ref, s1_ref, g2_ref, s2_ref, bi_ref, bo_ref,
    hold_ref, holdq_ref, holdf_ref, holdi_ref, holdo_ref, in_sem, out_sem,
):
    moves = []

    def move(src, hold, dst):
        n = len(moves)
        moves.append((
            pltpu.make_async_copy(src, hold, in_sem.at[n]),
            pltpu.make_async_copy(hold, dst, out_sem.at[n]),
        ))
        moves[n][0].start()

    for n, (src, dst) in enumerate(((act_in, act_ref), (grad_in, grad_ref))):
        for t in range(src.shape[0] // TILE):
            rows = pl.ds(t * TILE, TILE)
            move(src.at[rows], hold_ref.at[n, rows], dst.at[rows])
    move(gq_in, holdq_ref, gq_ref)
    move(gi_in, holdi_ref, gi_ref)
    move(go_in, holdo_ref, go_ref)
    for n in range(4):
        move(gf_in.at[n], holdf_ref.at[n], gf_ref.at[pl.ds(16 * n, 16)])
    me = lax.axis_index("dp") * 4 + lax.axis_index("fsdp")
    row = lax.broadcasted_iota(jnp.int32, (LANES, LANES), 0)
    lane = lane_ids(LANES)

    def cut(value, start):
        pick = jnp.where(row == lane + start, 1.0, 0.0)
        return lax.dot_general(
            value, pick, (((1,), (0,)), ((), ())), precision=lax.Precision.HIGHEST,
            preferred_element_type=F32,
        )

    def only(value, base, count, which):
        part = value[base : base + count]
        at = lax.broadcasted_iota(jnp.int32, part.shape, 0)
        return jnp.sum(jnp.where(at == which, part, 0.0), axis=0, keepdims=True)

    for come, go in moves:
        come.wait()
        go.start()
    pairs = first_in.shape[0] // 2
    spot = lax.rem(me, 8) * 16
    first, rest = cut(first_in[...], spot), cut(rest_in[...], spot)
    which = lax.div(me, 8)
    for n, ref in enumerate((g1_ref, s1_ref)):
        ref[...] = only(first, n * pairs, pairs, which)[:, :16]
    for n, ref in enumerate((g2_ref, s2_ref, bo_ref)):
        ref[...] = only(rest, n * pairs, pairs, which)[:, :16]
    wide = cut(rest_in[...], lax.rem(me, 2) * 64)
    each = pairs * pairs
    bi_ref[...] = only(wide, 3 * pairs, each, lax.div(me, 2))[:, :64]
    for _, go in moves:
        go.wait()


ANY = pl.BlockSpec(memory_space=pl.ANY)
VM = pl.BlockSpec(memory_space=pltpu.VMEM)


def call(kernel, outs, scratch, name, ins=None, out_specs=None, collective=None):
    extra = {} if ins is None else {"in_specs": ins, "out_specs": out_specs}
    params = {} if collective is None else {"collective_id": collective, "has_side_effects": True}
    return pl.pallas_call(
        kernel,
        out_shape=[jax.ShapeDtypeStruct(s, d) for s, d in outs],
        scratch_shapes=[pltpu.SemaphoreType.DMA(s) if d is None else pltpu.VMEM(s, d) for s, d in scratch],
        compiler_params=pltpu.CompilerParams(vmem_limit_bytes=60 * 2**20, **params),
        name=name,
        **extra,
    )


def padded_features(fm):
    heads, feats, _ = fm.shape
    zero = jnp.zeros_like(fm)
    even = (jnp.arange(heads) % 2 == 0)[:, None, None]
    return jnp.concatenate(
        [jnp.where(even, fm, zero), jnp.where(even, zero, fm), jnp.ones((heads, feats, LANES), BF)],
        axis=-1,
    )


def by_pair(columns, outer):
    rows, count = columns.shape
    split = columns.reshape(rows, outer, count // (outer * LANES), LANES)
    return split.swapaxes(1, 2).reshape(rows, count)


def middle(tokens, attr, cotangent, wo, wi, wf, prm, seq_weight):
    length, width = tokens.shape
    hidden = wi.shape[1]
    big, deep = (length, width), (length, hidden)
    chunks = 5 + hidden // width
    return call(
        middle_kernel,
        [(big, BF), (big, F32), (big, F32), ((16, width), F32), ((chunks, width // 64, 4, 16, width), BF)],
        [(deep, BF), (deep, BF), (big, BF), (big, BF), (big, BF), ((8, hidden), F32)],
        "middle",
    )(tokens, attr, cotangent, wo, wi, wf, prm, seq_weight)


def forward_outs(length, width, heads, feats):
    big = (length, width)
    deep = (length, heads * feats)
    low = (heads, length // BLOCK - 1, feats, 2 * LANES)
    return [(big, BF)] * 4 + [(deep, BF)] * 2 + [(big, BF), (big, F32), (low, BF)]


def backward_scratch(length, width):
    return [
        ((width, length), BF), ((length, 3 * width), BF),
        ((2, length, 2 * LANES), BF), ((2, length, 2 * LANES), BF), ((BLOCK, BLOCK), BF),
    ]


def plain_body(
    tokens, cotangent, group_id, w_qkv, w_out, w_ffn_in, w_ffn_out,
    gain_one, shift_one, gain_two, shift_two, bias_in, bias_out, feature_matrix,
):
    gather = functools.partial(lax.all_gather, axis_name=AXES, axis=0, tiled=True)
    scatter = functools.partial(
        lax.psum_scatter, axis_name=AXES, scatter_dimension=0, tiled=True
    )
    length, width = tokens.shape
    heads, feats, head_size = feature_matrix.shape
    hidden = w_ffn_in.shape[1]
    factor = head_size ** (-0.25)
    wq, wo, wi, wf = gather(w_qkv), gather(w_out), gather(w_ffn_in), gather(w_ffn_out)
    prm = gather(jnp.stack([gain_one, shift_one, gain_two, shift_two, bias_out], axis=1))
    prm = jnp.pad(prm.T.astype(F32), ((0, 3), (0, 0)))
    wf = jnp.concatenate([wf, jnp.pad(gather(bias_in)[:, None], ((0, 0), (0, LANES - 1)))], axis=1)

    slice_seqs = lax.axis_size("dp") * group_id.shape[0]
    labels = jnp.arange(slice_seqs // 2, dtype=jnp.int32)
    onehot = (group_id[:, None] == labels[None, :]).astype(F32)
    counts = lax.psum(jnp.sum(onehot, axis=0), "dp")
    group_size = jnp.sum(onehot * counts[None, :], axis=-1)
    groups = jnp.sum((counts > 0.5).astype(F32))
    seq_weight = jnp.broadcast_to((slice_seqs / (groups * group_size))[:, None], (8, LANES))

    fx = padded_features(feature_matrix)
    h1, q, k, v, pq, pk, attr, den, low = call(
        functools.partial(forward_kernel, factor),
        forward_outs(length, width, heads, feats), [], "forward",
    )(tokens, wq, prm, fx)
    act, dy, datt, gprm, grads = middle(tokens, attr, cotangent, wo, wi, wf, prm, seq_weight)
    input_grad, gq, gprm = call(
        functools.partial(backward_kernel, factor),
        [((length, width), BF), ((width, 3 * width), BF), ((16, width), F32)],
        backward_scratch(length, width), "backward",
    )(tokens, h1, q, k, v, pq, pk, attr, den, datt, dy, wq, fx, prm, gprm, low)
    gq = by_pair(gq, width // LANES)
    grads = grads.reshape(-1, width // 16, 16, width)
    gf = grads[:4].transpose(1, 0, 2, 3).reshape(hidden, width)
    gi = grads[4:-1].transpose(1, 2, 0, 3).reshape(width, hidden)
    go = grads[-1].reshape(width, width)
    small = scatter(gprm[:8].T)
    gbin = scatter(gprm[5 : 5 + hidden // width].reshape(hidden))
    part = [scatter(t).astype(F32) for t in (gq, go, gi, gf)]
    return (act, input_grad, *part, *(small[:, i] for i in range(4)), gbin, small[:, 4])


def ring_body(
    tokens, cotangent, group_id, w_qkv, w_out, w_ffn_in, w_ffn_out,
    gain_one, shift_one, gain_two, shift_two, bias_in, bias_out, feature_matrix,
):
    length, width = tokens.shape
    heads, feats, head_size = feature_matrix.shape
    hidden = w_ffn_in.shape[1]
    factor = head_size ** (-0.25)
    nz = lax.axis_size("dp") // 2
    grid = (nz, 2, 2, 2)
    wide = 3 * width
    pairs = width // LANES
    parts = hidden // width
    chunks, many = 5 + parts, 3 + pairs + 2 * parts
    wqs = (pairs, *grid, 16, 3 * LANES)
    big, deep, tall = (length, width), (length, heads * feats), (length, hidden)
    half = (-(-(3 + parts) * pairs // 8) * 8, LANES)
    pair_rows = (2 * pairs, LANES)
    near, far = 3, 2 * nz - 1
    act, input_grad, gq, gf, gi, go, rest, first = call(
        functools.partial(layer_kernel, nz, factor),
        [
            (big, BF), (big, BF), ((16, wide), F32), ((4, 16, width), F32), ((16, hidden), F32),
            ((16, width), F32), (half, F32), (pair_rows, F32),
        ],
        [
            *[(big, BF)] * 4, *[(deep, BF)] * 2, (big, BF), (big, F32),
            ((heads, length // BLOCK - 1, feats, 2 * LANES), BF),
            ((pairs, 16, 3 * LANES), BF), (wqs, BF), ((*grid, 16, width), BF),
            ((*grid, 16, hidden), BF), ((*grid, 64, width), BF), ((*grid, 16, LANES), BF), (big, BF),
            ((heads, feats, 2 * LANES), BF), ((16, LANES), F32), ((LANES, LANES), BF),
            ((8, width), F32),
            (big, BF), (big, F32), (big, F32), ((chunks, *grid, 16, width), BF), ((16, width), F32),
            (tall, BF), (tall, BF), (big, BF), (big, BF), (big, BF),
            ((8, width), F32), ((8, LANES), F32), ((4, 8, LANES), F32),
            ((pairs, *grid, 16, 3 * LANES), BF),
            *Reduce.shapes(chunks, nz, 16, width),
            *Reduce.shapes(pairs, nz, 16, 3 * LANES),
            (half, F32), (half, F32), ((near, *half), F32), ((far, *half), F32),
            (pair_rows, F32), (pair_rows, F32), ((near, *pair_rows), F32), ((far, *pair_rows), F32),
            ((4 * nz - 1, 16, 3 * LANES), BF),
            ((many, 4, nz - 1), None), ((many, 4, nz - 1), None), ((many,), None),
            ((chunks, 4, nz - 1), None), ((chunks, 4, nz - 1), None),
            ((pairs, 4, nz - 1), None), ((pairs, 4, nz - 1), None),
            ((2, far), None), ((2, far), None), ((2, far), None), ((2, far), None),
            ((4 * nz - 1,), None), ((4 * nz - 1,), None),
            ((), None), ((2, length // FFN_TILE), None),
        ],
        "layer",
        [VM, ANY, VM, ANY, ANY, ANY, VM, pl.BlockSpec(memory_space=pltpu.SMEM), *[VM] * 6],
        [ANY, ANY, *[VM] * 6],
        0,
    )(
        tokens, cotangent, w_qkv, w_out, w_ffn_in, w_ffn_out, feature_matrix.swapaxes(1, 2),
        group_id, *(t[None] for t in (gain_one, shift_one, gain_two, shift_two, bias_out, bias_in)),
    )
    act, input_grad, gq, go, gi, gf, *vecs = call(
        finish_kernel,
        [
            (big, BF), (big, BF), ((16, wide), F32), ((16, width), F32), ((16, hidden), F32),
            ((64, width), F32), *[((1, 16), F32)] * 4, ((1, 64), F32), ((1, 16), F32),
        ],
        [
            ((2, length, width), BF), ((16, wide), F32), ((4, 16, width), F32), ((16, hidden), F32),
            ((16, width), F32), ((2 * length // TILE + 7,), None), ((2 * length // TILE + 7,), None),
        ],
        "finish",
        [*[ANY] * 6, VM, VM],
        [*[ANY] * 6, *[VM] * 6],
    )(act, input_grad, gq, gf, gi, go, rest, first)
    return (act, input_grad, gq, go, gi, gf, *(t[0] for t in vecs))


def solution(mesh):
    rows, vec = P(AXES, None), P(AXES)
    devices = mesh.shape["dp"] * mesh.shape["fsdp"]

    def body(*args):
        width = args[0].shape[1]
        ring = mesh.shape["fsdp"] == 4 and mesh.shape["dp"] % 2 == 0 and width == 16 * devices
        return (ring_body if ring else plain_body)(*args)

    return jax.shard_map(
        body,
        mesh=mesh,
        in_specs=(rows, rows, vec, *[rows] * 4, *[vec] * 6, P()),
        out_specs=(*[rows] * 6, *[vec] * 6),
        check_vma=False,
    )
```
